128 devices in a mesh: shot: 16 (over y, x_lo, core), brick: 8 (over z, x_hi).
Axes of the slice: x: 4 (x_hi: 2, x_lo: 2; x = x_hi * 2 + x_lo), y: 4, z: 4, core: 2. Of those that a mesh axis runs over, the one named last changes fastest.
Arguments:
- latent: bfloat16 [16, 256, 32, 128], P(None, 'brick', 'shot'), may hold values from -6 to 6
- conv_in: bfloat16 [27, 16, 16], replicated, may hold values from -0.3125 to 0.3125
- conv_out: bfloat16 [27, 2, 16], replicated, may hold values from -0.3125 to 0.3125
- source_field: float32 [16, 256, 16, 128], P('shot', 'brick'), may hold values from -6 to 6
- observed: float32 [16, 3, 2048], P('shot'), may hold values from -6 to 6
- aperture: int32 [16], P('shot'), may hold values from 0 to 16, as said below
- receivers: int32 [16, 3, 2048], P('shot'), may hold values from 0 to 255, as said below
Outputs:
- grad_latent: float32 [16, 256, 32, 128], P(None, 'brick', 'shot')
- grad_first: float32 [27, 16, 16], replicated
- grad_second: float32 [27, 2, 16], replicated
The draws below stay inside these ranges and needn't reach their ends.
Inputs may be any that keep to these rules, and one draw needn't show every extreme that they name: Every shot's aperture lies inside the grid; some shot starts at 0 and some at 16. `receivers`: each receiver's first index is below 256, its third below 128, and its second lies inside its shot's aperture.
All inputs are finite; a program needn't handle non-finite values.
Results may differ from the reference program's by a relative error of at most 0.0023.
The reference program's roundings to bfloat16 on the way (of `hidden`, `grad_output` and `grad_inner`) count: a program that leaves them out, or rounds other values in their place, can miss the bound.
Values may be sent and summed in bfloat16 or wider, within the bound.
No kernel may reach another device: no remote copies, remote signals or barrier semaphores. Data moves between devices by JAX's collectives and lax.ppermute only.
A program may use at most 128 MiB of HBM per device.

```python
import jax
import jax.numpy as jnp
from jax import lax

CH = 16
NZ = 128
STEPS = 3
RECV = 2048
SHOTS = 16
NX = 256
NY = 32
AY = 16


def aperture_offsets(key):
    base = jax.random.fold_in(key, 17)
    first_key = jax.random.fold_in(base, 1)
    second_key = jax.random.fold_in(base, 2)
    spread = NY - AY
    drawn = jax.random.randint(first_key, (SHOTS,), 0, spread + 1, dtype=jnp.int32)
    fixed_ends = jnp.array([0, spread], dtype=jnp.int32)
    joined = jnp.concatenate([fixed_ends, drawn[2:]])
    order = jax.random.permutation(second_key, SHOTS)
    return joined[order]


def draw_aperture(key, part):
    return aperture_offsets(key)


def draw_receivers(key, part):
    offsets = aperture_offsets(key)
    base = jax.random.fold_in(key, 29)
    first_cells = jax.random.randint(jax.random.fold_in(base, 1), (SHOTS, RECV), 0, NX, dtype=jnp.int32)
    second_cells = offsets[:, None] + jax.random.randint(jax.random.fold_in(base, 2), (SHOTS, RECV), 0, AY, dtype=jnp.int32)
    third_cells = jax.random.randint(jax.random.fold_in(base, 3), (SHOTS, RECV), 0, NZ, dtype=jnp.int32)
    return jnp.stack([first_cells, second_cells, third_cells], axis=1)


def levels(rng, shape, shards, smallest, high):
    level, own = 1.0, jax.random.fold_in(rng, 6)
    for position, parts in shards:
        steps = jnp.exp(jax.random.uniform(jax.random.fold_in(own, position), (parts,), jnp.float32, smallest / len(shards), high / len(shards)))
        level = level * jnp.repeat(steps, shape[position] // parts).reshape([-1 if axis == position else 1 for axis in range(len(shape))])
    return level


def noise(rng, shape, width, bound, pieces=(), kind=jnp.bfloat16):
    factor_of = levels(rng, shape, pieces, -0.22, 0.18) if pieces else 1.0
    entries = jax.random.normal(rng, shape, jnp.float32) * width * factor_of
    return jnp.minimum(jnp.maximum(entries, -bound), bound).astype(kind)


def setup_inputs(seed: int = 0) -> dict:
    splits = jax.random.split(jax.random.key(seed), 8)
    return {
        "latent": noise(splits[0], (CH, NX, NY, NZ), 1.0, 6.0, ((1, 8), (2, 16))),
        "conv_in": noise(splits[1], (27, CH, CH), (27 * CH) ** -0.5, 0.3125),
        "conv_out": noise(splits[2], (27, 2, CH), (27 * CH) ** -0.5, 0.3125),
        "source_field": noise(splits[3], (SHOTS, NX, AY, NZ), 1.0, 6.0, ((0, 16), (1, 8)), jnp.float32),
        "observed": noise(splits[4], (SHOTS, STEPS, RECV), 1.0, 6.0, ((0, 16),), jnp.float32),
        "aperture": draw_aperture(jax.random.fold_in(splits[7], 71), 0),
        "receivers": draw_receivers(jax.random.fold_in(splits[7], 71), 0),
    }


stencil_taps = (1225.0 / 1024.0, -245.0 / 3072.0, 49.0 / 5120.0, -5.0 / 7168.0)
misfit_weight = 16.0
wave_rim = 8

def take_slab(array, first_index, length, which_axis):
    return lax.slice_in_dim(array, first_index, first_index + length, axis=which_axis)

def inner_part(array, which_axis):
    for other_axis in range(3):
        if other_axis != which_axis:
            array = take_slab(array, wave_rim, array.shape[other_axis] - 2 * wave_rim, other_axis)
    return array

def face_slope(array, which_axis):
    length = array.shape[which_axis] - 2 * wave_rim
    summed = jnp.zeros_like(take_slab(array, 0, length + 8, which_axis))
    for tap_index in range(1, 5):
        upper = take_slab(array, 3 + tap_index, length + 8, which_axis)
        lower = take_slab(array, 4 - tap_index, length + 8, which_axis)
        summed = summed + stencil_taps[tap_index - 1] * (upper - lower)
    return summed

def operate(wavefield_pad, buoyancy_pad):
    summed = 0.0
    for which_axis in range(3):
        field_part = inner_part(wavefield_pad, which_axis)
        weight_part = inner_part(buoyancy_pad, which_axis)
        length = field_part.shape[which_axis] - 2 * wave_rim
        face_weight = 0.5 * (take_slab(weight_part, 3, length + 8, which_axis) + take_slab(weight_part, 4, length + 8, which_axis))
        face_flux = face_weight * face_slope(field_part, which_axis)
        for tap_index in range(1, 5):
            upper = take_slab(face_flux, 4 + tap_index, length, which_axis)
            lower = take_slab(face_flux, 5 - tap_index, length, which_axis)
            summed = summed + stencil_taps[tap_index - 1] * (upper - lower)
    return summed

def buoyancy_slope(scaled_pad, wavefield_pad):
    summed = 0.0
    for which_axis in range(3):
        scaled_part = inner_part(scaled_pad, which_axis)
        length = scaled_part.shape[which_axis] - 2 * wave_rim
        face_product = -face_slope(scaled_part, which_axis) * face_slope(inner_part(wavefield_pad, which_axis), which_axis)
        summed = summed + 0.5 * (take_slab(face_product, 4, length, which_axis) + take_slab(face_product, 5, length, which_axis))
    return summed

def pad_rim(array):
    return jnp.pad(array, wave_rim)

def inject(values, cell_x, cell_y, cell_z, shape):
    return jnp.zeros(shape, jnp.float32).at[cell_x, cell_y, cell_z].add(values)

def shot_gradient(modulus, buoyancy, source, cell_x, cell_y, cell_z, observed):
    modulus_pad = pad_rim(modulus)
    buoyancy_pad = pad_rim(buoyancy)
    earlier = jnp.zeros_like(source)
    current = source
    fields = []
    images = []
    residuals = []
    for section_index in range(observed.shape[0]):
        wavefield_pad = pad_rim(current)
        operated = operate(wavefield_pad, buoyancy_pad)
        following = 2.0 * current - earlier + modulus * operated
        fields.append(wavefield_pad)
        images.append(operated)
        residuals.append(misfit_weight * (following[cell_x, cell_y, cell_z] - observed[section_index]))
        earlier = current
        current = following
    sections = len(residuals)
    adjoint = inject(residuals[sections - 1], cell_x, cell_y, cell_z, source.shape)
    adjoint_later = jnp.zeros_like(source)
    grad_modulus = jnp.zeros_like(source)
    grad_buoyancy = jnp.zeros_like(source)
    for section_index in reversed(range(sections)):
        scaled_pad = modulus_pad * pad_rim(adjoint)
        grad_modulus = grad_modulus + adjoint * images[section_index]
        grad_buoyancy = grad_buoyancy + buoyancy_slope(scaled_pad, fields[section_index])
        if section_index > 0:
            earlier_adjoint = inject(residuals[section_index - 1], cell_x, cell_y, cell_z, source.shape) + 2.0 * adjoint + operate(scaled_pad, buoyancy_pad) - adjoint_later
            adjoint_later = adjoint
            adjoint = earlier_adjoint
    return (grad_modulus, grad_buoyancy)

def kernel_shifts():
    listed = []
    for shift_x in range(3):
        for shift_y in range(3):
            for shift_z in range(3):
                listed.append((9 * shift_x + 3 * shift_y + shift_z, shift_x, shift_y, shift_z))
    return listed

def pad_one(array):
    return jnp.pad(array, ((0, 0), (1, 1), (1, 1), (1, 1)))

def conv_forward(padded, weights):
    extent = [padded.shape[dim_index] - 2 for dim_index in range(1, 4)]
    widened = padded.astype(jnp.float32)
    kernel = weights.astype(jnp.float32)
    summed = 0.0
    for kernel_index, shift_x, shift_y, shift_z in kernel_shifts():
        window = widened[:, shift_x:shift_x + extent[0], shift_y:shift_y + extent[1], shift_z:shift_z + extent[2]]
        summed = summed + jnp.einsum('oc,cxyz->oxyz', kernel[kernel_index], window, precision=lax.Precision.HIGHEST)
    return summed

def conv_back(grad_pad, weights):
    extent = [grad_pad.shape[dim_index] - 2 for dim_index in range(1, 4)]
    widened = grad_pad.astype(jnp.float32)
    kernel = weights.astype(jnp.float32)
    summed = 0.0
    for kernel_index, shift_x, shift_y, shift_z in kernel_shifts():
        window = widened[:, 2 - shift_x:2 - shift_x + extent[0], 2 - shift_y:2 - shift_y + extent[1], 2 - shift_z:2 - shift_z + extent[2]]
        summed = summed + jnp.einsum('oc,oxyz->cxyz', kernel[kernel_index], window, precision=lax.Precision.HIGHEST)
    return summed

def weight_grad(grads, padded):
    extent = grads.shape[1:]
    widened = padded.astype(jnp.float32)
    grads_wide = grads.astype(jnp.float32)
    listed = []
    for kernel_index, shift_x, shift_y, shift_z in kernel_shifts():
        window = widened[:, shift_x:shift_x + extent[0], shift_y:shift_y + extent[1], shift_z:shift_z + extent[2]]
        listed.append(jnp.einsum('oxyz,cxyz->oc', grads_wide, window, precision=lax.Precision.HIGHEST))
    return jnp.stack(listed)

def reference(latent, conv_in, conv_out, source_field, observed, aperture, receivers):
    latent_pad = pad_one(latent)
    hidden = jnp.tanh(conv_forward(latent_pad, conv_in)).astype(jnp.bfloat16)
    hidden = lax.optimization_barrier(hidden)
    hidden_pad = pad_one(hidden)
    output = conv_forward(hidden_pad, conv_out)
    squashed = jax.nn.sigmoid(output[0])
    modulus = 0.03 + 0.09 * squashed
    bent_part = jnp.tanh(output[1])
    buoyancy = jnp.exp(0.35 * bent_part)

    def one_shot(running, shot_index):
        first_row = aperture[shot_index]
        modulus_window = lax.dynamic_slice_in_dim(modulus, first_row, AY, 1)
        buoyancy_window = lax.dynamic_slice_in_dim(buoyancy, first_row, AY, 1)
        receiver_cells = receivers[shot_index]
        grad_modulus, grad_buoyancy = shot_gradient(modulus_window, buoyancy_window, source_field[shot_index], receiver_cells[0], receiver_cells[1] - first_row, receiver_cells[2], observed[shot_index])
        current_rows = lax.dynamic_slice_in_dim(running, first_row, AY, 2)
        running = lax.dynamic_update_slice_in_dim(running, current_rows + jnp.stack([grad_modulus, grad_buoyancy]), first_row, 2)
        return (running, None)
    coefficient_grad, unused = lax.scan(one_shot, jnp.zeros((2, NX, NY, NZ), jnp.float32), jnp.arange(SHOTS, dtype=jnp.int32))
    grad_output = jnp.stack([coefficient_grad[0] * 0.09 * squashed * (1.0 - squashed), coefficient_grad[1] * buoyancy * 0.35 * (1.0 - bent_part * bent_part)]).astype(jnp.bfloat16)
    grad_output = lax.optimization_barrier(grad_output)
    grad_hidden = conv_back(pad_one(grad_output), conv_out)
    hidden_wide = hidden.astype(jnp.float32)
    grad_inner = (grad_hidden * (1.0 - hidden_wide * hidden_wide)).astype(jnp.bfloat16)
    grad_inner = lax.optimization_barrier(grad_inner)
    grad_latent = conv_back(pad_one(grad_inner), conv_in)
    grad_first = weight_grad(grad_inner, latent_pad)
    grad_second = weight_grad(grad_output, hidden_pad)
    return (grad_latent, grad_first, grad_second)
```

```python
import functools

import jax
import jax.numpy as jnp
from jax import lax
from jax.experimental import pallas as pl
from jax.experimental.pallas import tpu as pltpu
from jax.sharding import PartitionSpec as P

F32 = jnp.float32
BF16 = jnp.bfloat16
stencil_taps = (1225.0 / 1024.0, -245.0 / 3072.0, 49.0 / 5120.0, -5.0 / 7168.0)
ratios = tuple(tap / stencil_taps[0] for tap in stencil_taps)
tap_square = stencil_taps[0] ** 2
misfit_weight = 16.0

bricks, shots = 8, 16
bx = 32
ay = 16
nz = 128
rim = 24
dom = bx + 2 * rim
lead = 8
xpad = dom + 24
ypad = ay + 8
gx = bx + 4
vmem = pltpu.CompilerParams(vmem_limit_bytes=40 * 1024 * 1024)


def whole(count):
    return [pl.BlockSpec(memory_space=pltpu.VMEM)] * count


scalars = pl.BlockSpec(memory_space=pltpu.SMEM)


def lane_index():
    return lax.broadcasted_iota(jnp.int32, (1, nz), 1)


def lane_shift(value, offset):
    if offset == 1:
        return value
    lane = lax.broadcasted_iota(jnp.int32, value.shape, 1)
    if offset == 0:
        return jnp.where(lane == 0, 0.0, pltpu.roll(value, 1, 1))
    return jnp.where(lane == nz - 1, 0.0, pltpu.roll(value, nz - 1, 1))


def generator_kernel(
    at_ref, lo_ref, mid_ref, hi_ref, w1_ref, w2_ref, coef_ref, out_ref, hid_ref, s1, s2
):
    shot, brick = at_ref[0], at_ref[1]
    y_fine = (shot > 0, True, shot < shots - 1)

    def spread(x, carry):
        x_fine = ((x >= 4) | (brick > 0)) & ((x < bx + 4) | (brick < bricks - 1))
        for part, ref in enumerate((lo_ref, mid_ref, hi_ref)):
            fine = x_fine & y_fine[part]
            for row in range(2):
                value = jnp.where(fine, ref[row, x].astype(F32), 0.0)
                for k in range(3):
                    s1[x, pl.ds((2 * part + row) * 48 + k * 16, 16), :] = lane_shift(
                        value, k
                    ).astype(BF16)
        return carry

    lax.fori_loop(0, bx + 8, spread, 0)

    def first_conv(block, carry):
        rows = s1[pl.ds(2 * block, 4)].reshape(4 * 288, nz)
        acc = jnp.tanh(jnp.dot(w1_ref[...], rows, preferred_element_type=F32))
        for xo in range(2):
            x = 2 * block + xo
            x_fine = ((x >= 3) | (brick > 0)) & ((x < bx + 3) | (brick < bricks - 1))
            for y in range(4):
                fine = x_fine
                if y == 0:
                    fine = fine & (shot > 0)
                if y == 3:
                    fine = fine & (shot < shots - 1)
                start = (xo * 4 + y) * 16
                value = jnp.where(fine, acc[start : start + 16], 0.0).astype(BF16)
                hid_ref[x, pl.ds(y * 16, 16), :] = value
                wide = value.astype(F32)
                for k in range(3):
                    s2[x, pl.ds(y * 48 + k * 16, 16), :] = lane_shift(wide, k).astype(BF16)
        return carry

    lax.fori_loop(0, (bx + 6) // 2, first_conv, 0)

    for block in range(gx // 6):
        rows = s2[pl.ds(6 * block, 8)].reshape(8 * 192, nz)
        acc = jnp.dot(w2_ref[...], rows, preferred_element_type=F32)
        for channel in range(2):
            for y in range(2):
                start = (channel * 2 + y) * 6
                out_ref[channel, y, pl.ds(6 * block, 6), :] = acc[start : start + 6]
    for y in range(2):
        modulus = 0.03 + 0.09 * jax.nn.sigmoid(out_ref[0, y, pl.ds(2, bx), :])
        buoyancy = jnp.exp(0.35 * jnp.tanh(out_ref[1, y, pl.ds(2, bx), :]))
        coef_ref[y, 0] = modulus
        coef_ref[y, 1] = buoyancy


def generator(at, lo, mid, hi, w1, w2):
    return pl.pallas_call(
        generator_kernel,
        out_shape=(
            jax.ShapeDtypeStruct((2, 2, bx, nz), F32),
            jax.ShapeDtypeStruct((2, 2, gx, nz), F32),
            jax.ShapeDtypeStruct((bx + 6, 64, nz), BF16),
        ),
        in_specs=[scalars] + whole(5),
        out_specs=tuple(whole(3)),
        scratch_shapes=[
            pltpu.VMEM((bx + 8, 288, nz), BF16),
            pltpu.VMEM((bx + 6, 192, nz), BF16),
        ],
        compiler_params=vmem,
        name="generator",
    )(at, lo, mid, hi, w1, w2)


def receiver_kernel(at_ref, cell_ref, seen_ref, out_ref, hot, spread):
    brick, first_row = at_ref[1], at_ref[2]
    count = cell_ref.shape[1]
    x = cell_ref[0:1] - brick * bx + rim
    row_of = jnp.where((x >= 0) & (x < dom), (cell_ref[1:2] - first_row) * dom + x, -1)
    z = cell_ref[2:3]

    def mark(chunk, carry):
        rows = chunk * 16 + lax.broadcasted_iota(jnp.int32, (16, count), 0)
        hot[pl.ds(chunk * 16, 16), :] = jnp.where(rows == row_of, 1.0, 0.0).astype(BF16)
        return carry

    lax.fori_loop(0, ay * dom // 16, mark, 0)
    parts = [jnp.ones((1, count), F32)]
    for step in range(3):
        value = seen_ref[step : step + 1]
        high = value.astype(BF16).astype(F32)
        parts += [high, value - high]

    def place(chunk, carry):
        same = chunk * 16 + lax.broadcasted_iota(jnp.int32, (16, count), 0) == z
        for index, part in enumerate(parts):
            spread[pl.ds(index * nz + chunk * 16, 16), :] = jnp.where(same, part, 0.0).astype(BF16)
        return carry

    lax.fori_loop(0, nz // 16, place, 0)
    size = 256

    def multiply(chunk, carry):
        left = hot[pl.ds(chunk * size, size), :]
        for field in range(4):
            first = 0 if field == 0 else (2 * field - 1) * nz
            right = spread[pl.ds(first, nz if field == 0 else 2 * nz), :]
            acc = lax.dot_general(
                left, right, (((1,), (1,)), ((), ())), preferred_element_type=F32
            )
            if field:
                acc = acc[:, :nz] + acc[:, nz:]
            out_ref[field, pl.ds(chunk * size, size), :] = acc
        return carry

    lax.fori_loop(0, ay * dom // size, multiply, 0)


def receiver_fields(at, cells, seen):
    count = cells.shape[1]
    return pl.pallas_call(
        receiver_kernel,
        out_shape=jax.ShapeDtypeStruct((4, ay * dom, nz), F32),
        in_specs=[scalars] + whole(2),
        out_specs=whole(1)[0],
        scratch_shapes=[
            pltpu.VMEM((ay * dom, count), BF16),
            pltpu.VMEM((7 * nz, count), BF16),
        ],
        compiler_params=vmem,
        cost_estimate=pl.CostEstimate(
            flops=2 * ay * dom * count * 7 * nz, bytes_accessed=4 * ay * dom * nz * 4, transcendentals=0
        ),
        name="receiver_fields",
    )(at, cells, seen)


def lane_factors():
    lane = lane_index()
    last = lane == nz - 1
    upper = [jnp.where((lane <= nz - 1 - t) | last, ratios[t - 1], 0.0) for t in range(1, 5)]
    lower = [jnp.where(lane >= t - 1, ratios[t - 1], 0.0) for t in range(1, 5)]
    above = [jnp.where(lane <= nz - t, ratios[t - 1], 0.0) for t in range(1, 5)]
    return last, upper, lower, above


def turn(value, shift):
    shift = shift % nz
    return value if shift == 0 else pltpu.roll(value, shift, 1)


def slope_z(value, factors):
    last, upper, lower, _ = factors
    up = sum(upper[t - 1] * turn(value, -t) for t in range(1, 5))
    low = sum(lower[t - 1] * turn(value, t - 1) for t in range(1, 5))
    slope = up - low
    return jnp.where(last, -low, slope), jnp.where(last, up, slope)


def differences(get):
    total = None
    for t in range(1, 5):
        upper, lower = get(t)
        term = upper - lower
        if t > 1:
            term = ratios[t - 1] * term
        total = term if total is None else total + term
    return total


def load_padded(ref, pieces):
    ref[...] = jnp.zeros(ref.shape, F32)

    def body(y, carry):
        for first, rows in pieces:
            value = rows(y)
            ref[y + 4, pl.ds(lead + first, value.shape[0]), :] = value
        return carry

    lax.fori_loop(0, ay, body, 0)


def face_weights(buoy, wx, wy, wz, wzl, factors):
    last = factors[0]
    half = 0.5 * tap_square

    def body(y, carry):
        value = buoy[y + 4, pl.ds(0, dom + 16), :]
        wx[y] = half * (value + buoy[y + 4, pl.ds(1, dom + 16), :])
        inner = buoy[y + 4, pl.ds(lead, dom), :]
        ahead = pltpu.roll(inner, nz - 1, 1)
        wz[y] = half * jnp.where(last, inner, inner + ahead)
        wzl[y] = half * jnp.where(last, ahead, inner + ahead)
        return carry

    lax.fori_loop(0, ay, body, 0)

    def faces(j, carry):
        wy[j] = half * (buoy[j + 3, pl.ds(lead, dom), :] + buoy[j + 4, pl.ds(lead, dom), :])
        return carry

    lax.fori_loop(0, ay + 1, faces, 0)


def slope_y(field, j, first, rows):
    return differences(
        lambda t: (
            field[j + 3 + t, pl.ds(lead + first, rows), :],
            field[j + 4 - t, pl.ds(lead + first, rows), :],
        )
    )


def apply_operator(field, weights, flux_y, flux_x, factors, first, rows, consume):
    wx, wy, wz, wzl = weights
    _, _, lower, above = factors

    def faces(j, carry):
        flux_y[j + 3, pl.ds(0, rows), :] = wy[j, pl.ds(first, rows), :] * slope_y(field, j, first, rows)
        return carry

    lax.fori_loop(0, ay + 1, faces, 0)
    base = lead + first - 4
    more = rows + 8

    def body(y, carry):
        flux_x[pl.ds(0, more), :] = wx[y, pl.ds(base, more), :] * differences(
            lambda t: (
                field[y + 4, pl.ds(base + t, more), :],
                field[y + 4, pl.ds(base + 1 - t, more), :],
            )
        )
        total = differences(
            lambda t: (
                flux_y[y + t + 3, pl.ds(0, rows), :],
                flux_y[y - t + 4, pl.ds(0, rows), :],
            )
        )
        here, before = slope_z(field[y + 4, pl.ds(lead + first, rows), :], factors)
        here = wz[y, pl.ds(first, rows), :] * here
        before = wzl[y, pl.ds(first, rows), :] * before
        total = total + sum(above[t - 1] * turn(here, 1 - t) for t in range(1, 5))
        total = total - sum(lower[t - 1] * turn(before, t) for t in range(1, 5))
        total = total + differences(
            lambda t: (flux_x[pl.ds(3 + t, rows), :], flux_x[pl.ds(4 - t, rows), :])
        )
        consume(y, total)
        return carry

    lax.fori_loop(0, ay, body, 0)


def clear_rims(flux_y):
    for j in (0, 1, 2, 20, 21, 22):
        flux_y[j] = jnp.zeros(flux_y.shape[1:], F32)


def halo_scale(at_ref):
    brick = at_ref[1]
    return (
        jnp.where(brick > 0, 1.0, 0.0).astype(F32),
        jnp.where(brick < bricks - 1, 1.0, 0.0).astype(F32),
    )


def load_window(at_ref, win_ref, clo_ref, chi_ref, modulus, buoy):
    low, high = halo_scale(at_ref)
    load_padded(
        buoy,
        (
            (0, lambda y: low * clo_ref[y, 1]),
            (rim, lambda y: win_ref[y, 1]),
            (rim + bx, lambda y: high * chi_ref[y, 1]),
        ),
    )

    def body(y, carry):
        modulus[y, pl.ds(0, rim), :] = low * clo_ref[y, 0]
        modulus[y, pl.ds(rim, bx), :] = win_ref[y, 0]
        modulus[y, pl.ds(rim + bx, rim), :] = high * chi_ref[y, 0]
        return carry

    lax.fori_loop(0, ay, body, 0)


weight_shapes = [
    pltpu.VMEM((ay, dom + 16, nz), F32),
    pltpu.VMEM((ay + 1, dom, nz), F32),
    pltpu.VMEM((ay, dom, nz), F32),
    pltpu.VMEM((ay, dom, nz), F32),
]
padded = pltpu.VMEM((ypad, xpad, nz), F32)


def forward_kernel(
    at_ref, win_ref, clo_ref, chi_ref, src_ref, plo_ref, phi_ref,
    p1_ref, p2_ref, p3_ref, p4_ref, image_ref, ahead_ref, behind_ref,
    modulus, buoy, f1, f2, f3, wx, wy, wz, wzl, flux_y, flux_x,
):
    factors = lane_factors()
    load_window(at_ref, win_ref, clo_ref, chi_ref, modulus, buoy)
    weights = (wx, wy, wz, wzl)
    face_weights(buoy, *weights, factors)
    clear_rims(flux_y)
    low, high = halo_scale(at_ref)
    load_padded(
        f1,
        (
            (0, lambda y: low * plo_ref[y]),
            (rim, lambda y: src_ref[y]),
            (rim + bx, lambda y: high * phi_ref[y]),
        ),
    )
    f2[...] = jnp.zeros(f2.shape, F32)
    f3[...] = jnp.zeros(f3.shape, F32)

    def first_step(y, image):
        f2[y + 4, pl.ds(lead + 8, 64), :] = (
            2.0 * f1[y + 4, pl.ds(lead + 8, 64), :] + modulus[y, pl.ds(8, 64), :] * image
        )
        image_ref[0, y] = image[8:56]

    def second_step(y, image):
        value = (
            2.0 * f2[y + 4, pl.ds(lead + 16, 48), :]
            - f1[y + 4, pl.ds(lead + 16, 48), :]
            + modulus[y, pl.ds(16, 48), :] * image
        )
        f3[y + 4, pl.ds(lead + 16, 48), :] = value
        image_ref[1, y] = image
        p3_ref[y] = value
        p1_ref[y] = f1[y + 4, pl.ds(lead + 8, 64), :]
        p2_ref[y] = f2[y + 4, pl.ds(lead + 8, 64), :]
        ahead_ref[y, pl.ds(rim, 8), :] = value[24:32]
        behind_ref[y, pl.ds(rim, 8), :] = value[16:24]

    def third_step(y, image):
        image_ref[2, y] = image
        value = (
            2.0 * f3[y + 4, pl.ds(lead + rim, bx), :]
            - f2[y + 4, pl.ds(lead + rim, bx), :]
            + modulus[y, pl.ds(rim, bx), :] * image[8:40]
        )
        p4_ref[y] = value
        ahead_ref[y, pl.ds(0, rim), :] = value[8:32]
        behind_ref[y, pl.ds(0, rim), :] = value[0:24]

    apply_operator(f1, weights, flux_y, flux_x, factors, 8, 64, first_step)
    apply_operator(f2, weights, flux_y, flux_x, factors, 16, 48, second_step)
    apply_operator(f3, weights, flux_y, flux_x, factors, 16, 48, third_step)


def forward_waves(at, window, clo, chi, source, plo, phi):
    shapes = [(ay, 64, nz), (ay, 64, nz), (ay, 48, nz), (ay, bx, nz), (3, ay, 48, nz), (ay, 32, nz), (ay, 32, nz)]
    return pl.pallas_call(
        forward_kernel,
        out_shape=tuple(jax.ShapeDtypeStruct(shape, F32) for shape in shapes),
        in_specs=[scalars] + whole(6),
        out_specs=tuple(whole(7)),
        scratch_shapes=[
            pltpu.VMEM((ay, dom, nz), F32),
            padded, padded, padded, padded,
            *weight_shapes,
            pltpu.VMEM((23, dom, nz), F32),
            pltpu.VMEM((dom + 16, nz), F32),
        ],
        compiler_params=vmem,
        name="forward_waves",
    )(at, window, clo, chi, source, plo, phi)


def adjoint_kernel(
    at_ref, win_ref, clo_ref, chi_ref, p1_ref, p2_ref, p3_ref, p4_ref, image_ref, back_ref, front_ref, seen_ref,
    column_ref,
    modulus, buoy, scaled, wave, later, late, grad_m, grad_b, wx, wy, wz, wzl, flux_y, flux_x, cross_y, cross_x,
):
    factors = lane_factors()
    load_window(at_ref, win_ref, clo_ref, chi_ref, modulus, buoy)
    weights = (wx, wy, wz, wzl)
    face_weights(buoy, *weights, factors)
    clear_rims(flux_y)
    low, high = halo_scale(at_ref)
    scaled[...] = jnp.zeros(scaled.shape, F32)
    wave[...] = jnp.zeros(wave.shape, F32)

    def residual(step, y, first, value):
        rows = value.shape[0]
        start = pl.multiple_of(y * dom + first, 8)
        count = seen_ref[0, pl.ds(start, rows), :]
        total = seen_ref[step, pl.ds(start, rows), :]
        return misfit_weight * (count * value - total)

    def seed(y, carry):
        for first, value in (
            (0, low * back_ref[y, pl.ds(0, rim), :]),
            (rim, p4_ref[y]),
            (rim + bx, high * front_ref[y, pl.ds(0, rim), :]),
        ):
            rows = value.shape[0]
            error = residual(3, y, first, value)
            later[y, pl.ds(first, rows), :] = error
            scaled[y + 4, pl.ds(lead + first, rows), :] = modulus[y, pl.ds(first, rows), :] * error
        return carry

    lax.fori_loop(0, ay, seed, 0)
    grad_m[...] = jnp.zeros(grad_m.shape, F32)
    grad_b[...] = jnp.zeros(grad_b.shape, F32)

    def set_wave(ref, first, offset):
        def body(y, carry):
            rows = ref.shape[1] - 2 * offset
            wave[y + 4, pl.ds(lead + first, rows), :] = ref[y, pl.ds(offset, rows), :]
            return carry

        lax.fori_loop(0, ay, body, 0)

    def gradients(adjoint_of, image):
        def faces(j, carry):
            cross_y[j] = slope_y(scaled, j, 16, 48) * slope_y(wave, j, 16, 48)
            return carry

        lax.fori_loop(0, ay + 1, faces, 0)
        base = lead + 8

        def body(y, carry):
            def slope_x(field):
                return differences(
                    lambda t: (
                        field[y + 4, pl.ds(base + t, 56), :],
                        field[y + 4, pl.ds(base + 1 - t, 56), :],
                    )
                )

            cross_x[...] = slope_x(scaled) * slope_x(wave)
            here_s, before_s = slope_z(scaled[y + 4, pl.ds(lead + 16, 48), :], factors)
            here_w, before_w = slope_z(wave[y + 4, pl.ds(lead + 16, 48), :], factors)
            total = here_s * here_w + pltpu.roll(before_s * before_w, 1, 1)
            total = total + cross_y[y] + cross_y[y + 1]
            total = total + cross_x[pl.ds(7, 48), :] + cross_x[pl.ds(8, 48), :]
            grad_b[y] = grad_b[y] - (0.5 * tap_square) * total
            grad_m[y] = grad_m[y] + adjoint_of(y) * image_ref[image, y]
            return carry

        lax.fori_loop(0, ay, body, 0)

    set_wave(p3_ref, 16, 0)
    gradients(lambda y: later[y, pl.ds(16, 48), :], 2)

    def step_three(y, image):
        value = jnp.concatenate(
            [
                low * back_ref[y, pl.ds(rim, 8), :],
                p3_ref[y],
                high * front_ref[y, pl.ds(rim, 8), :],
            ],
            axis=0,
        )
        late[y] = residual(2, y, 8, value) + 2.0 * later[y, pl.ds(8, 64), :] + image

    apply_operator(scaled, weights, flux_y, flux_x, factors, 8, 64, step_three)

    def rescale(y, carry):
        scaled[y + 4, pl.ds(lead + 8, 64), :] = modulus[y, pl.ds(8, 64), :] * late[y]
        return carry

    lax.fori_loop(0, ay, rescale, 0)
    set_wave(p2_ref, 8, 0)
    gradients(lambda y: late[y, pl.ds(8, 48), :], 1)

    def step_two(y, image):
        value = (
            residual(1, y, 16, p2_ref[y, pl.ds(8, 48), :])
            + 2.0 * late[y, pl.ds(8, 48), :]
            + image
            - later[y, pl.ds(16, 48), :]
        )
        later[y, pl.ds(16, 48), :] = value

    apply_operator(scaled, weights, flux_y, flux_x, factors, 16, 48, step_two)

    def rescale_last(y, carry):
        scaled[y + 4, pl.ds(lead + 16, 48), :] = modulus[y, pl.ds(16, 48), :] * later[y, pl.ds(16, 48), :]
        return carry

    lax.fori_loop(0, ay, rescale_last, 0)
    set_wave(p1_ref, 8, 0)
    gradients(lambda y: later[y, pl.ds(16, 48), :], 0)

    column_ref[...] = jnp.zeros(column_ref.shape, F32)
    first_row = at_ref[2]

    def place(y, carry):
        column_ref[first_row + y, pl.ds(0, gx), :] = grad_m[y, pl.ds(6, gx), :]
        column_ref[first_row + y, pl.ds(gx, gx), :] = grad_b[y, pl.ds(6, gx), :]
        return carry

    lax.fori_loop(0, ay, place, 0)


def adjoint_waves(at, window, clo, chi, fields, back, front, seen):
    return pl.pallas_call(
        adjoint_kernel,
        out_shape=jax.ShapeDtypeStruct((2 * shots, 2 * gx, nz), F32),
        in_specs=[scalars] + whole(11),
        out_specs=whole(1)[0],
        scratch_shapes=[
            pltpu.VMEM((ay, dom, nz), F32),
            padded, padded, padded,
            pltpu.VMEM((ay, dom, nz), F32),
            pltpu.VMEM((ay, 64, nz), F32),
            pltpu.VMEM((ay, 48, nz), F32),
            pltpu.VMEM((ay, 48, nz), F32),
            *weight_shapes,
            pltpu.VMEM((23, dom, nz), F32),
            pltpu.VMEM((dom + 16, nz), F32),
            pltpu.VMEM((ay + 1, 48, nz), F32),
            pltpu.VMEM((56, nz), F32),
        ],
        compiler_params=vmem,
        name="adjoint_waves",
    )(at, window, clo, chi, *fields, back, front, seen)


def chain_kernel(at_ref, got_ref, out_ref, grad_ref):
    brick = at_ref[1]
    row = lax.broadcasted_iota(jnp.int32, (gx, nz), 0)
    fine = ((row >= 2) | (brick > 0)) & ((row < gx - 2) | (brick < bricks - 1))
    for y in range(2):
        total = got_ref[0, y]
        for shot in range(1, shots):
            total = total + got_ref[shot, y]
        squashed = jax.nn.sigmoid(out_ref[0, y])
        bent = jnp.tanh(out_ref[1, y])
        buoyancy = jnp.exp(0.35 * bent)
        first = total[:gx] * 0.09 * squashed * (1.0 - squashed)
        second = total[gx:] * buoyancy * 0.35 * (1.0 - bent * bent)
        grad_ref[y, 0] = jnp.where(fine, first, 0.0).astype(BF16)
        grad_ref[y, 1] = jnp.where(fine, second, 0.0).astype(BF16)


def chain(at, got, output):
    return pl.pallas_call(
        chain_kernel,
        out_shape=jax.ShapeDtypeStruct((2, 2, gx, nz), BF16),
        in_specs=[scalars] + whole(2),
        out_specs=whole(1)[0],
        compiler_params=vmem,
        name="chain",
    )(at, got, output)


def backward_kernel(
    at_ref, glo_ref, gmid_ref, ghi_ref, hid_ref, lo_ref, mid_ref, hi_ref, w3_ref, w4_ref,
    latent_ref, kernel_ref,
    grads, own, s1, s2, s3, s4, inner,
):
    shot, brick = at_ref[0], at_ref[1]
    y_fine = (shot > 0, True, shot < shots - 1)
    grads[...] = jnp.zeros(grads.shape, F32)
    own[...] = jnp.zeros(own.shape, F32)
    for part, ref in enumerate((glo_ref, gmid_ref, ghi_ref)):
        for row in range(2):
            for channel in range(2):
                value = jnp.where(y_fine[part], ref[row, channel].astype(F32), 0.0)
                grads[(2 * part + row) * 2 + channel, pl.ds(0, gx), :] = value
                if part == 1:
                    own[:, channel * 2 + row, :] = value[2 : bx + 2]

    def hidden_grad(block, carry):
        for plane in range(12):
            value = grads[plane, pl.ds(8 * block, 16), :]
            for k in range(3):
                s3[pl.ds((plane * 3 + k) * 16, 16), :] = lane_shift(value, k).astype(BF16)
        acc = jnp.dot(w3_ref[...], s3[...], preferred_element_type=F32)
        for xo in range(8):
            x = 8 * block + xo
            x_fine = ((x >= 1) | (brick > 0)) & ((x < bx + 1) | (brick < bricks - 1))
            for y in range(4):
                fine = x_fine
                if y == 0:
                    fine = fine & (shot > 0)
                if y == 3:
                    fine = fine & (shot < shots - 1)
                hidden = hid_ref[jnp.minimum(x + 2, bx + 5), pl.ds(y * 16, 16), :].astype(F32)
                start = (xo * 4 + y) * 16
                value = acc[start : start + 16] * (1.0 - hidden * hidden)
                value = jnp.where(fine, value, 0.0).astype(BF16)
                if y in (1, 2):
                    inner[x, pl.ds((y - 1) * 16, 16), :] = value
                wide = value.astype(F32)
                for k in range(3):
                    s4[x, pl.ds(y * 48 + k * 16, 16), :] = lane_shift(wide, k).astype(BF16)
        return carry

    lax.fori_loop(0, 5, hidden_grad, 0)

    def latent_grad(block, carry):
        rows = s4[pl.ds(4 * block, 6)].reshape(6 * 192, nz)
        acc = jnp.dot(w4_ref[...], rows, preferred_element_type=F32)
        latent_ref[pl.ds(4 * block, 4)] = acc.reshape(4, 32, nz)
        return carry

    lax.fori_loop(0, bx // 4, latent_grad, 0)

    def spread(x, carry):
        x_fine = ((x >= 1) | (brick > 0)) & ((x < bx + 1) | (brick < bricks - 1))
        for y, (ref, row, part) in enumerate(((lo_ref, 1, 0), (mid_ref, 0, 1), (mid_ref, 1, 1), (hi_ref, 0, 2))):
            value = jnp.where(x_fine & y_fine[part], ref[row, x + 3].astype(F32), 0.0)
            hidden = hid_ref[x + 2, pl.ds(y * 16, 16), :].astype(F32)
            for k in range(3):
                s1[x, pl.ds(y * 48 + k * 16, 16), :] = lane_shift(value, k).astype(BF16)
                s2[x, pl.ds(y * 48 + k * 16, 16), :] = lane_shift(hidden, k).astype(BF16)
        return carry

    lax.fori_loop(0, bx + 2, spread, 0)

    def kernel_grad(x, carry):
        first, second = carry
        contract = (((1,), (1,)), ((), ()))
        first = first + lax.dot_general(
            inner[x + 1], s1[pl.ds(x, 3)].reshape(576, nz), contract, preferred_element_type=F32
        )
        second = second + lax.dot_general(
            own[x].astype(BF16), s2[pl.ds(x, 3)].reshape(576, nz), contract, preferred_element_type=F32
        )
        return first, second

    first, second = lax.fori_loop(
        0, bx, kernel_grad, (jnp.zeros((32, 576), F32), jnp.zeros((8, 576), F32))
    )
    kernel_ref[...] = jnp.zeros(kernel_ref.shape, F32)
    for dx in range(3):
        start = dx * 192
        one = first[:16, start : start + 144] + first[16:, start + 48 : start + 192]
        for channel in range(2):
            row = channel * 2
            two = (
                second[row : row + 1, start : start + 144]
                + second[row + 1 : row + 2, start + 48 : start + 192]
            )
            place = dx * 2 * 18 + 16 + channel
            kernel_ref[pl.ds(place, 1), :] = two[:, :128]
            kernel_ref[pl.ds(place + 18, 1), pl.ds(0, 16)] = two[:, 128:]
        kernel_ref[pl.ds(dx * 36, 16), :] = one[:, :128]
        kernel_ref[pl.ds(dx * 36 + 18, 16), pl.ds(0, 16)] = one[:, 128:]


def backward(at, glo, gmid, ghi, hidden, lo, mid, hi, w3, w4):
    return pl.pallas_call(
        backward_kernel,
        out_shape=(
            jax.ShapeDtypeStruct((bx, 32, nz), F32),
            jax.ShapeDtypeStruct((128, nz), F32),
        ),
        in_specs=[scalars] + whole(9),
        out_specs=tuple(whole(2)),
        scratch_shapes=[
            pltpu.VMEM((12, 48, nz), F32),
            pltpu.VMEM((bx, 8, nz), F32),
            pltpu.VMEM((bx + 2, 192, nz), BF16),
            pltpu.VMEM((bx + 2, 192, nz), BF16),
            pltpu.VMEM((576, nz), BF16),
            pltpu.VMEM((40, 192, nz), BF16),
            pltpu.VMEM((40, 32, nz), BF16),
        ],
        compiler_params=vmem,
        name="backward",
    )(at, glo, gmid, ghi, hidden, lo, mid, hi, w3, w4)


def both_ways(ahead, behind, axis):
    count = lax.axis_size(axis)
    forward = [(i, (i + 1) % count) for i in range(count)]
    backward_ = [(target, source) for source, target in forward]
    return lax.ppermute(ahead, axis, forward), lax.ppermute(behind, axis, backward_)


def banded(outputs, inputs):
    step = jnp.arange(inputs)[None, :] - jnp.arange(outputs)[:, None]
    return (step[:, :, None] == jnp.arange(3)[None, None, :]).astype(BF16)


def band_matrix(weights, x_out, y_out, form):
    rows = jnp.einsum("yjb,abkoc->yjakoc", banded(y_out, y_out + 2), weights)
    x_in = 16 if x_out == 8 else x_out + 2
    full = jnp.einsum("xia,yjakoc->" + form, banded(x_out, x_in), rows)
    return full


def per_device(latent, conv_in, conv_out, source_field, observed, aperture, receivers):
    shot = lax.axis_index("shot")
    brick = lax.axis_index("brick")
    at = jnp.stack([shot, brick, aperture[0]]).astype(jnp.int32)
    taps_in = conv_in.reshape(3, 3, 3, 16, 16)
    taps_out = conv_out.reshape(3, 3, 3, 2, 16)
    w1 = band_matrix(taps_in, 2, 4, "xyoijkc").reshape(128, 1152)
    w2 = band_matrix(taps_out, 6, 2, "oyxijkc").reshape(24, 1536)
    w3 = band_matrix(taps_out[::-1, ::-1, ::-1], 8, 4, "xycjoki").reshape(512, 576)
    w4 = band_matrix(taps_in[::-1, ::-1, ::-1], 4, 2, "xycijko").reshape(128, 1152)

    tile = jnp.transpose(latent, (2, 1, 0, 3))
    from_low, from_high = both_ways(tile[:, bx - 4 :], tile[:, :4], "brick")
    mid = jnp.concatenate([from_low, tile, from_high], axis=1)
    lo, hi = both_ways(mid, mid, "shot")
    source = jnp.transpose(source_field[0], (1, 0, 2))
    plo, phi = both_ways(source[:, bx - rim :], source[:, :rim], "brick")
    seen = receiver_fields(at, receivers[0], observed[0])

    coefficients, output, hidden = generator(at, lo, mid, hi, w1, w2)
    sent = jnp.broadcast_to(coefficients[None], (shots, 2, 2, bx, nz))
    column = lax.all_to_all(sent, "shot", 0, 0, tiled=True).reshape(2 * shots, 2, bx, nz)
    window = lax.dynamic_slice_in_dim(column, aperture[0], ay, 0)
    clo, chi = both_ways(window[:, :, bx - rim :], window[:, :, :rim], "brick")
    p1, p2, p3, p4, images, ahead, behind = forward_waves(at, window, clo, chi, source, plo, phi)
    back, front = both_ways(ahead, behind, "brick")
    grads = adjoint_waves(at, window, clo, chi, (p1, p2, p3, p4, images), back, front, seen)
    got = lax.all_to_all(grads, "shot", 0, 0, tiled=True).reshape(shots, 2, 2 * gx, nz)
    grad_output = chain(at, got, output)
    glo, ghi = both_ways(grad_output, grad_output, "shot")
    grad_latent, kernels = backward(at, glo, grad_output, ghi, hidden, lo, mid, hi, w3, w4)
    grad_latent = jnp.transpose(grad_latent.reshape(bx, 2, 16, nz), (2, 0, 1, 3))

    everyone = ("shot", "brick")
    slices = lax.all_to_all(kernels, everyone, 0, 0, tiled=True)
    mine = jnp.sum(slices, axis=0, keepdims=True)
    summed = lax.all_to_all(jnp.broadcast_to(mine, (128, nz)), everyone, 0, 0, tiled=True)
    folded = summed[:108].reshape(3, 2, 18, nz).transpose(0, 2, 1, 3).reshape(3, 18, 256)[:, :, :144]
    folded = folded.reshape(3, 18, 9, 16).transpose(0, 2, 1, 3).reshape(27, 18, 16)
    return (grad_latent, folded[:, :16], folded[:, 16:])


def solution(mesh):
    placed = (
        P(None, "brick", "shot", None),
        P(),
        P(),
        P("shot", "brick", None, None),
        P("shot", None, None),
        P("shot"),
        P("shot", None, None),
    )
    return jax.shard_map(
        per_device,
        mesh=mesh,
        in_specs=placed,
        out_specs=(P(None, "brick", "shot", None), P(), P()),
        check_vma=False,
    )
```

```python
import jax
import jax.numpy as jnp
import numpy as np
from jax import lax
from jax.experimental import pallas as pl
from jax.experimental.pallas import tpu as pltpu
from jax.sharding import PartitionSpec as P

F32 = jnp.float32
BF16 = jnp.bfloat16
stencil_taps = (1225.0 / 1024.0, -245.0 / 3072.0, 49.0 / 5120.0, -5.0 / 7168.0)
ratios = tuple(tap / stencil_taps[0] for tap in stencil_taps)
tap_square = stencil_taps[0] ** 2
misfit_weight = 16.0

bricks, shots = 8, 16
bx = 32
ay = 16
nz = 128
rim = 24
dom = bx + 2 * rim
lead = 8
xpad = dom + 24
ypad = ay + 8
gx = bx + 4
vmem = pltpu.CompilerParams(vmem_limit_bytes=40 * 1024 * 1024)


def cost(microseconds):
    return pl.CostEstimate(flops=0, bytes_accessed=int(microseconds * 3e6), transcendentals=0)


def whole(count):
    return [pl.BlockSpec(memory_space=pltpu.VMEM)] * count


scalars = pl.BlockSpec(memory_space=pltpu.SMEM)


def lane_index():
    return lax.broadcasted_iota(jnp.int32, (1, nz), 1)


def lane_shift(value, offset):
    if offset == 1:
        return value
    lane = lax.broadcasted_iota(jnp.int32, value.shape, 1)
    if offset == 0:
        return jnp.where(lane == 0, 0.0, pltpu.roll(value, 1, 1))
    return jnp.where(lane == nz - 1, 0.0, pltpu.roll(value, nz - 1, 1))


def generator_kernel(
    at_ref, lo_ref, mid_ref, hi_ref, w1_ref, w2_ref, coef_ref, out_ref, hid_ref, s1, s2
):
    shot, brick = at_ref[0], at_ref[1]
    y_fine = (shot > 0, True, shot < shots - 1)

    def spread(x, carry):
        x_fine = ((x >= 4) | (brick > 0)) & ((x < bx + 4) | (brick < bricks - 1))
        for part, ref in enumerate((lo_ref, mid_ref, hi_ref)):
            fine = x_fine & y_fine[part]
            for row in range(2):
                value = jnp.where(fine, ref[row, x].astype(F32), 0.0)
                for k in range(3):
                    s1[x, pl.ds((2 * part + row) * 48 + k * 16, 16), :] = lane_shift(
                        value, k
                    ).astype(BF16)
        return carry

    lax.fori_loop(0, bx + 8, spread, 0)

    def first_conv(block, carry):
        rows = s1[pl.ds(2 * block, 4)].reshape(4 * 288, nz)
        acc = jnp.tanh(jnp.dot(w1_ref[...], rows, preferred_element_type=F32))
        for xo in range(2):
            x = 2 * block + xo
            x_fine = ((x >= 3) | (brick > 0)) & ((x < bx + 3) | (brick < bricks - 1))
            for y in range(4):
                fine = x_fine
                if y == 0:
                    fine = fine & (shot > 0)
                if y == 3:
                    fine = fine & (shot < shots - 1)
                start = (xo * 4 + y) * 16
                value = jnp.where(fine, acc[start : start + 16], 0.0).astype(BF16)
                hid_ref[x, pl.ds(y * 16, 16), :] = value
                wide = value.astype(F32)
                for k in range(3):
                    s2[x, pl.ds(y * 48 + k * 16, 16), :] = lane_shift(wide, k).astype(BF16)
        return carry

    lax.fori_loop(0, (bx + 6) // 2, first_conv, 0)

    for block in range(gx // 6):
        rows = s2[pl.ds(6 * block, 8)].reshape(8 * 192, nz)
        acc = jnp.dot(w2_ref[...], rows, preferred_element_type=F32)
        for channel in range(2):
            for y in range(2):
                start = (channel * 2 + y) * 6
                out_ref[channel, y, pl.ds(6 * block, 6), :] = acc[start : start + 6]
    for y in range(2):
        modulus = 0.03 + 0.09 * jax.nn.sigmoid(out_ref[0, y, pl.ds(2, bx), :])
        buoyancy = jnp.exp(0.35 * jnp.tanh(out_ref[1, y, pl.ds(2, bx), :]))
        coef_ref[y, 0] = modulus
        coef_ref[y, 1] = buoyancy


def generator(at, lo, mid, hi, w1, w2):
    return pl.pallas_call(
        generator_kernel,
        out_shape=(
            jax.ShapeDtypeStruct((2, 2, bx, nz), F32),
            jax.ShapeDtypeStruct((2, 2, gx, nz), F32),
            jax.ShapeDtypeStruct((bx + 6, 64, nz), BF16),
        ),
        in_specs=[scalars] + whole(5),
        out_specs=tuple(whole(3)),
        scratch_shapes=[
            pltpu.VMEM((bx + 8, 288, nz), BF16),
            pltpu.VMEM((bx + 6, 192, nz), BF16),
        ],
        compiler_params=vmem,
        name="generator",
    )(at, lo, mid, hi, w1, w2)


def receiver_kernel(at_ref, cell_ref, seen_ref, out_ref, hot, spread):
    brick, first_row = at_ref[1], at_ref[2]
    count = cell_ref.shape[1]
    x = cell_ref[0:1] - brick * bx + rim
    row_of = jnp.where((x >= 0) & (x < dom), (cell_ref[1:2] - first_row) * dom + x, -1)
    z = cell_ref[2:3]

    def mark(chunk, carry):
        rows = chunk * 16 + lax.broadcasted_iota(jnp.int32, (16, count), 0)
        hot[pl.ds(chunk * 16, 16), :] = jnp.where(rows == row_of, 1.0, 0.0).astype(BF16)
        return carry

    lax.fori_loop(0, ay * dom // 16, mark, 0)
    parts = [jnp.ones((1, count), F32)]
    for step in range(3):
        value = seen_ref[step : step + 1]
        high = value.astype(BF16).astype(F32)
        parts += [high, value - high]

    def place(chunk, carry):
        same = chunk * 16 + lax.broadcasted_iota(jnp.int32, (16, count), 0) == z
        for index, part in enumerate(parts):
            spread[pl.ds(index * nz + chunk * 16, 16), :] = jnp.where(same, part, 0.0).astype(BF16)
        return carry

    lax.fori_loop(0, nz // 16, place, 0)
    size = 256

    def multiply(chunk, carry):
        left = hot[pl.ds(chunk * size, size), :]
        for field in range(4):
            first = 0 if field == 0 else (2 * field - 1) * nz
            right = spread[pl.ds(first, nz if field == 0 else 2 * nz), :]
            acc = lax.dot_general(
                left, right, (((1,), (1,)), ((), ())), preferred_element_type=F32
            )
            if field:
                acc = acc[:, :nz] + acc[:, nz:]
            out_ref[field, pl.ds(chunk * size, size), :] = acc
        return carry

    lax.fori_loop(0, ay * dom // size, multiply, 0)


def receiver_fields(at, cells, seen):
    count = cells.shape[1]
    return pl.pallas_call(
        receiver_kernel,
        out_shape=jax.ShapeDtypeStruct((4, ay * dom, nz), F32),
        in_specs=[scalars] + whole(2),
        out_specs=whole(1)[0],
        scratch_shapes=[
            pltpu.VMEM((ay * dom, count), BF16),
            pltpu.VMEM((7 * nz, count), BF16),
        ],
        compiler_params=vmem,
        cost_estimate=cost(9),
        name="receiver_fields",
    )(at, cells, seen)


def lane_factors():
    lane = lane_index()
    last = lane == nz - 1
    upper = [jnp.where((lane <= nz - 1 - t) | last, ratios[t - 1], 0.0) for t in range(1, 5)]
    lower = [jnp.where(lane >= t - 1, ratios[t - 1], 0.0) for t in range(1, 5)]
    above = [jnp.where(lane <= nz - t, ratios[t - 1], 0.0) for t in range(1, 5)]
    return last, upper, lower, above


def turn(value, shift):
    shift = shift % nz
    return value if shift == 0 else pltpu.roll(value, shift, 1)


def slope_z(value, factors):
    last, upper, lower, _ = factors
    up = sum(upper[t - 1] * turn(value, -t) for t in range(1, 5))
    low = sum(lower[t - 1] * turn(value, t - 1) for t in range(1, 5))
    slope = up - low
    return jnp.where(last, -low, slope), jnp.where(last, up, slope)


def differences(get):
    total = None
    for t in range(1, 5):
        upper, lower = get(t)
        term = upper - lower
        if t > 1:
            term = ratios[t - 1] * term
        total = term if total is None else total + term
    return total


def load_padded(ref, pieces):
    ref[...] = jnp.zeros(ref.shape, F32)

    def body(y, carry):
        for first, rows in pieces:
            value = rows(y)
            ref[y + 4, pl.ds(lead + first, value.shape[0]), :] = value
        return carry

    lax.fori_loop(0, ay, body, 0)


def face_weights(buoy, wx, wy, wz, wzl, factors):
    last = factors[0]
    half = 0.5 * tap_square

    def body(y, carry):
        value = buoy[y + 4, pl.ds(0, dom + 16), :]
        wx[y] = half * (value + buoy[y + 4, pl.ds(1, dom + 16), :])
        inner = buoy[y + 4, pl.ds(lead, dom), :]
        ahead = pltpu.roll(inner, nz - 1, 1)
        wz[y] = half * jnp.where(last, inner, inner + ahead)
        wzl[y] = half * jnp.where(last, ahead, inner + ahead)
        return carry

    lax.fori_loop(0, ay, body, 0)

    def faces(j, carry):
        wy[j] = half * (buoy[j + 3, pl.ds(lead, dom), :] + buoy[j + 4, pl.ds(lead, dom), :])
        return carry

    lax.fori_loop(0, ay + 1, faces, 0)


def slope_y(field, j, first, rows):
    return differences(
        lambda t: (
            field[j + 3 + t, pl.ds(lead + first, rows), :],
            field[j + 4 - t, pl.ds(lead + first, rows), :],
        )
    )


def apply_operator(field, weights, flux_y, flux_x, factors, first, rows, consume):
    wx, wy, wz, wzl = weights
    _, _, lower, above = factors

    def faces(j, carry):
        flux_y[j + 3, pl.ds(0, rows), :] = wy[j, pl.ds(first, rows), :] * slope_y(field, j, first, rows)
        return carry

    lax.fori_loop(0, ay + 1, faces, 0)
    base = lead + first - 4
    more = rows + 8

    def body(y, carry):
        flux_x[pl.ds(0, more), :] = wx[y, pl.ds(base, more), :] * differences(
            lambda t: (
                field[y + 4, pl.ds(base + t, more), :],
                field[y + 4, pl.ds(base + 1 - t, more), :],
            )
        )
        total = differences(
            lambda t: (
                flux_y[y + t + 3, pl.ds(0, rows), :],
                flux_y[y - t + 4, pl.ds(0, rows), :],
            )
        )
        here, before = slope_z(field[y + 4, pl.ds(lead + first, rows), :], factors)
        here = wz[y, pl.ds(first, rows), :] * here
        before = wzl[y, pl.ds(first, rows), :] * before
        total = total + sum(above[t - 1] * turn(here, 1 - t) for t in range(1, 5))
        total = total - sum(lower[t - 1] * turn(before, t) for t in range(1, 5))
        total = total + differences(
            lambda t: (flux_x[pl.ds(3 + t, rows), :], flux_x[pl.ds(4 - t, rows), :])
        )
        consume(y, total)
        return carry

    lax.fori_loop(0, ay, body, 0)


def clear_rims(flux_y):
    for j in (0, 1, 2, 20, 21, 22):
        flux_y[j] = jnp.zeros(flux_y.shape[1:], F32)


def halo_scale(at_ref):
    brick = at_ref[1]
    return (
        jnp.where(brick > 0, 1.0, 0.0).astype(F32),
        jnp.where(brick < bricks - 1, 1.0, 0.0).astype(F32),
    )


def load_window(at_ref, win_ref, clo_ref, chi_ref, modulus, buoy):
    low, high = halo_scale(at_ref)
    load_padded(
        buoy,
        (
            (0, lambda y: low * clo_ref[y, 1]),
            (rim, lambda y: win_ref[y, 1]),
            (rim + bx, lambda y: high * chi_ref[y, 1]),
        ),
    )

    def body(y, carry):
        modulus[y, pl.ds(0, rim), :] = low * clo_ref[y, 0]
        modulus[y, pl.ds(rim, bx), :] = win_ref[y, 0]
        modulus[y, pl.ds(rim + bx, rim), :] = high * chi_ref[y, 0]
        return carry

    lax.fori_loop(0, ay, body, 0)


weight_shapes = [
    pltpu.VMEM((ay, dom + 16, nz), F32),
    pltpu.VMEM((ay + 1, dom, nz), F32),
    pltpu.VMEM((ay, dom, nz), F32),
    pltpu.VMEM((ay, dom, nz), F32),
]
padded = pltpu.VMEM((ypad, xpad, nz), F32)


def forward_kernel(
    at_ref, win_ref, clo_ref, chi_ref, src_ref, plo_ref, phi_ref,
    p1_ref, p2_ref, p3_ref, p4_ref, image_ref, ahead_ref, behind_ref,
    modulus, buoy, f1, f2, f3, wx, wy, wz, wzl, flux_y, flux_x,
):
    factors = lane_factors()
    load_window(at_ref, win_ref, clo_ref, chi_ref, modulus, buoy)
    weights = (wx, wy, wz, wzl)
    face_weights(buoy, *weights, factors)
    clear_rims(flux_y)
    low, high = halo_scale(at_ref)
    load_padded(
        f1,
        (
            (0, lambda y: low * plo_ref[y]),
            (rim, lambda y: src_ref[y]),
            (rim + bx, lambda y: high * phi_ref[y]),
        ),
    )
    f2[...] = jnp.zeros(f2.shape, F32)
    f3[...] = jnp.zeros(f3.shape, F32)

    def first_step(y, image):
        f2[y + 4, pl.ds(lead + 8, 64), :] = (
            2.0 * f1[y + 4, pl.ds(lead + 8, 64), :] + modulus[y, pl.ds(8, 64), :] * image
        )
        image_ref[0, y] = image[8:56]

    def second_step(y, image):
        value = (
            2.0 * f2[y + 4, pl.ds(lead + 16, 48), :]
            - f1[y + 4, pl.ds(lead + 16, 48), :]
            + modulus[y, pl.ds(16, 48), :] * image
        )
        f3[y + 4, pl.ds(lead + 16, 48), :] = value
        image_ref[1, y] = image
        p3_ref[y] = value
        p1_ref[y] = f1[y + 4, pl.ds(lead + 8, 64), :]
        p2_ref[y] = f2[y + 4, pl.ds(lead + 8, 64), :]
        ahead_ref[y, pl.ds(rim, 8), :] = value[24:32]
        behind_ref[y, pl.ds(rim, 8), :] = value[16:24]

    def third_step(y, image):
        image_ref[2, y] = image
        value = (
            2.0 * f3[y + 4, pl.ds(lead + rim, bx), :]
            - f2[y + 4, pl.ds(lead + rim, bx), :]
            + modulus[y, pl.ds(rim, bx), :] * image[8:40]
        )
        p4_ref[y] = value
        ahead_ref[y, pl.ds(0, rim), :] = value[8:32]
        behind_ref[y, pl.ds(0, rim), :] = value[0:24]

    apply_operator(f1, weights, flux_y, flux_x, factors, 8, 64, first_step)
    apply_operator(f2, weights, flux_y, flux_x, factors, 16, 48, second_step)
    apply_operator(f3, weights, flux_y, flux_x, factors, 16, 48, third_step)


def forward_waves(at, window, clo, chi, source, plo, phi):
    shapes = [(ay, 64, nz), (ay, 64, nz), (ay, 48, nz), (ay, bx, nz), (3, ay, 48, nz), (ay, 32, nz), (ay, 32, nz)]
    return pl.pallas_call(
        forward_kernel,
        out_shape=tuple(jax.ShapeDtypeStruct(shape, F32) for shape in shapes),
        in_specs=[scalars] + whole(6),
        out_specs=tuple(whole(7)),
        scratch_shapes=[
            pltpu.VMEM((ay, dom, nz), F32),
            padded, padded, padded, padded,
            *weight_shapes,
            pltpu.VMEM((23, dom, nz), F32),
            pltpu.VMEM((dom + 16, nz), F32),
        ],
        compiler_params=vmem,
        name="forward_waves",
    )(at, window, clo, chi, source, plo, phi)


def adjoint_kernel(
    at_ref, win_ref, clo_ref, chi_ref, p1_ref, p2_ref, p3_ref, p4_ref, image_ref, back_ref, front_ref, seen_ref,
    column_ref,
    modulus, buoy, scaled, wave, later, late, grad_m, grad_b, wx, wy, wz, wzl, flux_y, flux_x, cross_y, cross_x,
):
    factors = lane_factors()
    load_window(at_ref, win_ref, clo_ref, chi_ref, modulus, buoy)
    weights = (wx, wy, wz, wzl)
    face_weights(buoy, *weights, factors)
    clear_rims(flux_y)
    low, high = halo_scale(at_ref)
    scaled[...] = jnp.zeros(scaled.shape, F32)
    wave[...] = jnp.zeros(wave.shape, F32)

    def residual(step, y, first, value):
        rows = value.shape[0]
        start = pl.multiple_of(y * dom + first, 8)
        count = seen_ref[0, pl.ds(start, rows), :]
        total = seen_ref[step, pl.ds(start, rows), :]
        return misfit_weight * (count * value - total)

    def seed(y, carry):
        for first, value in (
            (0, low * back_ref[y, pl.ds(0, rim), :]),
            (rim, p4_ref[y]),
            (rim + bx, high * front_ref[y, pl.ds(0, rim), :]),
        ):
            rows = value.shape[0]
            error = residual(3, y, first, value)
            later[y, pl.ds(first, rows), :] = error
            scaled[y + 4, pl.ds(lead + first, rows), :] = modulus[y, pl.ds(first, rows), :] * error
        return carry

    lax.fori_loop(0, ay, seed, 0)
    grad_m[...] = jnp.zeros(grad_m.shape, F32)
    grad_b[...] = jnp.zeros(grad_b.shape, F32)

    def set_wave(ref, first, offset):
        def body(y, carry):
            rows = ref.shape[1] - 2 * offset
            wave[y + 4, pl.ds(lead + first, rows), :] = ref[y, pl.ds(offset, rows), :]
            return carry

        lax.fori_loop(0, ay, body, 0)

    def gradients(adjoint_of, image):
        def faces(j, carry):
            cross_y[j] = slope_y(scaled, j, 16, 48) * slope_y(wave, j, 16, 48)
            return carry

        lax.fori_loop(0, ay + 1, faces, 0)
        base = lead + 8

        def body(y, carry):
            def slope_x(field):
                return differences(
                    lambda t: (
                        field[y + 4, pl.ds(base + t, 56), :],
                        field[y + 4, pl.ds(base + 1 - t, 56), :],
                    )
                )

            cross_x[...] = slope_x(scaled) * slope_x(wave)
            here_s, before_s = slope_z(scaled[y + 4, pl.ds(lead + 16, 48), :], factors)
            here_w, before_w = slope_z(wave[y + 4, pl.ds(lead + 16, 48), :], factors)
            total = here_s * here_w + pltpu.roll(before_s * before_w, 1, 1)
            total = total + cross_y[y] + cross_y[y + 1]
            total = total + cross_x[pl.ds(7, 48), :] + cross_x[pl.ds(8, 48), :]
            grad_b[y] = grad_b[y] - (0.5 * tap_square) * total
            grad_m[y] = grad_m[y] + adjoint_of(y) * image_ref[image, y]
            return carry

        lax.fori_loop(0, ay, body, 0)

    set_wave(p3_ref, 16, 0)
    gradients(lambda y: later[y, pl.ds(16, 48), :], 2)

    def step_three(y, image):
        value = jnp.concatenate(
            [
                low * back_ref[y, pl.ds(rim, 8), :],
                p3_ref[y],
                high * front_ref[y, pl.ds(rim, 8), :],
            ],
            axis=0,
        )
        late[y] = residual(2, y, 8, value) + 2.0 * later[y, pl.ds(8, 64), :] + image

    apply_operator(scaled, weights, flux_y, flux_x, factors, 8, 64, step_three)

    def rescale(y, carry):
        scaled[y + 4, pl.ds(lead + 8, 64), :] = modulus[y, pl.ds(8, 64), :] * late[y]
        return carry

    lax.fori_loop(0, ay, rescale, 0)
    set_wave(p2_ref, 8, 0)
    gradients(lambda y: late[y, pl.ds(8, 48), :], 1)

    def step_two(y, image):
        value = (
            residual(1, y, 16, p2_ref[y, pl.ds(8, 48), :])
            + 2.0 * late[y, pl.ds(8, 48), :]
            + image
            - later[y, pl.ds(16, 48), :]
        )
        later[y, pl.ds(16, 48), :] = value

    apply_operator(scaled, weights, flux_y, flux_x, factors, 16, 48, step_two)

    def rescale_last(y, carry):
        scaled[y + 4, pl.ds(lead + 16, 48), :] = modulus[y, pl.ds(16, 48), :] * later[y, pl.ds(16, 48), :]
        return carry

    lax.fori_loop(0, ay, rescale_last, 0)
    set_wave(p1_ref, 8, 0)
    gradients(lambda y: later[y, pl.ds(16, 48), :], 0)

    column_ref[...] = jnp.zeros(column_ref.shape, F32)
    first_row = at_ref[2]

    def place(y, carry):
        column_ref[first_row + y, pl.ds(0, gx), :] = grad_m[y, pl.ds(6, gx), :]
        column_ref[first_row + y, pl.ds(gx, gx), :] = grad_b[y, pl.ds(6, gx), :]
        return carry

    lax.fori_loop(0, ay, place, 0)


def adjoint_waves(at, window, clo, chi, fields, back, front, seen):
    return pl.pallas_call(
        adjoint_kernel,
        out_shape=jax.ShapeDtypeStruct((2 * shots, 2 * gx, nz), F32),
        in_specs=[scalars] + whole(11),
        out_specs=whole(1)[0],
        scratch_shapes=[
            pltpu.VMEM((ay, dom, nz), F32),
            padded, padded, padded,
            pltpu.VMEM((ay, dom, nz), F32),
            pltpu.VMEM((ay, 64, nz), F32),
            pltpu.VMEM((ay, 48, nz), F32),
            pltpu.VMEM((ay, 48, nz), F32),
            *weight_shapes,
            pltpu.VMEM((23, dom, nz), F32),
            pltpu.VMEM((dom + 16, nz), F32),
            pltpu.VMEM((ay + 1, 48, nz), F32),
            pltpu.VMEM((56, nz), F32),
        ],
        compiler_params=vmem,
        name="adjoint_waves",
    )(at, window, clo, chi, *fields, back, front, seen)


def chain_kernel(at_ref, got_ref, out_ref, grad_ref):
    brick = at_ref[1]
    row = lax.broadcasted_iota(jnp.int32, (gx, nz), 0)
    fine = ((row >= 2) | (brick > 0)) & ((row < gx - 2) | (brick < bricks - 1))
    for y in range(2):
        total = got_ref[0, y]
        for shot in range(1, shots):
            total = total + got_ref[shot, y]
        squashed = jax.nn.sigmoid(out_ref[0, y])
        bent = jnp.tanh(out_ref[1, y])
        buoyancy = jnp.exp(0.35 * bent)
        first = total[:gx] * 0.09 * squashed * (1.0 - squashed)
        second = total[gx:] * buoyancy * 0.35 * (1.0 - bent * bent)
        grad_ref[y, 0] = jnp.where(fine, first, 0.0).astype(BF16)
        grad_ref[y, 1] = jnp.where(fine, second, 0.0).astype(BF16)


def chain(at, got, output):
    return pl.pallas_call(
        chain_kernel,
        out_shape=jax.ShapeDtypeStruct((2, 2, gx, nz), BF16),
        in_specs=[scalars] + whole(2),
        out_specs=whole(1)[0],
        compiler_params=vmem,
        name="chain",
    )(at, got, output)


def spread_kernel(at_ref, lo_ref, mid_ref, hi_ref, hid_ref, s1, s2):
    shot, brick = at_ref[0], at_ref[1]
    y_fine = (shot > 0, True, shot < shots - 1)

    def spread(x, carry):
        x_fine = ((x >= 1) | (brick > 0)) & ((x < bx + 1) | (brick < bricks - 1))
        for y, (ref, row, part) in enumerate(((lo_ref, 1, 0), (mid_ref, 0, 1), (mid_ref, 1, 1), (hi_ref, 0, 2))):
            value = jnp.where(x_fine & y_fine[part], ref[row, x + 3].astype(F32), 0.0)
            hidden = hid_ref[x + 2, pl.ds(y * 16, 16), :].astype(F32)
            for k in range(3):
                s1[x, pl.ds(y * 48 + k * 16, 16), :] = lane_shift(value, k).astype(BF16)
                s2[x, pl.ds(y * 48 + k * 16, 16), :] = lane_shift(hidden, k).astype(BF16)
        return carry

    lax.fori_loop(0, bx + 2, spread, 0, unroll=2)


def spread_fields(at, lo, mid, hi, hidden):
    shape = jax.ShapeDtypeStruct((bx + 2, 192, nz), BF16)
    return pl.pallas_call(
        spread_kernel,
        out_shape=(shape, shape),
        in_specs=[scalars] + whole(4),
        out_specs=tuple(whole(2)),
        compiler_params=vmem,
        cost_estimate=cost(3),
        name="spread_fields",
    )(at, lo, mid, hi, hidden)


def kernel_grads_kernel(
    at_ref, glo_ref, gmid_ref, ghi_ref, hid_ref, s1, s2, w3_ref, s4, kernel_ref, grads, own, s3, inner
):
    shot, brick = at_ref[0], at_ref[1]
    y_fine = (shot > 0, True, shot < shots - 1)
    grads[:, pl.ds(gx, 12), :] = jnp.zeros((12, 12, nz), F32)
    own[...] = jnp.zeros(own.shape, F32)
    for part, ref in enumerate((glo_ref, gmid_ref, ghi_ref)):
        for row in range(2):
            for channel in range(2):
                value = jnp.where(y_fine[part], ref[row, channel].astype(F32), 0.0)
                grads[(2 * part + row) * 2 + channel, pl.ds(0, gx), :] = value
                if part == 1:
                    own[:, channel * 2 + row, :] = value[2 : bx + 2]

    def hidden_grad(block, carry):
        for plane in range(12):
            value = grads[plane, pl.ds(8 * block, 16), :]
            for k in range(3):
                s3[pl.ds((plane * 3 + k) * 16, 16), :] = lane_shift(value, k).astype(BF16)
        acc = jnp.dot(w3_ref[...], s3[...], preferred_element_type=F32)
        for xo in range(8):
            x = 8 * block + xo
            x_fine = ((x >= 1) | (brick > 0)) & ((x < bx + 1) | (brick < bricks - 1))
            for y in range(4):
                fine = x_fine
                if y == 0:
                    fine = fine & (shot > 0)
                if y == 3:
                    fine = fine & (shot < shots - 1)
                hidden = hid_ref[jnp.minimum(x + 2, bx + 5), pl.ds(y * 16, 16), :].astype(F32)
                start = (xo * 4 + y) * 16
                value = acc[start : start + 16] * (1.0 - hidden * hidden)
                value = jnp.where(fine, value, 0.0).astype(BF16)
                if y in (1, 2):
                    inner[x, pl.ds((y - 1) * 16, 16), :] = value
                wide = value.astype(F32)
                for k in range(3):
                    s4[x, pl.ds(y * 48 + k * 16, 16), :] = lane_shift(wide, k).astype(BF16)
        return carry

    lax.fori_loop(0, 5, hidden_grad, 0)

    def kernel_grad(x, carry):
        first, second = carry
        contract = (((1,), (1,)), ((), ()))
        first = first + lax.dot_general(
            inner[x + 1], s1[pl.ds(x, 3)].reshape(576, nz), contract, preferred_element_type=F32
        )
        second = second + lax.dot_general(
            own[x].astype(BF16), s2[pl.ds(x, 3)].reshape(576, nz), contract, preferred_element_type=F32
        )
        return first, second

    first, second = lax.fori_loop(
        0, bx, kernel_grad, (jnp.zeros((32, 576), F32), jnp.zeros((8, 576), F32)), unroll=4
    )
    kernel_ref[...] = jnp.zeros(kernel_ref.shape, F32)
    for dx in range(3):
        start = dx * 192
        one = first[:16, start : start + 144] + first[16:, start + 48 : start + 192]
        for channel in range(2):
            row = channel * 2
            two = (
                second[row : row + 1, start : start + 144]
                + second[row + 1 : row + 2, start + 48 : start + 192]
            )
            place = dx * 2 * 18 + 16 + channel
            kernel_ref[pl.ds(place, 1), :] = two[:, :128]
            kernel_ref[pl.ds(place + 18, 1), pl.ds(0, 16)] = two[:, 128:]
        kernel_ref[pl.ds(dx * 36, 16), :] = one[:, :128]
        kernel_ref[pl.ds(dx * 36 + 18, 16), pl.ds(0, 16)] = one[:, 128:]


def kernel_grads(at, glo, gmid, ghi, hidden, s1, s2, w3):
    return pl.pallas_call(
        kernel_grads_kernel,
        out_shape=(
            jax.ShapeDtypeStruct((40, 192, nz), BF16),
            jax.ShapeDtypeStruct((128, nz), F32),
        ),
        in_specs=[scalars] + whole(7),
        out_specs=tuple(whole(2)),
        scratch_shapes=[
            pltpu.VMEM((12, 48, nz), F32),
            pltpu.VMEM((bx, 8, nz), F32),
            pltpu.VMEM((576, nz), BF16),
            pltpu.VMEM((40, 32, nz), BF16),
        ],
        compiler_params=vmem,
        name="kernel_grads",
    )(at, glo, gmid, ghi, hidden, s1, s2, w3)


def latent_grad_kernel(s4, w4_ref, latent_ref):
    def latent_grad(block, carry):
        rows = s4[pl.ds(4 * block, 6)].reshape(6 * 192, nz)
        acc = jnp.dot(w4_ref[...], rows, preferred_element_type=F32)
        latent_ref[pl.ds(4 * block, 4)] = acc.reshape(4, 32, nz)
        return carry

    lax.fori_loop(0, bx // 4, latent_grad, 0)


def latent_grads(s4, w4):
    return pl.pallas_call(
        latent_grad_kernel,
        out_shape=jax.ShapeDtypeStruct((bx, 32, nz), F32),
        in_specs=whole(2),
        out_specs=whole(1)[0],
        compiler_params=vmem,
        cost_estimate=cost(4),
        name="latent_grads",
    )(s4, w4)


def column_codes(x_in, y_in, order):
    if order == "xykc":
        x, y, k, c = np.meshgrid(*map(np.arange, (x_in, y_in, 3, 16)), indexing="ij")
    else:
        y, c, k, x = np.meshgrid(*map(np.arange, (y_in, 2, 3, x_in)), indexing="ij")
    return np.stack([(8 * x + y).ravel(), (16 * k + c).ravel()]).astype(np.int32)


codes_1 = column_codes(4, 6, "xykc")
codes_2 = column_codes(8, 4, "xykc")
codes_3 = column_codes(16, 6, "yckx")
codes_4 = column_codes(6, 4, "xykc")


def expand(taps_ref, codes_ref, spare, flip):
    place = codes_ref[1:2]
    size = place.shape[1]
    rows = lax.broadcasted_iota(jnp.int32, (16, size), 0)
    picks = [jnp.where(place == rows + 16 * k, 1.0, 0.0).astype(BF16) for k in range(3)]
    for pair in range(9):
        total = None
        for k in range(3):
            q = 3 * pair + k
            term = jnp.dot(taps_ref[26 - q if flip else q], picks[k], preferred_element_type=F32)
            total = term if total is None else total + term
        spare[pair, :, pl.ds(0, size)] = total


def fill_blocks(out_ref, codes_ref, spare, x_out, y_out):
    code = codes_ref[0:1]
    size = code.shape[1]
    same = lax.broadcasted_iota(jnp.int32, (16, size), 0) * 0 + code
    for xo in range(x_out):
        for y in range(y_out):
            block = jnp.zeros((16, size), F32)
            for pair in range(9):
                wanted = (xo + pair // 3) * 8 + y + pair % 3
                block = jnp.where(same == wanted, spare[pair, :, pl.ds(0, size)], block)
            out_ref[pl.ds((xo * y_out + y) * 16, 16), :] = block.astype(BF16)


def forward_bands_kernel(in_ref, out_taps_ref, codes_1_ref, codes_2_ref, w1_ref, w2_ref, spare, rows):
    expand(in_ref, codes_1_ref, spare, False)
    fill_blocks(w1_ref, codes_1_ref, spare, 2, 4)
    expand(out_taps_ref, codes_2_ref, spare, False)
    size = codes_2_ref.shape[1]
    code = codes_2_ref[0:1] - 8 * lax.broadcasted_iota(jnp.int32, (6, size), 0)
    for channel in range(2):
        for y in range(2):
            block = jnp.zeros((6, size), F32)
            for pair in range(9):
                wanted = (pair // 3) * 8 + y + pair % 3
                block = jnp.where(code == wanted, spare[pair, channel : channel + 1, :], block)
            rows[pl.ds((channel * 2 + y) * 6, 6), :] = block
    w2_ref[...] = rows[...].astype(BF16)


def backward_bands_kernel(in_ref, out_taps_ref, codes_3_ref, codes_4_ref, w3_ref, w4_ref, spare):
    expand(out_taps_ref, codes_3_ref, spare, True)
    fill_blocks(w3_ref, codes_3_ref, spare, 8, 4)
    expand(in_ref, codes_4_ref, spare, True)
    fill_blocks(w4_ref, codes_4_ref, spare, 4, 2)


def forward_bands(taps_in, taps_out):
    return pl.pallas_call(
        forward_bands_kernel,
        out_shape=(
            jax.ShapeDtypeStruct((128, 1152), BF16),
            jax.ShapeDtypeStruct((24, 1536), BF16),
        ),
        in_specs=whole(4),
        out_specs=tuple(whole(2)),
        scratch_shapes=[pltpu.VMEM((9, 16, 1536), F32), pltpu.VMEM((24, 1536), F32)],
        compiler_params=vmem,
        cost_estimate=cost(3),
        name="forward_bands",
    )(taps_in, taps_out, codes_1, codes_2)


def backward_bands(taps_in, taps_out):
    return pl.pallas_call(
        backward_bands_kernel,
        out_shape=(
            jax.ShapeDtypeStruct((512, 576), BF16),
            jax.ShapeDtypeStruct((128, 1152), BF16),
        ),
        in_specs=whole(4),
        out_specs=tuple(whole(2)),
        scratch_shapes=[pltpu.VMEM((9, 16, 1152), F32)],
        compiler_params=vmem,
        cost_estimate=cost(4),
        name="backward_bands",
    )(taps_in, taps_out, codes_3, codes_4)


def both_ways(ahead, behind, axis):
    count = lax.axis_size(axis)
    forward = [(i, (i + 1) % count) for i in range(count)]
    backward_ = [(target, source) for source, target in forward]
    return lax.ppermute(ahead, axis, forward), lax.ppermute(behind, axis, backward_)


def per_device(latent, conv_in, conv_out, source_field, observed, aperture, receivers):
    shot = lax.axis_index("shot")
    brick = lax.axis_index("brick")
    at = jnp.stack([shot, brick, aperture[0]]).astype(jnp.int32)
    taps_out = jnp.pad(conv_out, ((0, 0), (0, 14), (0, 0)))
    w1, w2 = forward_bands(conv_in, taps_out)
    w3, w4 = backward_bands(conv_in.transpose(0, 2, 1), taps_out.transpose(0, 2, 1))

    tile = jnp.transpose(latent, (2, 1, 0, 3))
    from_low, from_high = both_ways(tile[:, bx - 4 :], tile[:, :4], "brick")
    mid = jnp.concatenate([from_low, tile, from_high], axis=1)
    lo, hi = both_ways(mid, mid, "shot")
    source = jnp.transpose(source_field[0], (1, 0, 2))
    plo, phi = both_ways(source[:, bx - rim :], source[:, :rim], "brick")
    seen = receiver_fields(at, receivers[0], observed[0])

    coefficients, output, hidden = generator(at, lo, mid, hi, w1, w2)
    coefficients, plo, phi = lax.optimization_barrier((coefficients, plo, phi))
    sent = jnp.broadcast_to(coefficients[None], (shots, 2, 2, bx, nz))
    column = lax.all_to_all(sent, "shot", 0, 0, tiled=True)
    column, seen, w3, w4 = lax.optimization_barrier((column, seen, w3, w4))
    column = column.reshape(2 * shots, 2, bx, nz)
    window = lax.dynamic_slice_in_dim(column, aperture[0], ay, 0)
    clo, chi = both_ways(window[:, :, bx - rim :], window[:, :, :rim], "brick")
    p1, p2, p3, p4, images, ahead, behind = forward_waves(at, window, clo, chi, source, plo, phi)
    back, front = both_ways(ahead, behind, "brick")
    grads = adjoint_waves(at, window, clo, chi, (p1, p2, p3, p4, images), back, front, seen)
    got = lax.all_to_all(grads, "shot", 0, 0, tiled=True)
    s1, s2 = spread_fields(at, lo, mid, hi, hidden)
    got, s1, s2 = lax.optimization_barrier((got, s1, s2))
    got = got.reshape(shots, 2, 2 * gx, nz)
    grad_output = chain(at, got, output)
    glo, ghi = both_ways(grad_output, grad_output, "shot")
    s4, kernels = kernel_grads(at, glo, grad_output, ghi, hidden, s1, s2, w3)
    grad_latent = latent_grads(s4, w4)
    grad_latent = jnp.transpose(grad_latent.reshape(bx, 2, 16, nz), (2, 0, 1, 3))

    everyone = ("shot", "brick")
    slices = lax.all_to_all(kernels, everyone, 0, 0, tiled=True)
    mine = jnp.sum(slices, axis=0, keepdims=True)
    summed = lax.all_to_all(jnp.broadcast_to(mine, (128, nz)), everyone, 0, 0, tiled=True)
    folded = summed[:108].reshape(3, 2, 18, nz).transpose(0, 2, 1, 3).reshape(3, 18, 256)[:, :, :144]
    folded = folded.reshape(3, 18, 9, 16).transpose(0, 2, 1, 3).reshape(27, 18, 16)
    return (grad_latent, folded[:, :16], folded[:, 16:])


def solution(mesh):
    placed = (
        P(None, "brick", "shot", None),
        P(),
        P(),
        P("shot", "brick", None, None),
        P("shot", None, None),
        P("shot"),
        P("shot", None, None),
    )
    return jax.shard_map(
        per_device,
        mesh=mesh,
        in_specs=placed,
        out_specs=(P(None, "brick", "shot", None), P(), P()),
        check_vma=False,
    )
```

```python
import jax
import jax.numpy as jnp
import numpy as np
from jax import lax
from jax.experimental import pallas as pl
from jax.experimental.pallas import tpu as pltpu
from jax.sharding import PartitionSpec as P

F32 = jnp.float32
BF16 = jnp.bfloat16
stencil_taps = (1225.0 / 1024.0, -245.0 / 3072.0, 49.0 / 5120.0, -5.0 / 7168.0)
ratios = tuple(tap / stencil_taps[0] for tap in stencil_taps)
tap_square = stencil_taps[0] ** 2
misfit_weight = 16.0

bricks, shots = 8, 16
bx = 32
ay = 16
nz = 128
rim = 24
dom = bx + 2 * rim
lead = 8
xpad = dom + 24
ypad = ay + 8
gx = bx + 4
vmem = pltpu.CompilerParams(vmem_limit_bytes=24 * 1024 * 1024)


def cost(microseconds):
    return pl.CostEstimate(flops=0, bytes_accessed=int(microseconds * 3e6), transcendentals=0)


def whole(count):
    return [pl.BlockSpec(memory_space=pltpu.VMEM)] * count


scalars = pl.BlockSpec(memory_space=pltpu.SMEM)


def lane_index():
    return lax.broadcasted_iota(jnp.int32, (1, nz), 1)


def lane_shift(value, offset):
    if offset == 1:
        return value
    lane = lax.broadcasted_iota(jnp.int32, value.shape, 1)
    if offset == 0:
        return jnp.where(lane == 0, 0.0, pltpu.roll(value, 1, 1))
    return jnp.where(lane == nz - 1, 0.0, pltpu.roll(value, nz - 1, 1))


def generator_kernel(
    at_ref, lo_ref, mid_ref, hi_ref, w1_ref, w2_ref, coef_ref, out_ref, hid_ref, s1, s2
):
    shot, brick = at_ref[0], at_ref[1]
    y_fine = (shot > 0, True, shot < shots - 1)

    def spread(x, carry):
        x_fine = ((x >= 4) | (brick > 0)) & ((x < bx + 4) | (brick < bricks - 1))
        for part, ref in enumerate((lo_ref, mid_ref, hi_ref)):
            fine = x_fine & y_fine[part]
            for row in range(2):
                value = jnp.where(fine, ref[row, x].astype(F32), 0.0)
                for k in range(3):
                    s1[x, pl.ds((2 * part + row) * 48 + k * 16, 16), :] = lane_shift(
                        value, k
                    ).astype(BF16)
        return carry

    lax.fori_loop(0, bx + 8, spread, 0)

    def first_conv(block, carry):
        rows = s1[pl.ds(2 * block, 4)].reshape(4 * 288, nz)
        acc = jnp.tanh(jnp.dot(w1_ref[...], rows, preferred_element_type=F32))
        for xo in range(2):
            x = 2 * block + xo
            x_fine = ((x >= 3) | (brick > 0)) & ((x < bx + 3) | (brick < bricks - 1))
            for y in range(4):
                fine = x_fine
                if y == 0:
                    fine = fine & (shot > 0)
                if y == 3:
                    fine = fine & (shot < shots - 1)
                start = (xo * 4 + y) * 16
                value = jnp.where(fine, acc[start : start + 16], 0.0).astype(BF16)
                hid_ref[x, pl.ds(y * 16, 16), :] = value
                wide = value.astype(F32)
                for k in range(3):
                    s2[x, pl.ds(y * 48 + k * 16, 16), :] = lane_shift(wide, k).astype(BF16)
        return carry

    lax.fori_loop(0, (bx + 6) // 2, first_conv, 0)

    for block in range(gx // 6):
        rows = s2[pl.ds(6 * block, 8)].reshape(8 * 192, nz)
        acc = jnp.dot(w2_ref[...], rows, preferred_element_type=F32)
        for channel in range(2):
            for y in range(2):
                start = (channel * 2 + y) * 6
                out_ref[channel, y, pl.ds(6 * block, 6), :] = acc[start : start + 6]
    for y in range(2):
        modulus = 0.03 + 0.09 * jax.nn.sigmoid(out_ref[0, y, pl.ds(2, bx), :])
        buoyancy = jnp.exp(0.35 * jnp.tanh(out_ref[1, y, pl.ds(2, bx), :]))
        coef_ref[y, 0] = modulus
        coef_ref[y, 1] = buoyancy


def generator(at, lo, mid, hi, w1, w2):
    return pl.pallas_call(
        generator_kernel,
        out_shape=(
            jax.ShapeDtypeStruct((2, 2, bx, nz), F32),
            jax.ShapeDtypeStruct((2, 2, gx, nz), F32),
            jax.ShapeDtypeStruct((bx + 6, 64, nz), BF16),
        ),
        in_specs=[scalars] + whole(5),
        out_specs=tuple(whole(3)),
        scratch_shapes=[
            pltpu.VMEM((bx + 8, 288, nz), BF16),
            pltpu.VMEM((bx + 6, 192, nz), BF16),
        ],
        compiler_params=vmem,
        name="generator",
    )(at, lo, mid, hi, w1, w2)


def receiver_kernel(at_ref, cell_ref, seen_ref, out_ref, hot, spread):
    brick, first_row = at_ref[1], at_ref[2]
    count = cell_ref.shape[1]
    x = cell_ref[0:1] - brick * bx + rim
    row_of = jnp.where((x >= 0) & (x < dom), (cell_ref[1:2] - first_row) * dom + x, -1)
    z = cell_ref[2:3]

    def mark(chunk, carry):
        rows = chunk * 16 + lax.broadcasted_iota(jnp.int32, (16, count), 0)
        hot[pl.ds(chunk * 16, 16), :] = jnp.where(rows == row_of, 1.0, 0.0).astype(BF16)
        return carry

    lax.fori_loop(0, ay * dom // 16, mark, 0)
    parts = [jnp.ones((1, count), F32)]
    for step in range(3):
        value = seen_ref[step : step + 1]
        high = value.astype(BF16).astype(F32)
        parts += [high, value - high]

    def place(chunk, carry):
        same = chunk * 16 + lax.broadcasted_iota(jnp.int32, (16, count), 0) == z
        for index, part in enumerate(parts):
            spread[pl.ds(index * nz + chunk * 16, 16), :] = jnp.where(same, part, 0.0).astype(BF16)
        return carry

    lax.fori_loop(0, nz // 16, place, 0)
    size = 256

    def multiply(chunk, carry):
        left = hot[pl.ds(chunk * size, size), :]
        for field in range(4):
            first = 0 if field == 0 else (2 * field - 1) * nz
            right = spread[pl.ds(first, nz if field == 0 else 2 * nz), :]
            acc = lax.dot_general(
                left, right, (((1,), (1,)), ((), ())), preferred_element_type=F32
            )
            if field:
                acc = acc[:, :nz] + acc[:, nz:]
            out_ref[field, pl.ds(chunk * size, size), :] = acc
        return carry

    lax.fori_loop(0, ay * dom // size, multiply, 0)


def receiver_fields(at, cells, seen):
    count = cells.shape[1]
    return pl.pallas_call(
        receiver_kernel,
        out_shape=jax.ShapeDtypeStruct((4, ay * dom, nz), F32),
        in_specs=[scalars] + whole(2),
        out_specs=whole(1)[0],
        scratch_shapes=[
            pltpu.VMEM((ay * dom, count), BF16),
            pltpu.VMEM((7 * nz, count), BF16),
        ],
        compiler_params=vmem,
        cost_estimate=cost(9),
        name="receiver_fields",
    )(at, cells, seen)


def lane_factors():
    lane = lane_index()
    last = lane == nz - 1
    upper = [jnp.where((lane <= nz - 1 - t) | last, ratios[t - 1], 0.0) for t in range(1, 5)]
    lower = [jnp.where(lane >= t - 1, ratios[t - 1], 0.0) for t in range(1, 5)]
    above = [jnp.where(lane <= nz - t, ratios[t - 1], 0.0) for t in range(1, 5)]
    return last, upper, lower, above


def turn(value, shift):
    shift = shift % nz
    return value if shift == 0 else pltpu.roll(value, shift, 1)


def differences(get):
    total = None
    for t in range(1, 5):
        upper, lower = get(t)
        term = upper - lower
        if t > 1:
            term = ratios[t - 1] * term
        total = term if total is None else total + term
    return total


def split_rows(value):
    high = value.astype(BF16).astype(F32)
    return jnp.concatenate([high, value - high], axis=0).astype(BF16)


def joined(rows):
    wide = rows.astype(F32)
    return wide[:8] + wide[8:]


def clear_sides(field):
    for y in (0, 1, 2, 3, ay + 4, ay + 5, ay + 6, ay + 7):
        field[y] = jnp.zeros(field.shape[1:], F32)


def clear_rims(flux_y):
    for j in (0, 1, 2, 20, 21, 22):
        flux_y[j] = jnp.zeros(flux_y.shape[1:], F32)


def halo_scale(at_ref):
    brick = at_ref[1]
    return (
        jnp.where(brick > 0, 1.0, 0.0).astype(F32),
        jnp.where(brick < bricks - 1, 1.0, 0.0).astype(F32),
    )


def window_kernel(at_ref, column_ref, win_ref, ahead_ref, behind_ref):
    first_row = at_ref[2]

    def body(y, carry):
        for channel in range(2):
            value = column_ref[first_row + y, channel]
            win_ref[y, channel] = value
            ahead_ref[y, channel, pl.ds(0, 16), :] = split_rows(value[24:])
            ahead_ref[y, channel, pl.ds(16, 16), :] = value[8:24].astype(BF16)
            behind_ref[y, channel, pl.ds(0, 16), :] = split_rows(value[:8])
            behind_ref[y, channel, pl.ds(16, 16), :] = value[8:24].astype(BF16)
        return carry

    lax.fori_loop(0, ay, body, 0, unroll=2)


def take_window(at, column):
    return pl.pallas_call(
        window_kernel,
        out_shape=(
            jax.ShapeDtypeStruct((ay, 2, bx, nz), F32),
            jax.ShapeDtypeStruct((ay, 2, bx, nz), BF16),
            jax.ShapeDtypeStruct((ay, 2, bx, nz), BF16),
        ),
        in_specs=[scalars] + whole(1),
        out_specs=tuple(whole(3)),
        compiler_params=vmem,
        name="take_window",
    )(at, column)


def slope_y(field, j, first, rows):
    return differences(
        lambda t: (
            field[j + 3 + t, pl.ds(lead + first, rows), :],
            field[j + 4 - t, pl.ds(lead + first, rows), :],
        )
    )


def slopes_at(field, y, first, rows, factors):
    value = field[y + 4, pl.ds(lead + first, rows), :]
    turned_up = [turn(value, -t) for t in range(1, 5)]
    turned_low = [turn(value, t - 1) for t in range(1, 5)]
    base, more = lead + first - 4, rows + 8
    sx = differences(
        lambda t: (
            field[y + 4, pl.ds(base + t, more), :],
            field[y + 4, pl.ds(base + 1 - t, more), :],
        )
    )
    sy = slope_y(field, y, first, rows)
    last, upper, lower, _ = factors
    up = sum(upper[t] * turned_up[t] for t in range(4))
    low = sum(lower[t] * turned_low[t] for t in range(4))
    slope = up - low
    return sx, sy, jnp.where(last, -low, slope), jnp.where(last, up, slope)


def flux_pass(field, weights, fluxes, first, rows, factors, also=None):
    wx, wy, wz, wzl = weights
    fx, fy, fh, fb = fluxes
    base, more = lead + first - 4, rows + 8

    def body(y, carry):
        sx, sy, here, before = slopes_at(field, y, first, rows, factors)
        fx[y, pl.ds(0, more), :] = wx[y, pl.ds(base, more), :] * sx
        fy[y + 3, pl.ds(0, rows), :] = wy[y, pl.ds(first, rows), :] * sy
        fh[y, pl.ds(0, rows), :] = wz[y, pl.ds(first, rows), :] * here
        fb[y, pl.ds(0, rows), :] = wzl[y, pl.ds(first, rows), :] * before
        if also is not None:
            also(y, sx, sy, here, before)
        return carry

    lax.fori_loop(0, ay, body, 0, unroll=2)
    sy = slope_y(field, ay, first, rows)
    fy[ay + 3, pl.ds(0, rows), :] = wy[ay, pl.ds(first, rows), :] * sy
    return sy


def divergence_pass(fluxes, rows, factors, consume):
    fx, fy, fh, fb = fluxes
    _, _, lower, above = factors

    def body(y, carry):
        here = fh[y, pl.ds(0, rows), :]
        before = fb[y, pl.ds(0, rows), :]
        turned_here = [turn(here, 1 - t) for t in range(1, 5)]
        turned_before = [turn(before, t) for t in range(1, 5)]
        total = differences(
            lambda t: (fx[y, pl.ds(3 + t, rows), :], fx[y, pl.ds(4 - t, rows), :])
        )
        total = total + differences(
            lambda t: (
                fy[y + t + 3, pl.ds(0, rows), :],
                fy[y - t + 4, pl.ds(0, rows), :],
            )
        )
        total = total + sum(above[t] * turned_here[t] for t in range(4))
        total = total - sum(lower[t] * turned_before[t] for t in range(4))
        consume(y, total)
        return carry

    lax.fori_loop(0, ay, body, 0, unroll=2)


weight_sizes = ((ay, dom + 16, nz), (ay + 1, dom, nz), (ay, dom, nz), (ay, dom, nz))
padded = pltpu.VMEM((ypad, xpad, nz), F32)
flux_shapes = [
    pltpu.VMEM((ay, 72, nz), F32),
    pltpu.VMEM((23, 64, nz), F32),
    pltpu.VMEM((ay, 64, nz), F32),
    pltpu.VMEM((ay, 64, nz), F32),
]


def forward_kernel(
    at_ref, win_ref, clo_ref, chi_ref, src_ref, plo_ref, phi_ref,
    p1_ref, p2_ref, p3_ref, p4_ref, image_ref, ahead_ref, behind_ref, modulus, wx, wy, wz, wzl,
    buoy, f1, f2, f3, fx, fy, fh, fb, message,
):
    factors = lane_factors()
    last = factors[0]
    weights = (wx, wy, wz, wzl)
    fluxes = (fx, fy, fh, fb)
    clear_rims(fy)
    for field in (buoy, f1, f2, f3):
        clear_sides(field)
    low, high = halo_scale(at_ref)
    half = 0.5 * tap_square

    def load(y, carry):
        for channel, ref, row, skip in ((0, modulus, y, 0), (1, buoy, y + 4, lead)):
            ref[row, pl.ds(skip, 16), :] = low * clo_ref[y, channel, pl.ds(16, 16), :].astype(F32)
            ref[row, pl.ds(skip + 16, 8), :] = low * joined(clo_ref[y, channel, pl.ds(0, 16), :])
            ref[row, pl.ds(skip + rim, bx), :] = win_ref[y, channel]
            ref[row, pl.ds(skip + rim + bx, 8), :] = high * joined(chi_ref[y, channel, pl.ds(0, 16), :])
            ref[row, pl.ds(skip + rim + bx + 8, 16), :] = high * chi_ref[y, channel, pl.ds(16, 16), :].astype(F32)
        f1[y + 4, pl.ds(lead, rim), :] = low * plo_ref[y]
        f1[y + 4, pl.ds(lead + rim, bx), :] = src_ref[y]
        f1[y + 4, pl.ds(lead + rim + bx, rim), :] = high * phi_ref[y]
        return carry

    lax.fori_loop(0, ay, load, 0)

    def weigh(y, carry):
        inner = buoy[y + 4, pl.ds(lead, dom), :]
        ahead = pltpu.roll(inner, nz - 1, 1)
        value = buoy[y + 4, pl.ds(0, dom + 16), :]
        wx[y] = half * (value + buoy[y + 4, pl.ds(1, dom + 16), :])
        wy[y] = half * (buoy[y + 3, pl.ds(lead, dom), :] + inner)
        wz[y] = half * jnp.where(last, inner, inner + ahead)
        wzl[y] = half * jnp.where(last, ahead, inner + ahead)
        return carry

    lax.fori_loop(0, ay, weigh, 0, unroll=2)
    wy[ay] = half * buoy[ay + 3, pl.ds(lead, dom), :]

    def first_step(y, image):
        f2[y + 4, pl.ds(lead + 8, 64), :] = (
            2.0 * f1[y + 4, pl.ds(lead + 8, 64), :] + modulus[y, pl.ds(8, 64), :] * image
        )
        image_ref[0, y] = image[8:56]

    def second_step(y, image):
        value = (
            2.0 * f2[y + 4, pl.ds(lead + 12, 56), :]
            - f1[y + 4, pl.ds(lead + 12, 56), :]
            + modulus[y, pl.ds(12, 56), :] * image
        )
        f3[y + 4, pl.ds(lead + 12, 56), :] = value
        image_ref[1, y] = image[4:52]
        p3_ref[y] = value[4:52]
        p1_ref[y] = f1[y + 4, pl.ds(lead + 8, 64), :]
        p2_ref[y] = f2[y + 4, pl.ds(lead + 8, 64), :]

    def third_step(y, image):
        image_ref[2, y] = image
        value = (
            2.0 * f3[y + 4, pl.ds(lead + rim, bx), :]
            - f2[y + 4, pl.ds(lead + rim, bx), :]
            + modulus[y, pl.ds(rim, bx), :] * image[8:40]
        )
        p4_ref[y] = value

    def pack(y, ref, near, further, third):
        value = p4_ref[y, pl.ds(near, 7), :]
        rounded = value.astype(BF16).astype(F32)
        message[pl.ds(0, 7), :] = rounded
        message[pl.ds(7, 7), :] = value - rounded
        message[pl.ds(14, 13), :] = p4_ref[y, pl.ds(further, 13), :]
        message[pl.ds(27, 5), :] = f3[y + 4, pl.ds(lead + rim + third, 5), :]
        ref[y] = message[...].astype(BF16)

    def send(y, carry):
        pack(y, ahead_ref, 25, 12, 19)
        pack(y, behind_ref, 0, 7, 8)
        return carry

    flux_pass(f1, weights, fluxes, 8, 64, factors)
    divergence_pass(fluxes, 64, factors, first_step)
    flux_pass(f2, weights, fluxes, 12, 56, factors)
    divergence_pass(fluxes, 56, factors, second_step)
    flux_pass(f3, weights, fluxes, 16, 48, factors)
    divergence_pass(fluxes, 48, factors, third_step)
    lax.fori_loop(0, ay, send, 0)


def forward_waves(at, window, clo, chi, source, plo, phi):
    shapes = [(ay, 64, nz), (ay, 64, nz), (ay, 48, nz), (ay, bx, nz), (3, ay, 48, nz)]
    return pl.pallas_call(
        forward_kernel,
        out_shape=tuple(jax.ShapeDtypeStruct(shape, F32) for shape in shapes)
        + (jax.ShapeDtypeStruct((ay, 32, nz), BF16),) * 2
        + (jax.ShapeDtypeStruct((ay, dom, nz), F32),)
        + tuple(jax.ShapeDtypeStruct(shape, F32) for shape in weight_sizes),
        in_specs=[scalars] + whole(6),
        out_specs=tuple(whole(12)),
        scratch_shapes=[padded, padded, padded, padded, *flux_shapes, pltpu.VMEM((32, nz), F32)],
        compiler_params=vmem,
        name="forward_waves",
    )(at, window, clo, chi, source, plo, phi)


def slopes_kernel(p1_ref, p2_ref, p3_ref, sx_ref, sy_ref, sh_ref, sb_ref, field):
    factors = lane_factors()
    clear_sides(field)
    for index, (ref, first) in enumerate(((p1_ref, 8), (p2_ref, 8), (p3_ref, 16))):
        rows = ref.shape[1]

        def load(y, carry):
            field[y + 4, pl.ds(lead + first, rows), :] = ref[y]
            return carry

        lax.fori_loop(0, ay, load, 0)

        def body(y, carry):
            sx, sy, here, before = slopes_at(field, y, 16, 48, factors)
            sx_ref[index, y] = sx[:48]
            sy_ref[index, y] = sy
            sh_ref[index, y] = here
            sb_ref[index, y] = before
            return carry

        lax.fori_loop(0, ay, body, 0, unroll=2)
        sy_ref[index, ay] = slope_y(field, ay, 16, 48)


def wave_slopes(p1, p2, p3):
    shapes = [(3, ay, 48, nz), (3, ay + 1, 48, nz), (3, ay, 48, nz), (3, ay, 48, nz)]
    return pl.pallas_call(
        slopes_kernel,
        out_shape=tuple(jax.ShapeDtypeStruct(shape, F32) for shape in shapes),
        in_specs=whole(3),
        out_specs=tuple(whole(4)),
        scratch_shapes=[padded],
        compiler_params=vmem,
        cost_estimate=cost(6),
        name="wave_slopes",
    )(p1, p2, p3)


def adjoint_kernel(
    at_ref, p2_ref, p3_ref, p4_ref, image_ref, back_ref, front_ref, seen_ref,
    modulus, wx, wy, wz, wzl, px_ref, py_ref, ph_ref, pb_ref,
    column_ref,
    scaled, later, late, grad_m, fx, fy, fh, fb, qx, qy, qh, qb, far,
):
    factors = lane_factors()
    weights = (wx, wy, wz, wzl)
    fluxes = (fx, fy, fh, fb)
    clear_rims(fy)
    clear_sides(scaled)
    low, high = halo_scale(at_ref)

    def residual(step, y, first, value):
        rows = value.shape[0]
        start = pl.multiple_of(y * dom + first, 8)
        count = seen_ref[0, pl.ds(start, rows), :]
        total = seen_ref[step, pl.ds(start, rows), :]
        return misfit_weight * (count * value - total)

    far[...] = jnp.zeros(far.shape, F32)

    def seed(y, carry):
        late[y, pl.ds(8, 48), :] = p3_ref[y]
        received = low * back_ref[y].astype(F32)
        far[pl.ds(4, 13), :] = received[14:27]
        far[pl.ds(17, 7), :] = received[:7] + received[7:14]
        late[y, pl.ds(3, 5), :] = received[27:]
        far[pl.ds(rim, bx), :] = p4_ref[y]
        received = high * front_ref[y].astype(F32)
        far[pl.ds(rim + bx, 7), :] = received[:7] + received[7:14]
        far[pl.ds(rim + bx + 7, 13), :] = received[14:27]
        late[y, pl.ds(56, 5), :] = received[27:]
        error = residual(3, y, 0, far[...])
        later[y] = error
        scaled[y + 4, pl.ds(lead, dom), :] = modulus[y] * error
        grad_m[y] = error[16:64] * image_ref[2, y]
        return carry

    lax.fori_loop(0, ay, seed, 0)

    def cross(index, offset):
        def also(y, sx, sy, here, before):
            products = (
                (qx, sx[offset : offset + 48] * px_ref[index, y]),
                (qy, sy[offset : offset + 48] * py_ref[index, y]),
                (qh, here[offset : offset + 48] * ph_ref[index, y]),
                (qb, before[offset : offset + 48] * pb_ref[index, y]),
            )
            for ref, product in products:
                ref[y] = product if index == 2 else ref[y] + product

        return also

    def cross_last(index, offset, sy):
        product = sy[offset : offset + 48] * py_ref[index, ay]
        qy[ay] = product if index == 2 else qy[ay] + product

    def step_three(y, image):
        value = late[y]
        value = residual(2, y, 8, value) + 2.0 * later[y, pl.ds(8, 64), :] + image
        late[y] = value
        grad_m[y] = grad_m[y] + value[8:56] * image_ref[1, y]

    def step_two(y, image):
        value = (
            residual(1, y, 16, p2_ref[y, pl.ds(8, 48), :])
            + 2.0 * late[y, pl.ds(8, 48), :]
            + image
            - later[y, pl.ds(16, 48), :]
        )
        grad_m[y] = grad_m[y] + value * image_ref[0, y]
        later[y, pl.ds(16, 48), :] = value

    sy = flux_pass(scaled, weights, fluxes, 8, 64, factors, cross(2, 8))
    cross_last(2, 8, sy)
    divergence_pass(fluxes, 64, factors, step_three)

    def rescale(y, carry):
        scaled[y + 4, pl.ds(lead + 8, 64), :] = modulus[y, pl.ds(8, 64), :] * late[y]
        return carry

    lax.fori_loop(0, ay, rescale, 0, unroll=2)
    sy = flux_pass(scaled, weights, fluxes, 16, 48, factors, cross(1, 0))
    cross_last(1, 0, sy)
    divergence_pass(fluxes, 48, factors, step_two)

    def rescale_last(y, carry):
        scaled[y + 4, pl.ds(lead + 16, 48), :] = modulus[y, pl.ds(16, 48), :] * later[y, pl.ds(16, 48), :]
        return carry

    lax.fori_loop(0, ay, rescale_last, 0, unroll=2)

    def last_slopes(y, carry):
        cross(0, 0)(y, *slopes_at(scaled, y, 16, 48, factors))
        return carry

    lax.fori_loop(0, ay, last_slopes, 0, unroll=2)
    cross_last(0, 0, slope_y(scaled, ay, 16, 48))

    first_row = at_ref[2]

    def blank(row, carry):
        column_ref[row] = jnp.zeros(column_ref.shape[1:], F32)
        return carry

    lax.fori_loop(0, first_row, blank, 0)
    lax.fori_loop(first_row + ay, 2 * shots, blank, 0)

    def place(y, carry):
        before = pltpu.roll(qb[y, pl.ds(6, gx), :], 1, 1)
        total = qh[y, pl.ds(6, gx), :] + before
        total = total + qy[y, pl.ds(6, gx), :] + qy[y + 1, pl.ds(6, gx), :]
        total = total + qx[y, pl.ds(9, gx), :] + qx[y, pl.ds(10, gx), :]
        column_ref[first_row + y, pl.ds(0, gx), :] = grad_m[y, pl.ds(6, gx), :]
        column_ref[first_row + y, pl.ds(gx, gx), :] = (-0.5 * tap_square) * total
        return carry

    lax.fori_loop(0, ay, place, 0, unroll=2)


def adjoint_waves(at, fields, images, back, front, seen, modulus, weights, slopes):
    near = pltpu.VMEM((ay, 48, nz), F32)
    return pl.pallas_call(
        adjoint_kernel,
        out_shape=jax.ShapeDtypeStruct((2 * shots, 2 * gx, nz), F32),
        in_specs=[scalars] + whole(16),
        out_specs=whole(1)[0],
        scratch_shapes=[
            padded,
            pltpu.VMEM((ay, dom, nz), F32),
            pltpu.VMEM((ay, 64, nz), F32),
            near,
            *flux_shapes,
            near,
            pltpu.VMEM((ay + 1, 48, nz), F32),
            near,
            near,
            pltpu.VMEM((dom, nz), F32),
        ],
        compiler_params=vmem,
        name="adjoint_waves",
    )(at, *fields, images, back, front, seen, modulus, *weights, *slopes)


def chain_kernel(at_ref, got_ref, out_ref, grad_ref):
    brick = at_ref[1]
    row = lax.broadcasted_iota(jnp.int32, (gx, nz), 0)
    fine = ((row >= 2) | (brick > 0)) & ((row < gx - 2) | (brick < bricks - 1))
    for y in range(2):
        total = got_ref[0, y]
        for shot in range(1, shots):
            total = total + got_ref[shot, y]
        squashed = jax.nn.sigmoid(out_ref[0, y])
        bent = jnp.tanh(out_ref[1, y])
        buoyancy = jnp.exp(0.35 * bent)
        first = total[:gx] * 0.09 * squashed * (1.0 - squashed)
        second = total[gx:] * buoyancy * 0.35 * (1.0 - bent * bent)
        grad_ref[y, 0] = jnp.where(fine, first, 0.0).astype(BF16)
        grad_ref[y, 1] = jnp.where(fine, second, 0.0).astype(BF16)


def chain(at, got, output):
    return pl.pallas_call(
        chain_kernel,
        out_shape=jax.ShapeDtypeStruct((2, 2, gx, nz), BF16),
        in_specs=[scalars] + whole(2),
        out_specs=whole(1)[0],
        compiler_params=vmem,
        name="chain",
    )(at, got, output)


def spread_kernel(at_ref, lo_ref, mid_ref, hi_ref, hid_ref, s1, s2):
    shot, brick = at_ref[0], at_ref[1]
    y_fine = (shot > 0, True, shot < shots - 1)

    def spread(x, carry):
        x_fine = ((x >= 1) | (brick > 0)) & ((x < bx + 1) | (brick < bricks - 1))
        for y, (ref, row, part) in enumerate(((lo_ref, 1, 0), (mid_ref, 0, 1), (mid_ref, 1, 1), (hi_ref, 0, 2))):
            value = jnp.where(x_fine & y_fine[part], ref[row, x + 3].astype(F32), 0.0)
            hidden = hid_ref[x + 2, pl.ds(y * 16, 16), :].astype(F32)
            for k in range(3):
                s1[x, pl.ds(y * 48 + k * 16, 16), :] = lane_shift(value, k).astype(BF16)
                s2[x, pl.ds(y * 48 + k * 16, 16), :] = lane_shift(hidden, k).astype(BF16)
        return carry

    lax.fori_loop(0, bx + 2, spread, 0, unroll=2)


def spread_fields(at, lo, mid, hi, hidden):
    shape = jax.ShapeDtypeStruct((bx + 2, 192, nz), BF16)
    return pl.pallas_call(
        spread_kernel,
        out_shape=(shape, shape),
        in_specs=[scalars] + whole(4),
        out_specs=tuple(whole(2)),
        compiler_params=vmem,
        cost_estimate=cost(3),
        name="spread_fields",
    )(at, lo, mid, hi, hidden)


def kernel_grads_kernel(
    at_ref, glo_ref, gmid_ref, ghi_ref, hid_ref, s1, s2, w3_ref, s4, kernel_ref, grads, own, s3, inner
):
    shot, brick = at_ref[0], at_ref[1]
    y_fine = (shot > 0, True, shot < shots - 1)
    grads[:, pl.ds(gx, 12), :] = jnp.zeros((12, 12, nz), F32)
    own[...] = jnp.zeros(own.shape, F32)
    for part, ref in enumerate((glo_ref, gmid_ref, ghi_ref)):
        for row in range(2):
            for channel in range(2):
                value = jnp.where(y_fine[part], ref[row, channel].astype(F32), 0.0)
                grads[(2 * part + row) * 2 + channel, pl.ds(0, gx), :] = value
                if part == 1:
                    own[:, channel * 2 + row, :] = value[2 : bx + 2]

    def hidden_grad(block, carry):
        for plane in range(12):
            value = grads[plane, pl.ds(8 * block, 16), :]
            for k in range(3):
                s3[pl.ds((plane * 3 + k) * 16, 16), :] = lane_shift(value, k).astype(BF16)
        acc = jnp.dot(w3_ref[...], s3[...], preferred_element_type=F32)
        for xo in range(8):
            x = 8 * block + xo
            x_fine = ((x >= 1) | (brick > 0)) & ((x < bx + 1) | (brick < bricks - 1))
            for y in range(4):
                fine = x_fine
                if y == 0:
                    fine = fine & (shot > 0)
                if y == 3:
                    fine = fine & (shot < shots - 1)
                hidden = hid_ref[jnp.minimum(x + 2, bx + 5), pl.ds(y * 16, 16), :].astype(F32)
                start = (xo * 4 + y) * 16
                value = acc[start : start + 16] * (1.0 - hidden * hidden)
                value = jnp.where(fine, value, 0.0).astype(BF16)
                if y in (1, 2):
                    inner[x, pl.ds((y - 1) * 16, 16), :] = value
                wide = value.astype(F32)
                for k in range(3):
                    s4[x, pl.ds(y * 48 + k * 16, 16), :] = lane_shift(wide, k).astype(BF16)
        return carry

    lax.fori_loop(0, 5, hidden_grad, 0)

    def kernel_grad(x, carry):
        first, second = carry
        contract = (((1,), (1,)), ((), ()))
        first = first + lax.dot_general(
            inner[x + 1], s1[pl.ds(x, 3)].reshape(576, nz), contract, preferred_element_type=F32
        )
        second = second + lax.dot_general(
            own[x].astype(BF16), s2[pl.ds(x, 3)].reshape(576, nz), contract, preferred_element_type=F32
        )
        return first, second

    first, second = lax.fori_loop(
        0, bx, kernel_grad, (jnp.zeros((32, 576), F32), jnp.zeros((8, 576), F32)), unroll=4
    )
    kernel_ref[...] = jnp.zeros(kernel_ref.shape, F32)
    for dx in range(3):
        start = dx * 192
        one = first[:16, start : start + 144] + first[16:, start + 48 : start + 192]
        for channel in range(2):
            row = channel * 2
            two = (
                second[row : row + 1, start : start + 144]
                + second[row + 1 : row + 2, start + 48 : start + 192]
            )
            place = dx * 2 * 18 + 16 + channel
            kernel_ref[pl.ds(place, 1), :] = two[:, :128]
            kernel_ref[pl.ds(place + 18, 1), pl.ds(0, 16)] = two[:, 128:]
        kernel_ref[pl.ds(dx * 36, 16), :] = one[:, :128]
        kernel_ref[pl.ds(dx * 36 + 18, 16), pl.ds(0, 16)] = one[:, 128:]


def kernel_grads(at, glo, gmid, ghi, hidden, s1, s2, w3):
    return pl.pallas_call(
        kernel_grads_kernel,
        out_shape=(
            jax.ShapeDtypeStruct((40, 192, nz), BF16),
            jax.ShapeDtypeStruct((128, nz), F32),
        ),
        in_specs=[scalars] + whole(7),
        out_specs=tuple(whole(2)),
        scratch_shapes=[
            pltpu.VMEM((12, 48, nz), F32),
            pltpu.VMEM((bx, 8, nz), F32),
            pltpu.VMEM((576, nz), BF16),
            pltpu.VMEM((40, 32, nz), BF16),
        ],
        compiler_params=vmem,
        name="kernel_grads",
    )(at, glo, gmid, ghi, hidden, s1, s2, w3)


def latent_grad_kernel(s4, w4_ref, latent_ref):
    def latent_grad(block, carry):
        rows = s4[pl.ds(4 * block, 6)].reshape(6 * 192, nz)
        acc = jnp.dot(w4_ref[...], rows, preferred_element_type=F32)
        latent_ref[pl.ds(4 * block, 4)] = acc.reshape(4, 32, nz)
        return carry

    lax.fori_loop(0, bx // 4, latent_grad, 0)


def latent_grads(s4, w4):
    return pl.pallas_call(
        latent_grad_kernel,
        out_shape=jax.ShapeDtypeStruct((bx, 32, nz), F32),
        in_specs=whole(2),
        out_specs=whole(1)[0],
        compiler_params=vmem,
        cost_estimate=cost(4),
        name="latent_grads",
    )(s4, w4)


def column_codes(x_in, y_in, order):
    if order == "xykc":
        x, y, k, c = np.meshgrid(*map(np.arange, (x_in, y_in, 3, 16)), indexing="ij")
    else:
        y, c, k, x = np.meshgrid(*map(np.arange, (y_in, 2, 3, x_in)), indexing="ij")
    return np.stack([(8 * x + y).ravel(), (16 * k + c).ravel()]).astype(np.int32)


codes_1 = column_codes(4, 6, "xykc")
codes_2 = column_codes(8, 4, "xykc")
codes_3 = column_codes(16, 6, "yckx")
codes_4 = column_codes(6, 4, "xykc")


def expand(taps_ref, codes_ref, spare, flip):
    place = codes_ref[1:2]
    size = place.shape[1]
    rows = lax.broadcasted_iota(jnp.int32, (16, size), 0)
    picks = [jnp.where(place == rows + 16 * k, 1.0, 0.0).astype(BF16) for k in range(3)]
    for pair in range(9):
        total = None
        for k in range(3):
            q = 3 * pair + k
            term = jnp.dot(taps_ref[26 - q if flip else q], picks[k], preferred_element_type=F32)
            total = term if total is None else total + term
        spare[pair, :, pl.ds(0, size)] = total


def fill_blocks(out_ref, codes_ref, spare, x_out, y_out):
    code = codes_ref[0:1]
    size = code.shape[1]
    same = lax.broadcasted_iota(jnp.int32, (16, size), 0) * 0 + code
    for xo in range(x_out):
        for y in range(y_out):
            block = jnp.zeros((16, size), F32)
            for pair in range(9):
                wanted = (xo + pair // 3) * 8 + y + pair % 3
                block = jnp.where(same == wanted, spare[pair, :, pl.ds(0, size)], block)
            out_ref[pl.ds((xo * y_out + y) * 16, 16), :] = block.astype(BF16)


def forward_bands_kernel(in_ref, out_taps_ref, codes_1_ref, codes_2_ref, w1_ref, w2_ref, spare, rows):
    expand(in_ref, codes_1_ref, spare, False)
    fill_blocks(w1_ref, codes_1_ref, spare, 2, 4)
    expand(out_taps_ref, codes_2_ref, spare, False)
    size = codes_2_ref.shape[1]
    code = codes_2_ref[0:1] - 8 * lax.broadcasted_iota(jnp.int32, (6, size), 0)
    for channel in range(2):
        for y in range(2):
            block = jnp.zeros((6, size), F32)
            for pair in range(9):
                wanted = (pair // 3) * 8 + y + pair % 3
                block = jnp.where(code == wanted, spare[pair, channel : channel + 1, :], block)
            rows[pl.ds((channel * 2 + y) * 6, 6), :] = block
    w2_ref[...] = rows[...].astype(BF16)


def backward_bands_kernel(in_ref, out_taps_ref, codes_3_ref, codes_4_ref, w3_ref, w4_ref, spare):
    expand(out_taps_ref, codes_3_ref, spare, True)
    fill_blocks(w3_ref, codes_3_ref, spare, 8, 4)
    expand(in_ref, codes_4_ref, spare, True)
    fill_blocks(w4_ref, codes_4_ref, spare, 4, 2)


def forward_bands(taps_in, taps_out):
    return pl.pallas_call(
        forward_bands_kernel,
        out_shape=(
            jax.ShapeDtypeStruct((128, 1152), BF16),
            jax.ShapeDtypeStruct((24, 1536), BF16),
        ),
        in_specs=whole(4),
        out_specs=tuple(whole(2)),
        scratch_shapes=[pltpu.VMEM((9, 16, 1536), F32), pltpu.VMEM((24, 1536), F32)],
        compiler_params=vmem,
        cost_estimate=cost(3),
        name="forward_bands",
    )(taps_in, taps_out, codes_1, codes_2)


def backward_bands(taps_in, taps_out):
    return pl.pallas_call(
        backward_bands_kernel,
        out_shape=(
            jax.ShapeDtypeStruct((512, 576), BF16),
            jax.ShapeDtypeStruct((128, 1152), BF16),
        ),
        in_specs=whole(4),
        out_specs=tuple(whole(2)),
        scratch_shapes=[pltpu.VMEM((9, 16, 1152), F32)],
        compiler_params=vmem,
        cost_estimate=cost(4),
        name="backward_bands",
    )(taps_in, taps_out, codes_3, codes_4)


def both_ways(ahead, behind, axis):
    count = lax.axis_size(axis)
    forward = [(i, (i + 1) % count) for i in range(count)]
    backward_ = [(target, source) for source, target in forward]
    return lax.ppermute(ahead, axis, forward), lax.ppermute(behind, axis, backward_)


def per_device(latent, conv_in, conv_out, source_field, observed, aperture, receivers):
    shot = lax.axis_index("shot")
    brick = lax.axis_index("brick")
    at = jnp.stack([shot, brick, aperture[0]]).astype(jnp.int32)
    taps_out = jnp.pad(conv_out, ((0, 0), (0, 14), (0, 0)))
    w1, w2 = forward_bands(conv_in, taps_out)
    w3, w4 = backward_bands(conv_in.transpose(0, 2, 1), taps_out.transpose(0, 2, 1))

    tile = jnp.transpose(latent, (2, 1, 0, 3))
    from_low, from_high = both_ways(tile[:, bx - 4 :], tile[:, :4], "brick")
    mid = jnp.concatenate([from_low, tile, from_high], axis=1)
    lo, hi = both_ways(mid, mid, "shot")
    source = jnp.transpose(source_field[0], (1, 0, 2))
    plo, phi = both_ways(source[:, bx - rim :], source[:, :rim], "brick")
    seen = receiver_fields(at, receivers[0], observed[0])

    coefficients, output, hidden = generator(at, lo, mid, hi, w1, w2)
    coefficients, plo, phi = lax.optimization_barrier((coefficients, plo, phi))
    sent = jnp.broadcast_to(coefficients[None], (shots, 2, 2, bx, nz))
    column = lax.all_to_all(sent, "shot", 0, 0, tiled=True)
    column, seen, w3, w4 = lax.optimization_barrier((column, seen, w3, w4))
    window, ahead, behind = take_window(at, column.reshape(2 * shots, 2, bx, nz))
    clo, chi = both_ways(ahead, behind, "brick")
    p1, p2, p3, p4, images, ahead, behind, modulus, *weights = forward_waves(
        at, window, clo, chi, source, plo, phi
    )
    back, front = both_ways(ahead, behind, "brick")
    slopes = wave_slopes(p1, p2, p3)
    back, front, slopes = lax.optimization_barrier((back, front, slopes))
    grads = adjoint_waves(at, (p2, p3, p4), images, back, front, seen, modulus, weights, slopes)
    got = lax.all_to_all(grads, "shot", 0, 0, tiled=True)
    s1, s2 = spread_fields(at, lo, mid, hi, hidden)
    got, s1, s2 = lax.optimization_barrier((got, s1, s2))
    got = got.reshape(shots, 2, 2 * gx, nz)
    grad_output = chain(at, got, output)
    glo, ghi = both_ways(grad_output, grad_output, "shot")
    s4, kernels = kernel_grads(at, glo, grad_output, ghi, hidden, s1, s2, w3)
    grad_latent = latent_grads(s4, w4)
    grad_latent = jnp.transpose(grad_latent.reshape(bx, 2, 16, nz), (2, 0, 1, 3))

    everyone = ("shot", "brick")
    slices = lax.all_to_all(kernels, everyone, 0, 0, tiled=True)
    mine = jnp.sum(slices, axis=0, keepdims=True)
    summed = lax.all_to_all(jnp.broadcast_to(mine, (128, nz)), everyone, 0, 0, tiled=True)
    folded = summed[:108].reshape(3, 2, 18, nz).transpose(0, 2, 1, 3).reshape(3, 18, 256)[:, :, :144]
    folded = folded.reshape(3, 18, 9, 16).transpose(0, 2, 1, 3).reshape(27, 18, 16)
    return (grad_latent, folded[:, :16], folded[:, 16:])


def solution(mesh):
    placed = (
        P(None, "brick", "shot", None),
        P(),
        P(),
        P("shot", "brick", None, None),
        P("shot", None, None),
        P("shot"),
        P("shot", None, None),
    )
    return jax.shard_map(
        per_device,
        mesh=mesh,
        in_specs=placed,
        out_specs=(P(None, "brick", "shot", None), P(), P()),
        check_vma=False,
    )
```

```python
import jax
import jax.numpy as jnp
import numpy as np
from jax import lax
from jax.experimental import pallas as pl
from jax.experimental.pallas import tpu as pltpu
from jax.sharding import PartitionSpec as P

F32 = jnp.float32
BF16 = jnp.bfloat16
stencil_taps = (1225.0 / 1024.0, -245.0 / 3072.0, 49.0 / 5120.0, -5.0 / 7168.0)
ratios = tuple(tap / stencil_taps[0] for tap in stencil_taps)
tap_square = stencil_taps[0] ** 2
misfit_weight = 16.0

bricks, shots = 8, 16
bx = 32
ay = 16
nz = 128
rim = 24
dom = bx + 2 * rim
lead = 8
xpad = dom + 24
ypad = ay + 8
gx = bx + 4
vmem = pltpu.CompilerParams(vmem_limit_bytes=24 * 1024 * 1024)


def cost(microseconds):
    return pl.CostEstimate(flops=0, bytes_accessed=int(microseconds * 3e6), transcendentals=0)


def whole(count):
    return [pl.BlockSpec(memory_space=pltpu.VMEM)] * count


scalars = pl.BlockSpec(memory_space=pltpu.SMEM)


def lane_index():
    return lax.broadcasted_iota(jnp.int32, (1, nz), 1)


def lane_shift(value, offset):
    if offset == 1:
        return value
    lane = lax.broadcasted_iota(jnp.int32, value.shape, 1)
    if offset == 0:
        return jnp.where(lane == 0, 0.0, pltpu.roll(value, 1, 1))
    return jnp.where(lane == nz - 1, 0.0, pltpu.roll(value, nz - 1, 1))


def generator_kernel(
    at_ref, lo_ref, mid_ref, hi_ref, w1_ref, w2_ref, coef_ref, out_ref, hid_ref, s1, s2
):
    shot, brick = at_ref[0], at_ref[1]
    y_fine = (shot > 0, True, shot < shots - 1)

    def spread(x, carry):
        x_fine = ((x >= 4) | (brick > 0)) & ((x < bx + 4) | (brick < bricks - 1))
        for part, ref in enumerate((lo_ref, mid_ref, hi_ref)):
            fine = x_fine & y_fine[part]
            for row in range(2):
                value = jnp.where(fine, ref[row, x].astype(F32), 0.0)
                for k in range(3):
                    s1[x, pl.ds((2 * part + row) * 48 + k * 16, 16), :] = lane_shift(
                        value, k
                    ).astype(BF16)
        return carry

    lax.fori_loop(0, bx + 8, spread, 0, unroll=4)
    last_block = (bx + 6) // 2 - 1

    def first_conv(block, before):
        before = jnp.tanh(before)
        for xo in range(2):
            x = jnp.maximum(2 * block - 2, 0) + xo
            x_fine = ((x >= 3) | (brick > 0)) & ((x < bx + 3) | (brick < bricks - 1))
            for y in range(4):
                fine = x_fine
                if y == 0:
                    fine = fine & (shot > 0)
                if y == 3:
                    fine = fine & (shot < shots - 1)
                start = (xo * 4 + y) * 16
                value = jnp.where(fine, before[start : start + 16], 0.0).astype(BF16)
                hid_ref[x, pl.ds(y * 16, 16), :] = value
                wide = value.astype(F32)
                for k in range(3):
                    s2[x, pl.ds(y * 48 + k * 16, 16), :] = lane_shift(wide, k).astype(BF16)
        rows = s1[pl.ds(2 * jnp.minimum(block, last_block), 4)].reshape(4 * 288, nz)
        return jnp.dot(w1_ref[...], rows, preferred_element_type=F32)

    lax.fori_loop(0, last_block + 2, first_conv, jnp.zeros((128, nz), F32))

    for block in range(gx // 6):
        rows = s2[pl.ds(6 * block, 8)].reshape(8 * 192, nz)
        acc = jnp.dot(w2_ref[...], rows, preferred_element_type=F32)
        for channel in range(2):
            for y in range(2):
                start = (channel * 2 + y) * 6
                out_ref[channel, y, pl.ds(6 * block, 6), :] = acc[start : start + 6]
    for y in range(2):
        modulus = 0.03 + 0.09 * jax.nn.sigmoid(out_ref[0, y, pl.ds(2, bx), :])
        buoyancy = jnp.exp(0.35 * jnp.tanh(out_ref[1, y, pl.ds(2, bx), :]))
        coef_ref[y, 0] = modulus
        coef_ref[y, 1] = buoyancy


def generator(at, lo, mid, hi, w1, w2):
    return pl.pallas_call(
        generator_kernel,
        out_shape=(
            jax.ShapeDtypeStruct((2, 2, bx, nz), F32),
            jax.ShapeDtypeStruct((2, 2, gx, nz), F32),
            jax.ShapeDtypeStruct((bx + 6, 64, nz), BF16),
        ),
        in_specs=[scalars] + whole(5),
        out_specs=tuple(whole(3)),
        scratch_shapes=[
            pltpu.VMEM((bx + 8, 288, nz), BF16),
            pltpu.VMEM((bx + 6, 192, nz), BF16),
        ],
        compiler_params=vmem,
        name="generator",
    )(at, lo, mid, hi, w1, w2)


def receiver_kernel(at_ref, cell_ref, seen_ref, out_ref, hot, spread):
    brick, first_row = at_ref[1], at_ref[2]
    count = cell_ref.shape[1]
    x = cell_ref[0:1] - brick * bx + rim
    row_of = jnp.where((x >= 0) & (x < dom), (cell_ref[1:2] - first_row) * dom + x, -1)
    z = cell_ref[2:3]

    def mark(chunk, carry):
        rows = chunk * 16 + lax.broadcasted_iota(jnp.int32, (16, count), 0)
        hot[pl.ds(chunk * 16, 16), :] = jnp.where(rows == row_of, 1.0, 0.0).astype(BF16)
        return carry

    lax.fori_loop(0, ay * dom // 16, mark, 0)
    parts = [jnp.ones((1, count), F32)]
    for step in range(3):
        value = seen_ref[step : step + 1]
        high = value.astype(BF16).astype(F32)
        parts += [high, value - high]

    def place(chunk, carry):
        same = chunk * 16 + lax.broadcasted_iota(jnp.int32, (16, count), 0) == z
        for index, part in enumerate(parts):
            spread[pl.ds(index * nz + chunk * 16, 16), :] = jnp.where(same, part, 0.0).astype(BF16)
        return carry

    lax.fori_loop(0, nz // 16, place, 0)
    size = 256

    def multiply(chunk, carry):
        left = hot[pl.ds(chunk * size, size), :]
        for field in range(4):
            first = 0 if field == 0 else (2 * field - 1) * nz
            right = spread[pl.ds(first, nz if field == 0 else 2 * nz), :]
            acc = lax.dot_general(
                left, right, (((1,), (1,)), ((), ())), preferred_element_type=F32
            )
            if field:
                acc = acc[:, :nz] + acc[:, nz:]
            out_ref[field, pl.ds(chunk * size, size), :] = acc
        return carry

    lax.fori_loop(0, ay * dom // size, multiply, 0)


def receiver_fields(at, cells, seen):
    count = cells.shape[1]
    return pl.pallas_call(
        receiver_kernel,
        out_shape=jax.ShapeDtypeStruct((4, ay * dom, nz), F32),
        in_specs=[scalars] + whole(2),
        out_specs=whole(1)[0],
        scratch_shapes=[
            pltpu.VMEM((ay * dom, count), BF16),
            pltpu.VMEM((7 * nz, count), BF16),
        ],
        compiler_params=vmem,
        cost_estimate=cost(9),
        name="receiver_fields",
    )(at, cells, seen)


def lane_factors():
    lane = lane_index()
    last = lane == nz - 1
    upper = [jnp.where((lane <= nz - 1 - t) | last, ratios[t - 1], 0.0) for t in range(1, 5)]
    lower = [jnp.where(lane >= t - 1, ratios[t - 1], 0.0) for t in range(1, 5)]
    above = [jnp.where(lane <= nz - t, ratios[t - 1], 0.0) for t in range(1, 5)]
    return last, upper, lower, above


def turn(value, shift):
    shift = shift % nz
    return value if shift == 0 else pltpu.roll(value, shift, 1)


def differences(get):
    total = None
    for t in range(1, 5):
        upper, lower = get(t)
        term = upper - lower
        if t > 1:
            term = ratios[t - 1] * term
        total = term if total is None else total + term
    return total


def clear_sides(field):
    for y in (0, 1, 2, 3, ay + 4, ay + 5, ay + 6, ay + 7):
        field[y] = jnp.zeros(field.shape[1:], F32)


def clear_rims(flux_y):
    for j in (0, 1, 2, 20, 21, 22):
        flux_y[j] = jnp.zeros(flux_y.shape[1:], F32)


def halo_scale(at_ref):
    brick = at_ref[1]
    return (
        jnp.where(brick > 0, 1.0, 0.0).astype(F32),
        jnp.where(brick < bricks - 1, 1.0, 0.0).astype(F32),
    )


def window_kernel(at_ref, column_ref, win_ref, ahead_ref, behind_ref, message):
    first_row = at_ref[2]

    def body(y, carry):
        for channel in range(2):
            value = column_ref[first_row + y, channel]
            win_ref[y, channel] = value
            rounded = value.astype(BF16).astype(F32)
            rest = value - rounded
            for slot, (ref, near, further) in enumerate(((ahead_ref, 28, 12), (behind_ref, 0, 4))):
                place = (channel * 2 + slot) * 24
                message[pl.ds(place, 4), :] = rounded[near : near + 4]
                message[pl.ds(place + 4, 4), :] = rest[near : near + 4]
                message[pl.ds(place + 8, 16), :] = value[further : further + 16]
                ref[y, channel] = message[pl.ds(place, 24), :].astype(BF16)
        return carry

    lax.fori_loop(0, ay, body, 0, unroll=2)


def take_window(at, column):
    return pl.pallas_call(
        window_kernel,
        out_shape=(
            jax.ShapeDtypeStruct((ay, 2, bx, nz), F32),
            jax.ShapeDtypeStruct((ay, 2, 24, nz), BF16),
            jax.ShapeDtypeStruct((ay, 2, 24, nz), BF16),
        ),
        in_specs=[scalars] + whole(1),
        out_specs=tuple(whole(3)),
        scratch_shapes=[pltpu.VMEM((96, nz), F32)],
        compiler_params=vmem,
        name="take_window",
    )(at, column)


def slope_y(field, j, first, rows):
    return differences(
        lambda t: (
            field[j + 3 + t, pl.ds(lead + first, rows), :],
            field[j + 4 - t, pl.ds(lead + first, rows), :],
        )
    )


def slopes_at(field, y, first, rows, factors):
    value = field[y + 4, pl.ds(lead + first, rows), :]
    turned_up = [turn(value, -t) for t in range(1, 5)]
    turned_low = [turn(value, t - 1) for t in range(1, 5)]
    base, more = lead + first - 4, rows + 8
    sx = differences(
        lambda t: (
            field[y + 4, pl.ds(base + t, more), :],
            field[y + 4, pl.ds(base + 1 - t, more), :],
        )
    )
    sy = slope_y(field, y, first, rows)
    last, upper, lower, _ = factors
    up = sum(upper[t] * turned_up[t] for t in range(4))
    low = sum(lower[t] * turned_low[t] for t in range(4))
    slope = up - low
    return sx, sy, jnp.where(last, -low, slope), jnp.where(last, up, slope)


def flux_pass(field, weights, fluxes, first, rows, factors, also=None):
    wx, wy, wz, wzl = weights
    fx, fy, fh, fb = fluxes
    base, more = lead + first - 4, rows + 8

    def body(y, carry):
        sx, sy, here, before = slopes_at(field, y, first, rows, factors)
        fx[y, pl.ds(0, more), :] = wx[y, pl.ds(base, more), :] * sx
        fy[y + 3, pl.ds(0, rows), :] = wy[y, pl.ds(first, rows), :] * sy
        fh[y, pl.ds(0, rows), :] = wz[y, pl.ds(first, rows), :] * here
        fb[y, pl.ds(0, rows), :] = wzl[y, pl.ds(first, rows), :] * before
        if also is not None:
            also(y, sx, sy, here, before)
        return carry

    lax.fori_loop(0, ay, body, 0, unroll=2)
    sy = slope_y(field, ay, first, rows)
    fy[ay + 3, pl.ds(0, rows), :] = wy[ay, pl.ds(first, rows), :] * sy
    return sy


def divergence_pass(fluxes, rows, factors, consume):
    fx, fy, fh, fb = fluxes
    _, _, lower, above = factors

    def body(y, carry):
        here = fh[y, pl.ds(0, rows), :]
        before = fb[y, pl.ds(0, rows), :]
        turned_here = [turn(here, 1 - t) for t in range(1, 5)]
        turned_before = [turn(before, t) for t in range(1, 5)]
        total = differences(
            lambda t: (fx[y, pl.ds(3 + t, rows), :], fx[y, pl.ds(4 - t, rows), :])
        )
        total = total + differences(
            lambda t: (
                fy[y + t + 3, pl.ds(0, rows), :],
                fy[y - t + 4, pl.ds(0, rows), :],
            )
        )
        total = total + sum(above[t] * turned_here[t] for t in range(4))
        total = total - sum(lower[t] * turned_before[t] for t in range(4))
        consume(y, total)
        return carry

    lax.fori_loop(0, ay, body, 0, unroll=2)


weight_sizes = ((ay, dom + 16, nz), (ay + 1, dom, nz), (ay, dom, nz), (ay, dom, nz))
padded = pltpu.VMEM((ypad, xpad, nz), F32)
flux_shapes = [
    pltpu.VMEM((ay, 72, nz), F32),
    pltpu.VMEM((23, 64, nz), F32),
    pltpu.VMEM((ay, 64, nz), F32),
    pltpu.VMEM((ay, 64, nz), F32),
]


def forward_kernel(
    at_ref, win_ref, clo_ref, chi_ref, src_ref, plo_ref, phi_ref,
    p1_ref, p2_ref, p3_ref, p4_ref, image_ref, ahead_ref, behind_ref, modulus, wx, wy, wz, wzl,
    buoy, f1, f2, f3, fx, fy, fh, fb, message,
):
    factors = lane_factors()
    last = factors[0]
    weights = (wx, wy, wz, wzl)
    fluxes = (fx, fy, fh, fb)
    clear_rims(fy)
    for field in (buoy, f1, f2, f3):
        clear_sides(field)
    low, high = halo_scale(at_ref)
    half = 0.5 * tap_square

    def load(y, carry):
        for channel, ref, row, skip in ((0, modulus, y, 0), (1, buoy, y + 4, lead)):
            received = low * clo_ref[y, channel].astype(F32)
            ref[row, pl.ds(skip + 4, 16), :] = received[8:]
            ref[row, pl.ds(skip + 20, 4), :] = received[:4] + received[4:8]
            ref[row, pl.ds(skip + rim, bx), :] = win_ref[y, channel]
            received = high * chi_ref[y, channel].astype(F32)
            ref[row, pl.ds(skip + rim + bx, 4), :] = received[:4] + received[4:8]
            ref[row, pl.ds(skip + rim + bx + 4, 16), :] = received[8:]
        f1[y + 4, pl.ds(lead, rim), :] = low * plo_ref[y]
        f1[y + 4, pl.ds(lead + rim, bx), :] = src_ref[y]
        f1[y + 4, pl.ds(lead + rim + bx, rim), :] = high * phi_ref[y]
        return carry

    lax.fori_loop(0, ay, load, 0)

    def weigh(y, carry):
        inner = buoy[y + 4, pl.ds(lead, dom), :]
        ahead = pltpu.roll(inner, nz - 1, 1)
        value = buoy[y + 4, pl.ds(0, dom + 16), :]
        wx[y] = half * (value + buoy[y + 4, pl.ds(1, dom + 16), :])
        wy[y] = half * (buoy[y + 3, pl.ds(lead, dom), :] + inner)
        wz[y] = half * jnp.where(last, inner, inner + ahead)
        wzl[y] = half * jnp.where(last, ahead, inner + ahead)
        return carry

    lax.fori_loop(0, ay, weigh, 0, unroll=2)
    wy[ay] = half * buoy[ay + 3, pl.ds(lead, dom), :]

    def first_step(y, image):
        f2[y + 4, pl.ds(lead + 8, 64), :] = (
            2.0 * f1[y + 4, pl.ds(lead + 8, 64), :] + modulus[y, pl.ds(8, 64), :] * image
        )
        image_ref[0, y] = image[8:56]

    def second_step(y, image):
        value = (
            2.0 * f2[y + 4, pl.ds(lead + 12, 56), :]
            - f1[y + 4, pl.ds(lead + 12, 56), :]
            + modulus[y, pl.ds(12, 56), :] * image
        )
        f3[y + 4, pl.ds(lead + 12, 56), :] = value
        image_ref[1, y] = image[4:52]
        p3_ref[y] = value[4:52]
        p1_ref[y] = f1[y + 4, pl.ds(lead + 8, 64), :]
        p2_ref[y] = f2[y + 4, pl.ds(lead + 8, 64), :]

    def third_step(y, image):
        image_ref[2, y] = image
        value = (
            2.0 * f3[y + 4, pl.ds(lead + rim, bx), :]
            - f2[y + 4, pl.ds(lead + rim, bx), :]
            + modulus[y, pl.ds(rim, bx), :] * image[8:40]
        )
        p4_ref[y] = value

    def pack(y, ref, near, further, third):
        value = p4_ref[y, pl.ds(near, 7), :]
        rounded = value.astype(BF16).astype(F32)
        message[pl.ds(0, 7), :] = rounded
        message[pl.ds(7, 7), :] = value - rounded
        message[pl.ds(14, 13), :] = p4_ref[y, pl.ds(further, 13), :]
        message[pl.ds(27, 5), :] = f3[y + 4, pl.ds(lead + rim + third, 5), :]
        ref[y] = message[...].astype(BF16)

    def send(y, carry):
        pack(y, ahead_ref, 25, 12, 19)
        pack(y, behind_ref, 0, 7, 8)
        return carry

    flux_pass(f1, weights, fluxes, 8, 64, factors)
    divergence_pass(fluxes, 64, factors, first_step)
    flux_pass(f2, weights, fluxes, 12, 56, factors)
    divergence_pass(fluxes, 56, factors, second_step)
    flux_pass(f3, weights, fluxes, 16, 48, factors)
    divergence_pass(fluxes, 48, factors, third_step)
    lax.fori_loop(0, ay, send, 0)


def forward_waves(at, window, clo, chi, source, plo, phi):
    shapes = [(ay, 64, nz), (ay, 64, nz), (ay, 48, nz), (ay, bx, nz), (3, ay, 48, nz)]
    return pl.pallas_call(
        forward_kernel,
        out_shape=tuple(jax.ShapeDtypeStruct(shape, F32) for shape in shapes)
        + (jax.ShapeDtypeStruct((ay, 32, nz), BF16),) * 2
        + (jax.ShapeDtypeStruct((ay, dom, nz), F32),)
        + tuple(jax.ShapeDtypeStruct(shape, F32) for shape in weight_sizes),
        in_specs=[scalars] + whole(6),
        out_specs=tuple(whole(12)),
        scratch_shapes=[padded, padded, padded, padded, *flux_shapes, pltpu.VMEM((32, nz), F32)],
        compiler_params=vmem,
        name="forward_waves",
    )(at, window, clo, chi, source, plo, phi)


def slopes_kernel(p1_ref, p2_ref, p3_ref, sx_ref, sy_ref, sh_ref, sb_ref, field):
    factors = lane_factors()
    clear_sides(field)
    for index, (ref, first) in enumerate(((p1_ref, 8), (p2_ref, 8), (p3_ref, 16))):
        rows = ref.shape[1]

        def load(y, carry):
            field[y + 4, pl.ds(lead + first, rows), :] = ref[y]
            return carry

        lax.fori_loop(0, ay, load, 0)

        def body(y, carry):
            sx, sy, here, before = slopes_at(field, y, 16, 48, factors)
            sx_ref[index, y] = sx[:48]
            sy_ref[index, y] = sy
            sh_ref[index, y] = here
            sb_ref[index, y] = before
            return carry

        lax.fori_loop(0, ay, body, 0, unroll=2)
        sy_ref[index, ay] = slope_y(field, ay, 16, 48)


def wave_slopes(p1, p2, p3):
    shapes = [(3, ay, 48, nz), (3, ay + 1, 48, nz), (3, ay, 48, nz), (3, ay, 48, nz)]
    return pl.pallas_call(
        slopes_kernel,
        out_shape=tuple(jax.ShapeDtypeStruct(shape, F32) for shape in shapes),
        in_specs=whole(3),
        out_specs=tuple(whole(4)),
        scratch_shapes=[padded],
        compiler_params=vmem,
        cost_estimate=cost(6),
        name="wave_slopes",
    )(p1, p2, p3)


def adjoint_kernel(
    at_ref, p2_ref, p3_ref, p4_ref, image_ref, back_ref, front_ref, seen_ref,
    modulus, wx, wy, wz, wzl, px_ref, py_ref, ph_ref, pb_ref,
    column_ref,
    scaled, later, late, grad_m, fx, fy, fh, fb, qx, qy, qh, qb, far,
):
    factors = lane_factors()
    weights = (wx, wy, wz, wzl)
    fluxes = (fx, fy, fh, fb)
    clear_rims(fy)
    clear_sides(scaled)
    low, high = halo_scale(at_ref)

    def residual(step, y, first, value):
        rows = value.shape[0]
        start = pl.multiple_of(y * dom + first, 8)
        count = seen_ref[0, pl.ds(start, rows), :]
        total = seen_ref[step, pl.ds(start, rows), :]
        return misfit_weight * (count * value - total)

    far[...] = jnp.zeros(far.shape, F32)

    def seed(y, carry):
        late[y, pl.ds(8, 48), :] = p3_ref[y]
        received = low * back_ref[y].astype(F32)
        far[pl.ds(4, 13), :] = received[14:27]
        far[pl.ds(17, 7), :] = received[:7] + received[7:14]
        late[y, pl.ds(3, 5), :] = received[27:]
        far[pl.ds(rim, bx), :] = p4_ref[y]
        received = high * front_ref[y].astype(F32)
        far[pl.ds(rim + bx, 7), :] = received[:7] + received[7:14]
        far[pl.ds(rim + bx + 7, 13), :] = received[14:27]
        late[y, pl.ds(56, 5), :] = received[27:]
        error = residual(3, y, 0, far[...])
        later[y] = error
        scaled[y + 4, pl.ds(lead, dom), :] = modulus[y] * error
        grad_m[y] = error[16:64] * image_ref[2, y]
        return carry

    lax.fori_loop(0, ay, seed, 0)

    def cross(index, offset):
        def also(y, sx, sy, here, before):
            products = (
                (qx, sx[offset : offset + 48] * px_ref[index, y]),
                (qy, sy[offset : offset + 48] * py_ref[index, y]),
                (qh, here[offset : offset + 48] * ph_ref[index, y]),
                (qb, before[offset : offset + 48] * pb_ref[index, y]),
            )
            for ref, product in products:
                ref[y] = product if index == 2 else ref[y] + product

        return also

    def cross_last(index, offset, sy):
        product = sy[offset : offset + 48] * py_ref[index, ay]
        qy[ay] = product if index == 2 else qy[ay] + product

    def step_three(y, image):
        value = late[y]
        value = residual(2, y, 8, value) + 2.0 * later[y, pl.ds(8, 64), :] + image
        late[y] = value
        grad_m[y] = grad_m[y] + value[8:56] * image_ref[1, y]

    def step_two(y, image):
        value = (
            residual(1, y, 16, p2_ref[y, pl.ds(8, 48), :])
            + 2.0 * late[y, pl.ds(8, 48), :]
            + image
            - later[y, pl.ds(16, 48), :]
        )
        grad_m[y] = grad_m[y] + value * image_ref[0, y]
        later[y, pl.ds(16, 48), :] = value

    sy = flux_pass(scaled, weights, fluxes, 8, 64, factors, cross(2, 8))
    cross_last(2, 8, sy)
    divergence_pass(fluxes, 64, factors, step_three)

    def rescale(y, carry):
        scaled[y + 4, pl.ds(lead + 8, 64), :] = modulus[y, pl.ds(8, 64), :] * late[y]
        return carry

    lax.fori_loop(0, ay, rescale, 0, unroll=2)
    sy = flux_pass(scaled, weights, fluxes, 16, 48, factors, cross(1, 0))
    cross_last(1, 0, sy)
    divergence_pass(fluxes, 48, factors, step_two)

    def rescale_last(y, carry):
        scaled[y + 4, pl.ds(lead + 16, 48), :] = modulus[y, pl.ds(16, 48), :] * later[y, pl.ds(16, 48), :]
        return carry

    lax.fori_loop(0, ay, rescale_last, 0, unroll=2)

    def last_slopes(y, carry):
        cross(0, 0)(y, *slopes_at(scaled, y, 16, 48, factors))
        return carry

    lax.fori_loop(0, ay, last_slopes, 0, unroll=2)
    cross_last(0, 0, slope_y(scaled, ay, 16, 48))

    first_row = at_ref[2]

    def blank(row, carry):
        column_ref[row] = jnp.zeros(column_ref.shape[1:], F32)
        return carry

    lax.fori_loop(0, first_row, blank, 0)
    lax.fori_loop(first_row + ay, 2 * shots, blank, 0)

    def place(y, carry):
        before = pltpu.roll(qb[y, pl.ds(6, gx), :], 1, 1)
        total = qh[y, pl.ds(6, gx), :] + before
        total = total + qy[y, pl.ds(6, gx), :] + qy[y + 1, pl.ds(6, gx), :]
        total = total + qx[y, pl.ds(9, gx), :] + qx[y, pl.ds(10, gx), :]
        column_ref[first_row + y, pl.ds(0, gx), :] = grad_m[y, pl.ds(6, gx), :]
        column_ref[first_row + y, pl.ds(gx, gx), :] = (-0.5 * tap_square) * total
        return carry

    lax.fori_loop(0, ay, place, 0, unroll=2)


def adjoint_waves(at, fields, images, back, front, seen, modulus, weights, slopes):
    near = pltpu.VMEM((ay, 48, nz), F32)
    return pl.pallas_call(
        adjoint_kernel,
        out_shape=jax.ShapeDtypeStruct((2 * shots, 2 * gx, nz), F32),
        in_specs=[scalars] + whole(16),
        out_specs=whole(1)[0],
        scratch_shapes=[
            padded,
            pltpu.VMEM((ay, dom, nz), F32),
            pltpu.VMEM((ay, 64, nz), F32),
            near,
            *flux_shapes,
            near,
            pltpu.VMEM((ay + 1, 48, nz), F32),
            near,
            near,
            pltpu.VMEM((dom, nz), F32),
        ],
        compiler_params=vmem,
        name="adjoint_waves",
    )(at, *fields, images, back, front, seen, modulus, *weights, *slopes)


def chain_kernel(at_ref, got_ref, out_ref, grad_ref):
    brick = at_ref[1]
    row = lax.broadcasted_iota(jnp.int32, (gx, nz), 0)
    fine = ((row >= 2) | (brick > 0)) & ((row < gx - 2) | (brick < bricks - 1))
    for y in range(2):
        total = got_ref[0, y]
        for shot in range(1, shots):
            total = total + got_ref[shot, y]
        squashed = jax.nn.sigmoid(out_ref[0, y])
        bent = jnp.tanh(out_ref[1, y])
        buoyancy = jnp.exp(0.35 * bent)
        first = total[:gx] * 0.09 * squashed * (1.0 - squashed)
        second = total[gx:] * buoyancy * 0.35 * (1.0 - bent * bent)
        grad_ref[y, 0] = jnp.where(fine, first, 0.0).astype(BF16)
        grad_ref[y, 1] = jnp.where(fine, second, 0.0).astype(BF16)


def chain(at, got, output):
    return pl.pallas_call(
        chain_kernel,
        out_shape=jax.ShapeDtypeStruct((2, 2, gx, nz), BF16),
        in_specs=[scalars] + whole(2),
        out_specs=whole(1)[0],
        compiler_params=vmem,
        name="chain",
    )(at, got, output)


def spread_kernel(at_ref, lo_ref, mid_ref, hi_ref, hid_ref, s1, s2):
    shot, brick = at_ref[0], at_ref[1]
    y_fine = (shot > 0, True, shot < shots - 1)

    def spread(x, carry):
        x_fine = ((x >= 1) | (brick > 0)) & ((x < bx + 1) | (brick < bricks - 1))
        for y, (ref, row, part) in enumerate(((lo_ref, 1, 0), (mid_ref, 0, 1), (mid_ref, 1, 1), (hi_ref, 0, 2))):
            value = jnp.where(x_fine & y_fine[part], ref[row, x + 3].astype(F32), 0.0)
            hidden = hid_ref[x + 2, pl.ds(y * 16, 16), :].astype(F32)
            for k in range(3):
                s1[x, pl.ds(y * 48 + k * 16, 16), :] = lane_shift(value, k).astype(BF16)
                s2[x, pl.ds(y * 48 + k * 16, 16), :] = lane_shift(hidden, k).astype(BF16)
        return carry

    lax.fori_loop(0, bx + 2, spread, 0, unroll=2)


def spread_fields(at, lo, mid, hi, hidden):
    shape = jax.ShapeDtypeStruct((bx + 2, 192, nz), BF16)
    return pl.pallas_call(
        spread_kernel,
        out_shape=(shape, shape),
        in_specs=[scalars] + whole(4),
        out_specs=tuple(whole(2)),
        compiler_params=vmem,
        cost_estimate=cost(3),
        name="spread_fields",
    )(at, lo, mid, hi, hidden)


contract_lanes = (((1,), (1,)), ((), ()))


def second_grads_kernel(gmid_ref, s2, second_ref, own):
    own[...] = jnp.zeros(own.shape, F32)
    for row in range(2):
        for channel in range(2):
            own[:, channel * 2 + row, :] = gmid_ref[row, channel].astype(F32)[2 : bx + 2]

    def kernel_grad(x, second):
        return second + lax.dot_general(
            own[x].astype(BF16), s2[pl.ds(x, 3)].reshape(576, nz), contract_lanes, preferred_element_type=F32
        )

    second_ref[...] = lax.fori_loop(0, bx, kernel_grad, jnp.zeros((8, 576), F32), unroll=4)


def second_grads(grad_output, s2):
    return pl.pallas_call(
        second_grads_kernel,
        out_shape=jax.ShapeDtypeStruct((8, 576), F32),
        in_specs=whole(2),
        out_specs=whole(1)[0],
        scratch_shapes=[pltpu.VMEM((bx, 8, nz), F32)],
        compiler_params=vmem,
        cost_estimate=cost(3),
        name="second_grads",
    )(grad_output, s2)


def first_grads_kernel(
    at_ref, glo_ref, gmid_ref, ghi_ref, hid_ref, second_ref, w3_ref, s1_any, inner_ref, kernel_ref, turned, s1, ready
):
    fetch = pltpu.make_async_copy(s1_any, s1, ready)
    fetch.start()
    shot, brick = at_ref[0], at_ref[1]
    y_fine = (shot > 0, True, shot < shots - 1)
    for part, ref in enumerate((glo_ref, gmid_ref, ghi_ref)):
        for row in range(2):
            for channel in range(2):
                value = jnp.where(y_fine[part], ref[row, channel].astype(F32), 0.0)
                value = jnp.concatenate([value, jnp.zeros((12, nz), F32)], axis=0)
                plane = (2 * part + row) * 2 + channel
                for k in range(3):
                    turned[plane * 3 + k] = lane_shift(value, k)

    def hidden_grad(block, carry):
        rows = turned[:, pl.ds(8 * block, 16), :].astype(BF16).reshape(576, nz)
        acc = jnp.dot(w3_ref[...], rows, preferred_element_type=F32)
        for xo in range(8):
            x = 8 * block + xo
            x_fine = ((x >= 1) | (brick > 0)) & ((x < bx + 1) | (brick < bricks - 1))
            hidden = hid_ref[jnp.minimum(x + 2, bx + 5)].astype(F32)
            value = acc[xo * 64 : xo * 64 + 64] * (1.0 - hidden * hidden)
            for y in range(4):
                fine = x_fine
                if y == 0:
                    fine = fine & (shot > 0)
                if y == 3:
                    fine = fine & (shot < shots - 1)
                inner_ref[x, pl.ds(y * 16, 16), :] = jnp.where(
                    fine, value[y * 16 : y * 16 + 16], 0.0
                ).astype(BF16)
        return carry

    lax.fori_loop(0, 5, hidden_grad, 0)
    fetch.wait()

    def kernel_grad(x, first):
        return first + lax.dot_general(
            inner_ref[x + 1, pl.ds(16, 32), :],
            s1[pl.ds(x, 3)].reshape(576, nz),
            contract_lanes,
            preferred_element_type=F32,
        )

    first = lax.fori_loop(0, bx, kernel_grad, jnp.zeros((32, 576), F32), unroll=4)
    second = second_ref[...]
    kernel_ref[...] = jnp.zeros(kernel_ref.shape, F32)
    for dx in range(3):
        start = dx * 192
        one = first[:16, start : start + 144] + first[16:, start + 48 : start + 192]
        for channel in range(2):
            row = channel * 2
            two = (
                second[row : row + 1, start : start + 144]
                + second[row + 1 : row + 2, start + 48 : start + 192]
            )
            place = dx * 2 * 18 + 16 + channel
            kernel_ref[pl.ds(place, 1), :] = two[:, :128]
            kernel_ref[pl.ds(place + 18, 1), pl.ds(0, 16)] = two[:, 128:]
        kernel_ref[pl.ds(dx * 36, 16), :] = one[:, :128]
        kernel_ref[pl.ds(dx * 36 + 18, 16), pl.ds(0, 16)] = one[:, 128:]


def first_grads(at, glo, gmid, ghi, hidden, second, w3, s1):
    return pl.pallas_call(
        first_grads_kernel,
        out_shape=(
            jax.ShapeDtypeStruct((40, 64, nz), BF16),
            jax.ShapeDtypeStruct((128, nz), F32),
        ),
        in_specs=[scalars] + whole(6) + [pl.BlockSpec(memory_space=pl.ANY)],
        out_specs=tuple(whole(2)),
        scratch_shapes=[
            pltpu.VMEM((36, 48, nz), F32),
            pltpu.VMEM((bx + 2, 192, nz), BF16),
            pltpu.SemaphoreType.DMA,
        ],
        compiler_params=vmem,
        name="first_grads",
    )(at, glo, gmid, ghi, hidden, second, w3, s1)


def latent_grad_kernel(inner_ref, w4_ref, latent_ref, s4):
    def spread(x, carry):
        for y in range(4):
            value = inner_ref[x, pl.ds(y * 16, 16), :].astype(F32)
            for k in range(3):
                s4[x, pl.ds(y * 48 + k * 16, 16), :] = lane_shift(value, k).astype(BF16)
        return carry

    lax.fori_loop(0, bx + 2, spread, 0, unroll=2)

    def latent_grad(block, carry):
        rows = s4[pl.ds(4 * block, 6)].reshape(6 * 192, nz)
        acc = jnp.dot(w4_ref[...], rows, preferred_element_type=F32)
        latent_ref[pl.ds(4 * block, 4)] = acc.reshape(4, 32, nz)
        return carry

    lax.fori_loop(0, bx // 4, latent_grad, 0)


def latent_grads(inner, w4):
    return pl.pallas_call(
        latent_grad_kernel,
        out_shape=jax.ShapeDtypeStruct((bx, 32, nz), F32),
        in_specs=whole(2),
        out_specs=whole(1)[0],
        scratch_shapes=[pltpu.VMEM((bx + 2, 192, nz), BF16)],
        compiler_params=vmem,
        cost_estimate=cost(4),
        name="latent_grads",
    )(inner, w4)


def column_codes(x_in, y_in, order):
    if order == "xykc":
        x, y, k, c = np.meshgrid(*map(np.arange, (x_in, y_in, 3, 16)), indexing="ij")
    else:
        y, c, k, x = np.meshgrid(*map(np.arange, (y_in, 2, 3, x_in)), indexing="ij")
    return np.stack([(8 * x + y).ravel(), (16 * k + c).ravel()]).astype(np.int32)


codes_1 = column_codes(4, 6, "xykc")
codes_2 = column_codes(8, 4, "xykc")
codes_3 = column_codes(16, 6, "yckx")
codes_4 = column_codes(6, 4, "xykc")


def expand(taps_ref, codes_ref, spare, flip):
    place = codes_ref[1:2]
    size = place.shape[1]
    rows = lax.broadcasted_iota(jnp.int32, (16, size), 0)
    picks = [jnp.where(place == rows + 16 * k, 1.0, 0.0).astype(BF16) for k in range(3)]
    for pair in range(9):
        total = None
        for k in range(3):
            q = 3 * pair + k
            term = jnp.dot(taps_ref[26 - q if flip else q], picks[k], preferred_element_type=F32)
            total = term if total is None else total + term
        spare[pair, :, pl.ds(0, size)] = total


def fill_blocks(out_ref, codes_ref, spare, x_out, y_out):
    code = codes_ref[0:1]
    size = code.shape[1]
    same = lax.broadcasted_iota(jnp.int32, (16, size), 0) * 0 + code
    for xo in range(x_out):
        for y in range(y_out):
            block = jnp.zeros((16, size), F32)
            for pair in range(9):
                wanted = (xo + pair // 3) * 8 + y + pair % 3
                block = jnp.where(same == wanted, spare[pair, :, pl.ds(0, size)], block)
            out_ref[pl.ds((xo * y_out + y) * 16, 16), :] = block.astype(BF16)


def forward_bands_kernel(in_ref, out_taps_ref, codes_1_ref, codes_2_ref, w1_ref, w2_ref, spare, rows):
    expand(in_ref, codes_1_ref, spare, False)
    fill_blocks(w1_ref, codes_1_ref, spare, 2, 4)
    expand(out_taps_ref, codes_2_ref, spare, False)
    size = codes_2_ref.shape[1]
    code = codes_2_ref[0:1] - 8 * lax.broadcasted_iota(jnp.int32, (6, size), 0)
    for channel in range(2):
        for y in range(2):
            block = jnp.zeros((6, size), F32)
            for pair in range(9):
                wanted = (pair // 3) * 8 + y + pair % 3
                block = jnp.where(code == wanted, spare[pair, channel : channel + 1, :], block)
            rows[pl.ds((channel * 2 + y) * 6, 6), :] = block
    w2_ref[...] = rows[...].astype(BF16)


def backward_bands_kernel(in_ref, out_taps_ref, codes_3_ref, codes_4_ref, w3_ref, w4_ref, spare):
    expand(out_taps_ref, codes_3_ref, spare, True)
    fill_blocks(w3_ref, codes_3_ref, spare, 8, 4)
    expand(in_ref, codes_4_ref, spare, True)
    fill_blocks(w4_ref, codes_4_ref, spare, 4, 2)


def forward_bands(taps_in, taps_out):
    return pl.pallas_call(
        forward_bands_kernel,
        out_shape=(
            jax.ShapeDtypeStruct((128, 1152), BF16),
            jax.ShapeDtypeStruct((24, 1536), BF16),
        ),
        in_specs=whole(4),
        out_specs=tuple(whole(2)),
        scratch_shapes=[pltpu.VMEM((9, 16, 1536), F32), pltpu.VMEM((24, 1536), F32)],
        compiler_params=vmem,
        cost_estimate=cost(3),
        name="forward_bands",
    )(taps_in, taps_out, codes_1, codes_2)


def backward_bands(taps_in, taps_out):
    return pl.pallas_call(
        backward_bands_kernel,
        out_shape=(
            jax.ShapeDtypeStruct((512, 576), BF16),
            jax.ShapeDtypeStruct((128, 1152), BF16),
        ),
        in_specs=whole(4),
        out_specs=tuple(whole(2)),
        scratch_shapes=[pltpu.VMEM((9, 16, 1152), F32)],
        compiler_params=vmem,
        cost_estimate=cost(4),
        name="backward_bands",
    )(taps_in, taps_out, codes_3, codes_4)


def both_ways(ahead, behind, axis):
    count = lax.axis_size(axis)
    forward = [(i, (i + 1) % count) for i in range(count)]
    backward_ = [(target, source) for source, target in forward]
    return lax.ppermute(ahead, axis, forward), lax.ppermute(behind, axis, backward_)


def per_device(latent, conv_in, conv_out, source_field, observed, aperture, receivers):
    shot = lax.axis_index("shot")
    brick = lax.axis_index("brick")
    at = jnp.stack([shot, brick, aperture[0]]).astype(jnp.int32)
    taps_out = jnp.pad(conv_out, ((0, 0), (0, 14), (0, 0)))
    w1, w2 = forward_bands(conv_in, taps_out)
    w3, w4 = backward_bands(conv_in.transpose(0, 2, 1), taps_out.transpose(0, 2, 1))

    tile = jnp.transpose(latent, (2, 1, 0, 3))
    from_low, from_high = both_ways(tile[:, bx - 4 :], tile[:, :4], "brick")
    mid = jnp.concatenate([from_low, tile, from_high], axis=1)
    lo, hi = both_ways(mid, mid, "shot")
    source = jnp.transpose(source_field[0], (1, 0, 2))
    plo, phi = both_ways(source[:, bx - rim :], source[:, :rim], "brick")
    seen = receiver_fields(at, receivers[0], observed[0])

    coefficients, output, hidden = generator(at, lo, mid, hi, w1, w2)
    coefficients, plo, phi = lax.optimization_barrier((coefficients, plo, phi))
    sent = jnp.broadcast_to(coefficients[None], (shots, 2, 2, bx, nz))
    column = lax.all_to_all(sent, "shot", 0, 0, tiled=True)
    column, seen, w3, w4 = lax.optimization_barrier((column, seen, w3, w4))
    window, ahead, behind = take_window(at, column.reshape(2 * shots, 2, bx, nz))
    clo, chi = both_ways(ahead, behind, "brick")
    p1, p2, p3, p4, images, ahead, behind, modulus, *weights = forward_waves(
        at, window, clo, chi, source, plo, phi
    )
    back, front = both_ways(ahead, behind, "brick")
    slopes = wave_slopes(p1, p2, p3)
    back, front, slopes = lax.optimization_barrier((back, front, slopes))
    grads = adjoint_waves(at, (p2, p3, p4), images, back, front, seen, modulus, weights, slopes)
    got = lax.all_to_all(grads, "shot", 0, 0, tiled=True)
    s1, s2 = spread_fields(at, lo, mid, hi, hidden)
    got, s1, s2 = lax.optimization_barrier((got, s1, s2))
    got = got.reshape(shots, 2, 2 * gx, nz)
    grad_output = chain(at, got, output)
    glo, ghi = both_ways(grad_output, grad_output, "shot")
    second = second_grads(grad_output, s2)
    inner, kernels = first_grads(at, glo, grad_output, ghi, hidden, second, w3, s1)
    grad_latent = latent_grads(inner, w4)
    grad_latent = jnp.transpose(grad_latent.reshape(bx, 2, 16, nz), (2, 0, 1, 3))

    everyone = ("shot", "brick")
    slices = lax.all_to_all(kernels, everyone, 0, 0, tiled=True)
    mine = jnp.sum(slices, axis=0, keepdims=True)
    summed = lax.all_to_all(jnp.broadcast_to(mine, (128, nz)), everyone, 0, 0, tiled=True)
    folded = summed[:108].reshape(3, 2, 18, nz).transpose(0, 2, 1, 3).reshape(3, 18, 256)[:, :, :144]
    folded = folded.reshape(3, 18, 9, 16).transpose(0, 2, 1, 3).reshape(27, 18, 16)
    return (grad_latent, folded[:, :16], folded[:, 16:])


def solution(mesh):
    placed = (
        P(None, "brick", "shot", None),
        P(),
        P(),
        P("shot", "brick", None, None),
        P("shot", None, None),
        P("shot"),
        P("shot", None, None),
    )
    return jax.shard_map(
        per_device,
        mesh=mesh,
        in_specs=placed,
        out_specs=(P(None, "brick", "shot", None), P(), P()),
        check_vma=False,
    )
```

```python
import jax
import jax.numpy as jnp
import numpy as np
from jax import lax
from jax.experimental import pallas as pl
from jax.experimental.pallas import tpu as pltpu
from jax.sharding import PartitionSpec as P

F32 = jnp.float32
BF16 = jnp.bfloat16
stencil_taps = (1225.0 / 1024.0, -245.0 / 3072.0, 49.0 / 5120.0, -5.0 / 7168.0)
ratios = tuple(tap / stencil_taps[0] for tap in stencil_taps)
tap_square = stencil_taps[0] ** 2
misfit_weight = 16.0

bricks, shots = 8, 16
bx = 32
ay = 16
nz = 128
rim = 24
dom = bx + 2 * rim
lead = 8
xpad = dom + 24
ypad = ay + 8
gx = bx + 4
vmem = pltpu.CompilerParams(vmem_limit_bytes=24 * 1024 * 1024)


def cost(microseconds):
    return pl.CostEstimate(flops=0, bytes_accessed=int(microseconds * 3e6), transcendentals=0)


def whole(count):
    return [pl.BlockSpec(memory_space=pltpu.VMEM)] * count


scalars = pl.BlockSpec(memory_space=pltpu.SMEM)


def lane_index():
    return lax.broadcasted_iota(jnp.int32, (1, nz), 1)


def lane_shift(value, offset):
    if offset == 1:
        return value
    lane = lax.broadcasted_iota(jnp.int32, value.shape, 1)
    if offset == 0:
        return jnp.where(lane == 0, 0.0, pltpu.roll(value, 1, 1))
    return jnp.where(lane == nz - 1, 0.0, pltpu.roll(value, nz - 1, 1))


def generator_kernel(
    at_ref, lo_ref, mid_ref, hi_ref, w1_ref, w2_ref, coef_ref, out_ref, hid_ref, s1, s2
):
    shot, brick = at_ref[0], at_ref[1]
    y_fine = (shot > 0, True, shot < shots - 1)

    def spread(x, carry):
        x_fine = ((x >= 4) | (brick > 0)) & ((x < bx + 4) | (brick < bricks - 1))
        for part, ref in enumerate((lo_ref, mid_ref, hi_ref)):
            fine = x_fine & y_fine[part]
            for row in range(2):
                value = jnp.where(fine, ref[row, x].astype(F32), 0.0)
                for k in range(3):
                    s1[x, pl.ds((2 * part + row) * 48 + k * 16, 16), :] = lane_shift(
                        value, k
                    ).astype(BF16)
        return carry

    lax.fori_loop(0, bx + 8, spread, 0, unroll=4)
    last_block = (bx + 6) // 2 - 1

    def first_conv(block, before):
        before = jnp.tanh(before)
        for xo in range(2):
            x = jnp.maximum(2 * block - 2, 0) + xo
            x_fine = ((x >= 3) | (brick > 0)) & ((x < bx + 3) | (brick < bricks - 1))
            for y in range(4):
                fine = x_fine
                if y == 0:
                    fine = fine & (shot > 0)
                if y == 3:
                    fine = fine & (shot < shots - 1)
                start = (xo * 4 + y) * 16
                value = jnp.where(fine, before[start : start + 16], 0.0).astype(BF16)
                hid_ref[x, pl.ds(y * 16, 16), :] = value
                wide = value.astype(F32)
                for k in range(3):
                    s2[x, pl.ds(y * 48 + k * 16, 16), :] = lane_shift(wide, k).astype(BF16)
        rows = s1[pl.ds(2 * jnp.minimum(block, last_block), 4)].reshape(4 * 288, nz)
        return jnp.dot(w1_ref[...], rows, preferred_element_type=F32)

    lax.fori_loop(0, last_block + 2, first_conv, jnp.zeros((128, nz), F32))

    for block in range(gx // 6):
        rows = s2[pl.ds(6 * block, 8)].reshape(8 * 192, nz)
        acc = jnp.dot(w2_ref[...], rows, preferred_element_type=F32)
        for channel in range(2):
            for y in range(2):
                start = (channel * 2 + y) * 6
                out_ref[channel, y, pl.ds(6 * block, 6), :] = acc[start : start + 6]
    for y in range(2):
        modulus = 0.03 + 0.09 * jax.nn.sigmoid(out_ref[0, y, pl.ds(2, bx), :])
        buoyancy = jnp.exp(0.35 * jnp.tanh(out_ref[1, y, pl.ds(2, bx), :]))
        coef_ref[y, 0] = modulus
        coef_ref[y, 1] = buoyancy


def generator(at, lo, mid, hi, w1, w2):
    return pl.pallas_call(
        generator_kernel,
        out_shape=(
            jax.ShapeDtypeStruct((2, 2, bx, nz), F32),
            jax.ShapeDtypeStruct((2, 2, gx, nz), F32),
            jax.ShapeDtypeStruct((bx + 6, 64, nz), BF16),
        ),
        in_specs=[scalars] + whole(5),
        out_specs=tuple(whole(3)),
        scratch_shapes=[
            pltpu.VMEM((bx + 8, 288, nz), BF16),
            pltpu.VMEM((bx + 6, 192, nz), BF16),
        ],
        compiler_params=vmem,
        name="generator",
    )(at, lo, mid, hi, w1, w2)


def receiver_kernel(at_ref, cell_ref, seen_ref, out_ref, hot, spread):
    brick, first_row = at_ref[1], at_ref[2]
    count = cell_ref.shape[1]
    x = cell_ref[0:1] - brick * bx + rim
    row_of = jnp.where((x >= 0) & (x < dom), (cell_ref[1:2] - first_row) * dom + x, -1)
    z = cell_ref[2:3]

    def mark(chunk, carry):
        rows = chunk * 16 + lax.broadcasted_iota(jnp.int32, (16, count), 0)
        hot[pl.ds(chunk * 16, 16), :] = jnp.where(rows == row_of, 1.0, 0.0).astype(BF16)
        return carry

    lax.fori_loop(0, ay * dom // 16, mark, 0)
    parts = [jnp.ones((1, count), F32)]
    for step in range(3):
        value = seen_ref[step : step + 1]
        high = value.astype(BF16).astype(F32)
        parts += [high, value - high]

    def place(chunk, carry):
        same = chunk * 16 + lax.broadcasted_iota(jnp.int32, (16, count), 0) == z
        for index, part in enumerate(parts):
            spread[pl.ds(index * nz + chunk * 16, 16), :] = jnp.where(same, part, 0.0).astype(BF16)
        return carry

    lax.fori_loop(0, nz // 16, place, 0)
    size = 256

    def multiply(chunk, carry):
        left = hot[pl.ds(chunk * size, size), :]
        for field in range(4):
            first = 0 if field == 0 else (2 * field - 1) * nz
            right = spread[pl.ds(first, nz if field == 0 else 2 * nz), :]
            acc = lax.dot_general(
                left, right, (((1,), (1,)), ((), ())), preferred_element_type=F32
            )
            if field:
                acc = acc[:, :nz] + acc[:, nz:]
            out_ref[field, pl.ds(chunk * size, size), :] = acc
        return carry

    lax.fori_loop(0, ay * dom // size, multiply, 0)


def receiver_fields(at, cells, seen):
    count = cells.shape[1]
    return pl.pallas_call(
        receiver_kernel,
        out_shape=jax.ShapeDtypeStruct((4, ay * dom, nz), F32),
        in_specs=[scalars] + whole(2),
        out_specs=whole(1)[0],
        scratch_shapes=[
            pltpu.VMEM((ay * dom, count), BF16),
            pltpu.VMEM((7 * nz, count), BF16),
        ],
        compiler_params=vmem,
        cost_estimate=cost(9),
        name="receiver_fields",
    )(at, cells, seen)


def third_dimension_matrices():
    slope = np.zeros((nz, 2 * nz))
    spread = np.zeros((2 * nz, nz))
    for t, ratio in enumerate(ratios, 1):
        for face in range(nz):
            for column, at in ((face, face), (nz + face, face if face < nz - 1 else -1)):
                if 0 <= at + t < nz:
                    slope[at + t, column] += ratio
                if 0 <= at + 1 - t < nz:
                    slope[at + 1 - t, column] -= ratio
        for cell in range(nz):
            if cell + t - 1 < nz:
                spread[cell + t - 1, cell] += ratio
            if cell - t >= -1:
                spread[nz + (cell - t) % nz, cell] -= ratio

    def parts(matrix):
        high = matrix.astype(jnp.bfloat16)
        return high, (matrix - high.astype(np.float64)).astype(jnp.bfloat16)

    high, low = parts(slope)
    slope = np.concatenate([high, high, low])
    blocks = []
    for half in (spread[:nz], spread[nz:]):
        high, low = parts(half)
        blocks += [high, high, low]
    return slope, np.concatenate(blocks)


slope_matrix, spread_matrix = third_dimension_matrices()


def halves(value):
    high = value.astype(BF16)
    return high, (value - high.astype(F32)).astype(BF16)


def slopes_z(value, slope_ref):
    high, low = halves(value)
    both = jnp.dot(
        jnp.concatenate([high, low, high], axis=1), slope_ref[...], preferred_element_type=F32
    )
    return both[:, :nz], both[:, nz:]


def rows_of(ref, y, count, first, rows):
    return ref[pl.ds(y, count), pl.ds(first, rows), :].reshape(count * rows, nz)


group = 4


def differences(get):
    total = None
    for t in range(1, 5):
        upper, lower = get(t)
        term = upper - lower
        if t > 1:
            term = ratios[t - 1] * term
        total = term if total is None else total + term
    return total


def clear_sides(field):
    for y in (0, 1, 2, 3, ay + 4, ay + 5, ay + 6, ay + 7):
        field[y] = jnp.zeros(field.shape[1:], F32)


def clear_rims(flux_y):
    for j in (0, 1, 2, 20, 21, 22):
        flux_y[j] = jnp.zeros(flux_y.shape[1:], F32)


def halo_scale(at_ref):
    brick = at_ref[1]
    return (
        jnp.where(brick > 0, 1.0, 0.0).astype(F32),
        jnp.where(brick < bricks - 1, 1.0, 0.0).astype(F32),
    )


def window_kernel(at_ref, column_ref, win_ref, ahead_ref, behind_ref, message):
    first_row = at_ref[2]

    def body(y, carry):
        for channel in range(2):
            value = column_ref[first_row + y, channel]
            win_ref[y, channel] = value
            rounded = value.astype(BF16).astype(F32)
            rest = value - rounded
            for slot, (ref, near, further) in enumerate(((ahead_ref, 28, 12), (behind_ref, 0, 4))):
                place = (channel * 2 + slot) * 24
                message[pl.ds(place, 4), :] = rounded[near : near + 4]
                message[pl.ds(place + 4, 4), :] = rest[near : near + 4]
                message[pl.ds(place + 8, 16), :] = value[further : further + 16]
                ref[y, channel] = message[pl.ds(place, 24), :].astype(BF16)
        return carry

    lax.fori_loop(0, ay, body, 0, unroll=2)


def take_window(at, column):
    return pl.pallas_call(
        window_kernel,
        out_shape=(
            jax.ShapeDtypeStruct((ay, 2, bx, nz), F32),
            jax.ShapeDtypeStruct((ay, 2, 24, nz), BF16),
            jax.ShapeDtypeStruct((ay, 2, 24, nz), BF16),
        ),
        in_specs=[scalars] + whole(1),
        out_specs=tuple(whole(3)),
        scratch_shapes=[pltpu.VMEM((96, nz), F32)],
        compiler_params=vmem,
        name="take_window",
    )(at, column)


def slope_y(field, j, first, rows):
    return differences(
        lambda t: (
            field[j + 3 + t, pl.ds(lead + first, rows), :],
            field[j + 4 - t, pl.ds(lead + first, rows), :],
        )
    )


def slopes_xy(field, y, first, rows):
    base, more = lead + first - 4, rows + 8
    sx = differences(
        lambda t: (
            field[y + 4, pl.ds(base + t, more), :],
            field[y + 4, pl.ds(base + 1 - t, more), :],
        )
    )
    return sx, slope_y(field, y, first, rows)


def third_pass(field, weights, matrices, out, first, rows, also=None):
    _, _, wz, wzl = weights
    slope_ref, spread_ref = matrices

    def body(index, carry):
        y = index * group
        here, before = slopes_z(rows_of(field, y + 4, group, lead + first, rows), slope_ref)
        if also is not None:
            also(y, here, before)
        high_h, low_h = halves(rows_of(wz, y, group, first, rows) * here)
        high_b, low_b = halves(rows_of(wzl, y, group, first, rows) * before)
        total = jnp.dot(
            jnp.concatenate([high_h, low_h, high_h, high_b, low_b, high_b], axis=1),
            spread_ref[...],
            preferred_element_type=F32,
        )
        out[pl.ds(y, group), pl.ds(0, rows), :] = total.reshape(group, rows, nz)
        return carry

    lax.fori_loop(0, ay // group, body, 0, unroll=2)


def flux_pass(field, weights, fluxes, first, rows, also=None):
    wx, wy, _, _ = weights
    fx, fy, _ = fluxes
    base, more = lead + first - 4, rows + 8

    def body(y, carry):
        sx, sy = slopes_xy(field, y, first, rows)
        fx[y, pl.ds(0, more), :] = wx[y, pl.ds(base, more), :] * sx
        fy[y + 3, pl.ds(0, rows), :] = wy[y, pl.ds(first, rows), :] * sy
        if also is not None:
            also(y, sx, sy)
        return carry

    lax.fori_loop(0, ay, body, 0, unroll=2)
    sy = slope_y(field, ay, first, rows)
    fy[ay + 3, pl.ds(0, rows), :] = wy[ay, pl.ds(first, rows), :] * sy
    return sy


def divergence_pass(fluxes, rows, consume):
    fx, fy, az = fluxes

    def body(y, carry):
        total = az[y, pl.ds(0, rows), :] + differences(
            lambda t: (fx[y, pl.ds(3 + t, rows), :], fx[y, pl.ds(4 - t, rows), :])
        )
        total = total + differences(
            lambda t: (
                fy[y + t + 3, pl.ds(0, rows), :],
                fy[y - t + 4, pl.ds(0, rows), :],
            )
        )
        consume(y, total)
        return carry

    lax.fori_loop(0, ay, body, 0, unroll=2)


weight_sizes = ((ay, dom + 16, nz), (ay + 1, dom, nz), (ay, dom, nz), (ay, dom, nz))
padded = pltpu.VMEM((ypad, xpad, nz), F32)
flux_shapes = [
    pltpu.VMEM((ay, 72, nz), F32),
    pltpu.VMEM((23, 64, nz), F32),
    pltpu.VMEM((ay, 64, nz), F32),
]


def forward_kernel(
    at_ref, win_ref, clo_ref, chi_ref, src_ref, plo_ref, phi_ref, slope_ref, spread_ref,
    p1_ref, p2_ref, p3_ref, p4_ref, image_ref, ahead_ref, behind_ref, modulus, wx, wy, wz, wzl,
    buoy, f1, f2, f3, fx, fy, az, message,
):
    last = lane_index() == nz - 1
    weights = (wx, wy, wz, wzl)
    fluxes = (fx, fy, az)
    matrices = (slope_ref, spread_ref)
    clear_rims(fy)
    for field in (buoy, f1, f2, f3):
        clear_sides(field)
    low, high = halo_scale(at_ref)
    half = 0.5 * tap_square

    def load(y, carry):
        for channel, ref, row, skip in ((0, modulus, y, 0), (1, buoy, y + 4, lead)):
            received = low * clo_ref[y, channel].astype(F32)
            ref[row, pl.ds(skip + 4, 16), :] = received[8:]
            ref[row, pl.ds(skip + 20, 4), :] = received[:4] + received[4:8]
            ref[row, pl.ds(skip + rim, bx), :] = win_ref[y, channel]
            received = high * chi_ref[y, channel].astype(F32)
            ref[row, pl.ds(skip + rim + bx, 4), :] = received[:4] + received[4:8]
            ref[row, pl.ds(skip + rim + bx + 4, 16), :] = received[8:]
        f1[y + 4, pl.ds(lead, rim), :] = low * plo_ref[y]
        f1[y + 4, pl.ds(lead + rim, bx), :] = src_ref[y]
        f1[y + 4, pl.ds(lead + rim + bx, rim), :] = high * phi_ref[y]
        return carry

    lax.fori_loop(0, ay, load, 0)

    def weigh(y, carry):
        inner = buoy[y + 4, pl.ds(lead, dom), :]
        ahead = pltpu.roll(inner, nz - 1, 1)
        value = buoy[y + 4, pl.ds(0, dom + 16), :]
        wx[y] = half * (value + buoy[y + 4, pl.ds(1, dom + 16), :])
        wy[y] = half * (buoy[y + 3, pl.ds(lead, dom), :] + inner)
        wz[y] = half * jnp.where(last, inner, inner + ahead)
        wzl[y] = half * jnp.where(last, ahead, inner + ahead)
        return carry

    lax.fori_loop(0, ay, weigh, 0, unroll=2)
    wy[ay] = half * buoy[ay + 3, pl.ds(lead, dom), :]

    def first_step(y, image):
        f2[y + 4, pl.ds(lead + 8, 64), :] = (
            2.0 * f1[y + 4, pl.ds(lead + 8, 64), :] + modulus[y, pl.ds(8, 64), :] * image
        )
        image_ref[0, y] = image[8:56]

    def second_step(y, image):
        value = (
            2.0 * f2[y + 4, pl.ds(lead + 12, 56), :]
            - f1[y + 4, pl.ds(lead + 12, 56), :]
            + modulus[y, pl.ds(12, 56), :] * image
        )
        f3[y + 4, pl.ds(lead + 12, 56), :] = value
        image_ref[1, y] = image[4:52]
        p3_ref[y] = value[4:52]
        p1_ref[y] = f1[y + 4, pl.ds(lead + 8, 64), :]
        p2_ref[y] = f2[y + 4, pl.ds(lead + 8, 64), :]

    def third_step(y, image):
        image_ref[2, y] = image
        value = (
            2.0 * f3[y + 4, pl.ds(lead + rim, bx), :]
            - f2[y + 4, pl.ds(lead + rim, bx), :]
            + modulus[y, pl.ds(rim, bx), :] * image[8:40]
        )
        p4_ref[y] = value

    def pack(y, ref, near, further, third):
        value = p4_ref[y, pl.ds(near, 7), :]
        rounded = value.astype(BF16).astype(F32)
        message[pl.ds(0, 7), :] = rounded
        message[pl.ds(7, 7), :] = value - rounded
        message[pl.ds(14, 13), :] = p4_ref[y, pl.ds(further, 13), :]
        message[pl.ds(27, 5), :] = f3[y + 4, pl.ds(lead + rim + third, 5), :]
        ref[y] = message[...].astype(BF16)

    def send(y, carry):
        pack(y, ahead_ref, 25, 12, 19)
        pack(y, behind_ref, 0, 7, 8)
        return carry

    for field, first, rows, consume in (
        (f1, 8, 64, first_step),
        (f2, 12, 56, second_step),
        (f3, 16, 48, third_step),
    ):
        third_pass(field, weights, matrices, az, first, rows)
        flux_pass(field, weights, fluxes, first, rows)
        divergence_pass(fluxes, rows, consume)
    lax.fori_loop(0, ay, send, 0)


def forward_waves(at, window, clo, chi, source, plo, phi):
    shapes = [(ay, 64, nz), (ay, 64, nz), (ay, 48, nz), (ay, bx, nz), (3, ay, 48, nz)]
    return pl.pallas_call(
        forward_kernel,
        out_shape=tuple(jax.ShapeDtypeStruct(shape, F32) for shape in shapes)
        + (jax.ShapeDtypeStruct((ay, 32, nz), BF16),) * 2
        + (jax.ShapeDtypeStruct((ay, dom, nz), F32),)
        + tuple(jax.ShapeDtypeStruct(shape, F32) for shape in weight_sizes),
        in_specs=[scalars] + whole(8),
        out_specs=tuple(whole(12)),
        scratch_shapes=[padded, padded, padded, padded, *flux_shapes, pltpu.VMEM((32, nz), F32)],
        compiler_params=vmem,
        name="forward_waves",
    )(at, window, clo, chi, source, plo, phi, slope_matrix, spread_matrix)


def slopes_kernel(p1_ref, p2_ref, p3_ref, slope_ref, sx_ref, sy_ref, sh_ref, sb_ref, field):
    clear_sides(field)
    for index, (ref, first) in enumerate(((p1_ref, 8), (p2_ref, 8), (p3_ref, 16))):
        rows = ref.shape[1]

        def load(y, carry):
            field[y + 4, pl.ds(lead + first, rows), :] = ref[y]
            return carry

        lax.fori_loop(0, ay, load, 0)

        def body(y, carry):
            sx, sy = slopes_xy(field, y, 16, 48)
            sx_ref[index, y] = sx[:48]
            sy_ref[index, y] = sy
            return carry

        lax.fori_loop(0, ay, body, 0, unroll=2)
        sy_ref[index, ay] = slope_y(field, ay, 16, 48)

        def third(part, carry):
            y = part * group
            here, before = slopes_z(rows_of(field, y + 4, group, lead + 16, 48), slope_ref)
            sh_ref[index, pl.ds(y, group)] = here.reshape(group, 48, nz)
            sb_ref[index, pl.ds(y, group)] = before.reshape(group, 48, nz)
            return carry

        lax.fori_loop(0, ay // group, third, 0)


def wave_slopes(p1, p2, p3):
    shapes = [(3, ay, 48, nz), (3, ay + 1, 48, nz), (3, ay, 48, nz), (3, ay, 48, nz)]
    return pl.pallas_call(
        slopes_kernel,
        out_shape=tuple(jax.ShapeDtypeStruct(shape, F32) for shape in shapes),
        in_specs=whole(4),
        out_specs=tuple(whole(4)),
        scratch_shapes=[padded],
        compiler_params=vmem,
        cost_estimate=cost(6),
        name="wave_slopes",
    )(p1, p2, p3, slope_matrix)


def adjoint_kernel(
    at_ref, p2_ref, p3_ref, p4_ref, image_ref, back_ref, front_ref, seen_ref,
    slope_ref, spread_ref, modulus, wx, wy, wz, wzl, px_ref, py_ref, ph_ref, pb_ref,
    column_ref,
    scaled, later, late, grad_m, fx, fy, az, qx, qy, qh, qb, far,
):
    weights = (wx, wy, wz, wzl)
    fluxes = (fx, fy, az)
    matrices = (slope_ref, spread_ref)
    clear_rims(fy)
    clear_sides(scaled)
    low, high = halo_scale(at_ref)

    def residual(step, y, first, value):
        rows = value.shape[0]
        start = pl.multiple_of(y * dom + first, 8)
        count = seen_ref[0, pl.ds(start, rows), :]
        total = seen_ref[step, pl.ds(start, rows), :]
        return misfit_weight * (count * value - total)

    far[...] = jnp.zeros(far.shape, F32)

    def seed(y, carry):
        late[y, pl.ds(8, 48), :] = p3_ref[y]
        received = low * back_ref[y].astype(F32)
        far[pl.ds(4, 13), :] = received[14:27]
        far[pl.ds(17, 7), :] = received[:7] + received[7:14]
        late[y, pl.ds(3, 5), :] = received[27:]
        far[pl.ds(rim, bx), :] = p4_ref[y]
        received = high * front_ref[y].astype(F32)
        far[pl.ds(rim + bx, 7), :] = received[:7] + received[7:14]
        far[pl.ds(rim + bx + 7, 13), :] = received[14:27]
        late[y, pl.ds(56, 5), :] = received[27:]
        error = residual(3, y, 0, far[...])
        later[y] = error
        scaled[y + 4, pl.ds(lead, dom), :] = modulus[y] * error
        grad_m[y] = error[16:64] * image_ref[2, y]
        return carry

    lax.fori_loop(0, ay, seed, 0)

    def add(ref, place, product, index):
        ref[place] = product if index == 2 else ref[place] + product

    def cross(index, offset):
        def also(y, sx, sy):
            add(qx, y, sx[offset : offset + 48] * px_ref[index, y], index)
            add(qy, y, sy[offset : offset + 48] * py_ref[index, y], index)

        return also

    def cross_third(index, offset):
        def also(y, here, before):
            for ref, slope, other in ((qh, here, ph_ref), (qb, before, pb_ref)):
                rows = slope.shape[0] // group
                near_rows = slope.reshape(group, rows, nz)[:, offset : offset + 48]
                add(ref, pl.ds(y, group), near_rows * other[index, pl.ds(y, group)], index)

        return also

    def cross_last(index, offset, sy):
        add(qy, ay, sy[offset : offset + 48] * py_ref[index, ay], index)

    def step_three(y, image):
        value = late[y]
        value = residual(2, y, 8, value) + 2.0 * later[y, pl.ds(8, 64), :] + image
        late[y] = value
        grad_m[y] = grad_m[y] + value[8:56] * image_ref[1, y]

    def step_two(y, image):
        value = (
            residual(1, y, 16, p2_ref[y, pl.ds(8, 48), :])
            + 2.0 * late[y, pl.ds(8, 48), :]
            + image
            - later[y, pl.ds(16, 48), :]
        )
        grad_m[y] = grad_m[y] + value * image_ref[0, y]
        later[y, pl.ds(16, 48), :] = value

    third_pass(scaled, weights, matrices, az, 8, 64, cross_third(2, 8))
    sy = flux_pass(scaled, weights, fluxes, 8, 64, cross(2, 8))
    cross_last(2, 8, sy)
    divergence_pass(fluxes, 64, step_three)

    def rescale(y, carry):
        scaled[y + 4, pl.ds(lead + 8, 64), :] = modulus[y, pl.ds(8, 64), :] * late[y]
        return carry

    lax.fori_loop(0, ay, rescale, 0, unroll=2)
    third_pass(scaled, weights, matrices, az, 16, 48, cross_third(1, 0))
    sy = flux_pass(scaled, weights, fluxes, 16, 48, cross(1, 0))
    cross_last(1, 0, sy)
    divergence_pass(fluxes, 48, step_two)

    def rescale_last(y, carry):
        scaled[y + 4, pl.ds(lead + 16, 48), :] = modulus[y, pl.ds(16, 48), :] * later[y, pl.ds(16, 48), :]
        return carry

    lax.fori_loop(0, ay, rescale_last, 0, unroll=2)

    def last_third(part, carry):
        y = part * group
        cross_third(0, 0)(y, *slopes_z(rows_of(scaled, y + 4, group, lead + 16, 48), slope_ref))
        return carry

    lax.fori_loop(0, ay // group, last_third, 0)

    def last_slopes(y, carry):
        cross(0, 0)(y, *slopes_xy(scaled, y, 16, 48))
        return carry

    lax.fori_loop(0, ay, last_slopes, 0, unroll=2)
    cross_last(0, 0, slope_y(scaled, ay, 16, 48))

    first_row = at_ref[2]

    def blank(row, carry):
        column_ref[row] = jnp.zeros(column_ref.shape[1:], F32)
        return carry

    lax.fori_loop(0, first_row, blank, 0)
    lax.fori_loop(first_row + ay, 2 * shots, blank, 0)

    def place(y, carry):
        before = pltpu.roll(qb[y, pl.ds(6, gx), :], 1, 1)
        total = qh[y, pl.ds(6, gx), :] + before
        total = total + qy[y, pl.ds(6, gx), :] + qy[y + 1, pl.ds(6, gx), :]
        total = total + qx[y, pl.ds(9, gx), :] + qx[y, pl.ds(10, gx), :]
        column_ref[first_row + y, pl.ds(0, gx), :] = grad_m[y, pl.ds(6, gx), :]
        column_ref[first_row + y, pl.ds(gx, gx), :] = (-0.5 * tap_square) * total
        return carry

    lax.fori_loop(0, ay, place, 0, unroll=2)


def adjoint_waves(at, fields, images, back, front, seen, modulus, weights, slopes):
    near = pltpu.VMEM((ay, 48, nz), F32)
    return pl.pallas_call(
        adjoint_kernel,
        out_shape=jax.ShapeDtypeStruct((2 * shots, 2 * gx, nz), F32),
        in_specs=[scalars] + whole(18),
        out_specs=whole(1)[0],
        scratch_shapes=[
            padded,
            pltpu.VMEM((ay, dom, nz), F32),
            pltpu.VMEM((ay, 64, nz), F32),
            near,
            *flux_shapes,
            near,
            pltpu.VMEM((ay + 1, 48, nz), F32),
            near,
            near,
            pltpu.VMEM((dom, nz), F32),
        ],
        compiler_params=vmem,
        name="adjoint_waves",
    )(at, *fields, images, back, front, seen, slope_matrix, spread_matrix, modulus, *weights, *slopes)


def chain_kernel(at_ref, got_ref, out_ref, grad_ref):
    brick = at_ref[1]
    row = lax.broadcasted_iota(jnp.int32, (gx, nz), 0)
    fine = ((row >= 2) | (brick > 0)) & ((row < gx - 2) | (brick < bricks - 1))
    for y in range(2):
        total = got_ref[0, y]
        for shot in range(1, shots):
            total = total + got_ref[shot, y]
        squashed = jax.nn.sigmoid(out_ref[0, y])
        bent = jnp.tanh(out_ref[1, y])
        buoyancy = jnp.exp(0.35 * bent)
        first = total[:gx] * 0.09 * squashed * (1.0 - squashed)
        second = total[gx:] * buoyancy * 0.35 * (1.0 - bent * bent)
        grad_ref[y, 0] = jnp.where(fine, first, 0.0).astype(BF16)
        grad_ref[y, 1] = jnp.where(fine, second, 0.0).astype(BF16)


def chain(at, got, output):
    return pl.pallas_call(
        chain_kernel,
        out_shape=jax.ShapeDtypeStruct((2, 2, gx, nz), BF16),
        in_specs=[scalars] + whole(2),
        out_specs=whole(1)[0],
        compiler_params=vmem,
        name="chain",
    )(at, got, output)


def spread_kernel(at_ref, lo_ref, mid_ref, hi_ref, hid_ref, s1, s2):
    shot, brick = at_ref[0], at_ref[1]
    y_fine = (shot > 0, True, shot < shots - 1)

    def spread(x, carry):
        x_fine = ((x >= 1) | (brick > 0)) & ((x < bx + 1) | (brick < bricks - 1))
        for y, (ref, row, part) in enumerate(((lo_ref, 1, 0), (mid_ref, 0, 1), (mid_ref, 1, 1), (hi_ref, 0, 2))):
            value = jnp.where(x_fine & y_fine[part], ref[row, x + 3].astype(F32), 0.0)
            hidden = hid_ref[x + 2, pl.ds(y * 16, 16), :].astype(F32)
            for k in range(3):
                s1[x, pl.ds(y * 48 + k * 16, 16), :] = lane_shift(value, k).astype(BF16)
                s2[x, pl.ds(y * 48 + k * 16, 16), :] = lane_shift(hidden, k).astype(BF16)
        return carry

    lax.fori_loop(0, bx + 2, spread, 0, unroll=2)


def spread_fields(at, lo, mid, hi, hidden):
    shape = jax.ShapeDtypeStruct((bx + 2, 192, nz), BF16)
    return pl.pallas_call(
        spread_kernel,
        out_shape=(shape, shape),
        in_specs=[scalars] + whole(4),
        out_specs=tuple(whole(2)),
        compiler_params=vmem,
        cost_estimate=cost(3),
        name="spread_fields",
    )(at, lo, mid, hi, hidden)


contract_lanes = (((1,), (1,)), ((), ()))


def second_grads_kernel(gmid_ref, s2, second_ref, own):
    own[...] = jnp.zeros(own.shape, F32)
    for row in range(2):
        for channel in range(2):
            own[:, channel * 2 + row, :] = gmid_ref[row, channel].astype(F32)[2 : bx + 2]

    def kernel_grad(x, second):
        return second + lax.dot_general(
            own[x].astype(BF16), s2[pl.ds(x, 3)].reshape(576, nz), contract_lanes, preferred_element_type=F32
        )

    second_ref[...] = lax.fori_loop(0, bx, kernel_grad, jnp.zeros((8, 576), F32), unroll=4)


def second_grads(grad_output, s2):
    return pl.pallas_call(
        second_grads_kernel,
        out_shape=jax.ShapeDtypeStruct((8, 576), F32),
        in_specs=whole(2),
        out_specs=whole(1)[0],
        scratch_shapes=[pltpu.VMEM((bx, 8, nz), F32)],
        compiler_params=vmem,
        cost_estimate=cost(3),
        name="second_grads",
    )(grad_output, s2)


def first_grads_kernel(
    at_ref, glo_ref, gmid_ref, ghi_ref, hid_ref, second_ref, w3_ref, s1_any, inner_ref, kernel_ref, turned, s1, ready
):
    fetch = pltpu.make_async_copy(s1_any, s1, ready)
    fetch.start()
    shot, brick = at_ref[0], at_ref[1]
    y_fine = (shot > 0, True, shot < shots - 1)
    for part, ref in enumerate((glo_ref, gmid_ref, ghi_ref)):
        for row in range(2):
            for channel in range(2):
                value = jnp.where(y_fine[part], ref[row, channel].astype(F32), 0.0)
                value = jnp.concatenate([value, jnp.zeros((12, nz), F32)], axis=0)
                plane = (2 * part + row) * 2 + channel
                for k in range(3):
                    turned[plane * 3 + k] = lane_shift(value, k)

    def hidden_grad(block, carry):
        rows = turned[:, pl.ds(8 * block, 16), :].astype(BF16).reshape(576, nz)
        acc = jnp.dot(w3_ref[...], rows, preferred_element_type=F32)
        for xo in range(8):
            x = 8 * block + xo
            x_fine = ((x >= 1) | (brick > 0)) & ((x < bx + 1) | (brick < bricks - 1))
            hidden = hid_ref[jnp.minimum(x + 2, bx + 5)].astype(F32)
            value = acc[xo * 64 : xo * 64 + 64] * (1.0 - hidden * hidden)
            for y in range(4):
                fine = x_fine
                if y == 0:
                    fine = fine & (shot > 0)
                if y == 3:
                    fine = fine & (shot < shots - 1)
                inner_ref[x, pl.ds(y * 16, 16), :] = jnp.where(
                    fine, value[y * 16 : y * 16 + 16], 0.0
                ).astype(BF16)
        return carry

    lax.fori_loop(0, 5, hidden_grad, 0)
    fetch.wait()

    def kernel_grad(x, first):
        return first + lax.dot_general(
            inner_ref[x + 1, pl.ds(16, 32), :],
            s1[pl.ds(x, 3)].reshape(576, nz),
            contract_lanes,
            preferred_element_type=F32,
        )

    first = lax.fori_loop(0, bx, kernel_grad, jnp.zeros((32, 576), F32), unroll=4)
    second = second_ref[...]
    kernel_ref[...] = jnp.zeros(kernel_ref.shape, F32)
    for dx in range(3):
        start = dx * 192
        one = first[:16, start : start + 144] + first[16:, start + 48 : start + 192]
        for channel in range(2):
            row = channel * 2
            two = (
                second[row : row + 1, start : start + 144]
                + second[row + 1 : row + 2, start + 48 : start + 192]
            )
            place = dx * 2 * 18 + 16 + channel
            kernel_ref[pl.ds(place, 1), :] = two[:, :128]
            kernel_ref[pl.ds(place + 18, 1), pl.ds(0, 16)] = two[:, 128:]
        kernel_ref[pl.ds(dx * 36, 16), :] = one[:, :128]
        kernel_ref[pl.ds(dx * 36 + 18, 16), pl.ds(0, 16)] = one[:, 128:]


def first_grads(at, glo, gmid, ghi, hidden, second, w3, s1):
    return pl.pallas_call(
        first_grads_kernel,
        out_shape=(
            jax.ShapeDtypeStruct((40, 64, nz), BF16),
            jax.ShapeDtypeStruct((128, nz), F32),
        ),
        in_specs=[scalars] + whole(6) + [pl.BlockSpec(memory_space=pl.ANY)],
        out_specs=tuple(whole(2)),
        scratch_shapes=[
            pltpu.VMEM((36, 48, nz), F32),
            pltpu.VMEM((bx + 2, 192, nz), BF16),
            pltpu.SemaphoreType.DMA,
        ],
        compiler_params=vmem,
        name="first_grads",
    )(at, glo, gmid, ghi, hidden, second, w3, s1)


def latent_grad_kernel(inner_ref, w4_ref, latent_ref, s4):
    def spread(x, carry):
        for y in range(4):
            value = inner_ref[x, pl.ds(y * 16, 16), :].astype(F32)
            for k in range(3):
                s4[x, pl.ds(y * 48 + k * 16, 16), :] = lane_shift(value, k).astype(BF16)
        return carry

    lax.fori_loop(0, bx + 2, spread, 0, unroll=2)

    def latent_grad(block, carry):
        rows = s4[pl.ds(4 * block, 6)].reshape(6 * 192, nz)
        acc = jnp.dot(w4_ref[...], rows, preferred_element_type=F32)
        latent_ref[pl.ds(4 * block, 4)] = acc.reshape(4, 32, nz)
        return carry

    lax.fori_loop(0, bx // 4, latent_grad, 0)


def latent_grads(inner, w4):
    return pl.pallas_call(
        latent_grad_kernel,
        out_shape=jax.ShapeDtypeStruct((bx, 32, nz), F32),
        in_specs=whole(2),
        out_specs=whole(1)[0],
        scratch_shapes=[pltpu.VMEM((bx + 2, 192, nz), BF16)],
        compiler_params=vmem,
        cost_estimate=cost(4),
        name="latent_grads",
    )(inner, w4)


def column_codes(x_in, y_in, order):
    if order == "xykc":
        x, y, k, c = np.meshgrid(*map(np.arange, (x_in, y_in, 3, 16)), indexing="ij")
    else:
        y, c, k, x = np.meshgrid(*map(np.arange, (y_in, 2, 3, x_in)), indexing="ij")
    return np.stack([(8 * x + y).ravel(), (16 * k + c).ravel()]).astype(np.int32)


codes_1 = column_codes(4, 6, "xykc")
codes_2 = column_codes(8, 4, "xykc")
codes_3 = column_codes(16, 6, "yckx")
codes_4 = column_codes(6, 4, "xykc")


def expand(taps_ref, codes_ref, spare, flip):
    place = codes_ref[1:2]
    size = place.shape[1]
    rows = lax.broadcasted_iota(jnp.int32, (16, size), 0)
    picks = [jnp.where(place == rows + 16 * k, 1.0, 0.0).astype(BF16) for k in range(3)]
    for pair in range(9):
        total = None
        for k in range(3):
            q = 3 * pair + k
            term = jnp.dot(taps_ref[26 - q if flip else q], picks[k], preferred_element_type=F32)
            total = term if total is None else total + term
        spare[pair, :, pl.ds(0, size)] = total


def fill_blocks(out_ref, codes_ref, spare, x_out, y_out):
    code = codes_ref[0:1]
    size = code.shape[1]
    same = lax.broadcasted_iota(jnp.int32, (16, size), 0) * 0 + code
    for xo in range(x_out):
        for y in range(y_out):
            block = jnp.zeros((16, size), F32)
            for pair in range(9):
                wanted = (xo + pair // 3) * 8 + y + pair % 3
                block = jnp.where(same == wanted, spare[pair, :, pl.ds(0, size)], block)
            out_ref[pl.ds((xo * y_out + y) * 16, 16), :] = block.astype(BF16)


def forward_bands_kernel(in_ref, out_taps_ref, codes_1_ref, codes_2_ref, w1_ref, w2_ref, spare, rows):
    expand(in_ref, codes_1_ref, spare, False)
    fill_blocks(w1_ref, codes_1_ref, spare, 2, 4)
    expand(out_taps_ref, codes_2_ref, spare, False)
    size = codes_2_ref.shape[1]
    code = codes_2_ref[0:1] - 8 * lax.broadcasted_iota(jnp.int32, (6, size), 0)
    for channel in range(2):
        for y in range(2):
            block = jnp.zeros((6, size), F32)
            for pair in range(9):
                wanted = (pair // 3) * 8 + y + pair % 3
                block = jnp.where(code == wanted, spare[pair, channel : channel + 1, :], block)
            rows[pl.ds((channel * 2 + y) * 6, 6), :] = block
    w2_ref[...] = rows[...].astype(BF16)


def backward_bands_kernel(in_ref, out_taps_ref, codes_3_ref, codes_4_ref, w3_ref, w4_ref, spare):
    expand(out_taps_ref, codes_3_ref, spare, True)
    fill_blocks(w3_ref, codes_3_ref, spare, 8, 4)
    expand(in_ref, codes_4_ref, spare, True)
    fill_blocks(w4_ref, codes_4_ref, spare, 4, 2)


def forward_bands(taps_in, taps_out):
    return pl.pallas_call(
        forward_bands_kernel,
        out_shape=(
            jax.ShapeDtypeStruct((128, 1152), BF16),
            jax.ShapeDtypeStruct((24, 1536), BF16),
        ),
        in_specs=whole(4),
        out_specs=tuple(whole(2)),
        scratch_shapes=[pltpu.VMEM((9, 16, 1536), F32), pltpu.VMEM((24, 1536), F32)],
        compiler_params=vmem,
        cost_estimate=cost(3),
        name="forward_bands",
    )(taps_in, taps_out, codes_1, codes_2)


def backward_bands(taps_in, taps_out):
    return pl.pallas_call(
        backward_bands_kernel,
        out_shape=(
            jax.ShapeDtypeStruct((512, 576), BF16),
            jax.ShapeDtypeStruct((128, 1152), BF16),
        ),
        in_specs=whole(4),
        out_specs=tuple(whole(2)),
        scratch_shapes=[pltpu.VMEM((9, 16, 1152), F32)],
        compiler_params=vmem,
        cost_estimate=cost(4),
        name="backward_bands",
    )(taps_in, taps_out, codes_3, codes_4)


def both_ways(ahead, behind, axis):
    count = lax.axis_size(axis)
    forward = [(i, (i + 1) % count) for i in range(count)]
    backward_ = [(target, source) for source, target in forward]
    return lax.ppermute(ahead, axis, forward), lax.ppermute(behind, axis, backward_)


def per_device(latent, conv_in, conv_out, source_field, observed, aperture, receivers):
    shot = lax.axis_index("shot")
    brick = lax.axis_index("brick")
    at = jnp.stack([shot, brick, aperture[0]]).astype(jnp.int32)
    taps_out = jnp.pad(conv_out, ((0, 0), (0, 14), (0, 0)))
    w1, w2 = forward_bands(conv_in, taps_out)
    w3, w4 = backward_bands(conv_in.transpose(0, 2, 1), taps_out.transpose(0, 2, 1))

    tile = jnp.transpose(latent, (2, 1, 0, 3))
    from_low, from_high = both_ways(tile[:, bx - 4 :], tile[:, :4], "brick")
    mid = jnp.concatenate([from_low, tile, from_high], axis=1)
    lo, hi = both_ways(mid, mid, "shot")
    source = jnp.transpose(source_field[0], (1, 0, 2))
    plo, phi = both_ways(source[:, bx - rim :], source[:, :rim], "brick")
    seen = receiver_fields(at, receivers[0], observed[0])

    coefficients, output, hidden = generator(at, lo, mid, hi, w1, w2)
    coefficients, plo, phi = lax.optimization_barrier((coefficients, plo, phi))
    sent = jnp.broadcast_to(coefficients[None], (shots, 2, 2, bx, nz))
    column = lax.all_to_all(sent, "shot", 0, 0, tiled=True)
    column, seen, w3, w4 = lax.optimization_barrier((column, seen, w3, w4))
    window, ahead, behind = take_window(at, column.reshape(2 * shots, 2, bx, nz))
    clo, chi = both_ways(ahead, behind, "brick")
    p1, p2, p3, p4, images, ahead, behind, modulus, *weights = forward_waves(
        at, window, clo, chi, source, plo, phi
    )
    back, front = both_ways(ahead, behind, "brick")
    slopes = wave_slopes(p1, p2, p3)
    back, front, slopes = lax.optimization_barrier((back, front, slopes))
    grads = adjoint_waves(at, (p2, p3, p4), images, back, front, seen, modulus, weights, slopes)
    got = lax.all_to_all(grads, "shot", 0, 0, tiled=True)
    s1, s2 = spread_fields(at, lo, mid, hi, hidden)
    got, s1, s2 = lax.optimization_barrier((got, s1, s2))
    got = got.reshape(shots, 2, 2 * gx, nz)
    grad_output = chain(at, got, output)
    glo, ghi = both_ways(grad_output, grad_output, "shot")
    second = second_grads(grad_output, s2)
    inner, kernels = first_grads(at, glo, grad_output, ghi, hidden, second, w3, s1)
    grad_latent = latent_grads(inner, w4)
    grad_latent = jnp.transpose(grad_latent.reshape(bx, 2, 16, nz), (2, 0, 1, 3))

    everyone = ("shot", "brick")
    slices = lax.all_to_all(kernels, everyone, 0, 0, tiled=True)
    mine = jnp.sum(slices, axis=0, keepdims=True)
    summed = lax.all_to_all(jnp.broadcast_to(mine, (128, nz)), everyone, 0, 0, tiled=True)
    folded = summed[:108].reshape(3, 2, 18, nz).transpose(0, 2, 1, 3).reshape(3, 18, 256)[:, :, :144]
    folded = folded.reshape(3, 18, 9, 16).transpose(0, 2, 1, 3).reshape(27, 18, 16)
    return (grad_latent, folded[:, :16], folded[:, 16:])


def solution(mesh):
    placed = (
        P(None, "brick", "shot", None),
        P(),
        P(),
        P("shot", "brick", None, None),
        P("shot", None, None),
        P("shot"),
        P("shot", None, None),
    )
    return jax.shard_map(
        per_device,
        mesh=mesh,
        in_specs=placed,
        out_specs=(P(None, "brick", "shot", None), P(), P()),
        check_vma=False,
    )
```

```python
import jax
import jax.numpy as jnp
import numpy as np
from jax import lax
from jax.experimental import pallas as pl
from jax.experimental.pallas import tpu as pltpu
from jax.sharding import PartitionSpec as P

F32 = jnp.float32
BF16 = jnp.bfloat16
stencil_taps = (1225.0 / 1024.0, -245.0 / 3072.0, 49.0 / 5120.0, -5.0 / 7168.0)
ratios = tuple(tap / stencil_taps[0] for tap in stencil_taps)
tap_square = stencil_taps[0] ** 2
misfit_weight = 16.0

bricks, shots = 8, 16
bx = 32
ay = 16
nz = 128
rim = 24
dom = bx + 2 * rim
lead = 8
xpad = dom + 24
ypad = ay + 8
gx = bx + 4
vmem = pltpu.CompilerParams(vmem_limit_bytes=24 * 1024 * 1024)


def cost(microseconds):
    return pl.CostEstimate(flops=0, bytes_accessed=int(microseconds * 3e6), transcendentals=0)


def whole(count):
    return [pl.BlockSpec(memory_space=pltpu.VMEM)] * count


scalars = pl.BlockSpec(memory_space=pltpu.SMEM)


def lane_index():
    return lax.broadcasted_iota(jnp.int32, (1, nz), 1)


def lane_shift(value, offset):
    if offset == 1:
        return value
    lane = lax.broadcasted_iota(jnp.int32, value.shape, 1)
    if offset == 0:
        return jnp.where(lane == 0, 0.0, pltpu.roll(value, 1, 1))
    return jnp.where(lane == nz - 1, 0.0, pltpu.roll(value, nz - 1, 1))


def generator_kernel(
    at_ref, lo_ref, mid_ref, hi_ref, w1_ref, w2_ref, coef_ref, out_ref, hid_ref, s1, s2
):
    shot, brick = at_ref[0], at_ref[1]
    y_fine = (shot > 0, True, shot < shots - 1)

    def spread(x, carry):
        x_fine = ((x >= 4) | (brick > 0)) & ((x < bx + 4) | (brick < bricks - 1))
        for part, ref in enumerate((lo_ref, mid_ref, hi_ref)):
            fine = x_fine & y_fine[part]
            for row in range(2):
                value = jnp.where(fine, ref[row, x].astype(F32), 0.0)
                for k in range(3):
                    s1[x, pl.ds((2 * part + row) * 48 + k * 16, 16), :] = lane_shift(
                        value, k
                    ).astype(BF16)
        return carry

    lax.fori_loop(0, bx + 8, spread, 0, unroll=4)
    last_block = (bx + 6) // 2 - 1

    def first_conv(block, before):
        before = jnp.tanh(before)
        for xo in range(2):
            x = jnp.maximum(2 * block - 2, 0) + xo
            x_fine = ((x >= 3) | (brick > 0)) & ((x < bx + 3) | (brick < bricks - 1))
            for y in range(4):
                fine = x_fine
                if y == 0:
                    fine = fine & (shot > 0)
                if y == 3:
                    fine = fine & (shot < shots - 1)
                start = (xo * 4 + y) * 16
                value = jnp.where(fine, before[start : start + 16], 0.0).astype(BF16)
                hid_ref[x, pl.ds(y * 16, 16), :] = value
                wide = value.astype(F32)
                for k in range(3):
                    s2[x, pl.ds(y * 48 + k * 16, 16), :] = lane_shift(wide, k).astype(BF16)
        rows = s1[pl.ds(2 * jnp.minimum(block, last_block), 4)].reshape(4 * 288, nz)
        return jnp.dot(w1_ref[...], rows, preferred_element_type=F32)

    lax.fori_loop(0, last_block + 2, first_conv, jnp.zeros((128, nz), F32))

    for block in range(gx // 6):
        rows = s2[pl.ds(6 * block, 8)].reshape(8 * 192, nz)
        acc = jnp.dot(w2_ref[...], rows, preferred_element_type=F32)
        for channel in range(2):
            for y in range(2):
                start = (channel * 2 + y) * 6
                out_ref[channel, y, pl.ds(6 * block, 6), :] = acc[start : start + 6]
    for y in range(2):
        modulus = 0.03 + 0.09 * jax.nn.sigmoid(out_ref[0, y, pl.ds(2, bx), :])
        buoyancy = jnp.exp(0.35 * jnp.tanh(out_ref[1, y, pl.ds(2, bx), :]))
        coef_ref[y, 0] = modulus
        coef_ref[y, 1] = buoyancy


def generator(at, lo, mid, hi, w1, w2):
    return pl.pallas_call(
        generator_kernel,
        out_shape=(
            jax.ShapeDtypeStruct((2, 2, bx, nz), F32),
            jax.ShapeDtypeStruct((2, 2, gx, nz), F32),
            jax.ShapeDtypeStruct((bx + 6, 64, nz), BF16),
        ),
        in_specs=[scalars] + whole(5),
        out_specs=tuple(whole(3)),
        scratch_shapes=[
            pltpu.VMEM((bx + 8, 288, nz), BF16),
            pltpu.VMEM((bx + 6, 192, nz), BF16),
        ],
        compiler_params=vmem,
        name="generator",
    )(at, lo, mid, hi, w1, w2)


def receiver_kernel(at_ref, cell_ref, seen_ref, out_ref, hot, spread):
    brick, first_row = at_ref[1], at_ref[2]
    count = cell_ref.shape[1]
    x = cell_ref[0:1] - brick * bx + rim
    row_of = jnp.where((x >= 0) & (x < dom), (cell_ref[1:2] - first_row) * dom + x, -1)
    z = cell_ref[2:3]

    def mark(chunk, carry):
        rows = chunk * 16 + lax.broadcasted_iota(jnp.int32, (16, count), 0)
        hot[pl.ds(chunk * 16, 16), :] = jnp.where(rows == row_of, 1.0, 0.0).astype(BF16)
        return carry

    lax.fori_loop(0, ay * dom // 16, mark, 0)
    parts = [jnp.ones((1, count), F32)]
    for step in range(3):
        value = seen_ref[step : step + 1]
        high = value.astype(BF16).astype(F32)
        parts += [high, value - high]

    def place(chunk, carry):
        same = chunk * 16 + lax.broadcasted_iota(jnp.int32, (16, count), 0) == z
        for index, part in enumerate(parts):
            spread[pl.ds(index * nz + chunk * 16, 16), :] = jnp.where(same, part, 0.0).astype(BF16)
        return carry

    lax.fori_loop(0, nz // 16, place, 0)
    size = 256

    def multiply(chunk, carry):
        left = hot[pl.ds(chunk * size, size), :]
        for field in range(4):
            first = 0 if field == 0 else (2 * field - 1) * nz
            right = spread[pl.ds(first, nz if field == 0 else 2 * nz), :]
            acc = lax.dot_general(
                left, right, (((1,), (1,)), ((), ())), preferred_element_type=F32
            )
            if field:
                acc = acc[:, :nz] + acc[:, nz:]
            out_ref[field, pl.ds(chunk * size, size), :] = acc
        return carry

    lax.fori_loop(0, ay * dom // size, multiply, 0)


def receiver_fields(at, cells, seen):
    count = cells.shape[1]
    return pl.pallas_call(
        receiver_kernel,
        out_shape=jax.ShapeDtypeStruct((4, ay * dom, nz), F32),
        in_specs=[scalars] + whole(2),
        out_specs=whole(1)[0],
        scratch_shapes=[
            pltpu.VMEM((ay * dom, count), BF16),
            pltpu.VMEM((7 * nz, count), BF16),
        ],
        compiler_params=vmem,
        cost_estimate=cost(9),
        name="receiver_fields",
    )(at, cells, seen)


def third_dimension_matrices():
    slope = np.zeros((nz, 2 * nz))
    spread = np.zeros((2 * nz, nz))
    for t, ratio in enumerate(ratios, 1):
        for face in range(nz):
            for column, at in ((face, face), (nz + face, face if face < nz - 1 else -1)):
                if 0 <= at + t < nz:
                    slope[at + t, column] += ratio
                if 0 <= at + 1 - t < nz:
                    slope[at + 1 - t, column] -= ratio
        for cell in range(nz):
            if cell + t - 1 < nz:
                spread[cell + t - 1, cell] += ratio
            if cell - t >= -1:
                spread[nz + (cell - t) % nz, cell] -= ratio

    def parts(matrix):
        high = matrix.astype(jnp.bfloat16)
        return high, (matrix - high.astype(np.float64)).astype(jnp.bfloat16)

    high, low = parts(slope)
    slope = np.concatenate([high, high, low])
    blocks = []
    for half in (spread[:nz], spread[nz:]):
        high, low = parts(half)
        blocks += [high, high, low]
    return slope, np.concatenate(blocks)


slope_matrix, spread_matrix = third_dimension_matrices()


def halves(value):
    high = value.astype(BF16)
    return high, (value - high.astype(F32)).astype(BF16)


def slopes_z(value, slope_ref):
    high, low = halves(value)
    both = jnp.dot(
        jnp.concatenate([high, low, high], axis=1), slope_ref[...], preferred_element_type=F32
    )
    return both[:, :nz], both[:, nz:]


def divergence_z(here, before, spread_ref):
    high_h, low_h = halves(here)
    high_b, low_b = halves(before)
    return jnp.dot(
        jnp.concatenate([high_h, low_h, high_h, high_b, low_b, high_b], axis=1),
        spread_ref[...],
        preferred_element_type=F32,
    )


def rows_of(ref, y, count, first, rows):
    return ref[pl.ds(y, count), pl.ds(first, rows), :].reshape(count * rows, nz)


group = 4


def differences(get):
    total = None
    for t in range(1, 5):
        upper, lower = get(t)
        term = upper - lower
        if t > 1:
            term = ratios[t - 1] * term
        total = term if total is None else total + term
    return total


def clear_sides(field):
    for y in (0, 1, 2, 3, ay + 4, ay + 5, ay + 6, ay + 7):
        field[y] = jnp.zeros(field.shape[1:], F32)


def clear_rims(flux_y):
    for j in (0, 1, 2, 20, 21, 22):
        flux_y[j] = jnp.zeros(flux_y.shape[1:], F32)


def halo_scale(at_ref):
    brick = at_ref[1]
    return (
        jnp.where(brick > 0, 1.0, 0.0).astype(F32),
        jnp.where(brick < bricks - 1, 1.0, 0.0).astype(F32),
    )


def window_kernel(at_ref, column_ref, win_ref, ahead_ref, behind_ref, message):
    first_row = at_ref[2]

    def body(y, carry):
        for channel in range(2):
            value = column_ref[first_row + y, channel]
            win_ref[y, channel] = value
            rounded = value.astype(BF16).astype(F32)
            rest = value - rounded
            for slot, (ref, near, further) in enumerate(((ahead_ref, 28, 12), (behind_ref, 0, 4))):
                place = (channel * 2 + slot) * 24
                message[pl.ds(place, 4), :] = rounded[near : near + 4]
                message[pl.ds(place + 4, 4), :] = rest[near : near + 4]
                message[pl.ds(place + 8, 16), :] = value[further : further + 16]
                ref[y, channel] = message[pl.ds(place, 24), :].astype(BF16)
        return carry

    lax.fori_loop(0, ay, body, 0, unroll=2)


def take_window(at, column):
    return pl.pallas_call(
        window_kernel,
        out_shape=(
            jax.ShapeDtypeStruct((ay, 2, bx, nz), F32),
            jax.ShapeDtypeStruct((ay, 2, 24, nz), BF16),
            jax.ShapeDtypeStruct((ay, 2, 24, nz), BF16),
        ),
        in_specs=[scalars] + whole(1),
        out_specs=tuple(whole(3)),
        scratch_shapes=[pltpu.VMEM((96, nz), F32)],
        compiler_params=vmem,
        name="take_window",
    )(at, column)


def slope_y(field, j, first, rows):
    return differences(
        lambda t: (
            field[j + 3 + t, pl.ds(lead + first, rows), :],
            field[j + 4 - t, pl.ds(lead + first, rows), :],
        )
    )


def slopes_xy(field, y, first, rows):
    base, more = lead + first - 4, rows + 8
    sx = differences(
        lambda t: (
            field[y + 4, pl.ds(base + t, more), :],
            field[y + 4, pl.ds(base + 1 - t, more), :],
        )
    )
    return sx, slope_y(field, y, first, rows)


def third_pass(field, weights, matrices, out, first, rows, also=None):
    _, _, wz, wzl = weights
    slope_ref, spread_ref = matrices

    def body(index, carry):
        y = index * group
        here, before = slopes_z(rows_of(field, y + 4, group, lead + first, rows), slope_ref)
        if also is not None:
            also(y, here, before)
        total = divergence_z(
            rows_of(wz, y, group, first, rows) * here,
            rows_of(wzl, y, group, first, rows) * before,
            spread_ref,
        )
        out[pl.ds(y, group), pl.ds(0, rows), :] = total.reshape(group, rows, nz)
        return carry

    lax.fori_loop(0, ay // group, body, 0, unroll=2)


def flux_pass(field, weights, fluxes, first, rows, also=None):
    wx, wy, _, _ = weights
    fx, fy, _ = fluxes
    base, more = lead + first - 4, rows + 8

    def body(y, carry):
        sx, sy = slopes_xy(field, y, first, rows)
        fx[y, pl.ds(0, more), :] = wx[y, pl.ds(base, more), :] * sx
        fy[y + 3, pl.ds(0, rows), :] = wy[y, pl.ds(first, rows), :] * sy
        if also is not None:
            also(y, sx, sy)
        return carry

    lax.fori_loop(0, ay, body, 0, unroll=2)
    sy = slope_y(field, ay, first, rows)
    fy[ay + 3, pl.ds(0, rows), :] = wy[ay, pl.ds(first, rows), :] * sy
    return sy


def divergence_pass(fluxes, rows, consume):
    fx, fy, az = fluxes

    def body(y, carry):
        total = az[y, pl.ds(0, rows), :] + differences(
            lambda t: (fx[y, pl.ds(3 + t, rows), :], fx[y, pl.ds(4 - t, rows), :])
        )
        total = total + differences(
            lambda t: (
                fy[y + t + 3, pl.ds(0, rows), :],
                fy[y - t + 4, pl.ds(0, rows), :],
            )
        )
        consume(y, total)
        return carry

    lax.fori_loop(0, ay, body, 0, unroll=2)


weight_sizes = ((ay, dom + 16, nz), (ay + 1, dom, nz), (ay, dom, nz), (ay, dom, nz))
padded = pltpu.VMEM((ypad, xpad, nz), F32)
flux_shapes = [
    pltpu.VMEM((ay, 72, nz), F32),
    pltpu.VMEM((23, 64, nz), F32),
    pltpu.VMEM((ay, 64, nz), F32),
]


def source_slopes_kernel(
    at_ref, src_ref, plo_ref, phi_ref, slope_ref, p1_ref, sx_ref, sy_ref, sh_ref, sb_ref, f1
):
    clear_sides(f1)
    low, high = halo_scale(at_ref)

    def load(y, carry):
        f1[y + 4, pl.ds(lead, rim), :] = low * plo_ref[y]
        f1[y + 4, pl.ds(lead + rim, bx), :] = src_ref[y]
        f1[y + 4, pl.ds(lead + rim + bx, rim), :] = high * phi_ref[y]
        p1_ref[y] = f1[y + 4, pl.ds(lead + 8, 64), :]
        return carry

    lax.fori_loop(0, ay, load, 0)

    def body(y, carry):
        sx_ref[y], sy_ref[y] = slopes_xy(f1, y, 8, 64)
        return carry

    lax.fori_loop(0, ay, body, 0, unroll=2)
    sy_ref[ay] = slope_y(f1, ay, 8, 64)

    def third(part, carry):
        y = part * group
        here, before = slopes_z(rows_of(f1, y + 4, group, lead + 8, 64), slope_ref)
        sh_ref[pl.ds(y, group)] = here.reshape(group, 64, nz)
        sb_ref[pl.ds(y, group)] = before.reshape(group, 64, nz)
        return carry

    lax.fori_loop(0, ay // group, third, 0)


def source_slopes(at, source, plo, phi):
    shapes = [(ay, 64, nz), (ay, 72, nz), (ay + 1, 64, nz), (ay, 64, nz), (ay, 64, nz)]
    return pl.pallas_call(
        source_slopes_kernel,
        out_shape=tuple(jax.ShapeDtypeStruct(shape, F32) for shape in shapes),
        in_specs=[scalars] + whole(4),
        out_specs=tuple(whole(5)),
        scratch_shapes=[padded],
        compiler_params=vmem,
        cost_estimate=cost(3),
        name="source_slopes",
    )(at, source, plo, phi, slope_matrix)


def forward_kernel(
    at_ref, win_ref, clo_ref, chi_ref, p1_ref, sx_ref, sy_ref, sh_ref, sb_ref, slope_ref, spread_ref,
    p2_ref, p3_ref, p4_ref, image_ref, ahead_ref, behind_ref, modulus, wx, wy, wz, wzl,
    buoy, f2, f3, fx, fy, az, message,
):
    last = lane_index() == nz - 1
    weights = (wx, wy, wz, wzl)
    fluxes = (fx, fy, az)
    matrices = (slope_ref, spread_ref)
    clear_rims(fy)
    for field in (buoy, f2, f3):
        clear_sides(field)
    low, high = halo_scale(at_ref)
    half = 0.5 * tap_square

    def load(y, carry):
        for channel, ref, row, skip in ((0, modulus, y, 0), (1, buoy, y + 4, lead)):
            received = low * clo_ref[y, channel].astype(F32)
            ref[row, pl.ds(skip + 4, 16), :] = received[8:]
            ref[row, pl.ds(skip + 20, 4), :] = received[:4] + received[4:8]
            ref[row, pl.ds(skip + rim, bx), :] = win_ref[y, channel]
            received = high * chi_ref[y, channel].astype(F32)
            ref[row, pl.ds(skip + rim + bx, 4), :] = received[:4] + received[4:8]
            ref[row, pl.ds(skip + rim + bx + 4, 16), :] = received[8:]
        return carry

    lax.fori_loop(0, ay, load, 0)

    def weigh(y, carry):
        inner = buoy[y + 4, pl.ds(lead, dom), :]
        ahead = pltpu.roll(inner, nz - 1, 1)
        value = buoy[y + 4, pl.ds(0, dom + 16), :]
        wx[y] = half * (value + buoy[y + 4, pl.ds(1, dom + 16), :])
        wy[y] = half * (buoy[y + 3, pl.ds(lead, dom), :] + inner)
        wz[y] = half * jnp.where(last, inner, inner + ahead)
        wzl[y] = half * jnp.where(last, ahead, inner + ahead)
        return carry

    lax.fori_loop(0, ay, weigh, 0, unroll=2)
    wy[ay] = half * buoy[ay + 3, pl.ds(lead, dom), :]

    def first_step(y, image):
        f2[y + 4, pl.ds(lead + 8, 64), :] = (
            2.0 * p1_ref[y] + modulus[y, pl.ds(8, 64), :] * image
        )
        image_ref[0, y] = image[8:56]

    def second_step(y, image):
        value = (
            2.0 * f2[y + 4, pl.ds(lead + 12, 56), :]
            - p1_ref[y, pl.ds(4, 56), :]
            + modulus[y, pl.ds(12, 56), :] * image
        )
        f3[y + 4, pl.ds(lead + 12, 56), :] = value
        image_ref[1, y] = image[4:52]
        p3_ref[y] = value[4:52]
        p2_ref[y] = f2[y + 4, pl.ds(lead + 8, 64), :]

    def third_step(y, image):
        image_ref[2, y] = image
        value = (
            2.0 * f3[y + 4, pl.ds(lead + rim, bx), :]
            - f2[y + 4, pl.ds(lead + rim, bx), :]
            + modulus[y, pl.ds(rim, bx), :] * image[8:40]
        )
        p4_ref[y] = value

    def pack(y, ref, near, further, third):
        value = p4_ref[y, pl.ds(near, 7), :]
        rounded = value.astype(BF16).astype(F32)
        message[pl.ds(0, 7), :] = rounded
        message[pl.ds(7, 7), :] = value - rounded
        message[pl.ds(14, 13), :] = p4_ref[y, pl.ds(further, 13), :]
        message[pl.ds(27, 5), :] = f3[y + 4, pl.ds(lead + rim + third, 5), :]
        ref[y] = message[...].astype(BF16)

    def send(y, carry):
        pack(y, ahead_ref, 25, 12, 19)
        pack(y, behind_ref, 0, 7, 8)
        return carry

    def first_third(part, carry):
        y = part * group
        total = divergence_z(
            rows_of(wz, y, group, 8, 64) * rows_of(sh_ref, y, group, 0, 64),
            rows_of(wzl, y, group, 8, 64) * rows_of(sb_ref, y, group, 0, 64),
            spread_ref,
        )
        az[pl.ds(y, group), pl.ds(0, 64), :] = total.reshape(group, 64, nz)
        return carry

    lax.fori_loop(0, ay // group, first_third, 0, unroll=2)

    def first_flux(y, carry):
        fx[y] = wx[y, pl.ds(lead + 4, 72), :] * sx_ref[y]
        fy[y + 3] = wy[y, pl.ds(8, 64), :] * sy_ref[y]
        return carry

    lax.fori_loop(0, ay, first_flux, 0, unroll=2)
    fy[ay + 3] = wy[ay, pl.ds(8, 64), :] * sy_ref[ay]
    divergence_pass(fluxes, 64, first_step)
    for field, first, rows, consume in (
        (f2, 12, 56, second_step),
        (f3, 16, 48, third_step),
    ):
        third_pass(field, weights, matrices, az, first, rows)
        flux_pass(field, weights, fluxes, first, rows)
        divergence_pass(fluxes, rows, consume)
    lax.fori_loop(0, ay, send, 0)


def forward_waves(at, window, clo, chi, first_slopes):
    shapes = [(ay, 64, nz), (ay, 48, nz), (ay, bx, nz), (3, ay, 48, nz)]
    return pl.pallas_call(
        forward_kernel,
        out_shape=tuple(jax.ShapeDtypeStruct(shape, F32) for shape in shapes)
        + (jax.ShapeDtypeStruct((ay, 32, nz), BF16),) * 2
        + (jax.ShapeDtypeStruct((ay, dom, nz), F32),)
        + tuple(jax.ShapeDtypeStruct(shape, F32) for shape in weight_sizes),
        in_specs=[scalars] + whole(10),
        out_specs=tuple(whole(11)),
        scratch_shapes=[padded, padded, padded, *flux_shapes, pltpu.VMEM((32, nz), F32)],
        compiler_params=vmem,
        name="forward_waves",
    )(at, window, clo, chi, *first_slopes, slope_matrix, spread_matrix)


def slopes_kernel(p1_ref, p2_ref, p3_ref, slope_ref, sx_ref, sy_ref, sh_ref, sb_ref, field):
    clear_sides(field)
    for index, (ref, first) in enumerate(((p1_ref, 8), (p2_ref, 8), (p3_ref, 16))):
        rows = ref.shape[1]

        def load(y, carry):
            field[y + 4, pl.ds(lead + first, rows), :] = ref[y]
            return carry

        lax.fori_loop(0, ay, load, 0)

        def body(y, carry):
            sx, sy = slopes_xy(field, y, 16, 48)
            sx_ref[index, y] = sx[:48]
            sy_ref[index, y] = sy
            return carry

        lax.fori_loop(0, ay, body, 0, unroll=2)
        sy_ref[index, ay] = slope_y(field, ay, 16, 48)

        def third(part, carry):
            y = part * group
            here, before = slopes_z(rows_of(field, y + 4, group, lead + 16, 48), slope_ref)
            sh_ref[index, pl.ds(y, group)] = here.reshape(group, 48, nz)
            sb_ref[index, pl.ds(y, group)] = before.reshape(group, 48, nz)
            return carry

        lax.fori_loop(0, ay // group, third, 0)


def wave_slopes(p1, p2, p3):
    shapes = [(3, ay, 48, nz), (3, ay + 1, 48, nz), (3, ay, 48, nz), (3, ay, 48, nz)]
    return pl.pallas_call(
        slopes_kernel,
        out_shape=tuple(jax.ShapeDtypeStruct(shape, F32) for shape in shapes),
        in_specs=whole(4),
        out_specs=tuple(whole(4)),
        scratch_shapes=[padded],
        compiler_params=vmem,
        cost_estimate=cost(6),
        name="wave_slopes",
    )(p1, p2, p3, slope_matrix)


def adjoint_kernel(
    at_ref, p2_ref, p3_ref, p4_ref, image_ref, back_ref, front_ref, seen_ref,
    slope_ref, spread_ref, modulus, wx, wy, wz, wzl, px_ref, py_ref, ph_ref, pb_ref,
    column_ref,
    scaled, later, late, grad_m, fx, fy, az, qx, qy, qh, qb, far,
):
    weights = (wx, wy, wz, wzl)
    fluxes = (fx, fy, az)
    matrices = (slope_ref, spread_ref)
    clear_rims(fy)
    clear_sides(scaled)
    low, high = halo_scale(at_ref)

    def residual(step, y, first, value):
        rows = value.shape[0]
        start = pl.multiple_of(y * dom + first, 8)
        count = seen_ref[0, pl.ds(start, rows), :]
        total = seen_ref[step, pl.ds(start, rows), :]
        return misfit_weight * (count * value - total)

    far[...] = jnp.zeros(far.shape, F32)

    def seed(y, carry):
        late[y, pl.ds(8, 48), :] = p3_ref[y]
        received = low * back_ref[y].astype(F32)
        far[pl.ds(4, 13), :] = received[14:27]
        far[pl.ds(17, 7), :] = received[:7] + received[7:14]
        late[y, pl.ds(3, 5), :] = received[27:]
        far[pl.ds(rim, bx), :] = p4_ref[y]
        received = high * front_ref[y].astype(F32)
        far[pl.ds(rim + bx, 7), :] = received[:7] + received[7:14]
        far[pl.ds(rim + bx + 7, 13), :] = received[14:27]
        late[y, pl.ds(56, 5), :] = received[27:]
        error = residual(3, y, 0, far[...])
        later[y] = error
        scaled[y + 4, pl.ds(lead, dom), :] = modulus[y] * error
        grad_m[y] = error[16:64] * image_ref[2, y]
        return carry

    lax.fori_loop(0, ay, seed, 0)

    def add(ref, place, product, index):
        ref[place] = product if index == 2 else ref[place] + product

    def cross(index, offset):
        def also(y, sx, sy):
            add(qx, y, sx[offset : offset + 48] * px_ref[index, y], index)
            add(qy, y, sy[offset : offset + 48] * py_ref[index, y], index)

        return also

    def cross_third(index, offset):
        def also(y, here, before):
            for ref, slope, other in ((qh, here, ph_ref), (qb, before, pb_ref)):
                rows = slope.shape[0] // group
                near_rows = slope.reshape(group, rows, nz)[:, offset : offset + 48]
                add(ref, pl.ds(y, group), near_rows * other[index, pl.ds(y, group)], index)

        return also

    def cross_last(index, offset, sy):
        add(qy, ay, sy[offset : offset + 48] * py_ref[index, ay], index)

    def step_three(y, image):
        value = late[y]
        value = residual(2, y, 8, value) + 2.0 * later[y, pl.ds(8, 64), :] + image
        late[y] = value
        grad_m[y] = grad_m[y] + value[8:56] * image_ref[1, y]

    def step_two(y, image):
        value = (
            residual(1, y, 16, p2_ref[y, pl.ds(8, 48), :])
            + 2.0 * late[y, pl.ds(8, 48), :]
            + image
            - later[y, pl.ds(16, 48), :]
        )
        grad_m[y] = grad_m[y] + value * image_ref[0, y]
        later[y, pl.ds(16, 48), :] = value

    third_pass(scaled, weights, matrices, az, 8, 64, cross_third(2, 8))
    sy = flux_pass(scaled, weights, fluxes, 8, 64, cross(2, 8))
    cross_last(2, 8, sy)
    divergence_pass(fluxes, 64, step_three)

    def rescale(y, carry):
        scaled[y + 4, pl.ds(lead + 8, 64), :] = modulus[y, pl.ds(8, 64), :] * late[y]
        return carry

    lax.fori_loop(0, ay, rescale, 0, unroll=2)
    third_pass(scaled, weights, matrices, az, 16, 48, cross_third(1, 0))
    sy = flux_pass(scaled, weights, fluxes, 16, 48, cross(1, 0))
    cross_last(1, 0, sy)
    divergence_pass(fluxes, 48, step_two)

    def rescale_last(y, carry):
        scaled[y + 4, pl.ds(lead + 16, 48), :] = modulus[y, pl.ds(16, 48), :] * later[y, pl.ds(16, 48), :]
        return carry

    lax.fori_loop(0, ay, rescale_last, 0, unroll=2)

    def last_third(part, carry):
        y = part * group
        cross_third(0, 0)(y, *slopes_z(rows_of(scaled, y + 4, group, lead + 16, 48), slope_ref))
        return carry

    lax.fori_loop(0, ay // group, last_third, 0)

    def last_slopes(y, carry):
        cross(0, 0)(y, *slopes_xy(scaled, y, 16, 48))
        return carry

    lax.fori_loop(0, ay, last_slopes, 0, unroll=2)
    cross_last(0, 0, slope_y(scaled, ay, 16, 48))

    first_row = at_ref[2]

    def blank(row, carry):
        column_ref[row] = jnp.zeros(column_ref.shape[1:], F32)
        return carry

    lax.fori_loop(0, first_row, blank, 0)
    lax.fori_loop(first_row + ay, 2 * shots, blank, 0)

    def place(y, carry):
        before = pltpu.roll(qb[y, pl.ds(6, gx), :], 1, 1)
        total = qh[y, pl.ds(6, gx), :] + before
        total = total + qy[y, pl.ds(6, gx), :] + qy[y + 1, pl.ds(6, gx), :]
        total = total + qx[y, pl.ds(9, gx), :] + qx[y, pl.ds(10, gx), :]
        column_ref[first_row + y, pl.ds(0, gx), :] = grad_m[y, pl.ds(6, gx), :]
        column_ref[first_row + y, pl.ds(gx, gx), :] = (-0.5 * tap_square) * total
        return carry

    lax.fori_loop(0, ay, place, 0, unroll=2)


def adjoint_waves(at, fields, images, back, front, seen, modulus, weights, slopes):
    near = pltpu.VMEM((ay, 48, nz), F32)
    return pl.pallas_call(
        adjoint_kernel,
        out_shape=jax.ShapeDtypeStruct((2 * shots, 2 * gx, nz), F32),
        in_specs=[scalars] + whole(18),
        out_specs=whole(1)[0],
        scratch_shapes=[
            padded,
            pltpu.VMEM((ay, dom, nz), F32),
            pltpu.VMEM((ay, 64, nz), F32),
            near,
            *flux_shapes,
            near,
            pltpu.VMEM((ay + 1, 48, nz), F32),
            near,
            near,
            pltpu.VMEM((dom, nz), F32),
        ],
        compiler_params=vmem,
        name="adjoint_waves",
    )(at, *fields, images, back, front, seen, slope_matrix, spread_matrix, modulus, *weights, *slopes)


def chain_kernel(at_ref, got_ref, out_ref, grad_ref):
    brick = at_ref[1]
    row = lax.broadcasted_iota(jnp.int32, (gx, nz), 0)
    fine = ((row >= 2) | (brick > 0)) & ((row < gx - 2) | (brick < bricks - 1))
    for y in range(2):
        total = got_ref[0, y]
        for shot in range(1, shots):
            total = total + got_ref[shot, y]
        squashed = jax.nn.sigmoid(out_ref[0, y])
        bent = jnp.tanh(out_ref[1, y])
        buoyancy = jnp.exp(0.35 * bent)
        first = total[:gx] * 0.09 * squashed * (1.0 - squashed)
        second = total[gx:] * buoyancy * 0.35 * (1.0 - bent * bent)
        grad_ref[y, 0] = jnp.where(fine, first, 0.0).astype(BF16)
        grad_ref[y, 1] = jnp.where(fine, second, 0.0).astype(BF16)


def chain(at, got, output):
    return pl.pallas_call(
        chain_kernel,
        out_shape=jax.ShapeDtypeStruct((2, 2, gx, nz), BF16),
        in_specs=[scalars] + whole(2),
        out_specs=whole(1)[0],
        compiler_params=vmem,
        name="chain",
    )(at, got, output)


def spread_kernel(at_ref, lo_ref, mid_ref, hi_ref, hid_ref, s1, s2):
    shot, brick = at_ref[0], at_ref[1]
    y_fine = (shot > 0, True, shot < shots - 1)

    def spread(x, carry):
        x_fine = ((x >= 1) | (brick > 0)) & ((x < bx + 1) | (brick < bricks - 1))
        for y, (ref, row, part) in enumerate(((lo_ref, 1, 0), (mid_ref, 0, 1), (mid_ref, 1, 1), (hi_ref, 0, 2))):
            value = jnp.where(x_fine & y_fine[part], ref[row, x + 3].astype(F32), 0.0)
            hidden = hid_ref[x + 2, pl.ds(y * 16, 16), :].astype(F32)
            for k in range(3):
                s1[x, pl.ds(y * 48 + k * 16, 16), :] = lane_shift(value, k).astype(BF16)
                s2[x, pl.ds(y * 48 + k * 16, 16), :] = lane_shift(hidden, k).astype(BF16)
        return carry

    lax.fori_loop(0, bx + 2, spread, 0, unroll=2)


def spread_fields(at, lo, mid, hi, hidden):
    shape = jax.ShapeDtypeStruct((bx + 2, 192, nz), BF16)
    return pl.pallas_call(
        spread_kernel,
        out_shape=(shape, shape),
        in_specs=[scalars] + whole(4),
        out_specs=tuple(whole(2)),
        compiler_params=vmem,
        cost_estimate=cost(3),
        name="spread_fields",
    )(at, lo, mid, hi, hidden)


contract_lanes = (((1,), (1,)), ((), ()))


def second_grads_kernel(gmid_ref, s2, second_ref, own):
    own[...] = jnp.zeros(own.shape, F32)
    for row in range(2):
        for channel in range(2):
            own[:, channel * 2 + row, :] = gmid_ref[row, channel].astype(F32)[2 : bx + 2]

    def kernel_grad(x, second):
        return second + lax.dot_general(
            own[x].astype(BF16), s2[pl.ds(x, 3)].reshape(576, nz), contract_lanes, preferred_element_type=F32
        )

    second_ref[...] = lax.fori_loop(0, bx, kernel_grad, jnp.zeros((8, 576), F32), unroll=4)


def second_grads(grad_output, s2):
    return pl.pallas_call(
        second_grads_kernel,
        out_shape=jax.ShapeDtypeStruct((8, 576), F32),
        in_specs=whole(2),
        out_specs=whole(1)[0],
        scratch_shapes=[pltpu.VMEM((bx, 8, nz), F32)],
        compiler_params=vmem,
        cost_estimate=cost(3),
        name="second_grads",
    )(grad_output, s2)


def first_grads_kernel(
    at_ref, glo_ref, gmid_ref, ghi_ref, hid_ref, second_ref, w3_ref, s1_any, inner_ref, kernel_ref, turned, s1, ready
):
    fetch = pltpu.make_async_copy(s1_any, s1, ready)
    fetch.start()
    shot, brick = at_ref[0], at_ref[1]
    y_fine = (shot > 0, True, shot < shots - 1)
    for part, ref in enumerate((glo_ref, gmid_ref, ghi_ref)):
        for row in range(2):
            for channel in range(2):
                value = jnp.where(y_fine[part], ref[row, channel].astype(F32), 0.0)
                value = jnp.concatenate([value, jnp.zeros((12, nz), F32)], axis=0)
                plane = (2 * part + row) * 2 + channel
                for k in range(3):
                    turned[plane * 3 + k] = lane_shift(value, k)

    def hidden_grad(block, carry):
        rows = turned[:, pl.ds(8 * block, 16), :].astype(BF16).reshape(576, nz)
        acc = jnp.dot(w3_ref[...], rows, preferred_element_type=F32)
        for xo in range(8):
            x = 8 * block + xo
            x_fine = ((x >= 1) | (brick > 0)) & ((x < bx + 1) | (brick < bricks - 1))
            hidden = hid_ref[jnp.minimum(x + 2, bx + 5)].astype(F32)
            value = acc[xo * 64 : xo * 64 + 64] * (1.0 - hidden * hidden)
            for y in range(4):
                fine = x_fine
                if y == 0:
                    fine = fine & (shot > 0)
                if y == 3:
                    fine = fine & (shot < shots - 1)
                inner_ref[x, pl.ds(y * 16, 16), :] = jnp.where(
                    fine, value[y * 16 : y * 16 + 16], 0.0
                ).astype(BF16)
        return carry

    lax.fori_loop(0, 5, hidden_grad, 0)
    fetch.wait()

    def kernel_grad(x, first):
        return first + lax.dot_general(
            inner_ref[x + 1, pl.ds(16, 32), :],
            s1[pl.ds(x, 3)].reshape(576, nz),
            contract_lanes,
            preferred_element_type=F32,
        )

    first = lax.fori_loop(0, bx, kernel_grad, jnp.zeros((32, 576), F32), unroll=4)
    second = second_ref[...]
    kernel_ref[...] = jnp.zeros(kernel_ref.shape, F32)
    for dx in range(3):
        start = dx * 192
        one = first[:16, start : start + 144] + first[16:, start + 48 : start + 192]
        for channel in range(2):
            row = channel * 2
            two = (
                second[row : row + 1, start : start + 144]
                + second[row + 1 : row + 2, start + 48 : start + 192]
            )
            place = dx * 2 * 18 + 16 + channel
            kernel_ref[pl.ds(place, 1), :] = two[:, :128]
            kernel_ref[pl.ds(place + 18, 1), pl.ds(0, 16)] = two[:, 128:]
        kernel_ref[pl.ds(dx * 36, 16), :] = one[:, :128]
        kernel_ref[pl.ds(dx * 36 + 18, 16), pl.ds(0, 16)] = one[:, 128:]


def first_grads(at, glo, gmid, ghi, hidden, second, w3, s1):
    return pl.pallas_call(
        first_grads_kernel,
        out_shape=(
            jax.ShapeDtypeStruct((40, 64, nz), BF16),
            jax.ShapeDtypeStruct((128, nz), F32),
        ),
        in_specs=[scalars] + whole(6) + [pl.BlockSpec(memory_space=pl.ANY)],
        out_specs=tuple(whole(2)),
        scratch_shapes=[
            pltpu.VMEM((36, 48, nz), F32),
            pltpu.VMEM((bx + 2, 192, nz), BF16),
            pltpu.SemaphoreType.DMA,
        ],
        compiler_params=vmem,
        name="first_grads",
    )(at, glo, gmid, ghi, hidden, second, w3, s1)


def latent_grad_kernel(inner_ref, w4_ref, latent_ref, s4):
    def spread(x, carry):
        for y in range(4):
            value = inner_ref[x, pl.ds(y * 16, 16), :].astype(F32)
            for k in range(3):
                s4[x, pl.ds(y * 48 + k * 16, 16), :] = lane_shift(value, k).astype(BF16)
        return carry

    lax.fori_loop(0, bx + 2, spread, 0, unroll=2)

    def latent_grad(block, carry):
        rows = s4[pl.ds(4 * block, 6)].reshape(6 * 192, nz)
        acc = jnp.dot(w4_ref[...], rows, preferred_element_type=F32)
        latent_ref[pl.ds(4 * block, 4)] = acc.reshape(4, 32, nz)
        return carry

    lax.fori_loop(0, bx // 4, latent_grad, 0)


def latent_grads(inner, w4):
    return pl.pallas_call(
        latent_grad_kernel,
        out_shape=jax.ShapeDtypeStruct((bx, 32, nz), F32),
        in_specs=whole(2),
        out_specs=whole(1)[0],
        scratch_shapes=[pltpu.VMEM((bx + 2, 192, nz), BF16)],
        compiler_params=vmem,
        cost_estimate=cost(4),
        name="latent_grads",
    )(inner, w4)


def column_codes(x_in, y_in, order):
    if order == "xykc":
        x, y, k, c = np.meshgrid(*map(np.arange, (x_in, y_in, 3, 16)), indexing="ij")
    else:
        y, c, k, x = np.meshgrid(*map(np.arange, (y_in, 2, 3, x_in)), indexing="ij")
    return np.stack([(8 * x + y).ravel(), (16 * k + c).ravel()]).astype(np.int32)


codes_1 = column_codes(4, 6, "xykc")
codes_2 = column_codes(8, 4, "xykc")
codes_3 = column_codes(16, 6, "yckx")
codes_4 = column_codes(6, 4, "xykc")


def expand(taps_ref, codes_ref, spare, flip):
    place = codes_ref[1:2]
    size = place.shape[1]
    rows = lax.broadcasted_iota(jnp.int32, (16, size), 0)
    picks = [jnp.where(place == rows + 16 * k, 1.0, 0.0).astype(BF16) for k in range(3)]
    for pair in range(9):
        total = None
        for k in range(3):
            q = 3 * pair + k
            term = jnp.dot(taps_ref[26 - q if flip else q], picks[k], preferred_element_type=F32)
            total = term if total is None else total + term
        spare[pair, :, pl.ds(0, size)] = total


def fill_blocks(out_ref, codes_ref, spare, x_out, y_out):
    code = codes_ref[0:1]
    size = code.shape[1]
    same = lax.broadcasted_iota(jnp.int32, (16, size), 0) * 0 + code
    for xo in range(x_out):
        for y in range(y_out):
            block = jnp.zeros((16, size), F32)
            for pair in range(9):
                wanted = (xo + pair // 3) * 8 + y + pair % 3
                block = jnp.where(same == wanted, spare[pair, :, pl.ds(0, size)], block)
            out_ref[pl.ds((xo * y_out + y) * 16, 16), :] = block.astype(BF16)


def forward_bands_kernel(in_ref, out_taps_ref, codes_1_ref, codes_2_ref, w1_ref, w2_ref, spare, rows):
    expand(in_ref, codes_1_ref, spare, False)
    fill_blocks(w1_ref, codes_1_ref, spare, 2, 4)
    expand(out_taps_ref, codes_2_ref, spare, False)
    size = codes_2_ref.shape[1]
    code = codes_2_ref[0:1] - 8 * lax.broadcasted_iota(jnp.int32, (6, size), 0)
    for channel in range(2):
        for y in range(2):
            block = jnp.zeros((6, size), F32)
            for pair in range(9):
                wanted = (pair // 3) * 8 + y + pair % 3
                block = jnp.where(code == wanted, spare[pair, channel : channel + 1, :], block)
            rows[pl.ds((channel * 2 + y) * 6, 6), :] = block
    w2_ref[...] = rows[...].astype(BF16)


def backward_bands_kernel(in_ref, out_taps_ref, codes_3_ref, codes_4_ref, w3_ref, w4_ref, spare):
    expand(out_taps_ref, codes_3_ref, spare, True)
    fill_blocks(w3_ref, codes_3_ref, spare, 8, 4)
    expand(in_ref, codes_4_ref, spare, True)
    fill_blocks(w4_ref, codes_4_ref, spare, 4, 2)


def forward_bands(taps_in, taps_out):
    return pl.pallas_call(
        forward_bands_kernel,
        out_shape=(
            jax.ShapeDtypeStruct((128, 1152), BF16),
            jax.ShapeDtypeStruct((24, 1536), BF16),
        ),
        in_specs=whole(4),
        out_specs=tuple(whole(2)),
        scratch_shapes=[pltpu.VMEM((9, 16, 1536), F32), pltpu.VMEM((24, 1536), F32)],
        compiler_params=vmem,
        cost_estimate=cost(3),
        name="forward_bands",
    )(taps_in, taps_out, codes_1, codes_2)


def backward_bands(taps_in, taps_out):
    return pl.pallas_call(
        backward_bands_kernel,
        out_shape=(
            jax.ShapeDtypeStruct((512, 576), BF16),
            jax.ShapeDtypeStruct((128, 1152), BF16),
        ),
        in_specs=whole(4),
        out_specs=tuple(whole(2)),
        scratch_shapes=[pltpu.VMEM((9, 16, 1152), F32)],
        compiler_params=vmem,
        cost_estimate=cost(4),
        name="backward_bands",
    )(taps_in, taps_out, codes_3, codes_4)


def both_ways(ahead, behind, axis):
    count = lax.axis_size(axis)
    forward = [(i, (i + 1) % count) for i in range(count)]
    backward_ = [(target, source) for source, target in forward]
    return lax.ppermute(ahead, axis, forward), lax.ppermute(behind, axis, backward_)


def per_device(latent, conv_in, conv_out, source_field, observed, aperture, receivers):
    shot = lax.axis_index("shot")
    brick = lax.axis_index("brick")
    at = jnp.stack([shot, brick, aperture[0]]).astype(jnp.int32)
    taps_out = jnp.pad(conv_out, ((0, 0), (0, 14), (0, 0)))
    w1, w2 = forward_bands(conv_in, taps_out)
    w3, w4 = backward_bands(conv_in.transpose(0, 2, 1), taps_out.transpose(0, 2, 1))

    tile = jnp.transpose(latent, (2, 1, 0, 3))
    from_low, from_high = both_ways(tile[:, bx - 4 :], tile[:, :4], "brick")
    mid = jnp.concatenate([from_low, tile, from_high], axis=1)
    lo, hi = both_ways(mid, mid, "shot")
    source = jnp.transpose(source_field[0], (1, 0, 2))
    plo, phi = both_ways(source[:, bx - rim :], source[:, :rim], "brick")
    seen = receiver_fields(at, receivers[0], observed[0])

    coefficients, output, hidden = generator(at, lo, mid, hi, w1, w2)
    coefficients, plo, phi = lax.optimization_barrier((coefficients, plo, phi))
    sent = jnp.broadcast_to(coefficients[None], (shots, 2, 2, bx, nz))
    column = lax.all_to_all(sent, "shot", 0, 0, tiled=True)
    column, seen, w3, w4 = lax.optimization_barrier((column, seen, w3, w4))
    window, ahead, behind = take_window(at, column.reshape(2 * shots, 2, bx, nz))
    clo, chi = both_ways(ahead, behind, "brick")
    s1, s2 = spread_fields(at, lo, mid, hi, hidden)
    first_slopes = source_slopes(at, source, plo, phi)
    clo, chi, s1, s2, first_slopes = lax.optimization_barrier((clo, chi, s1, s2, first_slopes))
    p2, p3, p4, images, ahead, behind, modulus, *weights = forward_waves(
        at, window, clo, chi, first_slopes
    )
    back, front = both_ways(ahead, behind, "brick")
    slopes = wave_slopes(first_slopes[0], p2, p3)
    back, front, slopes = lax.optimization_barrier((back, front, slopes))
    grads = adjoint_waves(at, (p2, p3, p4), images, back, front, seen, modulus, weights, slopes)
    got = lax.all_to_all(grads, "shot", 0, 0, tiled=True)
    got = got.reshape(shots, 2, 2 * gx, nz)
    grad_output = chain(at, got, output)
    glo, ghi = both_ways(grad_output, grad_output, "shot")
    second = second_grads(grad_output, s2)
    inner, kernels = first_grads(at, glo, grad_output, ghi, hidden, second, w3, s1)
    grad_latent = latent_grads(inner, w4)
    grad_latent = jnp.transpose(grad_latent.reshape(bx, 2, 16, nz), (2, 0, 1, 3))

    everyone = ("shot", "brick")
    slices = lax.all_to_all(kernels, everyone, 0, 0, tiled=True)
    mine = jnp.sum(slices, axis=0, keepdims=True)
    summed = lax.all_to_all(jnp.broadcast_to(mine, (128, nz)), everyone, 0, 0, tiled=True)
    folded = summed[:108].reshape(3, 2, 18, nz).transpose(0, 2, 1, 3).reshape(3, 18, 256)[:, :, :144]
    folded = folded.reshape(3, 18, 9, 16).transpose(0, 2, 1, 3).reshape(27, 18, 16)
    return (grad_latent, folded[:, :16], folded[:, 16:])


def solution(mesh):
    placed = (
        P(None, "brick", "shot", None),
        P(),
        P(),
        P("shot", "brick", None, None),
        P("shot", None, None),
        P("shot"),
        P("shot", None, None),
    )
    return jax.shard_map(
        per_device,
        mesh=mesh,
        in_specs=placed,
        out_specs=(P(None, "brick", "shot", None), P(), P()),
        check_vma=False,
    )
```

```python
import jax
import jax.numpy as jnp
import numpy as np
from jax import lax
from jax.experimental import pallas as pl
from jax.experimental.pallas import tpu as pltpu
from jax.sharding import PartitionSpec as P

F32 = jnp.float32
BF16 = jnp.bfloat16
stencil_taps = (1225.0 / 1024.0, -245.0 / 3072.0, 49.0 / 5120.0, -5.0 / 7168.0)
ratios = tuple(tap / stencil_taps[0] for tap in stencil_taps)
tap_square = stencil_taps[0] ** 2
misfit_weight = 16.0

bricks, shots = 8, 16
bx = 32
ay = 16
nz = 128
rim = 24
dom = bx + 2 * rim
lead = 8
xpad = dom + 24
ypad = ay + 8
gx = bx + 4
vmem = pltpu.CompilerParams(vmem_limit_bytes=24 * 1024 * 1024)


def cost(microseconds):
    return pl.CostEstimate(flops=0, bytes_accessed=int(microseconds * 3e6), transcendentals=0)


def whole(count):
    return [pl.BlockSpec(memory_space=pltpu.VMEM)] * count


scalars = pl.BlockSpec(memory_space=pltpu.SMEM)


def lane_index():
    return lax.broadcasted_iota(jnp.int32, (1, nz), 1)


def lane_shift(value, offset):
    if offset == 1:
        return value
    lane = lax.broadcasted_iota(jnp.int32, value.shape, 1)
    if offset == 0:
        return jnp.where(lane == 0, 0.0, pltpu.roll(value, 1, 1))
    return jnp.where(lane == nz - 1, 0.0, pltpu.roll(value, nz - 1, 1))


def generator_kernel(
    at_ref, lo_ref, mid_ref, hi_ref, w1_ref, w2_ref, coef_ref, out_ref, hid_ref, s1, s2
):
    shot, brick = at_ref[0], at_ref[1]
    y_fine = (shot > 0, True, shot < shots - 1)

    def spread(x, carry):
        x_fine = ((x >= 4) | (brick > 0)) & ((x < bx + 4) | (brick < bricks - 1))
        for part, ref in enumerate((lo_ref, mid_ref, hi_ref)):
            fine = x_fine & y_fine[part]
            for row in range(2):
                value = jnp.where(fine, ref[row, x].astype(F32), 0.0)
                for k in range(3):
                    s1[x, pl.ds((2 * part + row) * 48 + k * 16, 16), :] = lane_shift(
                        value, k
                    ).astype(BF16)
        return carry

    lax.fori_loop(0, bx + 8, spread, 0, unroll=4)
    last_block = (bx + 6) // 2 - 1

    def first_conv(block, before):
        before = jnp.tanh(before)
        for xo in range(2):
            x = jnp.maximum(2 * block - 2, 0) + xo
            x_fine = ((x >= 3) | (brick > 0)) & ((x < bx + 3) | (brick < bricks - 1))
            for y in range(4):
                fine = x_fine
                if y == 0:
                    fine = fine & (shot > 0)
                if y == 3:
                    fine = fine & (shot < shots - 1)
                start = (xo * 4 + y) * 16
                value = jnp.where(fine, before[start : start + 16], 0.0).astype(BF16)
                hid_ref[x, pl.ds(y * 16, 16), :] = value
                wide = value.astype(F32)
                for k in range(3):
                    s2[x, pl.ds(y * 48 + k * 16, 16), :] = lane_shift(wide, k).astype(BF16)
        rows = s1[pl.ds(2 * jnp.minimum(block, last_block), 4)].reshape(4 * 288, nz)
        return jnp.dot(w1_ref[...], rows, preferred_element_type=F32)

    lax.fori_loop(0, last_block + 2, first_conv, jnp.zeros((128, nz), F32))

    for block in range(gx // 6):
        rows = s2[pl.ds(6 * block, 8)].reshape(8 * 192, nz)
        acc = jnp.dot(w2_ref[...], rows, preferred_element_type=F32)
        for channel in range(2):
            for y in range(2):
                start = (channel * 2 + y) * 6
                out_ref[channel, y, pl.ds(6 * block, 6), :] = acc[start : start + 6]
    for y in range(2):
        modulus = 0.03 + 0.09 * jax.nn.sigmoid(out_ref[0, y, pl.ds(2, bx), :])
        buoyancy = jnp.exp(0.35 * jnp.tanh(out_ref[1, y, pl.ds(2, bx), :]))
        coef_ref[y, 0] = modulus
        coef_ref[y, 1] = buoyancy


def generator(at, lo, mid, hi, w1, w2):
    return pl.pallas_call(
        generator_kernel,
        out_shape=(
            jax.ShapeDtypeStruct((2, 2, bx, nz), F32),
            jax.ShapeDtypeStruct((2, 2, gx, nz), F32),
            jax.ShapeDtypeStruct((bx + 6, 64, nz), BF16),
        ),
        in_specs=[scalars] + whole(5),
        out_specs=tuple(whole(3)),
        scratch_shapes=[
            pltpu.VMEM((bx + 8, 288, nz), BF16),
            pltpu.VMEM((bx + 6, 192, nz), BF16),
        ],
        compiler_params=vmem,
        name="generator",
    )(at, lo, mid, hi, w1, w2)


def receiver_kernel(at_ref, cell_ref, seen_ref, out_ref, hot, spread):
    brick, first_row = at_ref[1], at_ref[2]
    count = cell_ref.shape[1]
    x = cell_ref[0:1] - brick * bx + rim
    row_of = jnp.where((x >= 0) & (x < dom), (cell_ref[1:2] - first_row) * dom + x, -1)
    z = cell_ref[2:3]

    def mark(chunk, carry):
        rows = chunk * 16 + lax.broadcasted_iota(jnp.int32, (16, count), 0)
        hot[pl.ds(chunk * 16, 16), :] = jnp.where(rows == row_of, 1.0, 0.0).astype(BF16)
        return carry

    lax.fori_loop(0, ay * dom // 16, mark, 0)
    parts = [jnp.ones((1, count), F32)]
    for step in range(3):
        value = seen_ref[step : step + 1]
        high = value.astype(BF16).astype(F32)
        parts += [high, value - high]

    def place(chunk, carry):
        same = chunk * 16 + lax.broadcasted_iota(jnp.int32, (16, count), 0) == z
        for index, part in enumerate(parts):
            spread[pl.ds(index * nz + chunk * 16, 16), :] = jnp.where(same, part, 0.0).astype(BF16)
        return carry

    lax.fori_loop(0, nz // 16, place, 0)
    size = 256

    def multiply(chunk, carry):
        left = hot[pl.ds(chunk * size, size), :]
        for field in range(4):
            first = 0 if field == 0 else (2 * field - 1) * nz
            right = spread[pl.ds(first, nz if field == 0 else 2 * nz), :]
            acc = lax.dot_general(
                left, right, (((1,), (1,)), ((), ())), preferred_element_type=F32
            )
            if field:
                acc = acc[:, :nz] + acc[:, nz:]
            out_ref[field, pl.ds(chunk * size, size), :] = acc
        return carry

    lax.fori_loop(0, ay * dom // size, multiply, 0)


def receiver_fields(at, cells, seen):
    count = cells.shape[1]
    return pl.pallas_call(
        receiver_kernel,
        out_shape=jax.ShapeDtypeStruct((4, ay * dom, nz), F32),
        in_specs=[scalars] + whole(2),
        out_specs=whole(1)[0],
        scratch_shapes=[
            pltpu.VMEM((ay * dom, count), BF16),
            pltpu.VMEM((7 * nz, count), BF16),
        ],
        compiler_params=vmem,
        cost_estimate=cost(9),
        name="receiver_fields",
    )(at, cells, seen)


def third_dimension_matrices():
    slope = np.zeros((nz, 2 * nz))
    spread = np.zeros((nz, nz))
    for t, ratio in enumerate(ratios, 1):
        slope[t - 1, nz:] += ratio
        for face in range(nz):
            if face + t < nz:
                slope[face + t, face] += ratio
            if face + 1 - t >= 0:
                slope[face + 1 - t, face] -= ratio
        for cell in range(nz):
            if cell + t - 1 < nz:
                spread[cell + t - 1, cell] += ratio
            if cell - t >= 0:
                spread[cell - t, cell] -= ratio

    def parts(matrix):
        high = matrix.astype(jnp.bfloat16)
        return np.concatenate([high, high, (matrix - high.astype(np.float64)).astype(jnp.bfloat16)])

    return parts(slope), parts(spread)


slope_matrix, spread_matrix = third_dimension_matrices()


def halves(value):
    high = value.astype(BF16)
    return high, (value - high.astype(F32)).astype(BF16)


def slopes_z(value, slope_ref):
    high, low = halves(value)
    both = jnp.dot(
        jnp.concatenate([high, low, high], axis=1), slope_ref[...], preferred_element_type=F32
    )
    return both[:, :nz], both[:, nz:]


def divergence_z(flux, first_part, spread_ref):
    high, low = halves(flux)
    return (
        jnp.dot(
            jnp.concatenate([high, low, high], axis=1), spread_ref[...], preferred_element_type=F32
        )
        - first_part
    )


def rows_of(ref, y, count, first, rows):
    return ref[pl.ds(y, count), pl.ds(first, rows), :].reshape(count * rows, nz)


group = 4


def differences(get):
    total = None
    for t in range(1, 5):
        upper, lower = get(t)
        term = upper - lower
        if t > 1:
            term = ratios[t - 1] * term
        total = term if total is None else total + term
    return total


def clear_sides(field):
    for y in (0, 1, 2, 3, ay + 4, ay + 5, ay + 6, ay + 7):
        field[y] = jnp.zeros(field.shape[1:], F32)


def clear_rims(flux_y):
    for j in (0, 1, 2, 20, 21, 22):
        flux_y[j] = jnp.zeros(flux_y.shape[1:], F32)


def halo_scale(at_ref):
    brick = at_ref[1]
    return (
        jnp.where(brick > 0, 1.0, 0.0).astype(F32),
        jnp.where(brick < bricks - 1, 1.0, 0.0).astype(F32),
    )


def window_kernel(at_ref, column_ref, win_ref, ahead_ref, behind_ref, message):
    first_row = at_ref[2]

    def body(y, carry):
        for channel in range(2):
            value = column_ref[first_row + y, channel]
            win_ref[y, channel] = value
            rounded = value.astype(BF16).astype(F32)
            rest = value - rounded
            for slot, (ref, near, further) in enumerate(((ahead_ref, 28, 12), (behind_ref, 0, 4))):
                place = (channel * 2 + slot) * 24
                message[pl.ds(place, 4), :] = rounded[near : near + 4]
                message[pl.ds(place + 4, 4), :] = rest[near : near + 4]
                message[pl.ds(place + 8, 16), :] = value[further : further + 16]
                ref[y, channel] = message[pl.ds(place, 24), :].astype(BF16)
        return carry

    lax.fori_loop(0, ay, body, 0, unroll=2)


def take_window(at, column):
    return pl.pallas_call(
        window_kernel,
        out_shape=(
            jax.ShapeDtypeStruct((ay, 2, bx, nz), F32),
            jax.ShapeDtypeStruct((ay, 2, 24, nz), BF16),
            jax.ShapeDtypeStruct((ay, 2, 24, nz), BF16),
        ),
        in_specs=[scalars] + whole(1),
        out_specs=tuple(whole(3)),
        scratch_shapes=[pltpu.VMEM((96, nz), F32)],
        compiler_params=vmem,
        name="take_window",
    )(at, column)


def slope_y(field, j, first, rows):
    return differences(
        lambda t: (
            field[j + 3 + t, pl.ds(lead + first, rows), :],
            field[j + 4 - t, pl.ds(lead + first, rows), :],
        )
    )


def slopes_xy(field, y, first, rows):
    base, more = lead + first - 4, rows + 8
    sx = differences(
        lambda t: (
            field[y + 4, pl.ds(base + t, more), :],
            field[y + 4, pl.ds(base + 1 - t, more), :],
        )
    )
    return sx, slope_y(field, y, first, rows)


def third_pass(field, weights, matrices, out, first, rows, also=None):
    _, _, wz, wzl = weights
    slope_ref, spread_ref = matrices

    def body(index, carry):
        y = index * group
        here, before = slopes_z(rows_of(field, y + 4, group, lead + first, rows), slope_ref)
        if also is not None:
            also(y, here, before)
        total = divergence_z(
            rows_of(wz, y, group, first, rows) * here,
            rows_of(wzl, y, group, first, rows) * before,
            spread_ref,
        )
        out[pl.ds(y, group), pl.ds(0, rows), :] = total.reshape(group, rows, nz)
        return carry

    lax.fori_loop(0, ay // group, body, 0, unroll=4)


def flux_pass(field, weights, fluxes, first, rows, also=None):
    wx, wy, _, _ = weights
    fx, fy, _ = fluxes
    base, more = lead + first - 4, rows + 8

    def body(y, carry):
        sx, sy = slopes_xy(field, y, first, rows)
        fx[y, pl.ds(0, more), :] = wx[y, pl.ds(base, more), :] * sx
        fy[y + 3, pl.ds(0, rows), :] = wy[y, pl.ds(first, rows), :] * sy
        if also is not None:
            also(y, sx, sy)
        return carry

    lax.fori_loop(0, ay, body, 0, unroll=2)
    sy = slope_y(field, ay, first, rows)
    fy[ay + 3, pl.ds(0, rows), :] = wy[ay, pl.ds(first, rows), :] * sy
    return sy


def divergence_pass(fluxes, rows, consume):
    fx, fy, az = fluxes

    def body(y, carry):
        total = az[y, pl.ds(0, rows), :] + differences(
            lambda t: (fx[y, pl.ds(3 + t, rows), :], fx[y, pl.ds(4 - t, rows), :])
        )
        total = total + differences(
            lambda t: (
                fy[y + t + 3, pl.ds(0, rows), :],
                fy[y - t + 4, pl.ds(0, rows), :],
            )
        )
        consume(y, total)
        return carry

    lax.fori_loop(0, ay, body, 0, unroll=2)


weight_sizes = ((ay, dom + 16, nz), (ay + 1, dom, nz), (ay, dom, nz), (ay, dom, nz))
padded = pltpu.VMEM((ypad, xpad, nz), F32)
flux_shapes = [
    pltpu.VMEM((ay, 72, nz), F32),
    pltpu.VMEM((23, 64, nz), F32),
    pltpu.VMEM((ay, 64, nz), F32),
]


def source_slopes_kernel(
    at_ref, src_ref, plo_ref, phi_ref, slope_ref, p1_ref, sx_ref, sy_ref, sh_ref, sb_ref, f1
):
    clear_sides(f1)
    low, high = halo_scale(at_ref)

    def load(y, carry):
        f1[y + 4, pl.ds(lead, rim), :] = low * plo_ref[y]
        f1[y + 4, pl.ds(lead + rim, bx), :] = src_ref[y]
        f1[y + 4, pl.ds(lead + rim + bx, rim), :] = high * phi_ref[y]
        p1_ref[y] = f1[y + 4, pl.ds(lead + 8, 64), :]
        return carry

    lax.fori_loop(0, ay, load, 0)

    def body(y, carry):
        sx_ref[y], sy_ref[y] = slopes_xy(f1, y, 8, 64)
        return carry

    lax.fori_loop(0, ay, body, 0, unroll=2)
    sy_ref[ay] = slope_y(f1, ay, 8, 64)

    def third(part, carry):
        y = part * group
        here, before = slopes_z(rows_of(f1, y + 4, group, lead + 8, 64), slope_ref)
        sh_ref[pl.ds(y, group)] = here.reshape(group, 64, nz)
        sb_ref[pl.ds(y, group)] = before.reshape(group, 64, nz)
        return carry

    lax.fori_loop(0, ay // group, third, 0)


def source_slopes(at, source, plo, phi):
    shapes = [(ay, 64, nz), (ay, 72, nz), (ay + 1, 64, nz), (ay, 64, nz), (ay, 64, nz)]
    return pl.pallas_call(
        source_slopes_kernel,
        out_shape=tuple(jax.ShapeDtypeStruct(shape, F32) for shape in shapes),
        in_specs=[scalars] + whole(4),
        out_specs=tuple(whole(5)),
        scratch_shapes=[padded],
        compiler_params=vmem,
        cost_estimate=cost(3),
        name="source_slopes",
    )(at, source, plo, phi, slope_matrix)


def forward_kernel(
    at_ref, win_ref, clo_ref, chi_ref, p1_ref, sx_ref, sy_ref, sh_ref, sb_ref, slope_ref, spread_ref,
    p2_ref, p3_ref, p4_ref, image_ref, ahead_ref, behind_ref, modulus, wx, wy, wz, wzl,
    buoy, f2, f3, fx, fy, az, message,
):
    half = 0.5 * tap_square
    last = lane_index() == nz - 1
    first_taps = sum(jnp.where(lane_index() == t, half * ratios[t], 0.0) for t in range(4))
    weights = (wx, wy, wz, wzl)
    fluxes = (fx, fy, az)
    matrices = (slope_ref, spread_ref)
    clear_rims(fy)
    for field in (buoy, f2, f3):
        clear_sides(field)
    low, high = halo_scale(at_ref)

    def load(y, carry):
        for channel, ref, row, skip in ((0, modulus, y, 0), (1, buoy, y + 4, lead)):
            received = low * clo_ref[y, channel].astype(F32)
            ref[row, pl.ds(skip + 4, 16), :] = received[8:]
            ref[row, pl.ds(skip + 20, 4), :] = received[:4] + received[4:8]
            ref[row, pl.ds(skip + rim, bx), :] = win_ref[y, channel]
            received = high * chi_ref[y, channel].astype(F32)
            ref[row, pl.ds(skip + rim + bx, 4), :] = received[:4] + received[4:8]
            ref[row, pl.ds(skip + rim + bx + 4, 16), :] = received[8:]
        return carry

    lax.fori_loop(0, ay, load, 0)

    def weigh(y, carry):
        inner = buoy[y + 4, pl.ds(lead, dom), :]
        ahead = pltpu.roll(inner, nz - 1, 1)
        value = buoy[y + 4, pl.ds(0, dom + 16), :]
        wx[y] = half * (value + buoy[y + 4, pl.ds(1, dom + 16), :])
        wy[y] = half * (buoy[y + 3, pl.ds(lead, dom), :] + inner)
        wz[y] = half * jnp.where(last, inner, inner + ahead)
        wzl[y] = inner[:, :1] * first_taps
        return carry

    lax.fori_loop(0, ay, weigh, 0, unroll=2)
    wy[ay] = half * buoy[ay + 3, pl.ds(lead, dom), :]

    def first_step(y, image):
        f2[y + 4, pl.ds(lead + 8, 64), :] = (
            2.0 * p1_ref[y] + modulus[y, pl.ds(8, 64), :] * image
        )
        image_ref[0, y] = image[8:56]

    def second_step(y, image):
        value = (
            2.0 * f2[y + 4, pl.ds(lead + 12, 56), :]
            - p1_ref[y, pl.ds(4, 56), :]
            + modulus[y, pl.ds(12, 56), :] * image
        )
        f3[y + 4, pl.ds(lead + 12, 56), :] = value
        image_ref[1, y] = image[4:52]
        p3_ref[y] = value[4:52]
        p2_ref[y] = f2[y + 4, pl.ds(lead + 8, 64), :]

    def third_step(y, image):
        image_ref[2, y] = image
        value = (
            2.0 * f3[y + 4, pl.ds(lead + rim, bx), :]
            - f2[y + 4, pl.ds(lead + rim, bx), :]
            + modulus[y, pl.ds(rim, bx), :] * image[8:40]
        )
        p4_ref[y] = value

    def pack(y, ref, near, further, third):
        value = p4_ref[y, pl.ds(near, 7), :]
        rounded = value.astype(BF16).astype(F32)
        message[pl.ds(0, 7), :] = rounded
        message[pl.ds(7, 7), :] = value - rounded
        message[pl.ds(14, 13), :] = p4_ref[y, pl.ds(further, 13), :]
        message[pl.ds(27, 5), :] = f3[y + 4, pl.ds(lead + rim + third, 5), :]
        ref[y] = message[...].astype(BF16)

    def send(y, carry):
        pack(y, ahead_ref, 25, 12, 19)
        pack(y, behind_ref, 0, 7, 8)
        return carry

    def first_third(part, carry):
        y = part * group
        total = divergence_z(
            rows_of(wz, y, group, 8, 64) * rows_of(sh_ref, y, group, 0, 64),
            rows_of(wzl, y, group, 8, 64) * rows_of(sb_ref, y, group, 0, 64),
            spread_ref,
        )
        az[pl.ds(y, group), pl.ds(0, 64), :] = total.reshape(group, 64, nz)
        return carry

    lax.fori_loop(0, ay // group, first_third, 0, unroll=4)

    def first_flux(y, carry):
        fx[y] = wx[y, pl.ds(lead + 4, 72), :] * sx_ref[y]
        fy[y + 3] = wy[y, pl.ds(8, 64), :] * sy_ref[y]
        return carry

    lax.fori_loop(0, ay, first_flux, 0, unroll=2)
    fy[ay + 3] = wy[ay, pl.ds(8, 64), :] * sy_ref[ay]
    divergence_pass(fluxes, 64, first_step)
    for field, first, rows, consume in (
        (f2, 12, 56, second_step),
        (f3, 16, 48, third_step),
    ):
        third_pass(field, weights, matrices, az, first, rows)
        flux_pass(field, weights, fluxes, first, rows)
        divergence_pass(fluxes, rows, consume)
    lax.fori_loop(0, ay, send, 0)


def forward_waves(at, window, clo, chi, first_slopes):
    shapes = [(ay, 64, nz), (ay, 48, nz), (ay, bx, nz), (3, ay, 48, nz)]
    return pl.pallas_call(
        forward_kernel,
        out_shape=tuple(jax.ShapeDtypeStruct(shape, F32) for shape in shapes)
        + (jax.ShapeDtypeStruct((ay, 32, nz), BF16),) * 2
        + (jax.ShapeDtypeStruct((ay, dom, nz), F32),)
        + tuple(jax.ShapeDtypeStruct(shape, F32) for shape in weight_sizes),
        in_specs=[scalars] + whole(10),
        out_specs=tuple(whole(11)),
        scratch_shapes=[padded, padded, padded, *flux_shapes, pltpu.VMEM((32, nz), F32)],
        compiler_params=vmem,
        name="forward_waves",
    )(at, window, clo, chi, *first_slopes, slope_matrix, spread_matrix)


def slopes_kernel(p1_ref, p2_ref, p3_ref, slope_ref, sx_ref, sy_ref, sh_ref, sb_ref, field):
    clear_sides(field)
    for index, (ref, first) in enumerate(((p1_ref, 8), (p2_ref, 8), (p3_ref, 16))):
        rows = ref.shape[1]

        def load(y, carry):
            field[y + 4, pl.ds(lead + first, rows), :] = ref[y]
            return carry

        lax.fori_loop(0, ay, load, 0)

        def body(y, carry):
            sx, sy = slopes_xy(field, y, 16, 48)
            sx_ref[index, y] = sx[:48]
            sy_ref[index, y] = sy
            return carry

        lax.fori_loop(0, ay, body, 0, unroll=2)
        sy_ref[index, ay] = slope_y(field, ay, 16, 48)

        def third(part, carry):
            y = part * group
            here, before = slopes_z(rows_of(field, y + 4, group, lead + 16, 48), slope_ref)
            sh_ref[index, pl.ds(y, group)] = here.reshape(group, 48, nz)
            sb_ref[index, pl.ds(y, group)] = before.reshape(group, 48, nz)
            return carry

        lax.fori_loop(0, ay // group, third, 0)


def wave_slopes(p1, p2, p3):
    shapes = [(3, ay, 48, nz), (3, ay + 1, 48, nz), (3, ay, 48, nz), (3, ay, 48, nz)]
    return pl.pallas_call(
        slopes_kernel,
        out_shape=tuple(jax.ShapeDtypeStruct(shape, F32) for shape in shapes),
        in_specs=whole(4),
        out_specs=tuple(whole(4)),
        scratch_shapes=[padded],
        compiler_params=vmem,
        cost_estimate=cost(6),
        name="wave_slopes",
    )(p1, p2, p3, slope_matrix)


def adjoint_kernel(
    at_ref, p2_ref, p3_ref, p4_ref, image_ref, back_ref, front_ref, seen_ref,
    slope_ref, spread_ref, modulus, wx, wy, wz, wzl, px_ref, py_ref, ph_ref, pb_ref,
    column_ref,
    scaled, later, late, grad_m, fx, fy, az, qx, qy, qh, qb, far,
):
    weights = (wx, wy, wz, wzl)
    fluxes = (fx, fy, az)
    matrices = (slope_ref, spread_ref)
    clear_rims(fy)
    clear_sides(scaled)
    low, high = halo_scale(at_ref)

    def residual(step, y, first, value):
        rows = value.shape[0]
        start = pl.multiple_of(y * dom + first, 8)
        count = seen_ref[0, pl.ds(start, rows), :]
        total = seen_ref[step, pl.ds(start, rows), :]
        return misfit_weight * (count * value - total)

    far[...] = jnp.zeros(far.shape, F32)

    def seed(y, carry):
        late[y, pl.ds(8, 48), :] = p3_ref[y]
        received = low * back_ref[y].astype(F32)
        far[pl.ds(4, 13), :] = received[14:27]
        far[pl.ds(17, 7), :] = received[:7] + received[7:14]
        late[y, pl.ds(3, 5), :] = received[27:]
        far[pl.ds(rim, bx), :] = p4_ref[y]
        received = high * front_ref[y].astype(F32)
        far[pl.ds(rim + bx, 7), :] = received[:7] + received[7:14]
        far[pl.ds(rim + bx + 7, 13), :] = received[14:27]
        late[y, pl.ds(56, 5), :] = received[27:]
        error = residual(3, y, 0, far[...])
        later[y] = error
        scaled[y + 4, pl.ds(lead, dom), :] = modulus[y] * error
        grad_m[y] = error[16:64] * image_ref[2, y]
        return carry

    lax.fori_loop(0, ay, seed, 0)

    def add(ref, place, product, index):
        ref[place] = product if index == 2 else ref[place] + product

    def cross(index, offset):
        def also(y, sx, sy):
            add(qx, y, sx[offset : offset + 48] * px_ref[index, y], index)
            add(qy, y, sy[offset : offset + 48] * py_ref[index, y], index)

        return also

    def cross_third(index, offset):
        def also(y, here, before):
            for ref, slope, other in ((qh, here, ph_ref), (qb, before, pb_ref)):
                rows = slope.shape[0] // group
                near_rows = slope.reshape(group, rows, nz)[:, offset : offset + 48]
                add(ref, pl.ds(y, group), near_rows * other[index, pl.ds(y, group)], index)

        return also

    def cross_last(index, offset, sy):
        add(qy, ay, sy[offset : offset + 48] * py_ref[index, ay], index)

    def step_three(y, image):
        value = late[y]
        value = residual(2, y, 8, value) + 2.0 * later[y, pl.ds(8, 64), :] + image
        late[y] = value
        grad_m[y] = grad_m[y] + value[8:56] * image_ref[1, y]

    def step_two(y, image):
        value = (
            residual(1, y, 16, p2_ref[y, pl.ds(8, 48), :])
            + 2.0 * late[y, pl.ds(8, 48), :]
            + image
            - later[y, pl.ds(16, 48), :]
        )
        grad_m[y] = grad_m[y] + value * image_ref[0, y]
        later[y, pl.ds(16, 48), :] = value

    third_pass(scaled, weights, matrices, az, 8, 64, cross_third(2, 8))
    sy = flux_pass(scaled, weights, fluxes, 8, 64, cross(2, 8))
    cross_last(2, 8, sy)
    divergence_pass(fluxes, 64, step_three)

    def rescale(y, carry):
        scaled[y + 4, pl.ds(lead + 8, 64), :] = modulus[y, pl.ds(8, 64), :] * late[y]
        return carry

    lax.fori_loop(0, ay, rescale, 0, unroll=2)
    third_pass(scaled, weights, matrices, az, 16, 48, cross_third(1, 0))
    sy = flux_pass(scaled, weights, fluxes, 16, 48, cross(1, 0))
    cross_last(1, 0, sy)
    divergence_pass(fluxes, 48, step_two)

    def rescale_last(y, carry):
        scaled[y + 4, pl.ds(lead + 16, 48), :] = modulus[y, pl.ds(16, 48), :] * later[y, pl.ds(16, 48), :]
        return carry

    lax.fori_loop(0, ay, rescale_last, 0, unroll=2)

    def last_third(part, carry):
        y = part * group
        cross_third(0, 0)(y, *slopes_z(rows_of(scaled, y + 4, group, lead + 16, 48), slope_ref))
        return carry

    lax.fori_loop(0, ay // group, last_third, 0)

    def last_slopes(y, carry):
        cross(0, 0)(y, *slopes_xy(scaled, y, 16, 48))
        return carry

    lax.fori_loop(0, ay, last_slopes, 0, unroll=2)
    cross_last(0, 0, slope_y(scaled, ay, 16, 48))

    first_row = at_ref[2]
    first_lane = lane_index() == 0

    def blank(row, carry):
        column_ref[row] = jnp.zeros(column_ref.shape[1:], F32)
        return carry

    lax.fori_loop(0, first_row, blank, 0)
    lax.fori_loop(first_row + ay, 2 * shots, blank, 0)

    def place(y, carry):
        here = qh[y, pl.ds(6, gx), :]
        total = here + jnp.where(first_lane, qb[y, pl.ds(6, gx), :], pltpu.roll(here, 1, 1))
        total = total + qy[y, pl.ds(6, gx), :] + qy[y + 1, pl.ds(6, gx), :]
        total = total + qx[y, pl.ds(9, gx), :] + qx[y, pl.ds(10, gx), :]
        column_ref[first_row + y, pl.ds(0, gx), :] = grad_m[y, pl.ds(6, gx), :]
        column_ref[first_row + y, pl.ds(gx, gx), :] = (-0.5 * tap_square) * total
        return carry

    lax.fori_loop(0, ay, place, 0, unroll=2)


def adjoint_waves(at, fields, images, back, front, seen, modulus, weights, slopes):
    near = pltpu.VMEM((ay, 48, nz), F32)
    return pl.pallas_call(
        adjoint_kernel,
        out_shape=jax.ShapeDtypeStruct((2 * shots, 2 * gx, nz), F32),
        in_specs=[scalars] + whole(18),
        out_specs=whole(1)[0],
        scratch_shapes=[
            padded,
            pltpu.VMEM((ay, dom, nz), F32),
            pltpu.VMEM((ay, 64, nz), F32),
            near,
            *flux_shapes,
            near,
            pltpu.VMEM((ay + 1, 48, nz), F32),
            near,
            near,
            pltpu.VMEM((dom, nz), F32),
        ],
        compiler_params=vmem,
        name="adjoint_waves",
    )(at, *fields, images, back, front, seen, slope_matrix, spread_matrix, modulus, *weights, *slopes)


def chain_kernel(at_ref, got_ref, out_ref, grad_ref):
    brick = at_ref[1]
    row = lax.broadcasted_iota(jnp.int32, (gx, nz), 0)
    fine = ((row >= 2) | (brick > 0)) & ((row < gx - 2) | (brick < bricks - 1))
    for y in range(2):
        total = got_ref[0, y]
        for shot in range(1, shots):
            total = total + got_ref[shot, y]
        squashed = jax.nn.sigmoid(out_ref[0, y])
        bent = jnp.tanh(out_ref[1, y])
        buoyancy = jnp.exp(0.35 * bent)
        first = total[:gx] * 0.09 * squashed * (1.0 - squashed)
        second = total[gx:] * buoyancy * 0.35 * (1.0 - bent * bent)
        grad_ref[y, 0] = jnp.where(fine, first, 0.0).astype(BF16)
        grad_ref[y, 1] = jnp.where(fine, second, 0.0).astype(BF16)


def chain(at, got, output):
    return pl.pallas_call(
        chain_kernel,
        out_shape=jax.ShapeDtypeStruct((2, 2, gx, nz), BF16),
        in_specs=[scalars] + whole(2),
        out_specs=whole(1)[0],
        compiler_params=vmem,
        name="chain",
    )(at, got, output)


def spread_kernel(at_ref, lo_ref, mid_ref, hi_ref, hid_ref, s1, s2):
    shot, brick = at_ref[0], at_ref[1]
    y_fine = (shot > 0, True, shot < shots - 1)

    def spread(x, carry):
        x_fine = ((x >= 1) | (brick > 0)) & ((x < bx + 1) | (brick < bricks - 1))
        for y, (ref, row, part) in enumerate(((lo_ref, 1, 0), (mid_ref, 0, 1), (mid_ref, 1, 1), (hi_ref, 0, 2))):
            value = jnp.where(x_fine & y_fine[part], ref[row, x + 3].astype(F32), 0.0)
            hidden = hid_ref[x + 2, pl.ds(y * 16, 16), :].astype(F32)
            for k in range(3):
                s1[x, pl.ds(y * 48 + k * 16, 16), :] = lane_shift(value, k).astype(BF16)
                s2[x, pl.ds(y * 48 + k * 16, 16), :] = lane_shift(hidden, k).astype(BF16)
        return carry

    lax.fori_loop(0, bx + 2, spread, 0, unroll=2)


def spread_fields(at, lo, mid, hi, hidden):
    shape = jax.ShapeDtypeStruct((bx + 2, 192, nz), BF16)
    return pl.pallas_call(
        spread_kernel,
        out_shape=(shape, shape),
        in_specs=[scalars] + whole(4),
        out_specs=tuple(whole(2)),
        compiler_params=vmem,
        cost_estimate=cost(3),
        name="spread_fields",
    )(at, lo, mid, hi, hidden)


contract_lanes = (((1,), (1,)), ((), ()))


def second_grads_kernel(gmid_ref, s2, second_ref, own):
    own[...] = jnp.zeros(own.shape, F32)
    for row in range(2):
        for channel in range(2):
            own[:, channel * 2 + row, :] = gmid_ref[row, channel].astype(F32)[2 : bx + 2]

    def kernel_grad(x, second):
        return second + lax.dot_general(
            own[x].astype(BF16), s2[pl.ds(x, 3)].reshape(576, nz), contract_lanes, preferred_element_type=F32
        )

    second_ref[...] = lax.fori_loop(0, bx, kernel_grad, jnp.zeros((8, 576), F32), unroll=4)


def second_grads(grad_output, s2):
    return pl.pallas_call(
        second_grads_kernel,
        out_shape=jax.ShapeDtypeStruct((8, 576), F32),
        in_specs=whole(2),
        out_specs=whole(1)[0],
        scratch_shapes=[pltpu.VMEM((bx, 8, nz), F32)],
        compiler_params=vmem,
        cost_estimate=cost(3),
        name="second_grads",
    )(grad_output, s2)


def first_grads_kernel(
    at_ref, glo_ref, gmid_ref, ghi_ref, hid_ref, second_ref, w3_ref, s1_any, inner_ref, kernel_ref, turned, s1, ready
):
    fetch = pltpu.make_async_copy(s1_any, s1, ready)
    fetch.start()
    shot, brick = at_ref[0], at_ref[1]
    y_fine = (shot > 0, True, shot < shots - 1)
    for part, ref in enumerate((glo_ref, gmid_ref, ghi_ref)):
        for row in range(2):
            for channel in range(2):
                value = jnp.where(y_fine[part], ref[row, channel].astype(F32), 0.0)
                value = jnp.concatenate([value, jnp.zeros((12, nz), F32)], axis=0)
                plane = (2 * part + row) * 2 + channel
                for k in range(3):
                    turned[plane * 3 + k] = lane_shift(value, k)

    def hidden_grad(block, carry):
        rows = turned[:, pl.ds(8 * block, 16), :].astype(BF16).reshape(576, nz)
        acc = jnp.dot(w3_ref[...], rows, preferred_element_type=F32)
        for xo in range(8):
            x = 8 * block + xo
            x_fine = ((x >= 1) | (brick > 0)) & ((x < bx + 1) | (brick < bricks - 1))
            hidden = hid_ref[jnp.minimum(x + 2, bx + 5)].astype(F32)
            value = acc[xo * 64 : xo * 64 + 64] * (1.0 - hidden * hidden)
            for y in range(4):
                fine = x_fine
                if y == 0:
                    fine = fine & (shot > 0)
                if y == 3:
                    fine = fine & (shot < shots - 1)
                inner_ref[x, pl.ds(y * 16, 16), :] = jnp.where(
                    fine, value[y * 16 : y * 16 + 16], 0.0
                ).astype(BF16)
        return carry

    lax.fori_loop(0, 5, hidden_grad, 0, unroll=5)
    fetch.wait()

    def kernel_grad(x, first):
        return first + lax.dot_general(
            inner_ref[x + 1, pl.ds(16, 32), :],
            s1[pl.ds(x, 3)].reshape(576, nz),
            contract_lanes,
            preferred_element_type=F32,
        )

    first = lax.fori_loop(0, bx, kernel_grad, jnp.zeros((32, 576), F32), unroll=4)
    second = second_ref[...]
    kernel_ref[...] = jnp.zeros(kernel_ref.shape, F32)
    for dx in range(3):
        start = dx * 192
        one = first[:16, start : start + 144] + first[16:, start + 48 : start + 192]
        for channel in range(2):
            row = channel * 2
            two = (
                second[row : row + 1, start : start + 144]
                + second[row + 1 : row + 2, start + 48 : start + 192]
            )
            place = dx * 2 * 18 + 16 + channel
            kernel_ref[pl.ds(place, 1), :] = two[:, :128]
            kernel_ref[pl.ds(place + 18, 1), pl.ds(0, 16)] = two[:, 128:]
        kernel_ref[pl.ds(dx * 36, 16), :] = one[:, :128]
        kernel_ref[pl.ds(dx * 36 + 18, 16), pl.ds(0, 16)] = one[:, 128:]


def first_grads(at, glo, gmid, ghi, hidden, second, w3, s1):
    return pl.pallas_call(
        first_grads_kernel,
        out_shape=(
            jax.ShapeDtypeStruct((40, 64, nz), BF16),
            jax.ShapeDtypeStruct((128, nz), F32),
        ),
        in_specs=[scalars] + whole(6) + [pl.BlockSpec(memory_space=pl.ANY)],
        out_specs=tuple(whole(2)),
        scratch_shapes=[
            pltpu.VMEM((36, 48, nz), F32),
            pltpu.VMEM((bx + 2, 192, nz), BF16),
            pltpu.SemaphoreType.DMA,
        ],
        compiler_params=vmem,
        name="first_grads",
    )(at, glo, gmid, ghi, hidden, second, w3, s1)


def latent_grad_kernel(inner_ref, w4_ref, latent_ref, s4):
    def spread(x, carry):
        for y in range(4):
            value = inner_ref[x, pl.ds(y * 16, 16), :].astype(F32)
            for k in range(3):
                s4[x, pl.ds(y * 48 + k * 16, 16), :] = lane_shift(value, k).astype(BF16)
        return carry

    lax.fori_loop(0, bx + 2, spread, 0, unroll=2)

    def latent_grad(block, carry):
        rows = s4[pl.ds(4 * block, 6)].reshape(6 * 192, nz)
        acc = jnp.dot(w4_ref[...], rows, preferred_element_type=F32)
        latent_ref[pl.ds(4 * block, 4)] = acc.reshape(4, 32, nz)
        return carry

    lax.fori_loop(0, bx // 4, latent_grad, 0)


def latent_grads(inner, w4):
    return pl.pallas_call(
        latent_grad_kernel,
        out_shape=jax.ShapeDtypeStruct((bx, 32, nz), F32),
        in_specs=whole(2),
        out_specs=whole(1)[0],
        scratch_shapes=[pltpu.VMEM((bx + 2, 192, nz), BF16)],
        compiler_params=vmem,
        cost_estimate=cost(4),
        name="latent_grads",
    )(inner, w4)


def column_codes(x_in, y_in, order):
    if order == "xykc":
        x, y, k, c = np.meshgrid(*map(np.arange, (x_in, y_in, 3, 16)), indexing="ij")
    else:
        y, c, k, x = np.meshgrid(*map(np.arange, (y_in, 2, 3, x_in)), indexing="ij")
    return np.stack([(8 * x + y).ravel(), (16 * k + c).ravel()]).astype(np.int32)


codes_1 = column_codes(4, 6, "xykc")
codes_2 = column_codes(8, 4, "xykc")
codes_3 = column_codes(16, 6, "yckx")
codes_4 = column_codes(6, 4, "xykc")


def expand(taps_ref, codes_ref, spare, flip):
    place = codes_ref[1:2]
    size = place.shape[1]
    rows = lax.broadcasted_iota(jnp.int32, (16, size), 0)
    picks = [jnp.where(place == rows + 16 * k, 1.0, 0.0).astype(BF16) for k in range(3)]
    for pair in range(9):
        total = None
        for k in range(3):
            q = 3 * pair + k
            term = jnp.dot(taps_ref[26 - q if flip else q], picks[k], preferred_element_type=F32)
            total = term if total is None else total + term
        spare[pair, :, pl.ds(0, size)] = total


def fill_blocks(out_ref, codes_ref, spare, x_out, y_out):
    code = codes_ref[0:1]
    size = code.shape[1]
    same = lax.broadcasted_iota(jnp.int32, (16, size), 0) * 0 + code
    for xo in range(x_out):
        for y in range(y_out):
            block = jnp.zeros((16, size), F32)
            for pair in range(9):
                wanted = (xo + pair // 3) * 8 + y + pair % 3
                block = jnp.where(same == wanted, spare[pair, :, pl.ds(0, size)], block)
            out_ref[pl.ds((xo * y_out + y) * 16, 16), :] = block.astype(BF16)


def forward_bands_kernel(in_ref, out_taps_ref, codes_1_ref, codes_2_ref, w1_ref, w2_ref, spare, rows):
    expand(in_ref, codes_1_ref, spare, False)
    fill_blocks(w1_ref, codes_1_ref, spare, 2, 4)
    expand(out_taps_ref, codes_2_ref, spare, False)
    size = codes_2_ref.shape[1]
    code = codes_2_ref[0:1] - 8 * lax.broadcasted_iota(jnp.int32, (6, size), 0)
    for channel in range(2):
        for y in range(2):
            block = jnp.zeros((6, size), F32)
            for pair in range(9):
                wanted = (pair // 3) * 8 + y + pair % 3
                block = jnp.where(code == wanted, spare[pair, channel : channel + 1, :], block)
            rows[pl.ds((channel * 2 + y) * 6, 6), :] = block
    w2_ref[...] = rows[...].astype(BF16)


def backward_bands_kernel(in_ref, out_taps_ref, codes_3_ref, codes_4_ref, w3_ref, w4_ref, spare):
    expand(out_taps_ref, codes_3_ref, spare, True)
    fill_blocks(w3_ref, codes_3_ref, spare, 8, 4)
    expand(in_ref, codes_4_ref, spare, True)
    fill_blocks(w4_ref, codes_4_ref, spare, 4, 2)


def forward_bands(taps_in, taps_out):
    return pl.pallas_call(
        forward_bands_kernel,
        out_shape=(
            jax.ShapeDtypeStruct((128, 1152), BF16),
            jax.ShapeDtypeStruct((24, 1536), BF16),
        ),
        in_specs=whole(4),
        out_specs=tuple(whole(2)),
        scratch_shapes=[pltpu.VMEM((9, 16, 1536), F32), pltpu.VMEM((24, 1536), F32)],
        compiler_params=vmem,
        cost_estimate=cost(3),
        name="forward_bands",
    )(taps_in, taps_out, codes_1, codes_2)


def backward_bands(taps_in, taps_out):
    return pl.pallas_call(
        backward_bands_kernel,
        out_shape=(
            jax.ShapeDtypeStruct((512, 576), BF16),
            jax.ShapeDtypeStruct((128, 1152), BF16),
        ),
        in_specs=whole(4),
        out_specs=tuple(whole(2)),
        scratch_shapes=[pltpu.VMEM((9, 16, 1152), F32)],
        compiler_params=vmem,
        cost_estimate=cost(4),
        name="backward_bands",
    )(taps_in, taps_out, codes_3, codes_4)


def both_ways(ahead, behind, axis):
    count = lax.axis_size(axis)
    forward = [(i, (i + 1) % count) for i in range(count)]
    backward_ = [(target, source) for source, target in forward]
    return lax.ppermute(ahead, axis, forward), lax.ppermute(behind, axis, backward_)


def per_device(latent, conv_in, conv_out, source_field, observed, aperture, receivers):
    shot = lax.axis_index("shot")
    brick = lax.axis_index("brick")
    at = jnp.stack([shot, brick, aperture[0]]).astype(jnp.int32)
    taps_out = jnp.pad(conv_out, ((0, 0), (0, 14), (0, 0)))
    w1, w2 = forward_bands(conv_in, taps_out)
    w3, w4 = backward_bands(conv_in.transpose(0, 2, 1), taps_out.transpose(0, 2, 1))

    tile = jnp.transpose(latent, (2, 1, 0, 3))
    from_low, from_high = both_ways(tile[:, bx - 4 :], tile[:, :4], "brick")
    mid = jnp.concatenate([from_low, tile, from_high], axis=1)
    lo, hi = both_ways(mid, mid, "shot")
    source = jnp.transpose(source_field[0], (1, 0, 2))
    plo, phi = both_ways(source[:, bx - rim :], source[:, :rim], "brick")
    seen = receiver_fields(at, receivers[0], observed[0])

    coefficients, output, hidden = generator(at, lo, mid, hi, w1, w2)
    coefficients, plo, phi = lax.optimization_barrier((coefficients, plo, phi))
    sent = jnp.broadcast_to(coefficients[None], (shots, 2, 2, bx, nz))
    column = lax.all_to_all(sent, "shot", 0, 0, tiled=True)
    column, seen, w3, w4 = lax.optimization_barrier((column, seen, w3, w4))
    window, ahead, behind = take_window(at, column.reshape(2 * shots, 2, bx, nz))
    clo, chi = both_ways(ahead, behind, "brick")
    s1, s2 = spread_fields(at, lo, mid, hi, hidden)
    first_slopes = source_slopes(at, source, plo, phi)
    clo, chi, s1, s2, first_slopes = lax.optimization_barrier((clo, chi, s1, s2, first_slopes))
    p2, p3, p4, images, ahead, behind, modulus, *weights = forward_waves(
        at, window, clo, chi, first_slopes
    )
    back, front = both_ways(ahead, behind, "brick")
    slopes = wave_slopes(first_slopes[0], p2, p3)
    back, front, slopes = lax.optimization_barrier((back, front, slopes))
    grads = adjoint_waves(at, (p2, p3, p4), images, back, front, seen, modulus, weights, slopes)
    got = lax.all_to_all(grads, "shot", 0, 0, tiled=True)
    got = got.reshape(shots, 2, 2 * gx, nz)
    grad_output = chain(at, got, output)
    glo, ghi = both_ways(grad_output, grad_output, "shot")
    second = second_grads(grad_output, s2)
    inner, kernels = first_grads(at, glo, grad_output, ghi, hidden, second, w3, s1)
    grad_latent = latent_grads(inner, w4)
    grad_latent = jnp.transpose(grad_latent.reshape(bx, 2, 16, nz), (2, 0, 1, 3))

    everyone = ("shot", "brick")
    slices = lax.all_to_all(kernels, everyone, 0, 0, tiled=True)
    mine = jnp.sum(slices, axis=0, keepdims=True)
    summed = lax.all_to_all(jnp.broadcast_to(mine, (128, nz)), everyone, 0, 0, tiled=True)
    folded = summed[:108].reshape(3, 2, 18, nz).transpose(0, 2, 1, 3).reshape(3, 18, 256)[:, :, :144]
    folded = folded.reshape(3, 18, 9, 16).transpose(0, 2, 1, 3).reshape(27, 18, 16)
    return (grad_latent, folded[:, :16], folded[:, 16:])


def solution(mesh):
    placed = (
        P(None, "brick", "shot", None),
        P(),
        P(),
        P("shot", "brick", None, None),
        P("shot", None, None),
        P("shot"),
        P("shot", None, None),
    )
    return jax.shard_map(
        per_device,
        mesh=mesh,
        in_specs=placed,
        out_specs=(P(None, "brick", "shot", None), P(), P()),
        check_vma=False,
    )
```

```python
import jax
import jax.numpy as jnp
import numpy as np
from jax import lax
from jax.experimental import pallas as pl
from jax.experimental.pallas import tpu as pltpu
from jax.sharding import PartitionSpec as P

F32 = jnp.float32
BF16 = jnp.bfloat16
stencil_taps = (1225.0 / 1024.0, -245.0 / 3072.0, 49.0 / 5120.0, -5.0 / 7168.0)
ratios = tuple(tap / stencil_taps[0] for tap in stencil_taps)
tap_square = stencil_taps[0] ** 2
misfit_weight = 16.0

bricks, shots = 8, 16
bx = 32
ay = 16
nz = 128
rim = 24
dom = bx + 2 * rim
lead = 8
xpad = dom + 24
ypad = ay + 8
gx = bx + 4
vmem = pltpu.CompilerParams(vmem_limit_bytes=24 * 1024 * 1024)


def cost(microseconds):
    return pl.CostEstimate(flops=0, bytes_accessed=int(microseconds * 3e6), transcendentals=0)


def whole(count):
    return [pl.BlockSpec(memory_space=pltpu.VMEM)] * count


scalars = pl.BlockSpec(memory_space=pltpu.SMEM)


def lane_index():
    return lax.broadcasted_iota(jnp.int32, (1, nz), 1)


def lane_shift(value, offset):
    if offset == 1:
        return value
    lane = lax.broadcasted_iota(jnp.int32, value.shape, 1)
    if offset == 0:
        return jnp.where(lane == 0, 0.0, pltpu.roll(value, 1, 1))
    return jnp.where(lane == nz - 1, 0.0, pltpu.roll(value, nz - 1, 1))


def generator_kernel(
    at_ref, lo_ref, mid_ref, hi_ref, w1_ref, w2_ref, coef_ref, out_ref, hid_ref, s1, s2
):
    shot, brick = at_ref[0], at_ref[1]
    y_fine = (shot > 0, True, shot < shots - 1)

    def spread(x, carry):
        x_fine = ((x >= 4) | (brick > 0)) & ((x < bx + 4) | (brick < bricks - 1))
        for part, ref in enumerate((lo_ref, mid_ref, hi_ref)):
            fine = x_fine & y_fine[part]
            for row in range(2):
                value = jnp.where(fine, ref[row, x].astype(F32), 0.0)
                for k in range(3):
                    s1[x, pl.ds((2 * part + row) * 48 + k * 16, 16), :] = lane_shift(
                        value, k
                    ).astype(BF16)
        return carry

    lax.fori_loop(0, bx + 8, spread, 0, unroll=4)
    last_block = (bx + 6) // 2 - 1

    def multiply(block):
        rows = s1[pl.ds(2 * block, 4)].reshape(4 * 288, nz)
        return jnp.dot(w1_ref[...], rows, preferred_element_type=F32)

    def finish(block, acc):
        acc = jnp.tanh(acc)
        for xo in range(2):
            x = 2 * block + xo
            x_fine = ((x >= 3) | (brick > 0)) & ((x < bx + 3) | (brick < bricks - 1))
            for y in range(4):
                fine = x_fine
                if y == 0:
                    fine = fine & (shot > 0)
                if y == 3:
                    fine = fine & (shot < shots - 1)
                start = (xo * 4 + y) * 16
                value = jnp.where(fine, acc[start : start + 16], 0.0).astype(BF16)
                hid_ref[x, pl.ds(y * 16, 16), :] = value
                wide = value.astype(F32)
                for k in range(3):
                    s2[x, pl.ds(y * 48 + k * 16, 16), :] = lane_shift(wide, k).astype(BF16)

    def first_conv(block, acc):
        finish(block, acc)
        return multiply(block + 1)

    finish(last_block, lax.fori_loop(0, last_block, first_conv, multiply(0), unroll=3))

    for block in range(gx // 6):
        rows = s2[pl.ds(6 * block, 8)].reshape(8 * 192, nz)
        acc = jnp.dot(w2_ref[...], rows, preferred_element_type=F32)
        for channel in range(2):
            for y in range(2):
                start = (channel * 2 + y) * 6
                out_ref[channel, y, pl.ds(6 * block, 6), :] = acc[start : start + 6]
    for y in range(2):
        modulus = 0.03 + 0.09 * jax.nn.sigmoid(out_ref[0, y, pl.ds(2, bx), :])
        buoyancy = jnp.exp(0.35 * jnp.tanh(out_ref[1, y, pl.ds(2, bx), :]))
        coef_ref[y, 0] = modulus
        coef_ref[y, 1] = buoyancy


def generator(at, lo, mid, hi, w1, w2):
    return pl.pallas_call(
        generator_kernel,
        out_shape=(
            jax.ShapeDtypeStruct((2, 2, bx, nz), F32),
            jax.ShapeDtypeStruct((2, 2, gx, nz), F32),
            jax.ShapeDtypeStruct((bx + 6, 64, nz), BF16),
        ),
        in_specs=[scalars] + whole(5),
        out_specs=tuple(whole(3)),
        scratch_shapes=[
            pltpu.VMEM((bx + 8, 288, nz), BF16),
            pltpu.VMEM((bx + 6, 192, nz), BF16),
        ],
        compiler_params=vmem,
        name="generator",
    )(at, lo, mid, hi, w1, w2)


def receiver_kernel(at_ref, cell_ref, seen_ref, out_ref, hot, spread):
    brick, first_row = at_ref[1], at_ref[2]
    count = cell_ref.shape[1]
    x = cell_ref[0:1] - brick * bx + rim
    row_of = jnp.where((x >= 0) & (x < dom), (cell_ref[1:2] - first_row) * dom + x, -1)
    z = cell_ref[2:3]

    def mark(chunk, carry):
        rows = chunk * 16 + lax.broadcasted_iota(jnp.int32, (16, count), 0)
        hot[pl.ds(chunk * 16, 16), :] = jnp.where(rows == row_of, 1.0, 0.0).astype(BF16)
        return carry

    lax.fori_loop(0, ay * dom // 16, mark, 0)
    parts = [jnp.ones((1, count), F32)]
    for step in range(3):
        value = seen_ref[step : step + 1]
        high = value.astype(BF16).astype(F32)
        parts += [high, value - high]

    def place(chunk, carry):
        same = chunk * 16 + lax.broadcasted_iota(jnp.int32, (16, count), 0) == z
        for index, part in enumerate(parts):
            spread[pl.ds(index * nz + chunk * 16, 16), :] = jnp.where(same, part, 0.0).astype(BF16)
        return carry

    lax.fori_loop(0, nz // 16, place, 0)
    size = 256

    def multiply(chunk, carry):
        left = hot[pl.ds(chunk * size, size), :]
        for field in range(4):
            first = 0 if field == 0 else (2 * field - 1) * nz
            right = spread[pl.ds(first, nz if field == 0 else 2 * nz), :]
            acc = lax.dot_general(
                left, right, (((1,), (1,)), ((), ())), preferred_element_type=F32
            )
            if field:
                acc = acc[:, :nz] + acc[:, nz:]
            out_ref[field, pl.ds(chunk * size, size), :] = acc
        return carry

    lax.fori_loop(0, ay * dom // size, multiply, 0)


def receiver_fields(at, cells, seen):
    count = cells.shape[1]
    return pl.pallas_call(
        receiver_kernel,
        out_shape=jax.ShapeDtypeStruct((4, ay * dom, nz), F32),
        in_specs=[scalars] + whole(2),
        out_specs=whole(1)[0],
        scratch_shapes=[
            pltpu.VMEM((ay * dom, count), BF16),
            pltpu.VMEM((7 * nz, count), BF16),
        ],
        compiler_params=vmem,
        cost_estimate=cost(9),
        name="receiver_fields",
    )(at, cells, seen)


def third_dimension_matrices():
    slope = np.zeros((nz, 2 * nz))
    spread = np.zeros((nz, nz))
    for t, ratio in enumerate(ratios, 1):
        slope[t - 1, nz:] += ratio
        for face in range(nz):
            if face + t < nz:
                slope[face + t, face] += ratio
            if face + 1 - t >= 0:
                slope[face + 1 - t, face] -= ratio
        for cell in range(nz):
            if cell + t - 1 < nz:
                spread[cell + t - 1, cell] += ratio
            if cell - t >= 0:
                spread[cell - t, cell] -= ratio

    def parts(matrix):
        high = matrix.astype(jnp.bfloat16)
        return np.concatenate([high, high, (matrix - high.astype(np.float64)).astype(jnp.bfloat16)])

    return parts(slope), parts(spread)


slope_matrix, spread_matrix = third_dimension_matrices()


def halves(value):
    high = value.astype(BF16)
    return high, (value - high.astype(F32)).astype(BF16)


def slopes_z(value, slope_ref):
    high, low = halves(value)
    both = jnp.dot(
        jnp.concatenate([high, low, high], axis=1), slope_ref[...], preferred_element_type=F32
    )
    return both[:, :nz], both[:, nz:]


def divergence_z(flux, first_part, spread_ref):
    high, low = halves(flux)
    return (
        jnp.dot(
            jnp.concatenate([high, low, high], axis=1), spread_ref[...], preferred_element_type=F32
        )
        - first_part
    )


def rows_of(ref, y, count, first, rows):
    return ref[pl.ds(y, count), pl.ds(first, rows), :].reshape(count * rows, nz)


group = 4


def differences(get):
    total = None
    for t in range(1, 5):
        upper, lower = get(t)
        term = upper - lower
        if t > 1:
            term = ratios[t - 1] * term
        total = term if total is None else total + term
    return total


def clear_sides(field):
    for y in (0, 1, 2, 3, ay + 4, ay + 5, ay + 6, ay + 7):
        field[y] = jnp.zeros(field.shape[1:], F32)


def clear_rims(flux_y):
    for j in (0, 1, 2, 20, 21, 22):
        flux_y[j] = jnp.zeros(flux_y.shape[1:], F32)


def halo_scale(at_ref):
    brick = at_ref[1]
    return (
        jnp.where(brick > 0, 1.0, 0.0).astype(F32),
        jnp.where(brick < bricks - 1, 1.0, 0.0).astype(F32),
    )


def window_kernel(at_ref, column_any, win_ref, ahead_ref, behind_ref, message, ready):
    fetch = pltpu.make_async_copy(column_any.at[pl.ds(at_ref[2], ay)], win_ref, ready)
    fetch.start()
    fetch.wait()

    def body(y, carry):
        for channel in range(2):
            value = win_ref[y, channel]
            rounded = value.astype(BF16).astype(F32)
            rest = value - rounded
            for slot, (ref, near, further) in enumerate(((ahead_ref, 28, 12), (behind_ref, 0, 4))):
                place = (channel * 2 + slot) * 24
                message[pl.ds(place, 4), :] = rounded[near : near + 4]
                message[pl.ds(place + 4, 4), :] = rest[near : near + 4]
                message[pl.ds(place + 8, 16), :] = value[further : further + 16]
                ref[y, channel] = message[pl.ds(place, 24), :].astype(BF16)
        return carry

    lax.fori_loop(0, ay, body, 0, unroll=2)


def take_window(at, column):
    return pl.pallas_call(
        window_kernel,
        out_shape=(
            jax.ShapeDtypeStruct((ay, 2, bx, nz), F32),
            jax.ShapeDtypeStruct((ay, 2, 24, nz), BF16),
            jax.ShapeDtypeStruct((ay, 2, 24, nz), BF16),
        ),
        in_specs=[scalars, pl.BlockSpec(memory_space=pl.ANY)],
        out_specs=tuple(whole(3)),
        scratch_shapes=[pltpu.VMEM((96, nz), F32), pltpu.SemaphoreType.DMA],
        compiler_params=vmem,
        name="take_window",
    )(at, column)


def slope_y(field, j, first, rows):
    return differences(
        lambda t: (
            field[j + 3 + t, pl.ds(lead + first, rows), :],
            field[j + 4 - t, pl.ds(lead + first, rows), :],
        )
    )


def slopes_xy(field, y, first, rows):
    base, more = lead + first - 4, rows + 8
    sx = differences(
        lambda t: (
            field[y + 4, pl.ds(base + t, more), :],
            field[y + 4, pl.ds(base + 1 - t, more), :],
        )
    )
    return sx, slope_y(field, y, first, rows)


def third_pass(field, weights, matrices, out, first, rows, also=None):
    _, _, wz, wzl = weights
    slope_ref, spread_ref = matrices

    def body(index, carry):
        y = index * group
        here, before = slopes_z(rows_of(field, y + 4, group, lead + first, rows), slope_ref)
        if also is not None:
            also(y, here, before)
        total = divergence_z(
            rows_of(wz, y, group, first, rows) * here,
            rows_of(wzl, y, group, first, rows) * before,
            spread_ref,
        )
        out[pl.ds(y, group), pl.ds(0, rows), :] = total.reshape(group, rows, nz)
        return carry

    lax.fori_loop(0, ay // group, body, 0, unroll=4)


def flux_pass(field, weights, fluxes, first, rows, also=None):
    wx, wy, _, _ = weights
    fx, fy, _ = fluxes
    base, more = lead + first - 4, rows + 8

    def body(y, carry):
        sx, sy = slopes_xy(field, y, first, rows)
        fx[y, pl.ds(0, more), :] = wx[y, pl.ds(base, more), :] * sx
        fy[y + 3, pl.ds(0, rows), :] = wy[y, pl.ds(first, rows), :] * sy
        if also is not None:
            also(y, sx, sy)
        return carry

    lax.fori_loop(0, ay, body, 0, unroll=2)
    sy = slope_y(field, ay, first, rows)
    fy[ay + 3, pl.ds(0, rows), :] = wy[ay, pl.ds(first, rows), :] * sy
    return sy


def divergence_pass(fluxes, rows, consume):
    fx, fy, az = fluxes

    def body(y, carry):
        total = az[y, pl.ds(0, rows), :] + differences(
            lambda t: (fx[y, pl.ds(3 + t, rows), :], fx[y, pl.ds(4 - t, rows), :])
        )
        total = total + differences(
            lambda t: (
                fy[y + t + 3, pl.ds(0, rows), :],
                fy[y - t + 4, pl.ds(0, rows), :],
            )
        )
        consume(y, total)
        return carry

    lax.fori_loop(0, ay, body, 0, unroll=2)


weight_sizes = ((ay, dom + 16, nz), (ay + 1, dom, nz), (ay, dom, nz), (ay, dom, nz))
padded = pltpu.VMEM((ypad, xpad, nz), F32)
flux_shapes = [
    pltpu.VMEM((ay, 72, nz), F32),
    pltpu.VMEM((23, 64, nz), F32),
    pltpu.VMEM((ay, 64, nz), F32),
]


def source_slopes_kernel(
    at_ref, src_ref, plo_ref, phi_ref, slope_ref, p1_ref, sx_ref, sy_ref, sh_ref, sb_ref, f1
):
    clear_sides(f1)
    low, high = halo_scale(at_ref)

    def load(y, carry):
        f1[y + 4, pl.ds(lead, rim), :] = low * plo_ref[y]
        f1[y + 4, pl.ds(lead + rim, bx), :] = src_ref[y]
        f1[y + 4, pl.ds(lead + rim + bx, rim), :] = high * phi_ref[y]
        p1_ref[y] = f1[y + 4, pl.ds(lead + 8, 64), :]
        return carry

    lax.fori_loop(0, ay, load, 0)

    def body(y, carry):
        sx_ref[y], sy_ref[y] = slopes_xy(f1, y, 8, 64)
        return carry

    lax.fori_loop(0, ay, body, 0, unroll=2)
    sy_ref[ay] = slope_y(f1, ay, 8, 64)

    def third(part, carry):
        y = part * group
        here, before = slopes_z(rows_of(f1, y + 4, group, lead + 8, 64), slope_ref)
        sh_ref[pl.ds(y, group)] = here.reshape(group, 64, nz)
        sb_ref[pl.ds(y, group)] = before.reshape(group, 64, nz)
        return carry

    lax.fori_loop(0, ay // group, third, 0)


def source_slopes(at, source, plo, phi):
    shapes = [(ay, 64, nz), (ay, 72, nz), (ay + 1, 64, nz), (ay, 64, nz), (ay, 64, nz)]
    return pl.pallas_call(
        source_slopes_kernel,
        out_shape=tuple(jax.ShapeDtypeStruct(shape, F32) for shape in shapes),
        in_specs=[scalars] + whole(4),
        out_specs=tuple(whole(5)),
        scratch_shapes=[padded],
        compiler_params=vmem,
        cost_estimate=cost(3),
        name="source_slopes",
    )(at, source, plo, phi, slope_matrix)


def forward_kernel(
    at_ref, win_ref, clo_ref, chi_ref, p1_ref, sx_ref, sy_ref, sh_ref, sb_ref, slope_ref, spread_ref,
    p2_ref, p3_ref, p4_ref, image_ref, ahead_ref, behind_ref, modulus, wx, wy, wz, wzl,
    buoy, f2, f3, fx, fy, az, message,
):
    half = 0.5 * tap_square
    last = lane_index() == nz - 1
    first_taps = sum(jnp.where(lane_index() == t, half * ratios[t], 0.0) for t in range(4))
    weights = (wx, wy, wz, wzl)
    fluxes = (fx, fy, az)
    matrices = (slope_ref, spread_ref)
    clear_rims(fy)
    for field in (buoy, f2, f3):
        clear_sides(field)
    low, high = halo_scale(at_ref)

    def load(y, carry):
        for channel, ref, row, skip in ((0, modulus, y, 0), (1, buoy, y + 4, lead)):
            received = low * clo_ref[y, channel].astype(F32)
            ref[row, pl.ds(skip + 4, 16), :] = received[8:]
            ref[row, pl.ds(skip + 20, 4), :] = received[:4] + received[4:8]
            ref[row, pl.ds(skip + rim, bx), :] = win_ref[y, channel]
            received = high * chi_ref[y, channel].astype(F32)
            ref[row, pl.ds(skip + rim + bx, 4), :] = received[:4] + received[4:8]
            ref[row, pl.ds(skip + rim + bx + 4, 16), :] = received[8:]
        return carry

    lax.fori_loop(0, ay, load, 0)

    def weigh(y, carry):
        inner = buoy[y + 4, pl.ds(lead, dom), :]
        ahead = pltpu.roll(inner, nz - 1, 1)
        value = buoy[y + 4, pl.ds(0, dom + 16), :]
        wx[y] = half * (value + buoy[y + 4, pl.ds(1, dom + 16), :])
        wy[y] = half * (buoy[y + 3, pl.ds(lead, dom), :] + inner)
        wz[y] = half * jnp.where(last, inner, inner + ahead)
        wzl[y] = inner[:, :1] * first_taps
        return carry

    lax.fori_loop(0, ay, weigh, 0, unroll=2)
    wy[ay] = half * buoy[ay + 3, pl.ds(lead, dom), :]

    def first_step(y, image):
        f2[y + 4, pl.ds(lead + 8, 64), :] = (
            2.0 * p1_ref[y] + modulus[y, pl.ds(8, 64), :] * image
        )
        image_ref[0, y] = image[8:56]

    def second_step(y, image):
        value = (
            2.0 * f2[y + 4, pl.ds(lead + 12, 56), :]
            - p1_ref[y, pl.ds(4, 56), :]
            + modulus[y, pl.ds(12, 56), :] * image
        )
        f3[y + 4, pl.ds(lead + 12, 56), :] = value
        image_ref[1, y] = image[4:52]
        p3_ref[y] = value[4:52]
        p2_ref[y] = f2[y + 4, pl.ds(lead + 8, 64), :]

    def third_step(y, image):
        image_ref[2, y] = image
        value = (
            2.0 * f3[y + 4, pl.ds(lead + rim, bx), :]
            - f2[y + 4, pl.ds(lead + rim, bx), :]
            + modulus[y, pl.ds(rim, bx), :] * image[8:40]
        )
        p4_ref[y] = value

    def pack(y, ref, near, further, third):
        value = p4_ref[y, pl.ds(near, 7), :]
        rounded = value.astype(BF16).astype(F32)
        message[pl.ds(0, 7), :] = rounded
        message[pl.ds(7, 7), :] = value - rounded
        message[pl.ds(14, 13), :] = p4_ref[y, pl.ds(further, 13), :]
        message[pl.ds(27, 5), :] = f3[y + 4, pl.ds(lead + rim + third, 5), :]
        ref[y] = message[...].astype(BF16)

    def send(y, carry):
        pack(y, ahead_ref, 25, 12, 19)
        pack(y, behind_ref, 0, 7, 8)
        return carry

    def first_third(part, carry):
        y = part * group
        total = divergence_z(
            rows_of(wz, y, group, 8, 64) * rows_of(sh_ref, y, group, 0, 64),
            rows_of(wzl, y, group, 8, 64) * rows_of(sb_ref, y, group, 0, 64),
            spread_ref,
        )
        az[pl.ds(y, group), pl.ds(0, 64), :] = total.reshape(group, 64, nz)
        return carry

    lax.fori_loop(0, ay // group, first_third, 0, unroll=4)

    def first_flux(y, carry):
        fx[y] = wx[y, pl.ds(lead + 4, 72), :] * sx_ref[y]
        fy[y + 3] = wy[y, pl.ds(8, 64), :] * sy_ref[y]
        return carry

    lax.fori_loop(0, ay, first_flux, 0, unroll=2)
    fy[ay + 3] = wy[ay, pl.ds(8, 64), :] * sy_ref[ay]
    divergence_pass(fluxes, 64, first_step)
    for field, first, rows, consume in (
        (f2, 12, 56, second_step),
        (f3, 16, 48, third_step),
    ):
        third_pass(field, weights, matrices, az, first, rows)
        flux_pass(field, weights, fluxes, first, rows)
        divergence_pass(fluxes, rows, consume)
    lax.fori_loop(0, ay, send, 0)


def forward_waves(at, window, clo, chi, first_slopes):
    shapes = [(ay, 64, nz), (ay, 48, nz), (ay, bx, nz), (3, ay, 48, nz)]
    return pl.pallas_call(
        forward_kernel,
        out_shape=tuple(jax.ShapeDtypeStruct(shape, F32) for shape in shapes)
        + (jax.ShapeDtypeStruct((ay, 32, nz), BF16),) * 2
        + (jax.ShapeDtypeStruct((ay, dom, nz), F32),)
        + tuple(jax.ShapeDtypeStruct(shape, F32) for shape in weight_sizes),
        in_specs=[scalars] + whole(10),
        out_specs=tuple(whole(11)),
        scratch_shapes=[padded, padded, padded, *flux_shapes, pltpu.VMEM((32, nz), F32)],
        compiler_params=vmem,
        name="forward_waves",
    )(at, window, clo, chi, *first_slopes, slope_matrix, spread_matrix)


def slopes_kernel(p1_ref, p2_ref, p3_ref, slope_ref, sx_ref, sy_ref, sh_ref, sb_ref, field):
    clear_sides(field)
    for index, (ref, first) in enumerate(((p1_ref, 8), (p2_ref, 8), (p3_ref, 16))):
        rows = ref.shape[1]

        def load(y, carry):
            field[y + 4, pl.ds(lead + first, rows), :] = ref[y]
            return carry

        lax.fori_loop(0, ay, load, 0)

        def body(y, carry):
            sx, sy = slopes_xy(field, y, 16, 48)
            sx_ref[index, y] = sx[:48]
            sy_ref[index, y] = sy
            return carry

        lax.fori_loop(0, ay, body, 0, unroll=2)
        sy_ref[index, ay] = slope_y(field, ay, 16, 48)

        def third(part, carry):
            y = part * group
            here, before = slopes_z(rows_of(field, y + 4, group, lead + 16, 48), slope_ref)
            sh_ref[index, pl.ds(y, group)] = here.reshape(group, 48, nz)
            sb_ref[index, pl.ds(y, group)] = before.reshape(group, 48, nz)
            return carry

        lax.fori_loop(0, ay // group, third, 0)


def wave_slopes(p1, p2, p3):
    shapes = [(3, ay, 48, nz), (3, ay + 1, 48, nz), (3, ay, 48, nz), (3, ay, 48, nz)]
    return pl.pallas_call(
        slopes_kernel,
        out_shape=tuple(jax.ShapeDtypeStruct(shape, F32) for shape in shapes),
        in_specs=whole(4),
        out_specs=tuple(whole(4)),
        scratch_shapes=[padded],
        compiler_params=vmem,
        cost_estimate=cost(6),
        name="wave_slopes",
    )(p1, p2, p3, slope_matrix)


def adjoint_kernel(
    at_ref, p2_ref, p3_ref, p4_ref, image_ref, back_ref, front_ref, seen_ref,
    slope_ref, spread_ref, modulus, wx, wy, wz, wzl, px_ref, py_ref, ph_ref, pb_ref,
    column_ref,
    scaled, later, late, grad_m, fx, fy, az, qx, qy, qh, qb, far,
):
    weights = (wx, wy, wz, wzl)
    fluxes = (fx, fy, az)
    matrices = (slope_ref, spread_ref)
    clear_rims(fy)
    clear_sides(scaled)
    low, high = halo_scale(at_ref)

    def residual(step, y, first, value):
        rows = value.shape[0]
        start = pl.multiple_of(y * dom + first, 8)
        count = seen_ref[0, pl.ds(start, rows), :]
        total = seen_ref[step, pl.ds(start, rows), :]
        return misfit_weight * (count * value - total)

    far[...] = jnp.zeros(far.shape, F32)

    def seed(y, carry):
        late[y, pl.ds(8, 48), :] = p3_ref[y]
        received = low * back_ref[y].astype(F32)
        far[pl.ds(4, 13), :] = received[14:27]
        far[pl.ds(17, 7), :] = received[:7] + received[7:14]
        late[y, pl.ds(3, 5), :] = received[27:]
        far[pl.ds(rim, bx), :] = p4_ref[y]
        received = high * front_ref[y].astype(F32)
        far[pl.ds(rim + bx, 7), :] = received[:7] + received[7:14]
        far[pl.ds(rim + bx + 7, 13), :] = received[14:27]
        late[y, pl.ds(56, 5), :] = received[27:]
        error = residual(3, y, 0, far[...])
        later[y] = error
        scaled[y + 4, pl.ds(lead, dom), :] = modulus[y] * error
        grad_m[y] = error[16:64] * image_ref[2, y]
        return carry

    lax.fori_loop(0, ay, seed, 0)

    def add(ref, place, product, index):
        ref[place] = product if index == 2 else ref[place] + product

    def cross(index, offset):
        def also(y, sx, sy):
            add(qx, y, sx[offset : offset + 48] * px_ref[index, y], index)
            add(qy, y, sy[offset : offset + 48] * py_ref[index, y], index)

        return also

    def cross_third(index, offset):
        def also(y, here, before):
            for ref, slope, other in ((qh, here, ph_ref), (qb, before, pb_ref)):
                rows = slope.shape[0] // group
                near_rows = slope.reshape(group, rows, nz)[:, offset : offset + 48]
                add(ref, pl.ds(y, group), near_rows * other[index, pl.ds(y, group)], index)

        return also

    def cross_last(index, offset, sy):
        add(qy, ay, sy[offset : offset + 48] * py_ref[index, ay], index)

    def step_three(y, image):
        value = late[y]
        value = residual(2, y, 8, value) + 2.0 * later[y, pl.ds(8, 64), :] + image
        late[y] = value
        grad_m[y] = grad_m[y] + value[8:56] * image_ref[1, y]

    def step_two(y, image):
        value = (
            residual(1, y, 16, p2_ref[y, pl.ds(8, 48), :])
            + 2.0 * late[y, pl.ds(8, 48), :]
            + image
            - later[y, pl.ds(16, 48), :]
        )
        grad_m[y] = grad_m[y] + value * image_ref[0, y]
        later[y, pl.ds(16, 48), :] = value

    third_pass(scaled, weights, matrices, az, 8, 64, cross_third(2, 8))
    sy = flux_pass(scaled, weights, fluxes, 8, 64, cross(2, 8))
    cross_last(2, 8, sy)
    divergence_pass(fluxes, 64, step_three)

    def rescale(y, carry):
        scaled[y + 4, pl.ds(lead + 8, 64), :] = modulus[y, pl.ds(8, 64), :] * late[y]
        return carry

    lax.fori_loop(0, ay, rescale, 0, unroll=2)
    third_pass(scaled, weights, matrices, az, 16, 48, cross_third(1, 0))
    sy = flux_pass(scaled, weights, fluxes, 16, 48, cross(1, 0))
    cross_last(1, 0, sy)
    divergence_pass(fluxes, 48, step_two)

    def rescale_last(y, carry):
        scaled[y + 4, pl.ds(lead + 16, 48), :] = modulus[y, pl.ds(16, 48), :] * later[y, pl.ds(16, 48), :]
        return carry

    lax.fori_loop(0, ay, rescale_last, 0, unroll=2)

    def last_third(part, carry):
        y = part * group
        cross_third(0, 0)(y, *slopes_z(rows_of(scaled, y + 4, group, lead + 16, 48), slope_ref))
        return carry

    lax.fori_loop(0, ay // group, last_third, 0)

    def last_slopes(y, carry):
        cross(0, 0)(y, *slopes_xy(scaled, y, 16, 48))
        return carry

    lax.fori_loop(0, ay, last_slopes, 0, unroll=2)
    cross_last(0, 0, slope_y(scaled, ay, 16, 48))

    first_row = at_ref[2]
    first_lane = lane_index() == 0

    def blank(row, carry):
        column_ref[row] = jnp.zeros(column_ref.shape[1:], F32)
        return carry

    lax.fori_loop(0, first_row, blank, 0)
    lax.fori_loop(first_row + ay, 2 * shots, blank, 0)

    def place(y, carry):
        here = qh[y, pl.ds(6, gx), :]
        total = here + jnp.where(first_lane, qb[y, pl.ds(6, gx), :], pltpu.roll(here, 1, 1))
        total = total + qy[y, pl.ds(6, gx), :] + qy[y + 1, pl.ds(6, gx), :]
        total = total + qx[y, pl.ds(9, gx), :] + qx[y, pl.ds(10, gx), :]
        column_ref[first_row + y, pl.ds(0, gx), :] = grad_m[y, pl.ds(6, gx), :]
        column_ref[first_row + y, pl.ds(gx, gx), :] = (-0.5 * tap_square) * total
        return carry

    lax.fori_loop(0, ay, place, 0, unroll=2)


def adjoint_waves(at, fields, images, back, front, seen, modulus, weights, slopes):
    near = pltpu.VMEM((ay, 48, nz), F32)
    return pl.pallas_call(
        adjoint_kernel,
        out_shape=jax.ShapeDtypeStruct((2 * shots, 2 * gx, nz), F32),
        in_specs=[scalars] + whole(18),
        out_specs=whole(1)[0],
        scratch_shapes=[
            padded,
            pltpu.VMEM((ay, dom, nz), F32),
            pltpu.VMEM((ay, 64, nz), F32),
            near,
            *flux_shapes,
            near,
            pltpu.VMEM((ay + 1, 48, nz), F32),
            near,
            near,
            pltpu.VMEM((dom, nz), F32),
        ],
        compiler_params=vmem,
        name="adjoint_waves",
    )(at, *fields, images, back, front, seen, slope_matrix, spread_matrix, modulus, *weights, *slopes)


def chain_kernel(at_ref, got_ref, out_ref, grad_ref):
    brick = at_ref[1]
    row = lax.broadcasted_iota(jnp.int32, (gx, nz), 0)
    fine = ((row >= 2) | (brick > 0)) & ((row < gx - 2) | (brick < bricks - 1))
    for y in range(2):
        total = got_ref[0, y]
        for shot in range(1, shots):
            total = total + got_ref[shot, y]
        squashed = jax.nn.sigmoid(out_ref[0, y])
        bent = jnp.tanh(out_ref[1, y])
        buoyancy = jnp.exp(0.35 * bent)
        first = total[:gx] * 0.09 * squashed * (1.0 - squashed)
        second = total[gx:] * buoyancy * 0.35 * (1.0 - bent * bent)
        grad_ref[y, 0] = jnp.where(fine, first, 0.0).astype(BF16)
        grad_ref[y, 1] = jnp.where(fine, second, 0.0).astype(BF16)


def chain(at, got, output):
    return pl.pallas_call(
        chain_kernel,
        out_shape=jax.ShapeDtypeStruct((2, 2, gx, nz), BF16),
        in_specs=[scalars] + whole(2),
        out_specs=whole(1)[0],
        compiler_params=vmem,
        name="chain",
    )(at, got, output)


def spread_kernel(at_ref, lo_ref, mid_ref, hi_ref, hid_ref, s1, s2):
    shot, brick = at_ref[0], at_ref[1]
    y_fine = (shot > 0, True, shot < shots - 1)

    def spread(x, carry):
        x_fine = ((x >= 1) | (brick > 0)) & ((x < bx + 1) | (brick < bricks - 1))
        for y, (ref, row, part) in enumerate(((lo_ref, 1, 0), (mid_ref, 0, 1), (mid_ref, 1, 1), (hi_ref, 0, 2))):
            value = jnp.where(x_fine & y_fine[part], ref[row, x + 3].astype(F32), 0.0)
            hidden = hid_ref[x + 2, pl.ds(y * 16, 16), :].astype(F32)
            for k in range(3):
                s1[x, pl.ds(y * 48 + k * 16, 16), :] = lane_shift(value, k).astype(BF16)
                s2[x, pl.ds(y * 48 + k * 16, 16), :] = lane_shift(hidden, k).astype(BF16)
        return carry

    lax.fori_loop(0, bx + 2, spread, 0, unroll=2)


def spread_fields(at, lo, mid, hi, hidden):
    shape = jax.ShapeDtypeStruct((bx + 2, 192, nz), BF16)
    return pl.pallas_call(
        spread_kernel,
        out_shape=(shape, shape),
        in_specs=[scalars] + whole(4),
        out_specs=tuple(whole(2)),
        compiler_params=vmem,
        cost_estimate=cost(3),
        name="spread_fields",
    )(at, lo, mid, hi, hidden)


contract_lanes = (((1,), (1,)), ((), ()))


def second_grads_kernel(gmid_ref, s2, second_ref, own):
    own[...] = jnp.zeros(own.shape, F32)
    for row in range(2):
        for channel in range(2):
            own[:, channel * 2 + row, :] = gmid_ref[row, channel].astype(F32)[2 : bx + 2]

    def kernel_grad(x, second):
        return second + lax.dot_general(
            own[x].astype(BF16), s2[pl.ds(x, 3)].reshape(576, nz), contract_lanes, preferred_element_type=F32
        )

    second_ref[...] = lax.fori_loop(0, bx, kernel_grad, jnp.zeros((8, 576), F32), unroll=8)


def second_grads(grad_output, s2):
    return pl.pallas_call(
        second_grads_kernel,
        out_shape=jax.ShapeDtypeStruct((8, 576), F32),
        in_specs=whole(2),
        out_specs=whole(1)[0],
        scratch_shapes=[pltpu.VMEM((bx, 8, nz), F32)],
        compiler_params=vmem,
        cost_estimate=cost(3),
        name="second_grads",
    )(grad_output, s2)


def first_grads_kernel(
    at_ref, glo_ref, gmid_ref, ghi_ref, hid_ref, second_ref, w3_ref, s1_any, inner_ref, kernel_ref, turned, s1, ready
):
    fetch = pltpu.make_async_copy(s1_any, s1, ready)
    fetch.start()
    shot, brick = at_ref[0], at_ref[1]
    y_fine = (shot > 0, True, shot < shots - 1)
    for part, ref in enumerate((glo_ref, gmid_ref, ghi_ref)):
        for row in range(2):
            for channel in range(2):
                value = jnp.where(y_fine[part], ref[row, channel].astype(F32), 0.0)
                value = jnp.concatenate([value, jnp.zeros((12, nz), F32)], axis=0)
                plane = (2 * part + row) * 2 + channel
                for k in range(3):
                    turned[plane * 3 + k] = lane_shift(value, k)

    def hidden_grad(block, carry):
        rows = turned[:, pl.ds(8 * block, 16), :].astype(BF16).reshape(576, nz)
        acc = jnp.dot(w3_ref[...], rows, preferred_element_type=F32)
        for xo in range(8):
            x = 8 * block + xo
            x_fine = ((x >= 1) | (brick > 0)) & ((x < bx + 1) | (brick < bricks - 1))
            hidden = hid_ref[jnp.minimum(x + 2, bx + 5)].astype(F32)
            value = acc[xo * 64 : xo * 64 + 64] * (1.0 - hidden * hidden)
            for y in range(4):
                fine = x_fine
                if y == 0:
                    fine = fine & (shot > 0)
                if y == 3:
                    fine = fine & (shot < shots - 1)
                inner_ref[x, pl.ds(y * 16, 16), :] = jnp.where(
                    fine, value[y * 16 : y * 16 + 16], 0.0
                ).astype(BF16)
        return carry

    lax.fori_loop(0, 5, hidden_grad, 0, unroll=5)
    fetch.wait()

    def kernel_grad(x, first):
        return first + lax.dot_general(
            inner_ref[x + 1, pl.ds(16, 32), :],
            s1[pl.ds(x, 3)].reshape(576, nz),
            contract_lanes,
            preferred_element_type=F32,
        )

    first = lax.fori_loop(0, bx, kernel_grad, jnp.zeros((32, 576), F32), unroll=8)
    second = second_ref[...]
    kernel_ref[...] = jnp.zeros(kernel_ref.shape, F32)
    for dx in range(3):
        start = dx * 192
        one = first[:16, start : start + 144] + first[16:, start + 48 : start + 192]
        for channel in range(2):
            row = channel * 2
            two = (
                second[row : row + 1, start : start + 144]
                + second[row + 1 : row + 2, start + 48 : start + 192]
            )
            place = dx * 2 * 18 + 16 + channel
            kernel_ref[pl.ds(place, 1), :] = two[:, :128]
            kernel_ref[pl.ds(place + 18, 1), pl.ds(0, 16)] = two[:, 128:]
        kernel_ref[pl.ds(dx * 36, 16), :] = one[:, :128]
        kernel_ref[pl.ds(dx * 36 + 18, 16), pl.ds(0, 16)] = one[:, 128:]


def first_grads(at, glo, gmid, ghi, hidden, second, w3, s1):
    return pl.pallas_call(
        first_grads_kernel,
        out_shape=(
            jax.ShapeDtypeStruct((40, 64, nz), BF16),
            jax.ShapeDtypeStruct((128, nz), F32),
        ),
        in_specs=[scalars] + whole(6) + [pl.BlockSpec(memory_space=pl.ANY)],
        out_specs=tuple(whole(2)),
        scratch_shapes=[
            pltpu.VMEM((36, 48, nz), F32),
            pltpu.VMEM((bx + 2, 192, nz), BF16),
            pltpu.SemaphoreType.DMA,
        ],
        compiler_params=vmem,
        name="first_grads",
    )(at, glo, gmid, ghi, hidden, second, w3, s1)


def latent_grad_kernel(inner_ref, w4_ref, latent_ref, s4):
    def spread(x, carry):
        for y in range(4):
            value = inner_ref[x, pl.ds(y * 16, 16), :].astype(F32)
            for k in range(3):
                s4[x, pl.ds(y * 48 + k * 16, 16), :] = lane_shift(value, k).astype(BF16)
        return carry

    lax.fori_loop(0, bx + 2, spread, 0, unroll=2)

    def latent_grad(block, carry):
        rows = s4[pl.ds(4 * block, 6)].reshape(6 * 192, nz)
        acc = jnp.dot(w4_ref[...], rows, preferred_element_type=F32)
        latent_ref[pl.ds(4 * block, 4)] = acc.reshape(4, 32, nz)
        return carry

    lax.fori_loop(0, bx // 4, latent_grad, 0)


def latent_grads(inner, w4):
    return pl.pallas_call(
        latent_grad_kernel,
        out_shape=jax.ShapeDtypeStruct((bx, 32, nz), F32),
        in_specs=whole(2),
        out_specs=whole(1)[0],
        scratch_shapes=[pltpu.VMEM((bx + 2, 192, nz), BF16)],
        compiler_params=vmem,
        cost_estimate=cost(4),
        name="latent_grads",
    )(inner, w4)


def column_codes(x_in, y_in, order):
    if order == "xykc":
        x, y, k, c = np.meshgrid(*map(np.arange, (x_in, y_in, 3, 16)), indexing="ij")
    else:
        y, c, k, x = np.meshgrid(*map(np.arange, (y_in, 2, 3, x_in)), indexing="ij")
    return np.stack([(8 * x + y).ravel(), (16 * k + c).ravel()]).astype(np.int32)


codes_1 = column_codes(4, 6, "xykc")
codes_2 = column_codes(8, 4, "xykc")
codes_3 = column_codes(16, 6, "yckx")
codes_4 = column_codes(6, 4, "xykc")


def expand(taps_ref, codes_ref, spare, flip):
    place = codes_ref[1:2]
    size = place.shape[1]
    rows = lax.broadcasted_iota(jnp.int32, (16, size), 0)
    picks = [jnp.where(place == rows + 16 * k, 1.0, 0.0).astype(BF16) for k in range(3)]
    for pair in range(9):
        total = None
        for k in range(3):
            q = 3 * pair + k
            term = jnp.dot(taps_ref[26 - q if flip else q], picks[k], preferred_element_type=F32)
            total = term if total is None else total + term
        spare[pair, :, pl.ds(0, size)] = total


def fill_blocks(out_ref, codes_ref, spare, x_out, y_out):
    code = codes_ref[0:1]
    size = code.shape[1]
    same = lax.broadcasted_iota(jnp.int32, (16, size), 0) * 0 + code
    for xo in range(x_out):
        for y in range(y_out):
            block = jnp.zeros((16, size), F32)
            for pair in range(9):
                wanted = (xo + pair // 3) * 8 + y + pair % 3
                block = jnp.where(same == wanted, spare[pair, :, pl.ds(0, size)], block)
            out_ref[pl.ds((xo * y_out + y) * 16, 16), :] = block.astype(BF16)


def forward_bands_kernel(in_ref, out_taps_ref, codes_1_ref, codes_2_ref, w1_ref, w2_ref, spare, rows):
    expand(in_ref, codes_1_ref, spare, False)
    fill_blocks(w1_ref, codes_1_ref, spare, 2, 4)
    expand(out_taps_ref, codes_2_ref, spare, False)
    size = codes_2_ref.shape[1]
    code = codes_2_ref[0:1] - 8 * lax.broadcasted_iota(jnp.int32, (6, size), 0)
    for channel in range(2):
        for y in range(2):
            block = jnp.zeros((6, size), F32)
            for pair in range(9):
                wanted = (pair // 3) * 8 + y + pair % 3
                block = jnp.where(code == wanted, spare[pair, channel : channel + 1, :], block)
            rows[pl.ds((channel * 2 + y) * 6, 6), :] = block
    w2_ref[...] = rows[...].astype(BF16)


def backward_bands_kernel(in_ref, out_taps_ref, codes_3_ref, codes_4_ref, w3_ref, w4_ref, spare):
    expand(out_taps_ref, codes_3_ref, spare, True)
    fill_blocks(w3_ref, codes_3_ref, spare, 8, 4)
    expand(in_ref, codes_4_ref, spare, True)
    fill_blocks(w4_ref, codes_4_ref, spare, 4, 2)


def forward_bands(taps_in, taps_out):
    return pl.pallas_call(
        forward_bands_kernel,
        out_shape=(
            jax.ShapeDtypeStruct((128, 1152), BF16),
            jax.ShapeDtypeStruct((24, 1536), BF16),
        ),
        in_specs=whole(4),
        out_specs=tuple(whole(2)),
        scratch_shapes=[pltpu.VMEM((9, 16, 1536), F32), pltpu.VMEM((24, 1536), F32)],
        compiler_params=vmem,
        cost_estimate=cost(3),
        name="forward_bands",
    )(taps_in, taps_out, codes_1, codes_2)


def backward_bands(taps_in, taps_out):
    return pl.pallas_call(
        backward_bands_kernel,
        out_shape=(
            jax.ShapeDtypeStruct((512, 576), BF16),
            jax.ShapeDtypeStruct((128, 1152), BF16),
        ),
        in_specs=whole(4),
        out_specs=tuple(whole(2)),
        scratch_shapes=[pltpu.VMEM((9, 16, 1152), F32)],
        compiler_params=vmem,
        cost_estimate=cost(4),
        name="backward_bands",
    )(taps_in, taps_out, codes_3, codes_4)


def both_ways(ahead, behind, axis):
    count = lax.axis_size(axis)
    forward = [(i, (i + 1) % count) for i in range(count)]
    backward_ = [(target, source) for source, target in forward]
    return lax.ppermute(ahead, axis, forward), lax.ppermute(behind, axis, backward_)


def per_device(latent, conv_in, conv_out, source_field, observed, aperture, receivers):
    shot = lax.axis_index("shot")
    brick = lax.axis_index("brick")
    at = jnp.stack([shot, brick, aperture[0]]).astype(jnp.int32)
    taps_out = jnp.pad(conv_out, ((0, 0), (0, 14), (0, 0)))
    w1, w2 = forward_bands(conv_in, taps_out)
    w3, w4 = backward_bands(conv_in.transpose(0, 2, 1), taps_out.transpose(0, 2, 1))

    tile = jnp.transpose(latent, (2, 1, 0, 3))
    from_low, from_high = both_ways(tile[:, bx - 4 :], tile[:, :4], "brick")
    mid = jnp.concatenate([from_low, tile, from_high], axis=1)
    lo, hi = both_ways(mid, mid, "shot")
    source = jnp.transpose(source_field[0], (1, 0, 2))
    plo, phi = both_ways(source[:, bx - rim :], source[:, :rim], "brick")
    seen = receiver_fields(at, receivers[0], observed[0])

    coefficients, output, hidden = generator(at, lo, mid, hi, w1, w2)
    coefficients, plo, phi = lax.optimization_barrier((coefficients, plo, phi))
    sent = jnp.broadcast_to(coefficients[None], (shots, 2, 2, bx, nz))
    column = lax.all_to_all(sent, "shot", 0, 0, tiled=True)
    column, seen, w3, w4 = lax.optimization_barrier((column, seen, w3, w4))
    window, ahead, behind = take_window(at, column.reshape(2 * shots, 2, bx, nz))
    clo, chi = both_ways(ahead, behind, "brick")
    s1, s2 = spread_fields(at, lo, mid, hi, hidden)
    first_slopes = source_slopes(at, source, plo, phi)
    clo, chi, s1, s2, first_slopes = lax.optimization_barrier((clo, chi, s1, s2, first_slopes))
    p2, p3, p4, images, ahead, behind, modulus, *weights = forward_waves(
        at, window, clo, chi, first_slopes
    )
    back, front = both_ways(ahead, behind, "brick")
    slopes = wave_slopes(first_slopes[0], p2, p3)
    back, front, slopes = lax.optimization_barrier((back, front, slopes))
    grads = adjoint_waves(at, (p2, p3, p4), images, back, front, seen, modulus, weights, slopes)
    got = lax.all_to_all(grads, "shot", 0, 0, tiled=True)
    got = got.reshape(shots, 2, 2 * gx, nz)
    grad_output = chain(at, got, output)
    glo, ghi = both_ways(grad_output, grad_output, "shot")
    second = second_grads(grad_output, s2)
    inner, kernels = first_grads(at, glo, grad_output, ghi, hidden, second, w3, s1)
    grad_latent = latent_grads(inner, w4)
    grad_latent = jnp.transpose(grad_latent.reshape(bx, 2, 16, nz), (2, 0, 1, 3))

    everyone = ("shot", "brick")
    slices = lax.all_to_all(kernels, everyone, 0, 0, tiled=True)
    mine = jnp.sum(slices, axis=0, keepdims=True)
    summed = lax.all_to_all(jnp.broadcast_to(mine, (128, nz)), everyone, 0, 0, tiled=True)
    folded = summed[:108].reshape(3, 2, 18, nz).transpose(0, 2, 1, 3).reshape(3, 18, 256)[:, :, :144]
    folded = folded.reshape(3, 18, 9, 16).transpose(0, 2, 1, 3).reshape(27, 18, 16)
    return (grad_latent, folded[:, :16], folded[:, 16:])


def solution(mesh):
    placed = (
        P(None, "brick", "shot", None),
        P(),
        P(),
        P("shot", "brick", None, None),
        P("shot", None, None),
        P("shot"),
        P("shot", None, None),
    )
    return jax.shard_map(
        per_device,
        mesh=mesh,
        in_specs=placed,
        out_specs=(P(None, "brick", "shot", None), P(), P()),
        check_vma=False,
    )
```

```python
import jax
import jax.numpy as jnp
import numpy as np
from jax import lax
from jax.experimental import pallas as pl
from jax.experimental.pallas import tpu as pltpu
from jax.sharding import PartitionSpec as P

F32 = jnp.float32
BF16 = jnp.bfloat16
stencil_taps = (1225.0 / 1024.0, -245.0 / 3072.0, 49.0 / 5120.0, -5.0 / 7168.0)
ratios = tuple(tap / stencil_taps[0] for tap in stencil_taps)
tap_square = stencil_taps[0] ** 2
misfit_weight = 16.0

bricks, shots = 8, 16
bx = 32
ay = 16
nz = 128
rim = 24
dom = bx + 2 * rim
lead = 8
xpad = dom + 24
ypad = ay + 8
gx = bx + 4
vmem = pltpu.CompilerParams(vmem_limit_bytes=24 * 1024 * 1024)


def cost(microseconds):
    return pl.CostEstimate(flops=0, bytes_accessed=int(microseconds * 3e6), transcendentals=0)


def whole(count):
    return [pl.BlockSpec(memory_space=pltpu.VMEM)] * count


scalars = pl.BlockSpec(memory_space=pltpu.SMEM)


def lane_index():
    return lax.broadcasted_iota(jnp.int32, (1, nz), 1)


def lane_shift(value, offset):
    if offset == 1:
        return value
    lane = lax.broadcasted_iota(jnp.int32, value.shape, 1)
    if offset == 0:
        return jnp.where(lane == 0, 0.0, pltpu.roll(value, 1, 1))
    return jnp.where(lane == nz - 1, 0.0, pltpu.roll(value, nz - 1, 1))


def generator_kernel(
    at_ref, lo_ref, mid_ref, hi_ref, w1_ref, w2_ref, coef_ref, out_ref, hid_ref, s1, s2
):
    shot, brick = at_ref[0], at_ref[1]
    y_fine = (shot > 0, True, shot < shots - 1)

    def spread(x, carry):
        x_fine = ((x >= 4) | (brick > 0)) & ((x < bx + 4) | (brick < bricks - 1))
        for part, ref in enumerate((lo_ref, mid_ref, hi_ref)):
            fine = x_fine & y_fine[part]
            for row in range(2):
                value = jnp.where(fine, ref[row, x].astype(F32), 0.0)
                for k in range(3):
                    s1[x, pl.ds((2 * part + row) * 48 + k * 16, 16), :] = lane_shift(
                        value, k
                    ).astype(BF16)
        return carry

    lax.fori_loop(0, bx + 8, spread, 0, unroll=4)
    last_block = (bx + 6) // 2 - 1

    def multiply(block):
        rows = s1[pl.ds(2 * block, 4)].reshape(4 * 288, nz)
        return jnp.dot(w1_ref[...], rows, preferred_element_type=F32)

    def finish(block, acc):
        acc = jnp.tanh(acc)
        for xo in range(2):
            x = 2 * block + xo
            x_fine = ((x >= 3) | (brick > 0)) & ((x < bx + 3) | (brick < bricks - 1))
            for y in range(4):
                fine = x_fine
                if y == 0:
                    fine = fine & (shot > 0)
                if y == 3:
                    fine = fine & (shot < shots - 1)
                start = (xo * 4 + y) * 16
                value = jnp.where(fine, acc[start : start + 16], 0.0).astype(BF16)
                hid_ref[x, pl.ds(y * 16, 16), :] = value
                wide = value.astype(F32)
                for k in range(3):
                    s2[x, pl.ds(y * 48 + k * 16, 16), :] = lane_shift(wide, k).astype(BF16)

    def first_conv(block, acc):
        finish(block, acc)
        return multiply(block + 1)

    finish(last_block, lax.fori_loop(0, last_block, first_conv, multiply(0), unroll=6))

    for block in range(gx // 6):
        rows = s2[pl.ds(6 * block, 8)].reshape(8 * 192, nz)
        acc = jnp.dot(w2_ref[...], rows, preferred_element_type=F32)
        for channel in range(2):
            for y in range(2):
                start = (channel * 2 + y) * 6
                out_ref[channel, y, pl.ds(6 * block, 6), :] = acc[start : start + 6]
    for y in range(2):
        modulus = 0.03 + 0.09 * jax.nn.sigmoid(out_ref[0, y, pl.ds(2, bx), :])
        buoyancy = jnp.exp(0.35 * jnp.tanh(out_ref[1, y, pl.ds(2, bx), :]))
        coef_ref[y, 0] = modulus
        coef_ref[y, 1] = buoyancy


def generator(at, lo, mid, hi, w1, w2):
    return pl.pallas_call(
        generator_kernel,
        out_shape=(
            jax.ShapeDtypeStruct((2, 2, bx, nz), F32),
            jax.ShapeDtypeStruct((2, 2, gx, nz), F32),
            jax.ShapeDtypeStruct((bx + 6, 64, nz), BF16),
        ),
        in_specs=[scalars] + whole(5),
        out_specs=tuple(whole(3)),
        scratch_shapes=[
            pltpu.VMEM((bx + 8, 288, nz), BF16),
            pltpu.VMEM((bx + 6, 192, nz), BF16),
        ],
        compiler_params=vmem,
        name="generator",
    )(at, lo, mid, hi, w1, w2)


def receiver_kernel(at_ref, cell_ref, seen_ref, out_ref, hot, spread):
    brick, first_row = at_ref[1], at_ref[2]
    count = cell_ref.shape[1]
    x = cell_ref[0:1] - brick * bx + rim
    row_of = jnp.where((x >= 0) & (x < dom), (cell_ref[1:2] - first_row) * dom + x, -1)
    z = cell_ref[2:3]

    def mark(chunk, carry):
        rows = chunk * 16 + lax.broadcasted_iota(jnp.int32, (16, count), 0)
        hot[pl.ds(chunk * 16, 16), :] = jnp.where(rows == row_of, 1.0, 0.0).astype(BF16)
        return carry

    lax.fori_loop(0, ay * dom // 16, mark, 0)
    parts = [jnp.ones((1, count), F32)]
    for step in range(3):
        value = seen_ref[step : step + 1]
        high = value.astype(BF16).astype(F32)
        parts += [high, value - high]

    def place(chunk, carry):
        same = chunk * 16 + lax.broadcasted_iota(jnp.int32, (16, count), 0) == z
        for index, part in enumerate(parts):
            spread[pl.ds(index * nz + chunk * 16, 16), :] = jnp.where(same, part, 0.0).astype(BF16)
        return carry

    lax.fori_loop(0, nz // 16, place, 0)
    size = 256

    def multiply(chunk, carry):
        left = hot[pl.ds(chunk * size, size), :]
        for field in range(4):
            first = 0 if field == 0 else (2 * field - 1) * nz
            right = spread[pl.ds(first, nz if field == 0 else 2 * nz), :]
            acc = lax.dot_general(
                left, right, (((1,), (1,)), ((), ())), preferred_element_type=F32
            )
            if field:
                acc = acc[:, :nz] + acc[:, nz:]
            out_ref[field, pl.ds(chunk * size, size), :] = acc
        return carry

    lax.fori_loop(0, ay * dom // size, multiply, 0)


def receiver_fields(at, cells, seen):
    count = cells.shape[1]
    return pl.pallas_call(
        receiver_kernel,
        out_shape=jax.ShapeDtypeStruct((4, ay * dom, nz), F32),
        in_specs=[scalars] + whole(2),
        out_specs=whole(1)[0],
        scratch_shapes=[
            pltpu.VMEM((ay * dom, count), BF16),
            pltpu.VMEM((7 * nz, count), BF16),
        ],
        compiler_params=vmem,
        cost_estimate=cost(9),
        name="receiver_fields",
    )(at, cells, seen)


def third_dimension_matrices():
    slope = np.zeros((nz, 2 * nz))
    spread = np.zeros((nz, nz))
    for t, ratio in enumerate(ratios, 1):
        slope[t - 1, nz:] += ratio
        for face in range(nz):
            if face + t < nz:
                slope[face + t, face] += ratio
            if face + 1 - t >= 0:
                slope[face + 1 - t, face] -= ratio
        for cell in range(nz):
            if cell + t - 1 < nz:
                spread[cell + t - 1, cell] += ratio
            if cell - t >= 0:
                spread[cell - t, cell] -= ratio

    def parts(matrix):
        high = matrix.astype(jnp.bfloat16)
        return np.concatenate([high, high, (matrix - high.astype(np.float64)).astype(jnp.bfloat16)])

    return parts(slope), parts(spread)


slope_matrix, spread_matrix = third_dimension_matrices()


def halves(value):
    high = value.astype(BF16)
    return high, (value - high.astype(F32)).astype(BF16)


def slopes_z(value, slope_ref):
    high, low = halves(value)
    both = jnp.dot(
        jnp.concatenate([high, low, high], axis=1), slope_ref[...], preferred_element_type=F32
    )
    return both[:, :nz], both[:, nz:]


def divergence_z(flux, first_part, spread_ref):
    high, low = halves(flux)
    return (
        jnp.dot(
            jnp.concatenate([high, low, high], axis=1), spread_ref[...], preferred_element_type=F32
        )
        - first_part
    )


def rows_of(ref, y, count, first, rows):
    return ref[pl.ds(y, count), pl.ds(first, rows), :].reshape(count * rows, nz)


group = 4


def differences(get):
    total = None
    for t in range(1, 5):
        upper, lower = get(t)
        term = upper - lower
        if t > 1:
            term = ratios[t - 1] * term
        total = term if total is None else total + term
    return total


def clear_sides(field):
    for y in (0, 1, 2, 3, ay + 4, ay + 5, ay + 6, ay + 7):
        field[y] = jnp.zeros(field.shape[1:], F32)


def clear_rims(flux_y):
    for j in (0, 1, 2, 20, 21, 22):
        flux_y[j] = jnp.zeros(flux_y.shape[1:], F32)


def halo_scale(at_ref):
    brick = at_ref[1]
    return (
        jnp.where(brick > 0, 1.0, 0.0).astype(F32),
        jnp.where(brick < bricks - 1, 1.0, 0.0).astype(F32),
    )


def window_kernel(at_ref, column_any, win_ref, ahead_ref, behind_ref, message, ready):
    fetch = pltpu.make_async_copy(column_any.at[pl.ds(at_ref[2], ay)], win_ref, ready)
    fetch.start()
    fetch.wait()

    def body(y, carry):
        for channel in range(2):
            value = win_ref[y, channel]
            rounded = value.astype(BF16).astype(F32)
            rest = value - rounded
            for slot, (ref, near, further) in enumerate(((ahead_ref, 28, 12), (behind_ref, 0, 4))):
                place = (channel * 2 + slot) * 24
                message[pl.ds(place, 4), :] = rounded[near : near + 4]
                message[pl.ds(place + 4, 4), :] = rest[near : near + 4]
                message[pl.ds(place + 8, 16), :] = value[further : further + 16]
                ref[y, channel] = message[pl.ds(place, 24), :].astype(BF16)
        return carry

    lax.fori_loop(0, ay, body, 0, unroll=2)


def take_window(at, column):
    return pl.pallas_call(
        window_kernel,
        out_shape=(
            jax.ShapeDtypeStruct((ay, 2, bx, nz), F32),
            jax.ShapeDtypeStruct((ay, 2, 24, nz), BF16),
            jax.ShapeDtypeStruct((ay, 2, 24, nz), BF16),
        ),
        in_specs=[scalars, pl.BlockSpec(memory_space=pl.ANY)],
        out_specs=tuple(whole(3)),
        scratch_shapes=[pltpu.VMEM((96, nz), F32), pltpu.SemaphoreType.DMA],
        compiler_params=vmem,
        name="take_window",
    )(at, column)


def slope_y(field, j, first, rows):
    return differences(
        lambda t: (
            field[j + 3 + t, pl.ds(lead + first, rows), :],
            field[j + 4 - t, pl.ds(lead + first, rows), :],
        )
    )


def slopes_xy(field, y, first, rows):
    base, more = lead + first - 4, rows + 8
    sx = differences(
        lambda t: (
            field[y + 4, pl.ds(base + t, more), :],
            field[y + 4, pl.ds(base + 1 - t, more), :],
        )
    )
    return sx, slope_y(field, y, first, rows)


def third_pass(field, weights, matrices, out, first, rows, also=None):
    _, _, wz, wzl = weights
    slope_ref, spread_ref = matrices

    def body(index, carry):
        y = index * group
        here, before = slopes_z(rows_of(field, y + 4, group, lead + first, rows), slope_ref)
        if also is not None:
            also(y, here, before)
        total = divergence_z(
            rows_of(wz, y, group, first, rows) * here,
            rows_of(wzl, y, group, first, rows) * before,
            spread_ref,
        )
        out[pl.ds(y, group), pl.ds(0, rows), :] = total.reshape(group, rows, nz)
        return carry

    lax.fori_loop(0, ay // group, body, 0, unroll=4)


def flux_pass(field, weights, fluxes, first, rows, also=None):
    wx, wy, _, _ = weights
    fx, fy, _ = fluxes
    base, more = lead + first - 4, rows + 8

    def body(y, carry):
        sx, sy = slopes_xy(field, y, first, rows)
        fx[y, pl.ds(0, more), :] = wx[y, pl.ds(base, more), :] * sx
        fy[y + 3, pl.ds(0, rows), :] = wy[y, pl.ds(first, rows), :] * sy
        if also is not None:
            also(y, sx, sy)
        return carry

    lax.fori_loop(0, ay, body, 0, unroll=2)
    sy = slope_y(field, ay, first, rows)
    fy[ay + 3, pl.ds(0, rows), :] = wy[ay, pl.ds(first, rows), :] * sy
    return sy


def divergence_pass(fluxes, rows, consume):
    fx, fy, az = fluxes

    def body(y, carry):
        total = az[y, pl.ds(0, rows), :] + differences(
            lambda t: (fx[y, pl.ds(3 + t, rows), :], fx[y, pl.ds(4 - t, rows), :])
        )
        total = total + differences(
            lambda t: (
                fy[y + t + 3, pl.ds(0, rows), :],
                fy[y - t + 4, pl.ds(0, rows), :],
            )
        )
        consume(y, total)
        return carry

    lax.fori_loop(0, ay, body, 0, unroll=2)


weight_sizes = ((ay, dom + 16, nz), (ay + 1, dom, nz), (ay, dom, nz), (ay, dom, nz))
padded = pltpu.VMEM((ypad, xpad, nz), F32)
flux_shapes = [
    pltpu.VMEM((ay, 72, nz), F32),
    pltpu.VMEM((23, 64, nz), F32),
    pltpu.VMEM((ay, 64, nz), F32),
]


def source_slopes_kernel(
    at_ref, src_ref, plo_ref, phi_ref, slope_ref, p1_ref, sx_ref, sy_ref, sh_ref, sb_ref, f1
):
    clear_sides(f1)
    low, high = halo_scale(at_ref)

    def load(y, carry):
        f1[y + 4, pl.ds(lead, rim), :] = low * plo_ref[y]
        f1[y + 4, pl.ds(lead + rim, bx), :] = src_ref[y]
        f1[y + 4, pl.ds(lead + rim + bx, rim), :] = high * phi_ref[y]
        p1_ref[y] = f1[y + 4, pl.ds(lead + 8, 64), :]
        return carry

    lax.fori_loop(0, ay, load, 0)

    def body(y, carry):
        sx_ref[y], sy_ref[y] = slopes_xy(f1, y, 8, 64)
        return carry

    lax.fori_loop(0, ay, body, 0, unroll=2)
    sy_ref[ay] = slope_y(f1, ay, 8, 64)

    def third(part, carry):
        y = part * group
        here, before = slopes_z(rows_of(f1, y + 4, group, lead + 8, 64), slope_ref)
        sh_ref[pl.ds(y, group)] = here.reshape(group, 64, nz)
        sb_ref[pl.ds(y, group)] = before.reshape(group, 64, nz)
        return carry

    lax.fori_loop(0, ay // group, third, 0)


def source_slopes(at, source, plo, phi):
    shapes = [(ay, 64, nz), (ay, 72, nz), (ay + 1, 64, nz), (ay, 64, nz), (ay, 64, nz)]
    return pl.pallas_call(
        source_slopes_kernel,
        out_shape=tuple(jax.ShapeDtypeStruct(shape, F32) for shape in shapes),
        in_specs=[scalars] + whole(4),
        out_specs=tuple(whole(5)),
        scratch_shapes=[padded],
        compiler_params=vmem,
        cost_estimate=cost(3),
        name="source_slopes",
    )(at, source, plo, phi, slope_matrix)


def forward_kernel(
    at_ref, win_ref, clo_ref, chi_ref, p1_ref, sx_ref, sy_ref, sh_ref, sb_ref, slope_ref, spread_ref,
    p2_ref, p3_ref, p4_ref, image_ref, ahead_ref, behind_ref, modulus, wx, wy, wz, wzl,
    buoy, f2, f3, fx, fy, az, message,
):
    half = 0.5 * tap_square
    last = lane_index() == nz - 1
    first_taps = sum(jnp.where(lane_index() == t, half * ratios[t], 0.0) for t in range(4))
    weights = (wx, wy, wz, wzl)
    fluxes = (fx, fy, az)
    matrices = (slope_ref, spread_ref)
    clear_rims(fy)
    for field in (buoy, f2, f3):
        clear_sides(field)
    low, high = halo_scale(at_ref)

    def load(y, carry):
        for channel, ref, row, skip in ((0, modulus, y, 0), (1, buoy, y + 4, lead)):
            received = low * clo_ref[y, channel].astype(F32)
            ref[row, pl.ds(skip + 4, 16), :] = received[8:]
            ref[row, pl.ds(skip + 20, 4), :] = received[:4] + received[4:8]
            ref[row, pl.ds(skip + rim, bx), :] = win_ref[y, channel]
            received = high * chi_ref[y, channel].astype(F32)
            ref[row, pl.ds(skip + rim + bx, 4), :] = received[:4] + received[4:8]
            ref[row, pl.ds(skip + rim + bx + 4, 16), :] = received[8:]
        return carry

    lax.fori_loop(0, ay, load, 0)

    def weigh(y, carry):
        inner = buoy[y + 4, pl.ds(lead, dom), :]
        ahead = pltpu.roll(inner, nz - 1, 1)
        value = buoy[y + 4, pl.ds(0, dom + 16), :]
        wx[y] = half * (value + buoy[y + 4, pl.ds(1, dom + 16), :])
        wy[y] = half * (buoy[y + 3, pl.ds(lead, dom), :] + inner)
        wz[y] = half * jnp.where(last, inner, inner + ahead)
        wzl[y] = inner[:, :1] * first_taps
        return carry

    lax.fori_loop(0, ay, weigh, 0, unroll=2)
    wy[ay] = half * buoy[ay + 3, pl.ds(lead, dom), :]

    def first_step(y, image):
        f2[y + 4, pl.ds(lead + 8, 64), :] = (
            2.0 * p1_ref[y] + modulus[y, pl.ds(8, 64), :] * image
        )
        image_ref[0, y] = image[8:56]

    def second_step(y, image):
        value = (
            2.0 * f2[y + 4, pl.ds(lead + 12, 56), :]
            - p1_ref[y, pl.ds(4, 56), :]
            + modulus[y, pl.ds(12, 56), :] * image
        )
        f3[y + 4, pl.ds(lead + 12, 56), :] = value
        image_ref[1, y] = image[4:52]
        p3_ref[y] = value[4:52]
        p2_ref[y] = f2[y + 4, pl.ds(lead + 8, 64), :]

    def third_step(y, image):
        image_ref[2, y] = image
        value = (
            2.0 * f3[y + 4, pl.ds(lead + rim, bx), :]
            - f2[y + 4, pl.ds(lead + rim, bx), :]
            + modulus[y, pl.ds(rim, bx), :] * image[8:40]
        )
        p4_ref[y] = value

    def pack(y, ref, near, further, third):
        value = p4_ref[y, pl.ds(near, 7), :]
        rounded = value.astype(BF16).astype(F32)
        message[pl.ds(0, 7), :] = rounded
        message[pl.ds(7, 7), :] = value - rounded
        message[pl.ds(14, 13), :] = p4_ref[y, pl.ds(further, 13), :]
        message[pl.ds(27, 5), :] = f3[y + 4, pl.ds(lead + rim + third, 5), :]
        ref[y] = message[...].astype(BF16)

    def send(y, carry):
        pack(y, ahead_ref, 25, 12, 19)
        pack(y, behind_ref, 0, 7, 8)
        return carry

    def first_third(part, carry):
        y = part * group
        total = divergence_z(
            rows_of(wz, y, group, 8, 64) * rows_of(sh_ref, y, group, 0, 64),
            rows_of(wzl, y, group, 8, 64) * rows_of(sb_ref, y, group, 0, 64),
            spread_ref,
        )
        az[pl.ds(y, group), pl.ds(0, 64), :] = total.reshape(group, 64, nz)
        return carry

    lax.fori_loop(0, ay // group, first_third, 0, unroll=4)

    def first_flux(y, carry):
        fx[y] = wx[y, pl.ds(lead + 4, 72), :] * sx_ref[y]
        fy[y + 3] = wy[y, pl.ds(8, 64), :] * sy_ref[y]
        return carry

    lax.fori_loop(0, ay, first_flux, 0, unroll=2)
    fy[ay + 3] = wy[ay, pl.ds(8, 64), :] * sy_ref[ay]
    divergence_pass(fluxes, 64, first_step)
    for field, first, rows, consume in (
        (f2, 12, 56, second_step),
        (f3, 16, 48, third_step),
    ):
        third_pass(field, weights, matrices, az, first, rows)
        flux_pass(field, weights, fluxes, first, rows)
        divergence_pass(fluxes, rows, consume)
    lax.fori_loop(0, ay, send, 0)


def forward_waves(at, window, clo, chi, first_slopes):
    shapes = [(ay, 64, nz), (ay, 48, nz), (ay, bx, nz), (3, ay, 48, nz)]
    return pl.pallas_call(
        forward_kernel,
        out_shape=tuple(jax.ShapeDtypeStruct(shape, F32) for shape in shapes)
        + (jax.ShapeDtypeStruct((ay, 32, nz), BF16),) * 2
        + (jax.ShapeDtypeStruct((ay, dom, nz), F32),)
        + tuple(jax.ShapeDtypeStruct(shape, F32) for shape in weight_sizes),
        in_specs=[scalars] + whole(10),
        out_specs=tuple(whole(11)),
        scratch_shapes=[padded, padded, padded, *flux_shapes, pltpu.VMEM((32, nz), F32)],
        compiler_params=vmem,
        name="forward_waves",
    )(at, window, clo, chi, *first_slopes, slope_matrix, spread_matrix)


def slopes_kernel(p1_ref, p2_ref, p3_ref, slope_ref, sx_ref, sy_ref, sh_ref, sb_ref, field):
    clear_sides(field)
    for index, (ref, first) in enumerate(((p1_ref, 8), (p2_ref, 8), (p3_ref, 16))):
        rows = ref.shape[1]

        def load(y, carry):
            field[y + 4, pl.ds(lead + first, rows), :] = ref[y]
            return carry

        lax.fori_loop(0, ay, load, 0)

        def body(y, carry):
            sx, sy = slopes_xy(field, y, 16, 48)
            sx_ref[index, y] = sx[:48]
            sy_ref[index, y] = sy
            return carry

        lax.fori_loop(0, ay, body, 0, unroll=2)
        sy_ref[index, ay] = slope_y(field, ay, 16, 48)

        def third(part, carry):
            y = part * group
            here, before = slopes_z(rows_of(field, y + 4, group, lead + 16, 48), slope_ref)
            sh_ref[index, pl.ds(y, group)] = here.reshape(group, 48, nz)
            sb_ref[index, pl.ds(y, group)] = before.reshape(group, 48, nz)
            return carry

        lax.fori_loop(0, ay // group, third, 0)


def wave_slopes(p1, p2, p3):
    shapes = [(3, ay, 48, nz), (3, ay + 1, 48, nz), (3, ay, 48, nz), (3, ay, 48, nz)]
    return pl.pallas_call(
        slopes_kernel,
        out_shape=tuple(jax.ShapeDtypeStruct(shape, F32) for shape in shapes),
        in_specs=whole(4),
        out_specs=tuple(whole(4)),
        scratch_shapes=[padded],
        compiler_params=vmem,
        cost_estimate=cost(6),
        name="wave_slopes",
    )(p1, p2, p3, slope_matrix)


def adjoint_kernel(
    at_ref, p2_ref, p3_ref, p4_ref, image_ref, back_ref, front_ref, seen_ref,
    slope_ref, spread_ref, modulus, wx, wy, wz, wzl, px_ref, py_ref, ph_ref, pb_ref,
    column_ref,
    scaled, later, late, grad_m, fx, fy, az, qx, qy, qh, qb, far,
):
    weights = (wx, wy, wz, wzl)
    fluxes = (fx, fy, az)
    matrices = (slope_ref, spread_ref)
    clear_rims(fy)
    clear_sides(scaled)
    low, high = halo_scale(at_ref)

    def residual(step, y, first, value):
        rows = value.shape[0]
        start = pl.multiple_of(y * dom + first, 8)
        count = seen_ref[0, pl.ds(start, rows), :]
        total = seen_ref[step, pl.ds(start, rows), :]
        return misfit_weight * (count * value - total)

    far[...] = jnp.zeros(far.shape, F32)

    def seed(y, carry):
        late[y, pl.ds(8, 48), :] = p3_ref[y]
        received = low * back_ref[y].astype(F32)
        far[pl.ds(4, 13), :] = received[14:27]
        far[pl.ds(17, 7), :] = received[:7] + received[7:14]
        late[y, pl.ds(3, 5), :] = received[27:]
        far[pl.ds(rim, bx), :] = p4_ref[y]
        received = high * front_ref[y].astype(F32)
        far[pl.ds(rim + bx, 7), :] = received[:7] + received[7:14]
        far[pl.ds(rim + bx + 7, 13), :] = received[14:27]
        late[y, pl.ds(56, 5), :] = received[27:]
        error = residual(3, y, 0, far[...])
        later[y] = error
        scaled[y + 4, pl.ds(lead, dom), :] = modulus[y] * error
        grad_m[y] = error[16:64] * image_ref[2, y]
        return carry

    lax.fori_loop(0, ay, seed, 0)

    def add(ref, place, product, index):
        ref[place] = product if index == 2 else ref[place] + product

    def cross(index, offset):
        def also(y, sx, sy):
            add(qx, y, sx[offset : offset + 48] * px_ref[index, y], index)
            add(qy, y, sy[offset : offset + 48] * py_ref[index, y], index)

        return also

    def cross_third(index, offset):
        def also(y, here, before):
            for ref, slope, other in ((qh, here, ph_ref), (qb, before, pb_ref)):
                rows = slope.shape[0] // group
                near_rows = slope.reshape(group, rows, nz)[:, offset : offset + 48]
                add(ref, pl.ds(y, group), near_rows * other[index, pl.ds(y, group)], index)

        return also

    def cross_last(index, offset, sy):
        add(qy, ay, sy[offset : offset + 48] * py_ref[index, ay], index)

    def step_three(y, image):
        value = late[y]
        value = residual(2, y, 8, value) + 2.0 * later[y, pl.ds(8, 64), :] + image
        late[y] = value
        grad_m[y] = grad_m[y] + value[8:56] * image_ref[1, y]

    def step_two(y, image):
        value = (
            residual(1, y, 16, p2_ref[y, pl.ds(8, 48), :])
            + 2.0 * late[y, pl.ds(8, 48), :]
            + image
            - later[y, pl.ds(16, 48), :]
        )
        grad_m[y] = grad_m[y] + value * image_ref[0, y]
        later[y, pl.ds(16, 48), :] = value

    third_pass(scaled, weights, matrices, az, 8, 64, cross_third(2, 8))
    sy = flux_pass(scaled, weights, fluxes, 8, 64, cross(2, 8))
    cross_last(2, 8, sy)
    divergence_pass(fluxes, 64, step_three)

    def rescale(y, carry):
        scaled[y + 4, pl.ds(lead + 8, 64), :] = modulus[y, pl.ds(8, 64), :] * late[y]
        return carry

    lax.fori_loop(0, ay, rescale, 0, unroll=2)
    third_pass(scaled, weights, matrices, az, 16, 48, cross_third(1, 0))
    sy = flux_pass(scaled, weights, fluxes, 16, 48, cross(1, 0))
    cross_last(1, 0, sy)
    divergence_pass(fluxes, 48, step_two)

    def rescale_last(y, carry):
        scaled[y + 4, pl.ds(lead + 16, 48), :] = modulus[y, pl.ds(16, 48), :] * later[y, pl.ds(16, 48), :]
        return carry

    lax.fori_loop(0, ay, rescale_last, 0, unroll=2)

    def last_third(part, carry):
        y = part * group
        cross_third(0, 0)(y, *slopes_z(rows_of(scaled, y + 4, group, lead + 16, 48), slope_ref))
        return carry

    lax.fori_loop(0, ay // group, last_third, 0, unroll=4)

    def last_slopes(y, carry):
        cross(0, 0)(y, *slopes_xy(scaled, y, 16, 48))
        return carry

    lax.fori_loop(0, ay, last_slopes, 0, unroll=2)
    cross_last(0, 0, slope_y(scaled, ay, 16, 48))

    first_row = at_ref[2]
    first_lane = lane_index() == 0

    def blank(row, carry):
        column_ref[row] = jnp.zeros(column_ref.shape[1:], F32)
        return carry

    lax.fori_loop(0, first_row, blank, 0)
    lax.fori_loop(first_row + ay, 2 * shots, blank, 0)

    def place(y, carry):
        here = qh[y, pl.ds(6, gx), :]
        total = here + jnp.where(first_lane, qb[y, pl.ds(6, gx), :], pltpu.roll(here, 1, 1))
        total = total + qy[y, pl.ds(6, gx), :] + qy[y + 1, pl.ds(6, gx), :]
        total = total + qx[y, pl.ds(9, gx), :] + qx[y, pl.ds(10, gx), :]
        column_ref[first_row + y, pl.ds(0, gx), :] = grad_m[y, pl.ds(6, gx), :]
        column_ref[first_row + y, pl.ds(gx, gx), :] = (-0.5 * tap_square) * total
        return carry

    lax.fori_loop(0, ay, place, 0, unroll=2)


def adjoint_waves(at, fields, images, back, front, seen, modulus, weights, slopes):
    near = pltpu.VMEM((ay, 48, nz), F32)
    return pl.pallas_call(
        adjoint_kernel,
        out_shape=jax.ShapeDtypeStruct((2 * shots, 2 * gx, nz), F32),
        in_specs=[scalars] + whole(18),
        out_specs=whole(1)[0],
        scratch_shapes=[
            padded,
            pltpu.VMEM((ay, dom, nz), F32),
            pltpu.VMEM((ay, 64, nz), F32),
            near,
            *flux_shapes,
            near,
            pltpu.VMEM((ay + 1, 48, nz), F32),
            near,
            near,
            pltpu.VMEM((dom, nz), F32),
        ],
        compiler_params=vmem,
        name="adjoint_waves",
    )(at, *fields, images, back, front, seen, slope_matrix, spread_matrix, modulus, *weights, *slopes)


def chain_kernel(at_ref, got_ref, out_ref, grad_ref):
    brick = at_ref[1]
    row = lax.broadcasted_iota(jnp.int32, (gx, nz), 0)
    fine = ((row >= 2) | (brick > 0)) & ((row < gx - 2) | (brick < bricks - 1))
    for y in range(2):
        total = got_ref[0, y]
        for shot in range(1, shots):
            total = total + got_ref[shot, y]
        squashed = jax.nn.sigmoid(out_ref[0, y])
        bent = jnp.tanh(out_ref[1, y])
        buoyancy = jnp.exp(0.35 * bent)
        first = total[:gx] * 0.09 * squashed * (1.0 - squashed)
        second = total[gx:] * buoyancy * 0.35 * (1.0 - bent * bent)
        grad_ref[y, 0] = jnp.where(fine, first, 0.0).astype(BF16)
        grad_ref[y, 1] = jnp.where(fine, second, 0.0).astype(BF16)


def chain(at, got, output):
    return pl.pallas_call(
        chain_kernel,
        out_shape=jax.ShapeDtypeStruct((2, 2, gx, nz), BF16),
        in_specs=[scalars] + whole(2),
        out_specs=whole(1)[0],
        compiler_params=vmem,
        name="chain",
    )(at, got, output)


def spread_kernel(at_ref, lo_ref, mid_ref, hi_ref, hid_ref, s1, s2):
    shot, brick = at_ref[0], at_ref[1]
    y_fine = (shot > 0, True, shot < shots - 1)

    def spread(x, carry):
        x_fine = ((x >= 1) | (brick > 0)) & ((x < bx + 1) | (brick < bricks - 1))
        for y, (ref, row, part) in enumerate(((lo_ref, 1, 0), (mid_ref, 0, 1), (mid_ref, 1, 1), (hi_ref, 0, 2))):
            value = jnp.where(x_fine & y_fine[part], ref[row, x + 3].astype(F32), 0.0)
            hidden = hid_ref[x + 2, pl.ds(y * 16, 16), :].astype(F32)
            for k in range(3):
                s1[x, pl.ds(y * 48 + k * 16, 16), :] = lane_shift(value, k).astype(BF16)
                s2[x, pl.ds(y * 48 + k * 16, 16), :] = lane_shift(hidden, k).astype(BF16)
        return carry

    lax.fori_loop(0, bx + 2, spread, 0, unroll=2)


def spread_fields(at, lo, mid, hi, hidden):
    shape = jax.ShapeDtypeStruct((bx + 2, 192, nz), BF16)
    return pl.pallas_call(
        spread_kernel,
        out_shape=(shape, shape),
        in_specs=[scalars] + whole(4),
        out_specs=tuple(whole(2)),
        compiler_params=vmem,
        cost_estimate=cost(3),
        name="spread_fields",
    )(at, lo, mid, hi, hidden)


contract_lanes = (((1,), (1,)), ((), ()))


def second_grads_kernel(gmid_ref, s2, second_ref, own):
    own[...] = jnp.zeros(own.shape, F32)
    for row in range(2):
        for channel in range(2):
            own[:, channel * 2 + row, :] = gmid_ref[row, channel].astype(F32)[2 : bx + 2]

    def kernel_grad(x, second):
        return second + lax.dot_general(
            own[x].astype(BF16), s2[pl.ds(x, 3)].reshape(576, nz), contract_lanes, preferred_element_type=F32
        )

    second_ref[...] = lax.fori_loop(0, bx, kernel_grad, jnp.zeros((8, 576), F32), unroll=8)


def second_grads(grad_output, s2):
    return pl.pallas_call(
        second_grads_kernel,
        out_shape=jax.ShapeDtypeStruct((8, 576), F32),
        in_specs=whole(2),
        out_specs=whole(1)[0],
        scratch_shapes=[pltpu.VMEM((bx, 8, nz), F32)],
        compiler_params=vmem,
        cost_estimate=cost(3),
        name="second_grads",
    )(grad_output, s2)


def first_grads_kernel(
    at_ref, glo_ref, gmid_ref, ghi_ref, hid_ref, second_ref, w3_ref, s1_any, inner_ref, kernel_ref, turned, s1, ready
):
    fetch = pltpu.make_async_copy(s1_any, s1, ready)
    fetch.start()
    shot, brick = at_ref[0], at_ref[1]
    y_fine = (shot > 0, True, shot < shots - 1)
    for part, ref in enumerate((glo_ref, gmid_ref, ghi_ref)):
        for row in range(2):
            for channel in range(2):
                value = jnp.where(y_fine[part], ref[row, channel].astype(F32), 0.0)
                value = jnp.concatenate([value, jnp.zeros((12, nz), F32)], axis=0)
                plane = (2 * part + row) * 2 + channel
                for k in range(3):
                    turned[plane * 3 + k] = lane_shift(value, k)

    def hidden_grad(block, carry):
        rows = turned[:, pl.ds(8 * block, 16), :].astype(BF16).reshape(576, nz)
        acc = jnp.dot(w3_ref[...], rows, preferred_element_type=F32)
        for xo in range(8):
            x = 8 * block + xo
            x_fine = ((x >= 1) | (brick > 0)) & ((x < bx + 1) | (brick < bricks - 1))
            hidden = hid_ref[jnp.minimum(x + 2, bx + 5)].astype(F32)
            value = acc[xo * 64 : xo * 64 + 64] * (1.0 - hidden * hidden)
            for y in range(4):
                fine = x_fine
                if y == 0:
                    fine = fine & (shot > 0)
                if y == 3:
                    fine = fine & (shot < shots - 1)
                inner_ref[x, pl.ds(y * 16, 16), :] = jnp.where(
                    fine, value[y * 16 : y * 16 + 16], 0.0
                ).astype(BF16)
        return carry

    lax.fori_loop(0, 5, hidden_grad, 0, unroll=5)
    fetch.wait()

    def kernel_grad(x, first):
        return first + lax.dot_general(
            inner_ref[x + 1, pl.ds(16, 32), :],
            s1[pl.ds(x, 3)].reshape(576, nz),
            contract_lanes,
            preferred_element_type=F32,
        )

    first = lax.fori_loop(0, bx, kernel_grad, jnp.zeros((32, 576), F32), unroll=8)
    second = second_ref[...]
    kernel_ref[...] = jnp.zeros(kernel_ref.shape, F32)
    for dx in range(3):
        start = dx * 192
        one = first[:16, start : start + 144] + first[16:, start + 48 : start + 192]
        for channel in range(2):
            row = channel * 2
            two = (
                second[row : row + 1, start : start + 144]
                + second[row + 1 : row + 2, start + 48 : start + 192]
            )
            place = dx * 2 * 18 + 16 + channel
            kernel_ref[pl.ds(place, 1), :] = two[:, :128]
            kernel_ref[pl.ds(place + 18, 1), pl.ds(0, 16)] = two[:, 128:]
        kernel_ref[pl.ds(dx * 36, 16), :] = one[:, :128]
        kernel_ref[pl.ds(dx * 36 + 18, 16), pl.ds(0, 16)] = one[:, 128:]


def first_grads(at, glo, gmid, ghi, hidden, second, w3, s1):
    return pl.pallas_call(
        first_grads_kernel,
        out_shape=(
            jax.ShapeDtypeStruct((40, 64, nz), BF16),
            jax.ShapeDtypeStruct((128, nz), F32),
        ),
        in_specs=[scalars] + whole(6) + [pl.BlockSpec(memory_space=pl.ANY)],
        out_specs=tuple(whole(2)),
        scratch_shapes=[
            pltpu.VMEM((36, 48, nz), F32),
            pltpu.VMEM((bx + 2, 192, nz), BF16),
            pltpu.SemaphoreType.DMA,
        ],
        compiler_params=vmem,
        name="first_grads",
    )(at, glo, gmid, ghi, hidden, second, w3, s1)


def latent_grad_kernel(inner_ref, w4_ref, latent_ref, s4):
    def spread(x, carry):
        for y in range(4):
            value = inner_ref[x, pl.ds(y * 16, 16), :].astype(F32)
            for k in range(3):
                s4[x, pl.ds(y * 48 + k * 16, 16), :] = lane_shift(value, k).astype(BF16)
        return carry

    lax.fori_loop(0, bx + 2, spread, 0, unroll=2)

    def latent_grad(block, carry):
        rows = s4[pl.ds(4 * block, 6)].reshape(6 * 192, nz)
        acc = jnp.dot(w4_ref[...], rows, preferred_element_type=F32)
        latent_ref[pl.ds(4 * block, 4)] = acc.reshape(4, 32, nz)
        return carry

    lax.fori_loop(0, bx // 4, latent_grad, 0)


def latent_grads(inner, w4):
    return pl.pallas_call(
        latent_grad_kernel,
        out_shape=jax.ShapeDtypeStruct((bx, 32, nz), F32),
        in_specs=whole(2),
        out_specs=whole(1)[0],
        scratch_shapes=[pltpu.VMEM((bx + 2, 192, nz), BF16)],
        compiler_params=vmem,
        cost_estimate=cost(4),
        name="latent_grads",
    )(inner, w4)


def column_codes(x_in, y_in, order):
    if order == "xykc":
        x, y, k, c = np.meshgrid(*map(np.arange, (x_in, y_in, 3, 16)), indexing="ij")
    else:
        y, c, k, x = np.meshgrid(*map(np.arange, (y_in, 2, 3, x_in)), indexing="ij")
    return np.stack([(8 * x + y).ravel(), (16 * k + c).ravel()]).astype(np.int32)


codes_1 = column_codes(4, 6, "xykc")
codes_2 = column_codes(8, 4, "xykc")
codes_3 = column_codes(16, 6, "yckx")
codes_4 = column_codes(6, 4, "xykc")


def expand(taps_ref, codes_ref, spare, flip):
    place = codes_ref[1:2]
    size = place.shape[1]
    rows = lax.broadcasted_iota(jnp.int32, (16, size), 0)
    picks = [jnp.where(place == rows + 16 * k, 1.0, 0.0).astype(BF16) for k in range(3)]
    for pair in range(9):
        total = None
        for k in range(3):
            q = 3 * pair + k
            term = jnp.dot(taps_ref[26 - q if flip else q], picks[k], preferred_element_type=F32)
            total = term if total is None else total + term
        spare[pair, :, pl.ds(0, size)] = total


def fill_blocks(out_ref, codes_ref, spare, x_out, y_out):
    code = codes_ref[0:1]
    size = code.shape[1]
    same = lax.broadcasted_iota(jnp.int32, (16, size), 0) * 0 + code
    for xo in range(x_out):
        for y in range(y_out):
            block = jnp.zeros((16, size), F32)
            for pair in range(9):
                wanted = (xo + pair // 3) * 8 + y + pair % 3
                block = jnp.where(same == wanted, spare[pair, :, pl.ds(0, size)], block)
            out_ref[pl.ds((xo * y_out + y) * 16, 16), :] = block.astype(BF16)


def forward_bands_kernel(in_ref, out_taps_ref, codes_1_ref, codes_2_ref, w1_ref, w2_ref, spare, rows):
    expand(in_ref, codes_1_ref, spare, False)
    fill_blocks(w1_ref, codes_1_ref, spare, 2, 4)
    expand(out_taps_ref, codes_2_ref, spare, False)
    size = codes_2_ref.shape[1]
    code = codes_2_ref[0:1] - 8 * lax.broadcasted_iota(jnp.int32, (6, size), 0)
    for channel in range(2):
        for y in range(2):
            block = jnp.zeros((6, size), F32)
            for pair in range(9):
                wanted = (pair // 3) * 8 + y + pair % 3
                block = jnp.where(code == wanted, spare[pair, channel : channel + 1, :], block)
            rows[pl.ds((channel * 2 + y) * 6, 6), :] = block
    w2_ref[...] = rows[...].astype(BF16)


def backward_bands_kernel(in_ref, out_taps_ref, codes_3_ref, codes_4_ref, w3_ref, w4_ref, spare):
    expand(out_taps_ref, codes_3_ref, spare, True)
    fill_blocks(w3_ref, codes_3_ref, spare, 8, 4)
    expand(in_ref, codes_4_ref, spare, True)
    fill_blocks(w4_ref, codes_4_ref, spare, 4, 2)


def forward_bands(taps_in, taps_out):
    return pl.pallas_call(
        forward_bands_kernel,
        out_shape=(
            jax.ShapeDtypeStruct((128, 1152), BF16),
            jax.ShapeDtypeStruct((24, 1536), BF16),
        ),
        in_specs=whole(4),
        out_specs=tuple(whole(2)),
        scratch_shapes=[pltpu.VMEM((9, 16, 1536), F32), pltpu.VMEM((24, 1536), F32)],
        compiler_params=vmem,
        cost_estimate=cost(3),
        name="forward_bands",
    )(taps_in, taps_out, codes_1, codes_2)


def backward_bands(taps_in, taps_out):
    return pl.pallas_call(
        backward_bands_kernel,
        out_shape=(
            jax.ShapeDtypeStruct((512, 576), BF16),
            jax.ShapeDtypeStruct((128, 1152), BF16),
        ),
        in_specs=whole(4),
        out_specs=tuple(whole(2)),
        scratch_shapes=[pltpu.VMEM((9, 16, 1152), F32)],
        compiler_params=vmem,
        cost_estimate=cost(4),
        name="backward_bands",
    )(taps_in, taps_out, codes_3, codes_4)


def both_ways(ahead, behind, axis):
    count = lax.axis_size(axis)
    forward = [(i, (i + 1) % count) for i in range(count)]
    backward_ = [(target, source) for source, target in forward]
    return lax.ppermute(ahead, axis, forward), lax.ppermute(behind, axis, backward_)


def per_device(latent, conv_in, conv_out, source_field, observed, aperture, receivers):
    shot = lax.axis_index("shot")
    brick = lax.axis_index("brick")
    at = jnp.stack([shot, brick, aperture[0]]).astype(jnp.int32)
    taps_out = jnp.pad(conv_out, ((0, 0), (0, 14), (0, 0)))
    w1, w2 = forward_bands(conv_in, taps_out)
    w3, w4 = backward_bands(conv_in.transpose(0, 2, 1), taps_out.transpose(0, 2, 1))

    tile = jnp.transpose(latent, (2, 1, 0, 3))
    from_low, from_high = both_ways(tile[:, bx - 4 :], tile[:, :4], "brick")
    mid = jnp.concatenate([from_low, tile, from_high], axis=1)
    lo, hi = both_ways(mid, mid, "shot")
    source = jnp.transpose(source_field[0], (1, 0, 2))
    plo, phi = both_ways(source[:, bx - rim :], source[:, :rim], "brick")
    seen = receiver_fields(at, receivers[0], observed[0])

    coefficients, output, hidden = generator(at, lo, mid, hi, w1, w2)
    coefficients, plo, phi = lax.optimization_barrier((coefficients, plo, phi))
    sent = jnp.broadcast_to(coefficients[None], (shots, 2, 2, bx, nz))
    column = lax.all_to_all(sent, "shot", 0, 0, tiled=True)
    column, seen, w3, w4 = lax.optimization_barrier((column, seen, w3, w4))
    window, ahead, behind = take_window(at, column.reshape(2 * shots, 2, bx, nz))
    clo, chi = both_ways(ahead, behind, "brick")
    s1, s2 = spread_fields(at, lo, mid, hi, hidden)
    first_slopes = source_slopes(at, source, plo, phi)
    clo, chi, s1, s2, first_slopes = lax.optimization_barrier((clo, chi, s1, s2, first_slopes))
    p2, p3, p4, images, ahead, behind, modulus, *weights = forward_waves(
        at, window, clo, chi, first_slopes
    )
    back, front = both_ways(ahead, behind, "brick")
    slopes = wave_slopes(first_slopes[0], p2, p3)
    back, front, slopes = lax.optimization_barrier((back, front, slopes))
    grads = adjoint_waves(at, (p2, p3, p4), images, back, front, seen, modulus, weights, slopes)
    got = lax.all_to_all(grads, "shot", 0, 0, tiled=True)
    got = got.reshape(shots, 2, 2 * gx, nz)
    grad_output = chain(at, got, output)
    glo, ghi = both_ways(grad_output, grad_output, "shot")
    second = second_grads(grad_output, s2)
    inner, kernels = first_grads(at, glo, grad_output, ghi, hidden, second, w3, s1)
    grad_latent = latent_grads(inner, w4)
    grad_latent = jnp.transpose(grad_latent.reshape(bx, 2, 16, nz), (2, 0, 1, 3))

    everyone = ("shot", "brick")
    slices = lax.all_to_all(kernels, everyone, 0, 0, tiled=True)
    mine = jnp.sum(slices, axis=0, keepdims=True)
    summed = lax.all_to_all(jnp.broadcast_to(mine, (128, nz)), everyone, 0, 0, tiled=True)
    folded = summed[:108].reshape(3, 2, 18, nz).transpose(0, 2, 1, 3).reshape(3, 18, 256)[:, :, :144]
    folded = folded.reshape(3, 18, 9, 16).transpose(0, 2, 1, 3).reshape(27, 18, 16)
    return (grad_latent, folded[:, :16], folded[:, 16:])


def solution(mesh):
    placed = (
        P(None, "brick", "shot", None),
        P(),
        P(),
        P("shot", "brick", None, None),
        P("shot", None, None),
        P("shot"),
        P("shot", None, None),
    )
    return jax.shard_map(
        per_device,
        mesh=mesh,
        in_specs=placed,
        out_specs=(P(None, "brick", "shot", None), P(), P()),
        check_vma=False,
    )
```
